32 devices in a mesh: rep: 8 (over y, x, core), shard: 4 (over z).
Axes of the slice: x: 2, y: 2, z: 4, core: 2. Of those that a mesh axis runs over, the one named last changes fastest.
Arguments:
- tokens: bfloat16 [16, 1024, 768], P('rep', 'shard'), may hold values from -6 to 6
- gain_attn: bfloat16 [768], P('shard'), may hold values from 0.25 to 1.75
- bias_attn: bfloat16 [768], P('shard'), may hold values from -1.5 to 1.5
- w_qkv: bfloat16 [768, 2304], P('shard'), may hold values from -0.21875 to 0.21875
- w_feature: bfloat16 [768, 128], P('shard'), may hold values from -1.5 to 1.5
- w_out: bfloat16 [768, 768], P('shard'), may hold values from -0.875 to 0.875
- gain_mlp: bfloat16 [768], P('shard'), may hold values from 0.25 to 1.75
- bias_mlp: bfloat16 [768], P('shard'), may hold values from -1.5 to 1.5
- w_up: bfloat16 [768, 3072], P('shard'), may hold values from -0.21875 to 0.21875
- w_down: bfloat16 [3072, 768], P('shard'), may hold values from -0.109375 to 0.109375
- cotangent: bfloat16 [16, 1024, 768], P('rep', 'shard'), may hold values from -6 to 6
Outputs:
- block_out: bfloat16 [16, 1024, 768], P('rep', 'shard')
- grad_tokens: bfloat16 [16, 1024, 768], P('rep', 'shard')
- grad_gain_attn: float32 [768], P('shard')
- grad_bias_attn: float32 [768], P('shard')
- grad_w_qkv: float32 [768, 2304], P('shard')
- grad_w_feature: float32 [768, 128], P('shard')
- grad_w_out: float32 [768, 768], P('shard')
- grad_gain_mlp: float32 [768], P('shard')
- grad_bias_mlp: float32 [768], P('shard')
- grad_w_up: float32 [768, 3072], P('shard')
- grad_w_down: float32 [3072, 768], P('shard')
The draws below stay inside these ranges and needn't reach their ends.
All inputs are finite; a program needn't handle non-finite values.
Results may differ from the reference program's by a relative error of at most 0.019.
Values may be sent and summed in bfloat16 or wider, within the bound.
No kernel may reach another device: no remote copies, remote signals or barrier semaphores. Data moves between devices by JAX's collectives and lax.ppermute only.
A program may use at most 192 MiB of HBM per device.

```python
import jax
import jax.numpy as jnp
from jax import lax

D = 768
HEADS = 12
HEAD = 64
FF = 3072
FEAT = 128
STRETCH = 64
LENGTH = 1024
SEQS = 16


def block_scale(key, dims, pieces, low, largest):
    def one(axis_at, blocks):
        steps = jax.random.uniform(jax.random.fold_in(jax.random.fold_in(key, 6), axis_at), (blocks,), jnp.float32, low / len(pieces), largest / len(pieces))
        return jnp.repeat(jnp.exp(steps), dims[axis_at] // blocks).reshape((-1,) + (1,) * (len(dims) - axis_at - 1))

    loudness = one(*pieces[0])
    for cut in pieces[1:]:
        loudness = loudness * one(*cut)
    return loudness


def noise(rng, dims, scale, bound, shards=(), dtype=jnp.bfloat16):
    array = scale * jax.random.normal(rng, dims, jnp.float32)
    if shards:
        array = array * block_scale(rng, dims, shards, -0.22, 0.18)
    return jnp.clip(array, -bound, bound).astype(dtype)


def setup_inputs(seed: int = 0) -> dict:
    streams_of = jax.random.split(jax.random.key(seed), 12)
    tokens = noise(streams_of[0], (SEQS, LENGTH, D), 1.0, 6.0, ((0, 8), (1, 4)))
    gain_attn = jnp.clip(1.0 + 0.15 * jax.random.normal(streams_of[1], (D,), jnp.float32), 0.25, 1.75).astype(jnp.bfloat16)
    bias_attn = noise(streams_of[2], (D,), 0.3, 1.5, ((0, 4),))
    w_qkv = noise(streams_of[3], (D, 3 * D), D ** -0.5, 0.21875, ((0, 4),))
    w_feature = noise(streams_of[4], (D, FEAT), (HEAD // 4) ** -0.5, 1.5, ((0, 4),))
    w_out = noise(streams_of[5], (D, D), (D // 16) ** -0.5, 0.875, ((0, 4),))
    gain_mlp = jnp.clip(1.0 + 0.15 * jax.random.normal(streams_of[6], (D,), jnp.float32), 0.25, 1.75).astype(jnp.bfloat16)
    bias_mlp = noise(streams_of[7], (D,), 0.3, 1.5, ((0, 4),))
    w_up = noise(streams_of[8], (D, FF), D ** -0.5, 0.21875, ((0, 4),))
    w_down = noise(streams_of[9], (FF, D), FF ** -0.5, 0.109375, ((0, 4),))
    cotangent = noise(streams_of[10], (SEQS, LENGTH, D), 1.0, 6.0, ((0, 8), (1, 4)))
    return {"tokens": tokens, "gain_attn": gain_attn, "bias_attn": bias_attn, "w_qkv": w_qkv, "w_feature": w_feature, "w_out": w_out, "gain_mlp": gain_mlp, "bias_mlp": bias_mlp, "w_up": w_up, "w_down": w_down, "cotangent": cotangent}


top_precision = lax.Precision.HIGHEST
norm_epsilon = 1e-05

@jax.custom_vjp
def low(v):
    return lax.optimization_barrier(v.astype(jnp.bfloat16)).astype(jnp.float32)

@jax.custom_vjp
def low_back(v):
    return v

def low_keep(v):
    return (low(v), None)

def low_pass(kept, grad):
    return (grad,)

def back_keep(v):
    return (v, None)

def back_low(kept, grad):
    return (low(grad),)
low.defvjp(low_keep, low_pass)
low_back.defvjp(back_keep, back_low)

def layer_norm(rows_in, gain, offset):
    centred = rows_in - lax.optimization_barrier(jnp.mean(rows_in, axis=-1, keepdims=True))
    spread = lax.optimization_barrier(jnp.mean(centred * centred, axis=-1, keepdims=True))
    return centred * lax.rsqrt(spread + norm_epsilon) * gain + offset

def featurize(inputs):
    return jnp.concatenate([jax.nn.softmax(inputs, axis=-1), jax.nn.softmax(-inputs, axis=-1)], axis=-1)

def block_attend(carry, block):
    kv_state, key_total = carry
    queries, key_rows, values = block
    positions = jnp.arange(queries.shape[0])
    causal = positions[:, None] >= positions[None, :]
    scores = jnp.where(causal[None], jnp.einsum('thf,shf->hts', queries, key_rows, precision=top_precision), 0.0)
    numerator = jnp.einsum('hts,she->the', scores, values, precision=top_precision) + jnp.einsum('thf,hfe->the', queries, kv_state, precision=top_precision)
    denominator = jnp.transpose(lax.optimization_barrier(jnp.sum(scores, axis=2))) + jnp.einsum('thf,hf->th', queries, key_total, precision=top_precision)
    kv_state = kv_state + jnp.einsum('shf,she->hfe', key_rows, values, precision=top_precision)
    key_total = key_total + lax.optimization_barrier(jnp.sum(key_rows, axis=0))
    return ((kv_state, key_total), numerator / denominator[:, :, None])

def forward(tokens, weights):
    gain_attn, bias_attn, w_qkv, w_feature, w_out, gain_mlp, bias_mlp, w_up, w_down = weights
    length = tokens.shape[0]
    normed = low(layer_norm(tokens, gain_attn, bias_attn))
    mixed = low(low_back(jnp.dot(normed, w_qkv, precision=top_precision)))
    queries = mixed[:, :D].reshape(length, HEADS, HEAD)
    key_rows = mixed[:, D:2 * D].reshape(length, HEADS, HEAD)
    values = mixed[:, 2 * D:].reshape(length, HEADS, HEAD)
    feature_maps = w_feature.reshape(HEADS, HEAD, 2, HEAD)
    u_query = low_back(jnp.einsum('thi,hio->tho', queries, feature_maps[:, :, 0], precision=top_precision))
    u_key = low_back(jnp.einsum('thi,hio->tho', key_rows, feature_maps[:, :, 1], precision=top_precision))
    f_query = low(featurize(u_query))
    f_key = low(featurize(u_key))
    blocks = length // STRETCH
    initial = (jnp.zeros((HEADS, FEAT, HEAD), jnp.float32), jnp.zeros((HEADS, FEAT), jnp.float32))
    carried, attended = lax.scan(jax.checkpoint(block_attend), initial, (f_query.reshape(blocks, STRETCH, HEADS, FEAT), f_key.reshape(blocks, STRETCH, HEADS, FEAT), values.reshape(blocks, STRETCH, HEADS, HEAD)))
    attended = low(attended.reshape(length, D))
    resid = tokens + low_back(jnp.dot(attended, w_out, precision=top_precision))
    normed_two = low(layer_norm(resid, gain_mlp, bias_mlp))
    hidden = low(jax.nn.gelu(low_back(jnp.dot(normed_two, w_up, precision=top_precision)), approximate=True))
    return resid + jnp.dot(hidden, w_down, precision=top_precision)

def reference(tokens, gain_attn, bias_attn, w_qkv, w_feature, w_out, gain_mlp, bias_mlp, w_up, w_down, cotangent):
    weights = (gain_attn.astype(jnp.float32), bias_attn.astype(jnp.float32), w_qkv.astype(jnp.float32), w_feature.astype(jnp.float32), w_out.astype(jnp.float32), gain_mlp.astype(jnp.float32), bias_mlp.astype(jnp.float32), w_up.astype(jnp.float32), w_down.astype(jnp.float32))

    def one_sequence(totals, paired):
        sequence, grad_out = paired
        result, pullback = jax.vjp(forward, sequence.astype(jnp.float32), weights)
        grad_input, grad_weights = pullback(grad_out.astype(jnp.float32))
        totals = tuple((total_sum + new_term for total_sum, new_term in zip(totals, grad_weights)))
        return (totals, (result.astype(jnp.bfloat16), grad_input.astype(jnp.bfloat16)))
    zero_sums = tuple((jnp.zeros_like(weight) for weight in weights))
    totals, (outputs, input_grads) = lax.scan(one_sequence, zero_sums, (tokens, cotangent))
    return (outputs, input_grads, totals[0], totals[1], totals[2], totals[3], totals[4], totals[5], totals[6], totals[7], totals[8])
```

```python
import jax
import jax.numpy as jnp
from jax import lax
from jax.sharding import PartitionSpec as P

D = 768
HEADS = 12
HEAD = 64
FEAT = 128
STRETCH = 64


top_precision = lax.Precision.DEFAULT
norm_epsilon = 1e-05


def prefix(value, axis, combine, identity):
    count, here = (lax.axis_size(axis), lax.axis_index(axis))
    everything = jax.tree.map(
        lambda part, kind: lax.all_gather(part.astype(kind), axis),
        value,
        (jnp.bfloat16, jnp.bfloat16),
    )
    start = jax.tree.map(
        lambda part, zero: jnp.broadcast_to(jnp.asarray(zero, part.dtype), part.shape),
        value,
        identity,
    )

    def lap(k, before):
        reached = k < here
        new = combine(
            before, jax.tree.map(lambda part, own: part[k].astype(own.dtype), everything, value)
        )
        return jax.tree.map(lambda a, b: jnp.where(reached, a, b), new, before)

    return lax.fori_loop(0, count, lap, start)


def prefix_2(value, axis, join, neutral):
    count = lax.axis_size(axis)
    place = lax.axis_index(axis)
    ahead = count - 1 - place
    gathered = jax.tree.map(
        lambda a, kind: lax.all_gather(a.astype(kind), axis),
        value,
        jax.tree.map(lambda a: jnp.bfloat16 if a.dtype == jnp.float32 else a.dtype, value),
    )
    state = jax.tree.map(lambda a, e: jnp.zeros_like(a) + jnp.asarray(e, a.dtype), value, neutral)

    def one(lap, state):
        source = count - 1 - lap
        return join(
            state,
            jax.tree.map(
                lambda a, own: lax.dynamic_index_in_dim(a, source, 0, False).astype(own.dtype),
                gathered,
                value,
            ),
        )

    return lax.fori_loop(0, ahead, one, state)


PIECES = 8


def flip(value, bit):
    count = lax.axis_size("rep")
    return lax.ppermute(value, "rep", [(i, i ^ bit) for i in range(count)])


def spin(value, step):
    count = lax.axis_size("shard")
    return lax.ppermute(value, "shard", [(i, (i + step) % count) for i in range(count)])


def spread(own):
    half = own.shape[0] // 2
    from_x = flip(own, 2)
    from_y = flip(own, 4)
    diagonal = jnp.concatenate([flip(from_x[:half], 4), flip(from_y[half:], 2)], axis=0)
    even = (own, from_x, from_y, diagonal)
    pieces = []
    for part in even:
        pieces += [part, flip(part, 1)]
    return pieces


def gather_pieces(part):
    count, here = lax.axis_size("shard"), lax.axis_index("shard")
    full = jnp.zeros((count,) + part.shape, part.dtype)
    full = lax.dynamic_update_index_in_dim(full, part, here, 0)
    for step in range(1, count):
        full = lax.dynamic_update_index_in_dim(full, spin(part, step), (here - step) % count, 0)
    return spread(full.reshape((count * part.shape[0],) + part.shape[1:]))


def sum_pieces(parts):
    wide = lambda a: a.astype(jnp.float32)
    low = lambda a: a.astype(jnp.bfloat16)
    odd = flip(jnp.stack([low(p) for p in parts[1::2]]), 1)
    mine, x_part, y_part, diagonal = (wide(p) + wide(odd[i]) for i, p in enumerate(parts[0::2]))
    half = diagonal.shape[0] // 2
    to_y, to_x = flip(low(diagonal[:half]), 4), flip(low(diagonal[half:]), 2)
    x_part = jnp.concatenate([x_part[:half] + wide(to_y), x_part[half:]], axis=0)
    y_part = jnp.concatenate([y_part[:half], y_part[half:] + wide(to_x)], axis=0)
    mine = mine + wide(flip(low(x_part), 2)) + wide(flip(low(y_part), 4))
    bit = PIECES
    while bit < lax.axis_size("rep"):
        mine = mine + wide(flip(low(mine), bit))
        bit *= 2
    count, here = lax.axis_size("shard"), lax.axis_index("shard")
    blocks = mine.reshape((count, mine.shape[0] // count) + mine.shape[1:])
    pick = lambda step: lax.dynamic_index_in_dim(blocks, (here + step) % count, 0, False)
    total = pick(0)
    for step in range(1, count):
        total = total + wide(spin(low(pick(step)), step))
    return spread(low(total))


def layer_norm(rows_in, gain, offset):
    centred = rows_in - jnp.mean(rows_in, axis=-1, keepdims=True)
    spread = jnp.mean(centred * centred, axis=-1, keepdims=True)
    return centred * lax.rsqrt(spread + norm_epsilon) * gain + offset


def featurize(inputs):
    return jnp.concatenate(
        [jax.nn.softmax(inputs, axis=-1), jax.nn.softmax(-inputs, axis=-1)], axis=-1
    )


def featurize_pair(u_query, u_key):
    return (featurize(u_query), featurize(u_key))


def gelu_tanh(pre_act):
    return jax.nn.gelu(pre_act, approximate=True)


def add_states(earlier, later):
    return jax.tree.map(jnp.add, earlier, later)


def shifted_sum(terms):
    running = jnp.cumsum(terms, axis=0)
    return jnp.concatenate([jnp.zeros_like(terms[:1]), running[:-1]], axis=0)


def attend_local(query_wide, key_wide, value_wide, prior_state, prior_total):
    length = query_wide.shape[0]
    blocks = length // STRETCH
    block_q = query_wide.reshape(blocks, STRETCH, HEADS, FEAT)
    block_k = key_wide.reshape(blocks, STRETCH, HEADS, FEAT)
    block_v = value_wide.reshape(blocks, STRETCH, HEADS, HEAD)
    state_terms = jnp.einsum("nshf,nshe->nhfe", block_k, block_v, precision=top_precision)
    total_terms = jnp.sum(block_k, axis=1)
    state_before = prior_state[None] + shifted_sum(state_terms)
    total_before = prior_total[None] + shifted_sum(total_terms)
    positions = jnp.arange(STRETCH)
    causal = positions[:, None] >= positions[None, :]
    scores = jnp.where(
        causal, jnp.einsum("nthf,nshf->nhts", block_q, block_k, precision=top_precision), 0.0
    )
    numerator = jnp.einsum("nhts,nshe->nthe", scores, block_v, precision=top_precision)
    numerator = numerator + jnp.einsum(
        "nthf,nhfe->nthe", block_q, state_before, precision=top_precision
    )
    denominator = jnp.transpose(jnp.sum(scores, axis=3), (0, 2, 1))
    denominator = denominator + jnp.einsum(
        "nthf,nhf->nth", block_q, total_before, precision=top_precision
    )
    return (numerator / denominator[..., None]).reshape(length, HEADS, HEAD)


def shards(
    tokens,
    gain_attn,
    bias_attn,
    w_qkv,
    w_feature,
    w_out,
    gain_mlp,
    bias_mlp,
    w_up,
    w_down,
    cotangent,
):
    shard_count = lax.axis_size("shard")
    place = lax.axis_index("rep") % PIECES
    rows = w_qkv.shape[0]
    chunk = w_up.shape[1] // PIECES
    fine = chunk // shard_count
    wide_in = jnp.concatenate([w_qkv, w_out], axis=1)
    part_in = lax.dynamic_slice_in_dim(wide_in, place * chunk, chunk, 1)
    in_pieces = gather_pieces(part_in)
    part_up = lax.dynamic_index_in_dim(
        w_up.reshape(rows, shard_count, PIECES, fine), place, 2, False
    ).reshape(rows, chunk)
    up_pieces = gather_pieces(part_up)
    down_rows = w_down.shape[0] // PIECES
    part_down = lax.dynamic_slice_in_dim(w_down, place * down_rows, down_rows, 0)
    down_pieces = gather_pieces(part_down)
    wide_weight = jnp.zeros((rows * shard_count, chunk * PIECES), jnp.bfloat16)
    for k, piece in enumerate(in_pieces):
        wide_weight = lax.dynamic_update_slice_in_dim(wide_weight, piece, (place ^ k) * chunk, 1)
    qkv_weight = wide_weight[:, : 3 * D]
    out_weight = wide_weight[:, 3 * D :]
    small = jnp.concatenate(
        [w_feature.reshape(-1), gain_attn, bias_attn, gain_mlp, bias_mlp]
    ).reshape(-1, rows)
    small = lax.all_gather(small, "shard", axis=0)
    feature_weight = small[:, :FEAT].reshape(D, FEAT)
    gain_one, bias_one, gain_two, bias_two = (small[:, FEAT + i].reshape(D) for i in range(4))
    totals = None
    results = []
    input_grads = []
    for batch_index in range(tokens.shape[0]):
        rows_in = tokens[batch_index].astype(jnp.float32)
        length = rows_in.shape[0]
        normed, norm_pull = jax.vjp(
            layer_norm, rows_in, gain_one.astype(jnp.float32), bias_one.astype(jnp.float32)
        )
        normed_low = normed.astype(jnp.bfloat16)
        mixed = jnp.dot(normed_low, qkv_weight, preferred_element_type=jnp.float32).astype(
            jnp.bfloat16
        )
        queries = mixed[:, :D].reshape(length, HEADS, HEAD)
        key_rows = mixed[:, D : 2 * D].reshape(length, HEADS, HEAD)
        values = mixed[:, 2 * D :].reshape(length, HEADS, HEAD)
        feature_maps = feature_weight.reshape(HEADS, HEAD, 2, HEAD)
        u_query = jnp.einsum(
            "thi,hio->tho", queries, feature_maps[:, :, 0], preferred_element_type=jnp.float32
        )
        u_key = jnp.einsum(
            "thi,hio->tho", key_rows, feature_maps[:, :, 1], preferred_element_type=jnp.float32
        )
        (f_query, f_key), feature_pull = jax.vjp(featurize_pair, u_query, u_key)
        query_low = f_query.astype(jnp.bfloat16)
        key_low = f_key.astype(jnp.bfloat16)
        query_wide = query_low.astype(jnp.float32)
        key_wide = key_low.astype(jnp.float32)
        value_wide = values.astype(jnp.float32)
        key_state = jnp.einsum("shf,she->hfe", key_low, values, preferred_element_type=jnp.float32)
        key_sum = jnp.sum(key_wide, axis=0)
        prior = prefix(
            (key_state, key_sum),
            "shard",
            add_states,
            (jnp.zeros_like(key_state), jnp.zeros_like(key_sum)),
        )
        attended, attend_pull = jax.vjp(
            attend_local, query_wide, key_wide, value_wide, prior[0], prior[1]
        )
        attended_low = attended.reshape(length, D).astype(jnp.bfloat16)
        resid = rows_in + jnp.dot(attended_low, out_weight, preferred_element_type=jnp.float32)
        normed_two, norm_two_pull = jax.vjp(
            layer_norm, resid, gain_two.astype(jnp.float32), bias_two.astype(jnp.float32)
        )
        normed_two_low = normed_two.astype(jnp.bfloat16)
        result = resid
        hidden_parts, gelu_pulls = [], []
        for up_piece, down_piece in zip(up_pieces, down_pieces):
            pre_act = jnp.dot(normed_two_low, up_piece, preferred_element_type=jnp.float32)
            hidden, gelu_pull = jax.vjp(gelu_tanh, pre_act)
            hidden_parts.append(hidden.astype(jnp.bfloat16))
            gelu_pulls.append(gelu_pull)
            result = result + jnp.dot(
                hidden_parts[-1], down_piece, preferred_element_type=jnp.float32
            )
        results.append(result.astype(jnp.bfloat16))
        grad_out = cotangent[batch_index]
        d_down, d_up = [], []
        d_normed_two = 0.0
        for hidden_low, gelu_pull, up_piece, down_piece in zip(
            hidden_parts, gelu_pulls, up_pieces, down_pieces
        ):
            d_down.append(jnp.dot(hidden_low.T, grad_out, preferred_element_type=jnp.float32))
            d_hidden = jnp.dot(grad_out, down_piece.T, preferred_element_type=jnp.float32)
            (d_pre,) = gelu_pull(d_hidden)
            d_pre_low = d_pre.astype(jnp.bfloat16)
            d_up.append(jnp.dot(normed_two_low.T, d_pre_low, preferred_element_type=jnp.float32))
            d_normed_two = d_normed_two + jnp.dot(
                d_pre_low, up_piece.T, preferred_element_type=jnp.float32
            )
        d_resid_two, d_gain_two, d_bias_two = norm_two_pull(d_normed_two)
        d_resid = grad_out.astype(jnp.float32) + d_resid_two
        d_resid_low = d_resid.astype(jnp.bfloat16)
        d_out = jnp.dot(attended_low.T, d_resid_low, preferred_element_type=jnp.float32)
        d_attended = jnp.dot(d_resid_low, out_weight.T, preferred_element_type=jnp.float32).reshape(
            length, HEADS, HEAD
        )
        d_query_f, d_key_f, d_value_f, local_state, local_sum = attend_pull(d_attended)
        later = prefix_2(
            (local_state, local_sum),
            "shard",
            add_states,
            (jnp.zeros_like(local_state), jnp.zeros_like(local_sum)),
        )
        d_key_f = (
            d_key_f
            + jnp.einsum("hfe,she->shf", later[0], value_wide, precision=top_precision)
            + later[1][None]
        )
        d_value_f = d_value_f + jnp.einsum(
            "hfe,shf->she", later[0], key_wide, precision=top_precision
        )
        d_u_query, d_u_key = feature_pull((d_query_f, d_key_f))
        d_uq_low = d_u_query.astype(jnp.bfloat16)
        d_uk_low = d_u_key.astype(jnp.bfloat16)
        back_maps = feature_weight.reshape(HEADS, HEAD, 2, HEAD)
        d_queries = jnp.einsum(
            "tho,hio->thi", d_uq_low, back_maps[:, :, 0], preferred_element_type=jnp.float32
        )
        d_keys = jnp.einsum(
            "tho,hio->thi", d_uk_low, back_maps[:, :, 1], preferred_element_type=jnp.float32
        )
        query_map_grad = jnp.einsum(
            "thi,tho->hio", queries, d_uq_low, preferred_element_type=jnp.float32
        )
        key_map_grad = jnp.einsum(
            "thi,tho->hio", key_rows, d_uk_low, preferred_element_type=jnp.float32
        )
        d_maps = jnp.stack([query_map_grad, key_map_grad], axis=2).reshape(D, FEAT)
        d_mixed = jnp.concatenate(
            [d_queries.reshape(length, D), d_keys.reshape(length, D), d_value_f.reshape(length, D)],
            axis=1,
        ).astype(jnp.bfloat16)
        d_qkv = jnp.dot(normed_low.T, d_mixed, preferred_element_type=jnp.float32)
        d_normed = jnp.dot(d_mixed, qkv_weight.T, preferred_element_type=jnp.float32)
        d_rows, d_gain_one, d_bias_one = norm_pull(d_normed)
        input_grads.append((d_resid + d_rows).astype(jnp.bfloat16))
        contributions = (
            jnp.concatenate([d_qkv, d_out], axis=1),
            d_up,
            d_down,
            (d_gain_one, d_bias_one, d_gain_two, d_bias_two, d_maps),
        )
        totals = (
            contributions
            if totals is None
            else jax.tree.map(jnp.add, totals, contributions)
        )
    grad_down = sum_pieces(totals[2])
    grad_up = sum_pieces(totals[1])
    grad_in = sum_pieces(
        [
            lax.dynamic_slice_in_dim(totals[0], (place ^ k) * chunk, chunk, 1)
            for k in range(PIECES)
        ]
    )
    ordered = []
    for parts in (grad_in, grad_up, grad_down):
        stack = jnp.zeros((PIECES,) + parts[0].shape, jnp.bfloat16)
        for k, part in enumerate(parts):
            stack = lax.dynamic_update_index_in_dim(stack, part, place ^ k, 0)
        ordered.append(stack.astype(jnp.float32))
    grad_wide = jnp.swapaxes(ordered[0], 0, 1).reshape(rows, -1)
    grad_up = (
        ordered[1]
        .reshape(PIECES, rows, shard_count, fine)
        .transpose(1, 2, 0, 3)
        .reshape(rows, -1)
    )
    grad_down = ordered[2].reshape(-1, D)
    tiny = jnp.concatenate([part.reshape(shard_count, -1) for part in totals[3]], axis=1)
    tiny = lax.psum_scatter(tiny.astype(jnp.bfloat16), "shard", scatter_dimension=0, tiled=True)
    tiny = lax.psum(tiny, "rep").astype(jnp.float32).reshape(-1)
    vectors = [tiny[i * rows : (i + 1) * rows] for i in range(4)]
    reduced = (
        vectors[0],
        vectors[1],
        grad_wide[:, : 3 * D],
        tiny[4 * rows :].reshape(rows, FEAT),
        grad_wide[:, 3 * D :],
        vectors[2],
        vectors[3],
        grad_up,
        grad_down,
    )
    return (
        jnp.stack(results),
        jnp.stack(input_grads),
        reduced[0],
        reduced[1],
        reduced[2],
        reduced[3],
        reduced[4],
        reduced[5],
        reduced[6],
        reduced[7],
        reduced[8],
    )


def solution(mesh):
    placed = (
        P("rep", "shard", None),
        P("shard"),
        P("shard"),
        P("shard", None),
        P("shard", None),
        P("shard", None),
        P("shard"),
        P("shard"),
        P("shard", None),
        P("shard", None),
        P("rep", "shard", None),
    )
    return jax.shard_map(
        shards,
        mesh=mesh,
        in_specs=placed,
        out_specs=(
            P("rep", "shard", None),
            P("rep", "shard", None),
            P("shard"),
            P("shard"),
            P("shard", None),
            P("shard", None),
            P("shard", None),
            P("shard"),
            P("shard"),
            P("shard", None),
            P("shard", None),
        ),
        check_vma=False,
    )
```

```python
import jax
import jax.numpy as jnp
from jax import lax
from jax.experimental import pallas as pl
from jax.experimental.pallas import tpu as pltpu
from jax.sharding import PartitionSpec as P

D = 768
HEADS = 12
HEAD = 64
FEAT = 128
PAIRS = HEADS // 2
GROUP = 4 * HEAD
PIECES = 8
CHUNK = 4 * D // PIECES
QKV_BLOCKS = 3 * D // CHUNK
SLAB = (PAIRS + 1) * FEAT

norm_epsilon = 1e-05
low_type = jnp.bfloat16
wide_type = jnp.float32


def flip(value, bit):
    count = lax.axis_size("rep")
    return lax.ppermute(value, "rep", [(i, i ^ bit) for i in range(count)])


def spin(value, step):
    count = lax.axis_size("shard")
    return lax.ppermute(value, "shard", [(i, (i + step) % count) for i in range(count)])


def slide(value, step):
    count = lax.axis_size("shard")
    pairs = [(i, i + step) for i in range(count) if 0 <= i + step < count]
    return lax.ppermute(value, "shard", pairs)


def wide(value):
    return value.astype(wide_type)


def low(value):
    return value.astype(low_type)


def spread(own):
    half = own.shape[0] // 2
    from_x = flip(own, 2)
    from_y = flip(own, 4)
    diagonal = jnp.concatenate([flip(from_x[:half], 4), flip(from_y[half:], 2)], axis=0)
    even = [own, from_x, from_y, diagonal]
    return even, [flip(part, 1) for part in even]


def around(part):
    count, here = lax.axis_size("shard"), lax.axis_index("shard")
    full = jnp.zeros((count,) + part.shape, part.dtype)
    full = lax.dynamic_update_index_in_dim(full, part, here, 0)
    for step in range(1, count):
        full = lax.dynamic_update_index_in_dim(full, spin(part, step), (here - step) % count, 0)
    return full


def gather_pieces(part):
    full = around(part)
    return spread(full.reshape((-1,) + part.shape[1:]))


def scatter_shards(total):
    count, here = lax.axis_size("shard"), lax.axis_index("shard")
    blocks = total.reshape((count, total.shape[0] // count) + total.shape[1:])
    pick = lambda step: lax.dynamic_index_in_dim(blocks, (here + step) % count, 0, False)
    result = pick(0)
    for step in range(1, count):
        result = result + wide(spin(low(pick(step)), step))
    return result


def sum_pieces(even, odd):
    other = flip(odd, 1)
    half = even.shape[1] // 2
    both = lambda i, rows: wide(even[i, rows]) + wide(other[i, rows])
    upper, lower, every = slice(None, half), slice(half, None), slice(None)
    to_y = flip(low(both(3, upper)), 4)
    to_x = flip(low(both(3, lower)), 2)
    x_part = jnp.concatenate([both(1, upper) + wide(to_y), both(1, lower)], axis=0)
    y_part = jnp.concatenate([both(2, upper), both(2, lower) + wide(to_x)], axis=0)
    mine = both(0, every) + wide(flip(low(x_part), 2)) + wide(flip(low(y_part), 4))
    bit = PIECES
    while bit < lax.axis_size("rep"):
        mine = mine + wide(flip(low(mine), bit))
        bit *= 2
    return spread(low(scatter_shards(mine)))


def dot(a, b):
    return jnp.dot(a, b, preferred_element_type=wide_type)


def dot_nt(a, b):
    return lax.dot_general(a, b, (((1,), (1,)), ((), ())), preferred_element_type=wide_type)


def dot_tn(a, b):
    return lax.dot_general(a, b, (((0,), (0,)), ((), ())), preferred_element_type=wide_type)


def normalize(rows):
    centred = rows - jnp.mean(rows, axis=-1, keepdims=True)
    scale = lax.rsqrt(jnp.mean(centred * centred, axis=-1, keepdims=True) + norm_epsilon)
    return centred * scale, scale


def norm_backward(grad, normal, scale, gain):
    e = grad * gain
    return scale * (
        e
        - jnp.mean(e, axis=-1, keepdims=True)
        - normal * jnp.mean(e * normal, axis=-1, keepdims=True)
    )


def lane_index(shape):
    return lax.broadcasted_iota(jnp.int32, shape, len(shape) - 1)


def row_index(shape):
    return lax.broadcasted_iota(jnp.int32, shape, len(shape) - 2)


def left_half(shape):
    return lane_index(shape) < HEAD


def aligned(index, unit):
    return pl.multiple_of(index * unit, unit)


def with_ones(pair):
    left = left_half(pair.shape)
    one = jnp.ones_like(pair)
    return jnp.where(left, pair, one), jnp.where(left, one, pair)


def pack_state(even, odd, p):
    lane = lane_index(even.shape)
    packed = jnp.where(lane < HEAD, even, odd)
    sums = jnp.where(lane == HEAD + 2 * p, even, jnp.where(lane == 2 * p + 1, odd, 0.0))
    return packed, sums


def unpack_state(packed, sums, p):
    shape = packed.shape
    lane, row = lane_index(shape), row_index(shape)
    pick_even = low(jnp.where((row == HEAD + 2 * p) & (lane >= HEAD), 1.0, 0.0))
    pick_odd = low(jnp.where((row == 2 * p + 1) & (lane < HEAD), 1.0, 0.0))
    even = jnp.where(lane < HEAD, packed, dot(sums, pick_even))
    odd = jnp.where(lane < HEAD, dot(sums, pick_odd), packed)
    return low(even), low(odd)


def added(refs, b, rows):
    total = wide(refs[0][b, rows, :])
    for ref in refs[1:]:
        total = total + wide(ref[b, rows, :])
    return total


def states_at(refs, b, p):
    packed = added(refs, b, pl.ds(aligned(p, FEAT), FEAT))
    sums = low(added(refs, b, slice(PAIRS * FEAT, SLAB)))
    return unpack_state(packed, sums, p)


def qkv_kernel(place, tokens, vectors, maps, *refs):
    pieces = refs[:PIECES]
    normed, normed_t, mixed, w_out, fq, fk, fq_t, fk_t, state = refs[PIECES:]
    seqs = state.shape[0]
    length = tokens.shape[0] // seqs
    normal, _ = normalize(wide(tokens[...]))
    normed[...] = low(normal * vectors[0:1, :] + vectors[1:2, :])
    normed_t[...] = normed[...].T
    for k in range(PIECES):
        block = place[0] ^ k

        @pl.when(block < QKV_BLOCKS)
        def _():
            mixed[:, pl.ds(aligned(block, CHUNK), CHUNK)] = low(dot(normed[...], pieces[k][...]))

        @pl.when(block >= QKV_BLOCKS)
        def _():
            w_out[:, pl.ds(aligned(block - QKV_BLOCKS, CHUNK), CHUNK)] = pieces[k][...]

    for which, (f_t, f) in enumerate(((fq_t, fq), (fk_t, fk))):

        def group(g, carry):
            columns = mixed[:, pl.ds(aligned(which * (D // GROUP) + g, GROUP), GROUP)]
            u_t = dot_nt(maps[which * (D // GROUP) + g], columns)
            for a in range(4):
                u = u_t[a * HEAD : (a + 1) * HEAD]
                up = jnp.exp(u - jnp.max(u, axis=0, keepdims=True))
                down = jnp.exp(jnp.min(u, axis=0, keepdims=True) - u)
                feature = jnp.concatenate(
                    [
                        up / jnp.sum(up, axis=0, keepdims=True),
                        down / jnp.sum(down, axis=0, keepdims=True),
                    ],
                    axis=0,
                )
                feature = low(feature)
                rows = pl.ds(aligned(g * 4 + a, FEAT), FEAT)
                f_t[rows, :] = feature
                f[:, rows] = feature.T
            return carry

        lax.fori_loop(0, D // GROUP, group, 0)

    def pair(p, sums):
        result = []
        for b in range(seqs):
            here = slice(b * length, (b + 1) * length)
            v_even, v_odd = with_ones(mixed[here, pl.ds(aligned(2 * D // FEAT + p, FEAT), FEAT)])
            even = dot(fk_t[pl.ds(aligned(2 * p, FEAT), FEAT), here], v_even)
            odd = dot(fk_t[pl.ds(aligned(2 * p + 1, FEAT), FEAT), here], v_odd)
            packed, new = pack_state(even, odd, p)
            state[b, pl.ds(aligned(p, FEAT), FEAT), :] = low(packed)
            result.append(sums[b] + new)
        return tuple(result)

    sums = lax.fori_loop(
        0, PAIRS, pair, tuple(jnp.zeros((FEAT, FEAT), wide_type) for _ in range(seqs))
    )
    for b in range(seqs):
        state[b, PAIRS * FEAT :, :] = low(sums[b])


def attend_kernel(tokens, vectors, mixed, fq, fk_t, w_out, *refs):
    priors, (attended, inverse, resid, second, second_t) = refs[:-5], refs[-5:]
    seqs = priors[0].shape[0]
    length = tokens.shape[0] // seqs

    def pair(p, carry):
        for b in range(seqs):
            here = slice(b * length, (b + 1) * length)
            values = with_ones(mixed[here, pl.ds(aligned(2 * D // FEAT + p, FEAT), FEAT)])
            states = states_at(priors, b, p)
            found = []
            for side in range(2):
                rows = pl.ds(aligned(2 * p + side, FEAT), FEAT)
                scores = dot(fq[here, rows], fk_t[rows, here])
                scores = jnp.where(row_index(scores.shape) >= lane_index(scores.shape), scores, 0.0)
                found.append(dot(low(scores), values[side]) + dot(fq[here, rows], states[side]))
            left = left_half(found[0].shape)
            turned = [pltpu.roll(a, HEAD, 1) for a in found]
            over = 1.0 / jnp.where(left, turned[0], turned[1])
            columns = pl.ds(aligned(p, FEAT), FEAT)
            attended[here, columns] = low(jnp.where(left, found[0], found[1]) * over)
            inverse[here, columns] = over
        return carry

    lax.fori_loop(0, PAIRS, pair, 0)
    resid[...] = wide(tokens[...]) + dot(attended[...], w_out[...])
    normal, _ = normalize(resid[...])
    second[...] = low(normal * vectors[2:3, :] + vectors[3:4, :])
    second_t[...] = second[...].T


def mlp_kernel(second, second_t, cotangent, out_before, back_before, *refs):
    pieces = refs[:4]
    out_after, back_after, grads, up, down, ready = refs[4:]
    step = pl.program_id(0)
    block = pieces[0].shape[0]

    parts = grads_layout(second.shape[1], block)

    def copies(k, source):
        listed = []
        for i, (src, dst) in enumerate(parts):
            if dst[0] == "up":
                target = up.at[k, pl.ds(dst[1], dst[2]), :]
            else:
                target = down.at[k, pl.ds(dst[1], dst[2]), pl.ds(dst[3], CHUNK)]
            listed.append(
                pltpu.make_async_copy(source.at[pl.ds(src, dst[2]), :], target, ready.at[k, i])
            )
        return listed

    @pl.when(step == 0)
    def _():
        for k in range(4):
            for copy in copies(k, pieces[k]):
                copy.start()
        out_after[...] = out_before[...]
        back_after[...] = back_before[...]

    for copy in copies(step, pieces[0]):
        copy.wait()

    up_weight, down_weight = up[step], down[step]
    pre = dot(second[...], up_weight)
    inner = 0.7978845608 * (pre + 0.044715 * pre * pre * pre)
    bent = jnp.tanh(inner)
    hidden = low(0.5 * pre * (1.0 + bent))
    slope = 0.5 * (1.0 + bent) + 0.5 * pre * (1.0 - bent * bent) * (
        0.7978845608 * (1.0 + 3.0 * 0.044715 * pre * pre)
    )
    out_after[...] += dot(hidden, down_weight)
    d_pre = low(dot_nt(cotangent[...], down_weight) * slope)
    back_after[...] += dot_nt(d_pre, up_weight)
    d_up = low(dot(second_t[...], d_pre))
    d_down = low(dot_tn(hidden, cotangent[...]))
    for src, dst in parts:
        if dst[0] == "up":
            grads[0, src : src + dst[2], :] = d_up[dst[1] : dst[1] + dst[2]]
        else:
            grads[0, src : src + dst[2], :] = d_down[dst[1] : dst[1] + dst[2], dst[3] : dst[3] + CHUNK]


def grads_layout(width, block):
    shards = block // CHUNK
    up_rows = width // shards
    down_rows = CHUNK // shards
    parts = []
    for s in range(shards):
        base = s * (up_rows + 2 * down_rows)
        parts.append((base, ("up", s * up_rows, up_rows)))
        for side in range(2):
            parts.append(
                (
                    base + up_rows + side * down_rows,
                    ("down", s * down_rows, down_rows, side * CHUNK),
                )
            )
    return parts


def resid_kernel(out_sum, back_sum, resid, cotangent, vectors, w_out, attended, inverse, fq_t, *refs):
    block_out, d_resid, d_resid_low, d_vectors, d_num, d_den, state = refs
    seqs = state.shape[0]
    length = resid.shape[0] // seqs
    block_out[...] = low(out_sum[...])
    normal, scale = normalize(resid[...])
    grad = back_sum[...]
    d_vectors[0:1, :] = jnp.sum(grad * normal, axis=0, keepdims=True)
    d_vectors[1:2, :] = jnp.sum(grad, axis=0, keepdims=True)
    d_resid[...] = wide(cotangent[...]) + norm_backward(grad, normal, scale, vectors[2:3, :])
    d_resid_low[...] = low(d_resid[...])
    d_attended = dot_nt(d_resid_low[...], w_out[...])
    shape = (FEAT, FEAT)
    cross = low(
        jnp.where(left_half(shape) != (row_index(shape) < HEAD), -1.0 / HEAD, 0.0)
    )
    for p in range(PAIRS):
        columns = slice(p * FEAT, (p + 1) * FEAT)
        num = d_attended[:, columns] * inverse[:, columns]
        product = num * wide(attended[:, columns])
        top = low(product)
        rest = low(product - wide(top))
        d_num[:, columns] = low(num)
        d_den[:, columns] = low(dot(top, cross) + dot(rest, cross))

    def pair(p, sums):
        result = []
        for b in range(seqs):
            here = slice(b * length, (b + 1) * length)
            d_even, d_odd = joined(d_num, d_den, here, p)
            even = dot(fq_t[pl.ds(aligned(2 * p, FEAT), FEAT), here], d_even)
            odd = dot(fq_t[pl.ds(aligned(2 * p + 1, FEAT), FEAT), here], d_odd)
            packed, new = pack_state(even, odd, p)
            state[b, pl.ds(aligned(p, FEAT), FEAT), :] = low(packed)
            result.append(sums[b] + new)
        return tuple(result)

    sums = lax.fori_loop(
        0, PAIRS, pair, tuple(jnp.zeros((FEAT, FEAT), wide_type) for _ in range(seqs))
    )
    for b in range(seqs):
        state[b, PAIRS * FEAT :, :] = low(sums[b])


def joined(d_num, d_den, here, p):
    columns = pl.ds(aligned(p, FEAT), FEAT)
    num, den = d_num[here, columns], d_den[here, columns]
    left = left_half(num.shape)
    return jnp.where(left, num, den), jnp.where(left, den, num)


def softmax_backward(feature, grad):
    plus, minus = wide(feature[:HEAD]), wide(feature[HEAD:])
    d_plus, d_minus = grad[:HEAD], grad[HEAD:]
    d_plus = plus * (d_plus - jnp.sum(d_plus * plus, axis=0, keepdims=True))
    d_minus = minus * (d_minus - jnp.sum(d_minus * minus, axis=0, keepdims=True))
    return low(d_plus - d_minus)


def local_kernel(mixed, fq_t, fk, fk_t, d_num, d_den, *refs):
    priors, (d_uq_t, d_fk_t, d_values) = refs[:-3], refs[-3:]
    seqs = priors[0].shape[0]
    length = mixed.shape[0] // seqs

    def pair(p, carry):
        for b in range(seqs):
            here = slice(b * length, (b + 1) * length)
            values = with_ones(mixed[here, pl.ds(aligned(2 * D // FEAT + p, FEAT), FEAT)])
            outer = joined(d_num, d_den, here, p)
            states = states_at(priors, b, p)
            found = []
            for side in range(2):
                rows = pl.ds(aligned(2 * p + side, FEAT), FEAT)
                q_t, k_t = fq_t[rows, here], fk_t[rows, here]
                link = dot_nt(outer[side], values[side])
                row, lane = row_index(link.shape), lane_index(link.shape)
                link = low(jnp.where(row >= lane, link, 0.0))
                d_q = dot_nt(k_t, link) + dot_nt(states[side], outer[side])
                d_uq_t[pl.ds(aligned(2 * p + side, HEAD), HEAD), here] = softmax_backward(q_t, d_q)
                d_fk_t[rows, here] = dot(q_t, link)
                scores = dot(fk[here, rows], q_t)
                scores = low(jnp.where(row <= lane, scores, 0.0))
                found.append(dot(scores, outer[side]))
            left = left_half(found[0].shape)
            d_values[here, pl.ds(aligned(p, FEAT), FEAT)] = jnp.where(left, found[0], found[1])
        return carry

    lax.fori_loop(0, PAIRS, pair, 0)


def mixed_kernel(mixed, fk, fk_t, maps, d_uq_t, d_fk_t, d_values, *refs):
    laters, (d_mixed, d_maps, d_uk_t) = refs[:-3], refs[-3:]
    seqs = laters[0].shape[0]
    length = mixed.shape[0] // seqs

    def pair(p, carry):
        for b in range(seqs):
            here = slice(b * length, (b + 1) * length)
            values = with_ones(mixed[here, pl.ds(aligned(2 * D // FEAT + p, FEAT), FEAT)])
            states = states_at(laters, b, p)
            found = []
            for side in range(2):
                rows = pl.ds(aligned(2 * p + side, FEAT), FEAT)
                d_k = d_fk_t[rows, here] + dot_nt(states[side], values[side])
                d_uk_t[pl.ds(aligned(2 * p + side, HEAD), HEAD), here] = softmax_backward(
                    fk_t[rows, here], d_k
                )
                found.append(dot(fk[here, rows], states[side]))
            left = left_half(found[0].shape)
            total = d_values[here, pl.ds(aligned(p, FEAT), FEAT)] + jnp.where(
                left, found[0], found[1]
            )
            d_mixed[here, pl.ds(aligned(2 * D // FEAT + p, FEAT), FEAT)] = low(total)
        return carry

    lax.fori_loop(0, PAIRS, pair, 0)
    for which, d_u_t in enumerate((d_uq_t, d_uk_t)):

        def group(g, carry):
            index = which * (D // GROUP) + g
            d_u = d_u_t[pl.ds(aligned(g, GROUP), GROUP), :]
            columns = pl.ds(aligned(index, GROUP), GROUP)
            d_maps[index] = low(dot(d_u, mixed[:, columns]))
            d_mixed[:, columns] = low(dot(d_u.T, maps[index]))
            return carry

        lax.fori_loop(0, D // GROUP, group, 0)


def in_grads_kernel(place, normed_t, d_mixed, attended, d_resid_low, grads, *, first):
    for i in range(PIECES // 2):
        block = place[0] ^ (2 * i + first)

        @pl.when(block < QKV_BLOCKS)
        def _():
            columns = pl.ds(aligned(block, CHUNK), CHUNK)
            grads[i] = low(dot(normed_t[...], d_mixed[:, columns]))

        @pl.when(block >= QKV_BLOCKS)
        def _():
            columns = pl.ds(aligned(block - QKV_BLOCKS, CHUNK), CHUNK)
            grads[i] = low(dot_tn(attended[...], d_resid_low[:, columns]))


def input_kernel(place, tokens, vectors, d_mixed, d_resid, *refs):
    pieces = refs[:PIECES]
    grad_tokens, d_vectors, total = refs[PIECES:]
    total[...] = jnp.zeros_like(total)
    for k in range(PIECES):
        block = place[0] ^ k

        @pl.when(block < QKV_BLOCKS)
        def _():
            columns = pl.ds(aligned(block, CHUNK), CHUNK)
            total[...] += dot_nt(d_mixed[:, columns], pieces[k][...])

    normal, scale = normalize(wide(tokens[...]))
    grad = total[...]
    d_vectors[0:1, :] = jnp.sum(grad * normal, axis=0, keepdims=True)
    d_vectors[1:2, :] = jnp.sum(grad, axis=0, keepdims=True)
    grad_tokens[...] = low(d_resid[...] + norm_backward(grad, normal, scale, vectors[0:1, :]))


def lay_in_kernel(place, *refs):
    pieces, (qkv, out) = refs[:PIECES], refs[PIECES:]
    for k in range(PIECES):
        block = place[0] ^ k

        @pl.when(block < QKV_BLOCKS)
        def _():
            qkv[:, pl.ds(aligned(block, CHUNK), CHUNK)] = wide(pieces[k][...])

        @pl.when(block >= QKV_BLOCKS)
        def _():
            out[:, pl.ds(aligned(block - QKV_BLOCKS, CHUNK), CHUNK)] = wide(pieces[k][...])


def lay_mlp_kernel(place, *refs):
    pieces, (up, down) = refs[:PIECES], refs[PIECES:]
    up_rows, down_rows = up.shape[1], down.shape[1]
    for k in range(PIECES):
        block = place[0] ^ k
        up[block] = pieces[k][:up_rows, :]
        for side in range(2):
            start = up_rows + side * down_rows
            down[block, :, side * CHUNK : (side + 1) * CHUNK] = wide(
                pieces[k][start : start + down_rows, :]
            )


def whole(shape, dtype=low_type):
    return jax.ShapeDtypeStruct(shape, dtype)


def scalar_first(count):
    return [pl.BlockSpec(memory_space=pltpu.SMEM)] + [
        pl.BlockSpec(memory_space=pltpu.VMEM) for _ in range(count)
    ]


def interleave(even, odd):
    return [part for both in zip(even, odd) for part in both]


def shards(
    tokens,
    gain_attn,
    bias_attn,
    w_qkv,
    w_feature,
    w_out,
    gain_mlp,
    bias_mlp,
    w_up,
    w_down,
    cotangent,
):
    shard_count = lax.axis_size("shard")
    place = lax.axis_index("rep") % PIECES
    spot = place.reshape(1).astype(jnp.int32)
    seqs, length, _ = tokens.shape
    count = seqs * length
    rows = w_qkv.shape[0]
    fine = CHUNK // shard_count

    small = jnp.concatenate(
        [w_feature.reshape(-1), gain_attn, bias_attn, gain_mlp, bias_mlp]
    ).reshape(-1, rows)
    small = around(small)
    feature_weight = small[:, :FEAT].reshape(shard_count, rows, FEAT).reshape(D, FEAT)
    vectors = wide(small[:, FEAT:].transpose(1, 0, 2).reshape(4, D))
    blocks = feature_weight.reshape(D // GROUP, 4, HEAD, 2, HEAD)
    maps = (
        jnp.einsum("gaiwo,ab->wgaobi", blocks, jnp.eye(4, dtype=low_type))
        .reshape(2 * D // GROUP, GROUP, GROUP)
        .astype(low_type)
    )

    part_in = lax.dynamic_slice_in_dim(
        jnp.concatenate([w_qkv, w_out], axis=1), place * CHUNK, CHUNK, 1
    )
    in_even, in_odd = gather_pieces(part_in)
    in_pieces = interleave(in_even, in_odd)
    part_up = lax.dynamic_index_in_dim(
        w_up.reshape(rows, shard_count, PIECES, fine), place, 2, False
    ).reshape(rows, CHUNK)
    part_down = lax.dynamic_slice_in_dim(w_down, place * fine, fine, 0)
    mlp_even, mlp_odd = gather_pieces(
        jnp.concatenate([part_up, part_down[:, :CHUNK], part_down[:, CHUNK:]], axis=0)
    )

    flat = tokens.reshape(count, D)
    flat_cotangent = cotangent.reshape(count, D)
    normed, normed_t, mixed, out_weight, fq, fk, fq_t, fk_t, key_state = pl.pallas_call(
        qkv_kernel,
        out_shape=(
            whole((count, D)),
            whole((D, count)),
            whole((count, 3 * D)),
            whole((D, D)),
            whole((count, HEADS * FEAT)),
            whole((count, HEADS * FEAT)),
            whole((HEADS * FEAT, count)),
            whole((HEADS * FEAT, count)),
            whole((seqs, SLAB, FEAT)),
        ),
        in_specs=scalar_first(3 + PIECES),
        name="qkv",
    )(spot, flat, vectors, maps, *in_pieces)
    priors = [slide(key_state, step) for step in range(1, shard_count)]
    attended, inverse, resid, second, second_t = pl.pallas_call(
        attend_kernel,
        out_shape=(
            whole((count, D)),
            whole((count, D), wide_type),
            whole((count, D), wide_type),
            whole((count, D)),
            whole((D, count)),
        ),
        name="attend",
    )(flat, vectors, mixed, fq, fk_t, out_weight, *priors)

    def mlp(out_before, back_before, pieces, name):
        block = pieces[0].shape[0]
        fixed = lambda shape: pl.BlockSpec(shape, lambda i: (0, 0))
        return pl.pallas_call(
            mlp_kernel,
            grid=(4,),
            in_specs=[
                fixed((count, D)),
                fixed((D, count)),
                fixed((count, D)),
                fixed((count, D)),
                fixed((count, D)),
            ]
            + [pl.BlockSpec(memory_space=pl.ANY)] * 4,
            out_specs=(
                fixed((count, D)),
                fixed((count, D)),
                pl.BlockSpec((1, block, CHUNK), lambda i: (i, 0, 0)),
            ),
            out_shape=(
                whole((count, D), wide_type),
                whole((count, D), wide_type),
                whole((4, block, CHUNK)),
            ),
            scratch_shapes=[
                pltpu.VMEM((4, D, CHUNK), low_type),
                pltpu.VMEM((4, CHUNK, D), low_type),
                pltpu.SemaphoreType.DMA((4, 3 * shard_count)),
            ],
            name=name,
        )(second, second_t, flat_cotangent, out_before, back_before, *pieces)

    out_sum, back_sum, mlp_grads_odd = mlp(resid, jnp.zeros_like(resid), mlp_odd, "mlp_odd")
    out_sum, back_sum, mlp_grads_even = mlp(out_sum, back_sum, mlp_even, "mlp_even")
    block_out, d_resid, d_resid_low, d_vectors_two, d_num, d_den, query_state = pl.pallas_call(
        resid_kernel,
        out_shape=(
            whole((count, D)),
            whole((count, D), wide_type),
            whole((count, D)),
            whole((2, D), wide_type),
            whole((count, D)),
            whole((count, D)),
            whole((seqs, SLAB, FEAT)),
        ),
        name="resid",
    )(out_sum, back_sum, resid, flat_cotangent, vectors, out_weight, attended, inverse, fq_t)
    laters = [slide(query_state, -step) for step in range(1, shard_count)]
    d_uq_t, d_fk_t, d_values = pl.pallas_call(
        local_kernel,
        out_shape=(
            whole((D, count)),
            whole((HEADS * FEAT, count), wide_type),
            whole((count, D), wide_type),
        ),
        name="local",
    )(mixed, fq_t, fk, fk_t, d_num, d_den, *priors)
    d_mixed, d_maps, _ = pl.pallas_call(
        mixed_kernel,
        out_shape=(
            whole((count, 3 * D)),
            whole((2 * D // GROUP, GROUP, GROUP)),
            whole((D, count)),
        ),
        name="mixed",
    )(mixed, fk, fk_t, maps, d_uq_t, d_fk_t, d_values, *laters)

    def in_grads(first):
        return pl.pallas_call(
            lambda *refs: in_grads_kernel(*refs, first=first),
            out_shape=whole((PIECES // 2, D, CHUNK)),
            in_specs=scalar_first(4),
            name="in_grads",
        )(spot, normed_t, d_mixed, attended, d_resid_low)

    in_grads_odd = in_grads(1)
    in_grads_even = in_grads(0)
    grad_tokens, d_vectors_one = pl.pallas_call(
        input_kernel,
        out_shape=(whole((count, D)), whole((2, D), wide_type)),
        in_specs=scalar_first(4 + PIECES),
        scratch_shapes=[pltpu.VMEM((count, D), wide_type)],
        name="input",
    )(spot, flat, vectors, d_mixed, d_resid, *in_pieces)

    mlp_sums = interleave(*sum_pieces(mlp_grads_even, mlp_grads_odd))
    in_sums = interleave(*sum_pieces(in_grads_even, in_grads_odd))
    grad_qkv, grad_out = pl.pallas_call(
        lay_in_kernel,
        out_shape=(whole((rows, 3 * D), wide_type), whole((rows, D), wide_type)),
        in_specs=scalar_first(PIECES),
        name="lay_in",
    )(spot, *in_sums)
    grad_up, grad_down = pl.pallas_call(
        lay_mlp_kernel,
        out_shape=(whole((PIECES, rows, CHUNK)), whole((PIECES, fine, D), wide_type)),
        in_specs=scalar_first(PIECES),
        name="lay_mlp",
    )(spot, *mlp_sums)
    grad_up = (
        wide(grad_up)
        .reshape(PIECES, rows, shard_count, fine)
        .transpose(1, 2, 0, 3)
        .reshape(rows, -1)
    )
    grad_down = grad_down.reshape(-1, D)

    d_maps = d_maps.reshape(2, D // GROUP, 4, HEAD, 4, HEAD)
    d_maps = jnp.stack([d_maps[:, :, a, :, a, :] for a in range(4)], axis=2)
    d_maps = d_maps.transpose(1, 2, 4, 0, 3).reshape(shard_count, -1)
    d_vectors = jnp.concatenate([d_vectors_one, d_vectors_two], axis=0)
    d_vectors = d_vectors.reshape(4, shard_count, rows).transpose(1, 0, 2)
    tiny = jnp.concatenate([wide(d_maps), d_vectors.reshape(shard_count, -1)], axis=1)
    tiny = tiny.reshape(-1, rows)
    bit = 1
    while bit < lax.axis_size("rep"):
        tiny = tiny + wide(flip(low(tiny), bit))
        bit *= 2
    tiny = scatter_shards(tiny)
    grad_feature = tiny[:FEAT].reshape(rows, FEAT)
    return (
        block_out.reshape(tokens.shape),
        grad_tokens.reshape(tokens.shape),
        tiny[FEAT],
        tiny[FEAT + 1],
        grad_qkv,
        grad_feature,
        grad_out,
        tiny[FEAT + 2],
        tiny[FEAT + 3],
        grad_up,
        grad_down,
    )


def solution(mesh):
    placed = (
        P("rep", "shard", None),
        P("shard"),
        P("shard"),
        P("shard", None),
        P("shard", None),
        P("shard", None),
        P("shard"),
        P("shard"),
        P("shard", None),
        P("shard", None),
        P("rep", "shard", None),
    )
    return jax.shard_map(
        shards,
        mesh=mesh,
        in_specs=placed,
        out_specs=(
            P("rep", "shard", None),
            P("rep", "shard", None),
            P("shard"),
            P("shard"),
            P("shard", None),
            P("shard", None),
            P("shard", None),
            P("shard"),
            P("shard"),
            P("shard", None),
            P("shard", None),
        ),
        check_vma=False,
    )
```

```python
import jax
import jax.numpy as jnp
from jax import lax
from jax.experimental import pallas as pl
from jax.experimental.pallas import tpu as pltpu
from jax.sharding import PartitionSpec as P

D = 768
HEADS = 12
HEAD = 64
FEAT = 128
PAIRS = HEADS // 2
GROUP = 4 * HEAD
PIECES = 8
CHUNK = 4 * D // PIECES
QKV_BLOCKS = 3 * D // CHUNK
SLAB = (PAIRS + 1) * FEAT

norm_epsilon = 1e-05
low_type = jnp.bfloat16
wide_type = jnp.float32


def flip(value, bit):
    count = lax.axis_size("rep")
    return lax.ppermute(value, "rep", [(i, i ^ bit) for i in range(count)])


def spin(value, step):
    count = lax.axis_size("shard")
    return lax.ppermute(value, "shard", [(i, (i + step) % count) for i in range(count)])


def slide(value, step):
    count = lax.axis_size("shard")
    pairs = [(i, i + step) for i in range(count) if 0 <= i + step < count]
    return lax.ppermute(value, "shard", pairs)


def wide(value):
    return value.astype(wide_type)


def low(value):
    return value.astype(low_type)


def spread(own):
    half = own.shape[0] // 2
    from_x = flip(own, 2)
    from_y = flip(own, 4)
    diagonal = jnp.concatenate([flip(from_x[:half], 4), flip(from_y[half:], 2)], axis=0)
    even = [own, from_x, from_y, diagonal]
    return even, [flip(part, 1) for part in even]


def around(part):
    count, here = lax.axis_size("shard"), lax.axis_index("shard")
    full = jnp.zeros((count,) + part.shape, part.dtype)
    full = lax.dynamic_update_index_in_dim(full, part, here, 0)
    for step in range(1, count):
        full = lax.dynamic_update_index_in_dim(full, spin(part, step), (here - step) % count, 0)
    return full


def scatter_shards(total):
    count, here = lax.axis_size("shard"), lax.axis_index("shard")
    blocks = total.reshape((count, total.shape[0] // count) + total.shape[1:])
    pick = lambda step: lax.dynamic_index_in_dim(blocks, (here + step) % count, 0, False)
    result = pick(0)
    for step in range(1, count):
        result = result + wide(spin(low(pick(step)), step))
    return result


def both(even, other, i, rows):
    return wide(even[i, rows]) + wide(other[i, rows])


def split_rows(even):
    half = even.shape[1] // 2
    return slice(None, half), slice(half, None)


def diagonal_halves(even, other):
    upper, lower = split_rows(even)
    return low(both(even, other, 3, upper)), low(both(even, other, 3, lower))


def send_diagonal(halves):
    return flip(halves[0], 4), flip(halves[1], 2)


def side_parts(even, other, received):
    upper, lower = split_rows(even)
    x_part = [both(even, other, 1, upper) + wide(received[0]), both(even, other, 1, lower)]
    y_part = [both(even, other, 2, upper), both(even, other, 2, lower) + wide(received[1])]
    return low(jnp.concatenate(x_part, axis=0)), low(jnp.concatenate(y_part, axis=0))


def send_sides(sides):
    return flip(sides[0], 2), flip(sides[1], 4)


def join_parts(even, other, joined_parts):
    mine = both(even, other, 0, slice(None)) + wide(joined_parts[0]) + wide(joined_parts[1])
    bit = PIECES
    while bit < lax.axis_size("rep"):
        mine = mine + wide(flip(low(mine), bit))
        bit *= 2
    return mine


def dot(a, b):
    return jnp.dot(a, b, preferred_element_type=wide_type)


def dot_nt(a, b):
    return lax.dot_general(a, b, (((1,), (1,)), ((), ())), preferred_element_type=wide_type)


def dot_tn(a, b):
    return lax.dot_general(a, b, (((0,), (0,)), ((), ())), preferred_element_type=wide_type)


def normalize(rows):
    centred = rows - jnp.mean(rows, axis=-1, keepdims=True)
    scale = lax.rsqrt(jnp.mean(centred * centred, axis=-1, keepdims=True) + norm_epsilon)
    return centred * scale, scale


def norm_backward(grad, normal, scale, gain):
    e = grad * gain
    return scale * (
        e
        - jnp.mean(e, axis=-1, keepdims=True)
        - normal * jnp.mean(e * normal, axis=-1, keepdims=True)
    )


def lane_index(shape):
    return lax.broadcasted_iota(jnp.int32, shape, len(shape) - 1)


def row_index(shape):
    return lax.broadcasted_iota(jnp.int32, shape, len(shape) - 2)


def left_half(shape):
    return lane_index(shape) < HEAD


def aligned(index, unit):
    return pl.multiple_of(index * unit, unit)


def with_ones(pair):
    left = left_half(pair.shape)
    one = jnp.ones_like(pair)
    return jnp.where(left, pair, one), jnp.where(left, one, pair)


def pack_state(even, odd, p):
    lane = lane_index(even.shape)
    packed = jnp.where(lane < HEAD, even, odd)
    sums = jnp.where(lane == HEAD + 2 * p, even, jnp.where(lane == 2 * p + 1, odd, 0.0))
    return packed, sums


def unpack_state(packed, sums, p):
    shape = packed.shape
    lane, row = lane_index(shape), row_index(shape)
    pick_even = low(jnp.where((row == HEAD + 2 * p) & (lane >= HEAD), 1.0, 0.0))
    pick_odd = low(jnp.where((row == 2 * p + 1) & (lane < HEAD), 1.0, 0.0))
    even = jnp.where(lane < HEAD, packed, dot(sums, pick_even))
    odd = jnp.where(lane < HEAD, dot(sums, pick_odd), packed)
    return low(even), low(odd)


def added(refs, b, rows):
    total = wide(refs[0][b, rows, :])
    for ref in refs[1:]:
        total = total + wide(ref[b, rows, :])
    return total


def states_at(refs, b, p):
    packed = added(refs, b, pl.ds(aligned(p, FEAT), FEAT))
    sums = low(added(refs, b, slice(PAIRS * FEAT, SLAB)))
    return unpack_state(packed, sums, p)


def features(maps, base, columns, f_t, f):
    def group(g, carry):
        u_t = dot_nt(maps[base + g], columns[:, pl.ds(aligned(g, GROUP), GROUP)])
        for a in range(4):
            u = u_t[a * HEAD : (a + 1) * HEAD]
            up = jnp.exp(u - jnp.max(u, axis=0, keepdims=True))
            down = jnp.exp(jnp.min(u, axis=0, keepdims=True) - u)
            plus = up / jnp.sum(up, axis=0, keepdims=True)
            minus = down / jnp.sum(down, axis=0, keepdims=True)
            feature = low(jnp.concatenate([plus, minus], axis=0))
            rows = pl.ds(aligned(g * 4 + a, FEAT), FEAT)
            f_t[rows, :] = feature
            f[:, rows] = feature.T
        return carry

    lax.fori_loop(0, D // GROUP, group, 0)


def wanted(place, k, first, last):
    block = place[0] ^ k
    return block, (block >= first) & (block < last)


def fetch(place, pieces, held, ready, first, last):
    for k in range(PIECES):
        _, use = wanted(place, k, first, last)

        @pl.when(use)
        def _():
            pltpu.make_async_copy(pieces[k], held.at[k], ready.at[k]).start()


def each_piece(place, pieces, held, ready, first, last, work):
    for k in range(PIECES):
        block, use = wanted(place, k, first, last)

        @pl.when(use)
        def _():
            pltpu.make_async_copy(pieces[k], held.at[k], ready.at[k]).wait()
            work(block - first, held.at[k])


def chunk_at(index):
    return pl.ds(aligned(index, CHUNK), CHUNK)


def pair_at(index):
    return pl.ds(aligned(index, FEAT), FEAT)


VALUES = D // FEAT
QUERY_BLOCKS = D // CHUNK


def keys_kernel(place, tokens, vectors, maps, *refs):
    pieces = refs[:PIECES]
    normed, normed_t, keyed, fk, fk_t, state, held, ready = refs[PIECES:]
    fetch(place, pieces, held, ready, QUERY_BLOCKS, QKV_BLOCKS)
    seqs = state.shape[0]
    length = tokens.shape[0] // seqs
    normal, _ = normalize(wide(tokens[...]))
    normed[...] = low(normal * vectors[0:1, :] + vectors[1:2, :])

    def project(index, weight):
        keyed[:, chunk_at(index)] = low(dot(normed[...], weight[...]))

    each_piece(place, pieces, held, ready, QUERY_BLOCKS, QKV_BLOCKS, project)
    features(maps, D // GROUP, keyed, fk_t, fk)
    state_sums(state, length, lambda p, here: with_ones(keyed[here, pair_at(VALUES + p)]), fk_t)
    normed_t[...] = normed[...].T


def state_sums(state, length, sides, f_t):
    seqs = state.shape[0]

    def pair(p, sums):
        result = []
        for b in range(seqs):
            here = slice(b * length, (b + 1) * length)
            first, second = sides(p, here)
            even = dot(f_t[pair_at(2 * p), here], first)
            odd = dot(f_t[pair_at(2 * p + 1), here], second)
            packed, new = pack_state(even, odd, p)
            state[b, pair_at(p), :] = low(packed)
            result.append(sums[b] + new)
        return tuple(result)

    empty = tuple(jnp.zeros((FEAT, FEAT), wide_type) for _ in range(seqs))
    sums = lax.fori_loop(0, PAIRS, pair, empty)
    for b in range(seqs):
        state[b, PAIRS * FEAT :, :] = low(sums[b])


def queries_kernel(place, normed, keyed, fk_t, maps, *refs):
    pieces = refs[:PIECES]
    queries, fq, fq_t, partial, w_out, held, ready = refs[PIECES:]
    fetch(place, pieces, held, ready, 0, QUERY_BLOCKS)
    for k in range(PIECES):
        block, use = wanted(place, k, QKV_BLOCKS, PIECES)

        @pl.when(use)
        def _():
            target = w_out.at[:, chunk_at(block - QKV_BLOCKS)]
            pltpu.make_async_copy(pieces[k], target, ready.at[k]).start()

    def project(index, weight):
        queries[:, chunk_at(index)] = low(dot(normed[...], weight[...]))

    each_piece(place, pieces, held, ready, 0, QUERY_BLOCKS, project)
    features(maps, 0, queries, fq_t, fq)
    count = normed.shape[0]
    length = count // partial.shape[0]

    def pair(p, carry):
        for b in range(count // length):
            here = slice(b * length, (b + 1) * length)
            values = with_ones(keyed[here, pair_at(VALUES + p)])
            for side in range(2):
                rows = pair_at(2 * p + side)
                scores = dot(fq[here, rows], fk_t[rows, here])
                scores = jnp.where(row_index(scores.shape) >= lane_index(scores.shape), scores, 0.0)
                partial[b, :, rows] = dot(low(scores), values[side])
        return carry

    lax.fori_loop(0, PAIRS, pair, 0)
    for k in range(PIECES):
        block, use = wanted(place, k, QKV_BLOCKS, PIECES)

        @pl.when(use)
        def _():
            target = w_out.at[:, chunk_at(block - QKV_BLOCKS)]
            pltpu.make_async_copy(pieces[k], target, ready.at[k]).wait()


def attend_kernel(tokens, vectors, partial, fq, w_out, *refs):
    priors, (attended, inverse, resid, second, second_t) = refs[:-5], refs[-5:]
    seqs = priors[0].shape[0]
    length = tokens.shape[0] // seqs

    def pair(p, carry):
        for b in range(seqs):
            here = slice(b * length, (b + 1) * length)
            states = states_at(priors, b, p)
            found = []
            for side in range(2):
                rows = pair_at(2 * p + side)
                found.append(partial[b, :, rows] + dot(fq[here, rows], states[side]))
            left = left_half(found[0].shape)
            turned = [pltpu.roll(a, HEAD, 1) for a in found]
            over = 1.0 / jnp.where(left, turned[0], turned[1])
            attended[here, pair_at(p)] = low(jnp.where(left, found[0], found[1]) * over)
            inverse[here, pair_at(p)] = over
        return carry

    lax.fori_loop(0, PAIRS, pair, 0)
    resid[...] = wide(tokens[...]) + dot(attended[...], w_out[...])
    normal, _ = normalize(resid[...])
    second[...] = low(normal * vectors[2:3, :] + vectors[3:4, :])
    second_t[...] = second[...].T


def mlp_kernel(second, cotangent, resid, *refs):
    pieces = refs[:PIECES]
    out_sum, back_sum, hiddens, d_pres, up, down, ready = refs[PIECES:]
    step = pl.program_id(0)
    parts = grads_layout(second.shape[1], pieces[0].shape[0])

    def copies(k, source):
        listed = []
        for i, (src, dst) in enumerate(parts):
            if dst[0] == "up":
                target = up.at[k, pl.ds(dst[1], dst[2]), :]
            else:
                target = down.at[k, pl.ds(dst[1], dst[2]), pl.ds(dst[3], CHUNK)]
            listed.append(
                pltpu.make_async_copy(source.at[pl.ds(src, dst[2]), :], target, ready.at[k, i])
            )
        return listed

    @pl.when(step == 0)
    def _():
        for k in range(PIECES):
            for copy in copies(k, pieces[k]):
                copy.start()
        out_sum[...] = resid[...]
        back_sum[...] = jnp.zeros_like(back_sum)

    for copy in copies(step, pieces[0]):
        copy.wait()

    up_weight, down_weight = up[step], down[step]
    pre = dot(second[...], up_weight)
    square = pre * pre
    bent = jnp.tanh(0.7978845608 * (pre + 0.044715 * square * pre))
    half = 0.5 * (1.0 + bent)
    hidden = low(pre * half)
    slope = half + (0.5 * 0.7978845608) * pre * (1.0 - bent * bent) * (
        1.0 + 3.0 * 0.044715 * square
    )
    hiddens[0] = hidden
    out_sum[...] += dot(hidden, down_weight)
    d_pre = low(dot_nt(cotangent[...], down_weight) * slope)
    d_pres[0] = d_pre
    back_sum[...] += dot_nt(d_pre, up_weight)


def mlp_grads_kernel(second_t, cotangent, hidden, d_pre, grads):
    d_up = low(dot(second_t[...], d_pre[0]))
    d_down = low(dot_tn(hidden[0], cotangent[...]))
    for src, dst in grads_layout(second_t.shape[0], grads.shape[1]):
        if dst[0] == "up":
            grads[0, src : src + dst[2], :] = d_up[dst[1] : dst[1] + dst[2]]
        else:
            grads[0, src : src + dst[2], :] = d_down[dst[1] : dst[1] + dst[2], dst[3] : dst[3] + CHUNK]


def grads_layout(width, block):
    shards = block // CHUNK
    up_rows = width // shards
    down_rows = CHUNK // shards
    parts = []
    for s in range(shards):
        base = s * (up_rows + 2 * down_rows)
        parts.append((base, ("up", s * up_rows, up_rows)))
        for side in range(2):
            parts.append(
                (
                    base + up_rows + side * down_rows,
                    ("down", s * down_rows, down_rows, side * CHUNK),
                )
            )
    return parts


def resid_kernel(out_sum, back_sum, resid, cotangent, vectors, w_out, attended, inverse, fq_t, *refs):
    block_out, d_resid, d_resid_low, d_vectors, d_num, d_den, state = refs
    seqs = state.shape[0]
    length = resid.shape[0] // seqs
    block_out[...] = low(out_sum[...])
    normal, scale = normalize(resid[...])
    grad = back_sum[...]
    d_vectors[0:1, :] = jnp.sum(grad * normal, axis=0, keepdims=True)
    d_vectors[1:2, :] = jnp.sum(grad, axis=0, keepdims=True)
    d_resid[...] = wide(cotangent[...]) + norm_backward(grad, normal, scale, vectors[2:3, :])
    d_resid_low[...] = low(d_resid[...])
    d_attended = dot_nt(d_resid_low[...], w_out[...])
    shape = (FEAT, FEAT)
    cross = low(
        jnp.where(left_half(shape) != (row_index(shape) < HEAD), -1.0 / HEAD, 0.0)
    )
    for p in range(PAIRS):
        columns = slice(p * FEAT, (p + 1) * FEAT)
        num = d_attended[:, columns] * inverse[:, columns]
        product = num * wide(attended[:, columns])
        top = low(product)
        rest = low(product - wide(top))
        d_num[:, columns] = low(num)
        d_den[:, columns] = low(dot(top, cross) + dot(rest, cross))

    state_sums(state, length, lambda p, here: joined(d_num, d_den, here, p), fq_t)


def joined(d_num, d_den, here, p):
    columns = pl.ds(aligned(p, FEAT), FEAT)
    num, den = d_num[here, columns], d_den[here, columns]
    left = left_half(num.shape)
    return jnp.where(left, num, den), jnp.where(left, den, num)


def softmax_backward(feature, grad):
    plus, minus = wide(feature[:HEAD]), wide(feature[HEAD:])
    d_plus, d_minus = grad[:HEAD], grad[HEAD:]
    d_plus = plus * (d_plus - jnp.sum(d_plus * plus, axis=0, keepdims=True))
    d_minus = minus * (d_minus - jnp.sum(d_minus * minus, axis=0, keepdims=True))
    return low(d_plus - d_minus)


def local_kernel(keyed, fq_t, fk, fk_t, d_num, d_den, *refs):
    priors, (d_uq_t, d_fk_t, d_values) = refs[:-3], refs[-3:]
    seqs = priors[0].shape[0]
    length = keyed.shape[0] // seqs

    def pair(p, carry):
        for b in range(seqs):
            here = slice(b * length, (b + 1) * length)
            values = with_ones(keyed[here, pair_at(VALUES + p)])
            outer = joined(d_num, d_den, here, p)
            states = states_at(priors, b, p)
            found = []
            for side in range(2):
                rows = pl.ds(aligned(2 * p + side, FEAT), FEAT)
                q_t, k_t = fq_t[rows, here], fk_t[rows, here]
                link = dot_nt(outer[side], values[side])
                row, lane = row_index(link.shape), lane_index(link.shape)
                link = low(jnp.where(row >= lane, link, 0.0))
                d_q = dot_nt(k_t, link) + dot_nt(states[side], outer[side])
                d_uq_t[pl.ds(aligned(2 * p + side, HEAD), HEAD), here] = softmax_backward(q_t, d_q)
                d_fk_t[rows, here] = dot(q_t, link)
                scores = dot(fk[here, rows], q_t)
                scores = low(jnp.where(row <= lane, scores, 0.0))
                found.append(dot(scores, outer[side]))
            left = left_half(found[0].shape)
            d_values[here, pl.ds(aligned(p, FEAT), FEAT)] = jnp.where(left, found[0], found[1])
        return carry

    lax.fori_loop(0, PAIRS, pair, 0)


def mixed_kernel(queries, keyed, fk, fk_t, maps, d_uq_t, d_fk_t, d_values, *refs):
    laters, (d_mixed, d_maps, d_uk_t) = refs[:-3], refs[-3:]
    seqs = laters[0].shape[0]
    length = keyed.shape[0] // seqs

    def pair(p, carry):
        for b in range(seqs):
            here = slice(b * length, (b + 1) * length)
            values = with_ones(keyed[here, pair_at(VALUES + p)])
            states = states_at(laters, b, p)
            found = []
            for side in range(2):
                rows = pl.ds(aligned(2 * p + side, FEAT), FEAT)
                d_k = d_fk_t[rows, here] + dot_nt(states[side], values[side])
                d_uk_t[pl.ds(aligned(2 * p + side, HEAD), HEAD), here] = softmax_backward(
                    fk_t[rows, here], d_k
                )
                found.append(dot(fk[here, rows], states[side]))
            left = left_half(found[0].shape)
            total = d_values[here, pl.ds(aligned(p, FEAT), FEAT)] + jnp.where(
                left, found[0], found[1]
            )
            d_mixed[here, pl.ds(aligned(2 * D // FEAT + p, FEAT), FEAT)] = low(total)
        return carry

    lax.fori_loop(0, PAIRS, pair, 0)
    for which, (d_u_t, source) in enumerate(((d_uq_t, queries), (d_uk_t, keyed))):

        def group(g, carry):
            index = which * (D // GROUP) + g
            d_u = d_u_t[pl.ds(aligned(g, GROUP), GROUP), :]
            columns = pl.ds(aligned(index, GROUP), GROUP)
            d_maps[index] = low(dot(d_u, source[:, pl.ds(aligned(g, GROUP), GROUP)]))
            d_mixed[:, columns] = low(dot(d_u.T, maps[index]))
            return carry

        lax.fori_loop(0, D // GROUP, group, 0)


def in_grads_kernel(place, normed_t, d_mixed, attended, d_resid_low, grads, *, first):
    for i in range(PIECES // 2):
        block = place[0] ^ (2 * i + first)

        @pl.when(block < QKV_BLOCKS)
        def _():
            columns = pl.ds(aligned(block, CHUNK), CHUNK)
            grads[i] = low(dot(normed_t[...], d_mixed[:, columns]))

        @pl.when(block >= QKV_BLOCKS)
        def _():
            columns = pl.ds(aligned(block - QKV_BLOCKS, CHUNK), CHUNK)
            grads[i] = low(dot_tn(attended[...], d_resid_low[:, columns]))


def input_kernel(place, tokens, vectors, d_mixed, d_resid, *refs):
    pieces = refs[:PIECES]
    grad_tokens, d_vectors, total, held, ready = refs[PIECES:]
    fetch(place, pieces, held, ready, 0, QKV_BLOCKS)
    total[...] = jnp.zeros_like(total)

    def add(index, weight):
        total[...] += dot_nt(d_mixed[:, chunk_at(index)], weight[...])

    each_piece(place, pieces, held, ready, 0, QKV_BLOCKS, add)
    normal, scale = normalize(wide(tokens[...]))
    grad = total[...]
    d_vectors[0:1, :] = jnp.sum(grad * normal, axis=0, keepdims=True)
    d_vectors[1:2, :] = jnp.sum(grad, axis=0, keepdims=True)
    grad_tokens[...] = low(d_resid[...] + norm_backward(grad, normal, scale, vectors[0:1, :]))


def lay_in_kernel(place, *refs):
    pieces, (qkv, out) = refs[:PIECES], refs[PIECES:]
    for k in range(PIECES):
        block = place[0] ^ k

        @pl.when(block < QKV_BLOCKS)
        def _():
            qkv[:, pl.ds(aligned(block, CHUNK), CHUNK)] = wide(pieces[k][...])

        @pl.when(block >= QKV_BLOCKS)
        def _():
            out[:, pl.ds(aligned(block - QKV_BLOCKS, CHUNK), CHUNK)] = wide(pieces[k][...])


def lay_mlp_kernel(place, *refs):
    pieces, (up, down, ordered) = refs[:PIECES], refs[PIECES:]
    up_rows, down_rows = ordered.shape[1], down.shape[1]
    for k in range(PIECES):
        block = place[0] ^ k
        ordered[block] = pieces[k][:up_rows, :]
        for side in range(2):
            start = up_rows + side * down_rows
            down[block, :, side * CHUNK : (side + 1) * CHUNK] = wide(
                pieces[k][start : start + down_rows, :]
            )
    for s in range(CHUNK // down_rows):
        columns = slice(s * down_rows, (s + 1) * down_rows)
        row = jnp.concatenate([ordered[r][:, columns] for r in range(PIECES)], axis=1)
        up[:, s * PIECES * down_rows : (s + 1) * PIECES * down_rows] = wide(row)


def whole(shape, dtype=low_type):
    return jax.ShapeDtypeStruct(shape, dtype)


def scalar_first(count):
    return [pl.BlockSpec(memory_space=pltpu.SMEM)] + [
        pl.BlockSpec(memory_space=pltpu.VMEM) for _ in range(count)
    ]


def piece_scratch():
    return [pltpu.VMEM((PIECES, D, CHUNK), low_type), pltpu.SemaphoreType.DMA((PIECES,))]


def call(kernel, weight, out_shape, in_specs=None, scratch=(), **rest):
    if in_specs is not None:
        rest["in_specs"] = in_specs
    return pl.pallas_call(
        kernel,
        out_shape=out_shape,
        scratch_shapes=list(scratch),
        compiler_params=pltpu.CompilerParams(vmem_limit_bytes=36 << 20),
        cost_estimate=pl.CostEstimate(
            flops=weight * 10**9, transcendentals=0, bytes_accessed=weight * 3 * 10**6
        ),
        **rest,
    )


def interleave(even, odd):
    return [part for both in zip(even, odd) for part in both]


def shards(
    tokens,
    gain_attn,
    bias_attn,
    w_qkv,
    w_feature,
    w_out,
    gain_mlp,
    bias_mlp,
    w_up,
    w_down,
    cotangent,
):
    shard_count = lax.axis_size("shard")
    place = lax.axis_index("rep") % PIECES
    spot = place.reshape(1).astype(jnp.int32)
    seqs, length, _ = tokens.shape
    count = seqs * length
    rows = w_qkv.shape[0]
    fine = CHUNK // shard_count
    flat = tokens.reshape(count, D)
    flat_cotangent = cotangent.reshape(count, D)
    anywhere = [pl.BlockSpec(memory_space=pl.ANY)] * PIECES

    small = jnp.concatenate(
        [w_feature.reshape(-1), gain_attn, bias_attn, gain_mlp, bias_mlp]
    ).reshape(-1, rows)
    part_in = lax.dynamic_slice_in_dim(
        jnp.concatenate([w_qkv, w_out], axis=1), place * CHUNK, CHUNK, 1
    )
    part_up = lax.dynamic_index_in_dim(
        w_up.reshape(rows, shard_count, PIECES, fine), place, 2, False
    ).reshape(rows, CHUNK)
    part_down = lax.dynamic_slice_in_dim(w_down, place * fine, fine, 0)
    part_mlp = jnp.concatenate([part_up, part_down[:, :CHUNK], part_down[:, CHUNK:]], axis=0)

    small = around(small)
    in_full = around(part_in)
    feature_weight = small[:, :FEAT].reshape(shard_count, rows, FEAT).reshape(D, FEAT)
    vectors = wide(small[:, FEAT:].transpose(1, 0, 2).reshape(4, D))
    blocks = feature_weight.reshape(D // GROUP, 4, HEAD, 2, HEAD)
    maps = (
        jnp.einsum("gaiwo,ab->wgaobi", blocks, jnp.eye(4, dtype=low_type))
        .reshape(2 * D // GROUP, GROUP, GROUP)
        .astype(low_type)
    )
    in_full, maps, vectors, part_mlp = lax.optimization_barrier((in_full, maps, vectors, part_mlp))
    in_pieces = interleave(*spread(in_full.reshape(-1, CHUNK)))
    mlp_full = around(part_mlp).reshape(-1, CHUNK)

    normed, normed_t, keyed, fk, fk_t, key_state = call(
        keys_kernel,
        9,
        (
            whole((count, D)),
            whole((D, count)),
            whole((count, 2 * D)),
            whole((count, HEADS * FEAT)),
            whole((HEADS * FEAT, count)),
            whole((seqs, SLAB, FEAT)),
        ),
        scalar_first(3) + anywhere,
        piece_scratch(),
    )(spot, flat, vectors, maps, *in_pieces)
    priors = [slide(key_state, step) for step in range(1, shard_count)]
    mlp_full, normed = lax.optimization_barrier((mlp_full, normed))
    mlp_pieces = spread(mlp_full)
    queries, fq, fq_t, partial, out_weight = call(
        queries_kernel,
        9,
        (
            whole((count, D)),
            whole((count, HEADS * FEAT)),
            whole((HEADS * FEAT, count)),
            whole((seqs, length, HEADS * FEAT), wide_type),
            whole((D, D)),
        ),
        scalar_first(4) + anywhere,
        piece_scratch(),
    )(spot, normed, keyed, fk_t, maps, *in_pieces)
    attended, inverse, resid, second, second_t = call(
        attend_kernel,
        5,
        (
            whole((count, D)),
            whole((count, D), wide_type),
            whole((count, D), wide_type),
            whole((count, D)),
            whole((D, count)),
        ),
    )(flat, vectors, partial, fq, out_weight, *priors)

    fixed = lambda shape: pl.BlockSpec(shape, lambda i: (0, 0))
    stacked = lambda shape: pl.BlockSpec((1,) + shape, lambda i: (i, 0, 0))
    mlp_odd, mlp_even = mlp_pieces[1], mlp_pieces[0]
    out_sum, back_sum, hiddens, d_pres = call(
        mlp_kernel,
        20,
        (
            whole((count, D), wide_type),
            whole((count, D), wide_type),
            whole((PIECES, count, CHUNK)),
            whole((PIECES, count, CHUNK)),
        ),
        [fixed((count, D)), fixed((count, D)), fixed((count, D))] + anywhere,
        [
            pltpu.VMEM((PIECES, D, CHUNK), low_type),
            pltpu.VMEM((PIECES, CHUNK, D), low_type),
            pltpu.SemaphoreType.DMA((PIECES, 3 * shard_count)),
        ],
        grid=(PIECES,),
        out_specs=(
            fixed((count, D)),
            fixed((count, D)),
            stacked((count, CHUNK)),
            stacked((count, CHUNK)),
        ),
    )(second, flat_cotangent, resid, *mlp_odd, *mlp_even)
    block_out, d_resid, d_resid_low, d_vectors_two, d_num, d_den, query_state = call(
        resid_kernel,
        5,
        (
            whole((count, D)),
            whole((count, D), wide_type),
            whole((count, D)),
            whole((2, D), wide_type),
            whole((count, D)),
            whole((count, D)),
            whole((seqs, SLAB, FEAT)),
        ),
    )(out_sum, back_sum, resid, flat_cotangent, vectors, out_weight, attended, inverse, fq_t)
    laters = [slide(query_state, -step) for step in range(1, shard_count)]

    def mlp_grads(first, second_t):
        taken = pl.BlockSpec((1, count, CHUNK), lambda i: (i + first, 0, 0))
        block = mlp_full.shape[0]
        return call(
            mlp_grads_kernel,
            6,
            whole((PIECES // 2, block, CHUNK)),
            [fixed((D, count)), fixed((count, D)), taken, taken],
            grid=(PIECES // 2,),
            out_specs=stacked((block, CHUNK)),
        )(second_t, flat_cotangent, hiddens, d_pres)

    second_t, query_state = lax.optimization_barrier((second_t, query_state))
    mlp_grads_odd = mlp_grads(0, second_t)
    mlp_other = flip(mlp_grads_odd, 1)
    second_t, mlp_grads_odd = lax.optimization_barrier((second_t, mlp_grads_odd))
    mlp_grads_even = mlp_grads(PIECES // 2, second_t)
    mlp_halves = diagonal_halves(mlp_grads_even, mlp_other)
    mlp_halves, fk = lax.optimization_barrier((mlp_halves, fk))
    mlp_received = send_diagonal(mlp_halves)
    d_uq_t, d_fk_t, d_values = call(
        local_kernel,
        10,
        (
            whole((D, count)),
            whole((HEADS * FEAT, count), wide_type),
            whole((count, D), wide_type),
        ),
    )(keyed, fq_t, fk, fk_t, d_num, d_den, *priors)
    mlp_sides = side_parts(mlp_grads_even, mlp_other, mlp_received)
    mlp_sides, d_uq_t = lax.optimization_barrier((mlp_sides, d_uq_t))
    mlp_joined = send_sides(mlp_sides)
    d_mixed, d_maps, _ = call(
        mixed_kernel,
        7,
        (
            whole((count, 3 * D)),
            whole((2 * D // GROUP, GROUP, GROUP)),
            whole((D, count)),
        ),
    )(queries, keyed, fk, fk_t, maps, d_uq_t, d_fk_t, d_values, *laters)

    def in_grads(first, d_mixed):
        return call(
            lambda *refs: in_grads_kernel(*refs, first=first),
            4,
            whole((PIECES // 2, D, CHUNK)),
            scalar_first(4),
        )(spot, normed_t, d_mixed, attended, d_resid_low)

    in_grads_odd = in_grads(1, d_mixed)
    in_other = flip(in_grads_odd, 1)
    d_mixed, in_grads_odd = lax.optimization_barrier((d_mixed, in_grads_odd))
    in_grads_even = in_grads(0, d_mixed)
    in_halves = diagonal_halves(in_grads_even, in_other)
    in_halves, d_mixed = lax.optimization_barrier((in_halves, d_mixed))
    in_received = send_diagonal(in_halves)
    grad_tokens, d_vectors_one = call(
        input_kernel,
        8,
        (whole((count, D)), whole((2, D), wide_type)),
        scalar_first(4) + anywhere,
        [pltpu.VMEM((count, D), wide_type)] + piece_scratch(),
    )(spot, flat, vectors, d_mixed, d_resid, *in_pieces)
    in_sides = side_parts(in_grads_even, in_other, in_received)
    in_sides, mlp_joined = lax.optimization_barrier((in_sides, mlp_joined))
    in_joined = send_sides(in_sides)
    mlp_mine = join_parts(mlp_grads_even, mlp_other, mlp_joined)
    mlp_sums = interleave(*spread(low(scatter_shards(mlp_mine))))
    in_mine = join_parts(in_grads_even, in_other, in_joined)
    in_sums = interleave(*spread(low(scatter_shards(in_mine))))
    grad_qkv, grad_out = call(
        lay_in_kernel,
        2,
        (whole((rows, 3 * D), wide_type), whole((rows, D), wide_type)),
        scalar_first(PIECES),
    )(spot, *in_sums)
    grad_up, grad_down = call(
        lay_mlp_kernel,
        3,
        (whole((rows, 4 * D), wide_type), whole((PIECES, fine, D), wide_type)),
        scalar_first(PIECES),
        [pltpu.VMEM((PIECES, rows, CHUNK), low_type)],
    )(spot, *mlp_sums)
    grad_down = grad_down.reshape(-1, D)

    d_maps = d_maps.reshape(2, D // GROUP, 4, HEAD, 4, HEAD)
    d_maps = jnp.stack([d_maps[:, :, a, :, a, :] for a in range(4)], axis=2)
    d_maps = d_maps.transpose(1, 2, 4, 0, 3).reshape(shard_count, -1)
    d_vectors = jnp.concatenate([d_vectors_one, d_vectors_two], axis=0)
    d_vectors = d_vectors.reshape(4, shard_count, rows).transpose(1, 0, 2)
    tiny = jnp.concatenate([wide(d_maps), d_vectors.reshape(shard_count, -1)], axis=1)
    tiny = tiny.reshape(-1, rows)
    bit = 1
    while bit < lax.axis_size("rep"):
        tiny = tiny + wide(flip(low(tiny), bit))
        bit *= 2
    tiny = scatter_shards(tiny)
    grad_feature = tiny[:FEAT].reshape(rows, FEAT)
    return (
        block_out.reshape(tokens.shape),
        grad_tokens.reshape(tokens.shape),
        tiny[FEAT],
        tiny[FEAT + 1],
        grad_qkv,
        grad_feature,
        grad_out,
        tiny[FEAT + 2],
        tiny[FEAT + 3],
        grad_up,
        grad_down,
    )


def solution(mesh):
    placed = (
        P("rep", "shard", None),
        P("shard"),
        P("shard"),
        P("shard", None),
        P("shard", None),
        P("shard", None),
        P("shard"),
        P("shard"),
        P("shard", None),
        P("shard", None),
        P("rep", "shard", None),
    )
    return jax.shard_map(
        shards,
        mesh=mesh,
        in_specs=placed,
        out_specs=(
            P("rep", "shard", None),
            P("rep", "shard", None),
            P("shard"),
            P("shard"),
            P("shard", None),
            P("shard", None),
            P("shard", None),
            P("shard"),
            P("shard"),
            P("shard", None),
            P("shard", None),
        ),
        check_vma=False,
    )
```

```python
import jax
import jax.numpy as jnp
from jax import lax
from jax.experimental import pallas as pl
from jax.experimental.pallas import tpu as pltpu
from jax.sharding import PartitionSpec as P

D = 768
HEADS = 12
HEAD = 64
FEAT = 128
PAIRS = HEADS // 2
GROUP = 4 * HEAD
PIECES = 8
CHUNK = 4 * D // PIECES
QKV_BLOCKS = 3 * D // CHUNK
SLAB = (PAIRS + 1) * FEAT

norm_epsilon = 1e-05
low_type = jnp.bfloat16
wide_type = jnp.float32


def flip(value, bit):
    count = lax.axis_size("rep")
    return lax.ppermute(value, "rep", [(i, i ^ bit) for i in range(count)])


def spin(value, step):
    count = lax.axis_size("shard")
    return lax.ppermute(value, "shard", [(i, (i + step) % count) for i in range(count)])


def slide(value, step):
    count = lax.axis_size("shard")
    pairs = [(i, i + step) for i in range(count) if 0 <= i + step < count]
    return lax.ppermute(value, "shard", pairs)


def wide(value):
    return value.astype(wide_type)


def low(value):
    return value.astype(low_type)


def place_kernel(slots, *refs):
    parts, full = refs[:-1], refs[-1]
    for i, part in enumerate(parts):
        size = part.shape[0]
        full[pl.ds(slots[i] * size, size)] = part[...]


def place_parts(parts, slots):
    shape = (len(parts) * parts[0].shape[0],) + parts[0].shape[1:]
    slots = jnp.stack([jnp.asarray(slot, jnp.int32) for slot in slots])
    return call(place_kernel, 1, whole(shape, parts[0].dtype), scalar_first(len(parts)))(
        slots, *parts
    )


def around_parts(part):
    count, here = lax.axis_size("shard"), lax.axis_index("shard")
    parts = [part[None]] + [spin(part, step)[None] for step in range(1, count)]
    return parts, [(here - step) % count for step in range(count)]


def around(part):
    return place_parts(*around_parts(part))


def scan_first(state, direction):
    received = slide(state, direction)
    return received, low(wide(state) + wide(received))


def scan_rest(received, running, direction):
    found, step = [received], 2
    while step < lax.axis_size("shard"):
        found.append(slide(running, direction * step))
        running = low(wide(running) + wide(found[-1]))
        step *= 2
    return found


def sides_of(own):
    return flip(own, 2), flip(own, 4)


def halves_of(from_x, from_y):
    half = from_x.shape[0] // 2
    return from_x[:half], from_y[half:]


def diagonal_of(halves):
    return jnp.concatenate([flip(halves[0], 4), flip(halves[1], 2)], axis=0)


def spread(own):
    from_x, from_y = sides_of(own)
    even = [own, from_x, from_y, diagonal_of(halves_of(from_x, from_y))]
    return even, [flip(part, 1) for part in even]


def sides_kernel(x_part, y_part, to_x, to_y, x_sum, y_sum):
    half = to_x.shape[0]
    x_sum[:half] = low(wide(x_part[:half]) + wide(to_x[...]))
    x_sum[half:] = x_part[half:]
    y_sum[:half] = y_part[:half]
    y_sum[half:] = low(wide(y_part[half:]) + wide(to_y[...]))


def join_parts(parts):
    count, here = lax.axis_size("shard"), lax.axis_index("shard")
    bit = PIECES
    if bit < lax.axis_size("rep"):
        mine = sum(wide(part) for part in parts)
        while bit < lax.axis_size("rep"):
            mine = mine + wide(flip(low(mine), bit))
            bit *= 2
        parts = [mine]
    rows, columns = parts[0].shape
    rows //= count

    def kernel(spot, *refs):
        sources, outs = refs[: len(parts)], refs[len(parts) :]
        for step in range(count):
            block = lax.rem(spot[0] + step, count)
            chosen = pl.ds(pl.multiple_of(block * rows, rows), rows)
            total = wide(sources[0][chosen, :])
            for source in sources[1:]:
                total = total + wide(source[chosen, :])
            outs[step][...] = total if step == 0 else low(total)

    shapes = [whole((rows, columns), wide_type)] + [whole((rows, columns))] * (count - 1)
    return call(kernel, 2, tuple(shapes), scalar_first(len(parts)))(
        here.reshape(1).astype(jnp.int32), *parts
    )


def settle(own, *sends):
    received = [spin(part, step + 1) for step, part in enumerate(sends)]

    def kernel(own, *refs):
        total = own[...]
        for ref in refs[:-1]:
            total = total + wide(ref[...])
        refs[-1][...] = low(total)

    return call(kernel, 1, whole(own.shape))(own, *received)


def scatter_shards(total):
    count, here = lax.axis_size("shard"), lax.axis_index("shard")
    blocks = total.reshape((count, total.shape[0] // count) + total.shape[1:])
    pick = lambda step: lax.dynamic_index_in_dim(blocks, (here + step) % count, 0, False)
    result = pick(0)
    for step in range(1, count):
        result = result + wide(spin(low(pick(step)), step))
    return result


def dot(a, b):
    return jnp.dot(a, b, preferred_element_type=wide_type)


def dot_nt(a, b):
    return lax.dot_general(a, b, (((1,), (1,)), ((), ())), preferred_element_type=wide_type)


def dot_tn(a, b):
    return lax.dot_general(a, b, (((0,), (0,)), ((), ())), preferred_element_type=wide_type)


def normalize(rows):
    centred = rows - jnp.mean(rows, axis=-1, keepdims=True)
    scale = lax.rsqrt(jnp.mean(centred * centred, axis=-1, keepdims=True) + norm_epsilon)
    return centred * scale, scale


def norm_backward(grad, normal, scale, gain):
    e = grad * gain
    return scale * (
        e
        - jnp.mean(e, axis=-1, keepdims=True)
        - normal * jnp.mean(e * normal, axis=-1, keepdims=True)
    )


def lane_index(shape):
    return lax.broadcasted_iota(jnp.int32, shape, len(shape) - 1)


def row_index(shape):
    return lax.broadcasted_iota(jnp.int32, shape, len(shape) - 2)


def left_half(shape):
    return lane_index(shape) < HEAD


def aligned(index, unit):
    return pl.multiple_of(index * unit, unit)


def with_ones(pair):
    left = left_half(pair.shape)
    one = jnp.ones_like(pair)
    return jnp.where(left, pair, one), jnp.where(left, one, pair)


def pack_state(even, odd, p):
    lane = lane_index(even.shape)
    packed = jnp.where(lane < HEAD, even, odd)
    sums = jnp.where(lane == HEAD + 2 * p, even, jnp.where(lane == 2 * p + 1, odd, 0.0))
    return packed, sums


def unpack_state(packed, sums, p):
    shape = packed.shape
    lane, row = lane_index(shape), row_index(shape)
    pick_even = low(jnp.where((row == HEAD + 2 * p) & (lane >= HEAD), 1.0, 0.0))
    pick_odd = low(jnp.where((row == 2 * p + 1) & (lane < HEAD), 1.0, 0.0))
    even = jnp.where(lane < HEAD, packed, dot(sums, pick_even))
    odd = jnp.where(lane < HEAD, dot(sums, pick_odd), packed)
    return low(even), low(odd)


def added(refs, b, rows):
    total = wide(refs[0][b, rows, :])
    for ref in refs[1:]:
        total = total + wide(ref[b, rows, :])
    return total


def states_at(refs, b, p):
    packed = added(refs, b, pl.ds(aligned(p, FEAT), FEAT))
    sums = low(added(refs, b, slice(PAIRS * FEAT, SLAB)))
    return unpack_state(packed, sums, p)


def features(maps, base, columns, f_t, f):
    def group(g, carry):
        u_t = dot_nt(maps[base + g], columns[:, pl.ds(aligned(g, GROUP), GROUP)])
        for a in range(4):
            u = u_t[a * HEAD : (a + 1) * HEAD]
            up = jnp.exp(u - jnp.max(u, axis=0, keepdims=True))
            down = jnp.exp(jnp.min(u, axis=0, keepdims=True) - u)
            plus = up / jnp.sum(up, axis=0, keepdims=True)
            minus = down / jnp.sum(down, axis=0, keepdims=True)
            feature = low(jnp.concatenate([plus, minus], axis=0))
            rows = pl.ds(aligned(g * 4 + a, FEAT), FEAT)
            f_t[rows, :] = feature
            f[:, rows] = feature.T
        return carry

    lax.fori_loop(0, D // GROUP, group, 0)


def wanted(place, k, first, last):
    block = place[0] ^ k
    return block, (block >= first) & (block < last)


def each_piece(place, pieces, first, last, work):
    for k in range(PIECES):
        block, use = wanted(place, k, first, last)

        @pl.when(use)
        def _():
            work(block - first, pieces[k])


def chunk_at(index):
    return pl.ds(aligned(index, CHUNK), CHUNK)


def pair_at(index):
    return pl.ds(aligned(index, FEAT), FEAT)


VALUES = D // FEAT
QUERY_BLOCKS = D // CHUNK


def keys_kernel(place, tokens, vectors, maps, *refs):
    pieces = refs[:PIECES]
    normed, normed_t, queries, keyed, fk, fk_t, state, w_out = refs[PIECES:]
    seqs = state.shape[0]
    length = tokens.shape[0] // seqs
    normal, _ = normalize(wide(tokens[...]))
    normed[...] = low(normal * vectors[0:1, :] + vectors[1:2, :])

    def project_keys(index, weight):
        keyed[:, chunk_at(index)] = low(dot(normed[...], weight[...]))

    def project_queries(index, weight):
        queries[:, chunk_at(index)] = low(dot(normed[...], weight[...]))

    each_piece(place, pieces, QUERY_BLOCKS, QKV_BLOCKS, project_keys)
    features(maps, D // GROUP, keyed, fk_t, fk)
    state_sums(state, length, lambda p, here: with_ones(keyed[here, pair_at(VALUES + p)]), fk_t)
    each_piece(place, pieces, 0, QUERY_BLOCKS, project_queries)
    normed_t[...] = normed[...].T

    def keep_out(index, weight):
        w_out[:, chunk_at(index)] = weight[...]

    each_piece(place, pieces, QKV_BLOCKS, PIECES, keep_out)


def state_sums(state, length, sides, f_t):
    seqs = state.shape[0]

    def pair(p, sums):
        result = []
        for b in range(seqs):
            here = slice(b * length, (b + 1) * length)
            first, second = sides(p, here)
            even = dot(f_t[pair_at(2 * p), here], first)
            odd = dot(f_t[pair_at(2 * p + 1), here], second)
            packed, new = pack_state(even, odd, p)
            state[b, pair_at(p), :] = low(packed)
            result.append(sums[b] + new)
        return tuple(result)

    empty = tuple(jnp.zeros((FEAT, FEAT), wide_type) for _ in range(seqs))
    sums = lax.fori_loop(0, PAIRS, pair, empty)
    for b in range(seqs):
        state[b, PAIRS * FEAT :, :] = low(sums[b])


def queries_kernel(queries, keyed, fk_t, maps, fq, fq_t, partial):
    features(maps, 0, queries, fq_t, fq)
    seqs, length, _ = partial.shape

    def pair(p, carry):
        for b in range(seqs):
            here = slice(b * length, (b + 1) * length)
            values = with_ones(keyed[here, pair_at(VALUES + p)])
            for side in range(2):
                rows = pair_at(2 * p + side)
                scores = dot(fq[here, rows], fk_t[rows, here])
                scores = jnp.where(row_index(scores.shape) >= lane_index(scores.shape), scores, 0.0)
                partial[b, :, rows] = dot(low(scores), values[side])
        return carry

    lax.fori_loop(0, PAIRS, pair, 0)


def attend_kernel(tokens, vectors, partial, fq, w_out, *refs):
    priors, (attended, inverse, resid, second, second_t) = refs[:-5], refs[-5:]
    seqs = priors[0].shape[0]
    length = tokens.shape[0] // seqs

    def pair(p, carry):
        for b in range(seqs):
            here = slice(b * length, (b + 1) * length)
            states = states_at(priors, b, p)
            found = []
            for side in range(2):
                rows = pair_at(2 * p + side)
                found.append(partial[b, :, rows] + dot(fq[here, rows], states[side]))
            left = left_half(found[0].shape)
            turned = [pltpu.roll(a, HEAD, 1) for a in found]
            over = 1.0 / jnp.where(left, turned[0], turned[1])
            attended[here, pair_at(p)] = low(jnp.where(left, found[0], found[1]) * over)
            inverse[here, pair_at(p)] = over
        return carry

    lax.fori_loop(0, PAIRS, pair, 0)
    resid[...] = wide(tokens[...]) + dot(attended[...], w_out[...])
    normal, _ = normalize(resid[...])
    second[...] = low(normal * vectors[2:3, :] + vectors[3:4, :])
    second_t[...] = second[...].T


def mlp_kernel(second, second_other, cotangent, cotangent_other, resid, *refs):
    pieces = refs[:4]
    out_sum, out_send, back_sum, back_send, hiddens, d_pres, second_other_t = refs[4:11]
    out_other, back_other, up, down, ready = refs[11:]
    count = second.shape[0]
    parts = grads_layout(second.shape[1], pieces[0].shape[0])

    def copies(k, source):
        listed = []
        for i, (src, dst) in enumerate(parts):
            if dst[0] == "up":
                target = up.at[k, pl.ds(dst[1], dst[2]), :]
            else:
                target = down.at[k, pl.ds(dst[1], dst[2]), pl.ds(dst[3], CHUNK)]
            listed.append(
                pltpu.make_async_copy(source.at[pl.ds(src, dst[2]), :], target, ready.at[k, i])
            )
        return listed

    for k in range(4):
        for copy in copies(k, pieces[k]):
            copy.start()
    out_sum[...] = resid[...]
    for total in (out_other, back_sum, back_other):
        total[...] = jnp.zeros_like(total)
    second_other_t[...] = second_other[...].T
    sides = (
        (second, cotangent, out_sum, back_sum),
        (second_other, cotangent_other, out_other, back_other),
    )

    def piece(k, carry):
        for copy in copies(k, pieces[0]):
            copy.wait()
        for side, (source, grad, out_total, back_total) in enumerate(sides):
            here = slice(side * count, (side + 1) * count)
            pre = dot(source[...], up[k])
            square = pre * pre
            bent = jnp.tanh(0.7978845608 * (pre + 0.044715 * square * pre))
            half = 0.5 * (1.0 + bent)
            hidden = low(pre * half)
            slope = half + (0.5 * 0.7978845608) * pre * (1.0 - bent * bent) * (
                1.0 + 3.0 * 0.044715 * square
            )
            hiddens[k, here] = hidden
            out_total[...] += dot(hidden, down[k])
            d_pre = low(dot_nt(grad[...], down[k]) * slope)
            d_pres[k, here] = d_pre
            back_total[...] += dot_nt(d_pre, up[k])
        return carry

    lax.fori_loop(0, 4, piece, 0)
    out_send[...] = low(out_other[...])
    back_send[...] = low(back_other[...])


def store_piece(outs, k, row, value):
    half = outs[3].shape[0]
    if k < 3:
        outs[k][row : row + value.shape[0], :] = value
    elif row < half:
        outs[3][row : row + value.shape[0], :] = value
    else:
        outs[4][row - half : row - half + value.shape[0], :] = value


def mlp_grads_kernel(second_t, second_other_t, cotangent, cotangent_other, hiddens, d_pres, *outs):
    count = cotangent.shape[0]
    own, other = slice(0, count), slice(count, 2 * count)
    layout = grads_layout(second_t.shape[0], outs[0].shape[0])
    for k in range(4):
        d_up = dot(second_t[...], d_pres[k, own]) + dot(second_other_t[...], d_pres[k, other])
        d_down = dot_tn(hiddens[k, own], cotangent[...])
        d_down = d_down + dot_tn(hiddens[k, other], cotangent_other[...])
        d_up, d_down = low(d_up), low(d_down)
        for src, dst in layout:
            rows = slice(dst[1], dst[1] + dst[2])
            if dst[0] == "up":
                store_piece(outs, k, src, d_up[rows])
            else:
                store_piece(outs, k, src, d_down[rows, dst[3] : dst[3] + CHUNK])


def grads_layout(width, block):
    shards = block // CHUNK
    up_rows = width // shards
    down_rows = CHUNK // shards
    parts = []
    for s in range(shards):
        base = s * (up_rows + 2 * down_rows)
        parts.append((base, ("up", s * up_rows, up_rows)))
        for side in range(2):
            parts.append(
                (
                    base + up_rows + side * down_rows,
                    ("down", s * down_rows, down_rows, side * CHUNK),
                )
            )
    return parts


def resid_kernel(back_sum, back_other, resid, cotangent, vectors, w_out, attended, inverse, fq_t, *refs):
    d_resid, d_resid_low, d_vectors, d_num, d_den, state = refs
    seqs = state.shape[0]
    length = resid.shape[0] // seqs
    normal, scale = normalize(resid[...])
    grad = back_sum[...] + wide(back_other[...])
    d_vectors[0:1, :] = jnp.sum(grad * normal, axis=0, keepdims=True)
    d_vectors[1:2, :] = jnp.sum(grad, axis=0, keepdims=True)
    d_resid[...] = wide(cotangent[...]) + norm_backward(grad, normal, scale, vectors[2:3, :])
    d_resid_low[...] = low(d_resid[...])
    d_attended = dot_nt(d_resid_low[...], w_out[...])
    shape = (FEAT, FEAT)
    cross = low(
        jnp.where(left_half(shape) != (row_index(shape) < HEAD), -1.0 / HEAD, 0.0)
    )
    for p in range(PAIRS):
        columns = slice(p * FEAT, (p + 1) * FEAT)
        num = d_attended[:, columns] * inverse[:, columns]
        product = num * wide(attended[:, columns])
        top = low(product)
        rest = low(product - wide(top))
        d_num[:, columns] = low(num)
        d_den[:, columns] = low(dot(top, cross) + dot(rest, cross))

    state_sums(state, length, lambda p, here: joined(d_num, d_den, here, p), fq_t)


def joined(d_num, d_den, here, p):
    columns = pl.ds(aligned(p, FEAT), FEAT)
    num, den = d_num[here, columns], d_den[here, columns]
    left = left_half(num.shape)
    return jnp.where(left, num, den), jnp.where(left, den, num)


def softmax_backward(feature, grad):
    plus, minus = wide(feature[:HEAD]), wide(feature[HEAD:])
    d_plus, d_minus = grad[:HEAD], grad[HEAD:]
    d_plus = plus * (d_plus - jnp.sum(d_plus * plus, axis=0, keepdims=True))
    d_minus = minus * (d_minus - jnp.sum(d_minus * minus, axis=0, keepdims=True))
    return low(d_plus - d_minus)


def local_kernel(keyed, fq_t, fk, fk_t, d_num, d_den, *refs):
    priors, (d_uq_t, d_fk_t, d_values) = refs[:-3], refs[-3:]
    seqs = priors[0].shape[0]
    length = keyed.shape[0] // seqs

    def pair(p, carry):
        for b in range(seqs):
            here = slice(b * length, (b + 1) * length)
            values = with_ones(keyed[here, pair_at(VALUES + p)])
            outer = joined(d_num, d_den, here, p)
            states = states_at(priors, b, p)
            found = []
            for side in range(2):
                rows = pl.ds(aligned(2 * p + side, FEAT), FEAT)
                q_t, k_t = fq_t[rows, here], fk_t[rows, here]
                link = dot_nt(outer[side], values[side])
                row, lane = row_index(link.shape), lane_index(link.shape)
                link = low(jnp.where(row >= lane, link, 0.0))
                d_q = dot_nt(k_t, link) + dot_nt(states[side], outer[side])
                d_uq_t[pl.ds(aligned(2 * p + side, HEAD), HEAD), here] = softmax_backward(q_t, d_q)
                d_fk_t[rows, here] = dot(q_t, link)
                scores = dot(fk[here, rows], q_t)
                scores = low(jnp.where(row <= lane, scores, 0.0))
                found.append(dot(scores, outer[side]))
            left = left_half(found[0].shape)
            d_values[here, pl.ds(aligned(p, FEAT), FEAT)] = jnp.where(left, found[0], found[1])
        return carry

    lax.fori_loop(0, PAIRS, pair, 0)


def mixed_kernel(
    place, queries, keyed, fk, fk_t, maps, d_uq_t, d_fk_t, d_values, d_resid_low, *refs
):
    laters, (d_mixed, d_features, sends, d_uk_t) = refs[:-4], refs[-4:]
    seqs = laters[0].shape[0]
    length = keyed.shape[0] // seqs

    def pair(p, carry):
        for b in range(seqs):
            here = slice(b * length, (b + 1) * length)
            values = with_ones(keyed[here, pair_at(VALUES + p)])
            states = states_at(laters, b, p)
            found = []
            for side in range(2):
                rows = pl.ds(aligned(2 * p + side, FEAT), FEAT)
                d_k = d_fk_t[rows, here] + dot_nt(states[side], values[side])
                d_uk_t[pl.ds(aligned(2 * p + side, HEAD), HEAD), here] = softmax_backward(
                    fk_t[rows, here], d_k
                )
                found.append(dot(fk[here, rows], states[side]))
            left = left_half(found[0].shape)
            total = d_values[here, pl.ds(aligned(p, FEAT), FEAT)] + jnp.where(
                left, found[0], found[1]
            )
            d_mixed[here, pl.ds(aligned(2 * D // FEAT + p, FEAT), FEAT)] = low(total)
        return carry

    lax.fori_loop(0, PAIRS, pair, 0)
    for which, (d_u_t, source) in enumerate(((d_uq_t, queries), (d_uk_t, keyed))):

        def group(g, carry):
            index = which * (D // GROUP) + g
            d_u = d_u_t[pl.ds(aligned(g, GROUP), GROUP), :]
            columns = pl.ds(aligned(index, GROUP), GROUP)
            product = dot(d_u, source[:, pl.ds(aligned(g, GROUP), GROUP)]).T
            for a in range(4):
                block = slice(a * HEAD, (a + 1) * HEAD)
                rows = pl.ds(aligned(g * 4 + a, HEAD), HEAD)
                d_features[rows, which * HEAD : (which + 1) * HEAD] = product[block, block]
            d_mixed[:, columns] = low(dot(d_u.T, maps[index]))
            return carry

        lax.fori_loop(0, D // GROUP, group, 0)
    for i in range(PIECES // 2):
        block = place[0] ^ (2 * i + 1)

        @pl.when(block < QKV_BLOCKS)
        def _():
            sends[i] = d_mixed[:, chunk_at(block)]

        @pl.when(block >= QKV_BLOCKS)
        def _():
            sends[i] = d_resid_low[:, chunk_at(block - QKV_BLOCKS)]


def in_grads_kernel(
    place, normed_t, normed_other_t, attended, attended_other, d_mixed, d_resid_low, received, *outs
):
    for i in range(PIECES // 2):
        block = place[0] ^ (2 * i)

        def store(value):
            half = outs[3].shape[0]
            value = low(value)
            store_piece(outs, i, 0, value[:half])
            store_piece(outs, i, half, value[half:])

        @pl.when(block < QKV_BLOCKS)
        def _():
            own = dot(normed_t[...], d_mixed[:, chunk_at(block)])
            store(own + dot(normed_other_t[...], received[i]))

        @pl.when(block >= QKV_BLOCKS)
        def _():
            own = dot_tn(attended[...], d_resid_low[:, chunk_at(block - QKV_BLOCKS)])
            store(own + dot_tn(attended_other[...], received[i]))


def input_kernel(place, tokens, vectors, d_mixed, d_resid, out_sum, out_other, *refs):
    pieces = refs[:PIECES]
    block_out, grad_tokens, d_vectors, total = refs[PIECES:]
    total[...] = jnp.zeros_like(total)
    block_out[...] = low(out_sum[...] + wide(out_other[...]))

    def add(index, weight):
        total[...] += dot_nt(d_mixed[:, chunk_at(index)], weight[...])

    each_piece(place, pieces, 0, QKV_BLOCKS, add)
    normal, scale = normalize(wide(tokens[...]))
    grad = total[...]
    d_vectors[0:1, :] = jnp.sum(grad * normal, axis=0, keepdims=True)
    d_vectors[1:2, :] = jnp.sum(grad, axis=0, keepdims=True)
    grad_tokens[...] = low(d_resid[...] + norm_backward(grad, normal, scale, vectors[0:1, :]))


def lay_in_kernel(place, *refs):
    pieces, (qkv, out) = refs[:PIECES], refs[PIECES:]
    for k in range(PIECES):
        block = place[0] ^ k

        @pl.when(block < QKV_BLOCKS)
        def _():
            qkv[:, pl.ds(aligned(block, CHUNK), CHUNK)] = wide(pieces[k][...])

        @pl.when(block >= QKV_BLOCKS)
        def _():
            out[:, pl.ds(aligned(block - QKV_BLOCKS, CHUNK), CHUNK)] = wide(pieces[k][...])


def lay_mlp_kernel(place, *refs):
    pieces, (up, down, ordered) = refs[:PIECES], refs[PIECES:]
    up_rows, down_rows = ordered.shape[1], down.shape[1]
    for k in range(PIECES):
        block = place[0] ^ k
        ordered[block] = pieces[k][:up_rows, :]
        for side in range(2):
            start = up_rows + side * down_rows
            down[block, :, side * CHUNK : (side + 1) * CHUNK] = wide(
                pieces[k][start : start + down_rows, :]
            )
    for s in range(CHUNK // down_rows):
        columns = slice(s * down_rows, (s + 1) * down_rows)
        row = jnp.concatenate([ordered[r][:, columns] for r in range(PIECES)], axis=1)
        up[:, s * PIECES * down_rows : (s + 1) * PIECES * down_rows] = wide(row)


def whole(shape, dtype=low_type):
    return jax.ShapeDtypeStruct(shape, dtype)


def scalar_first(count):
    return [pl.BlockSpec(memory_space=pltpu.SMEM)] + [
        pl.BlockSpec(memory_space=pltpu.VMEM) for _ in range(count)
    ]


def call(kernel, weight, out_shape, in_specs=None, scratch=(), limit=16, **rest):
    if in_specs is not None:
        rest["in_specs"] = in_specs
    return pl.pallas_call(
        kernel,
        out_shape=out_shape,
        scratch_shapes=list(scratch),
        compiler_params=pltpu.CompilerParams(vmem_limit_bytes=limit << 20),
        cost_estimate=pl.CostEstimate(
            flops=weight * 10**9, transcendentals=0, bytes_accessed=weight * 3 * 10**6
        ),
        **rest,
    )


def interleave(even, odd):
    return [part for both in zip(even, odd) for part in both]


def shards(
    tokens,
    gain_attn,
    bias_attn,
    w_qkv,
    w_feature,
    w_out,
    gain_mlp,
    bias_mlp,
    w_up,
    w_down,
    cotangent,
):
    shard_count = lax.axis_size("shard")
    place = lax.axis_index("rep") % PIECES
    spot = place.reshape(1).astype(jnp.int32)
    seqs, length, _ = tokens.shape
    count = seqs * length
    rows = w_qkv.shape[0]
    fine = CHUNK // shard_count
    flat = tokens.reshape(count, D)
    flat_cotangent = cotangent.reshape(count, D)
    anywhere = [pl.BlockSpec(memory_space=pl.ANY)] * PIECES

    part_in = lax.dynamic_slice_in_dim(
        jnp.concatenate([w_qkv, w_out], axis=1), place * CHUNK, CHUNK, 1
    )
    vectors = jnp.concatenate([gain_attn, bias_attn, gain_mlp, bias_mlp]).reshape(-1, FEAT)
    small = jnp.concatenate([w_feature, vectors], axis=0)
    part_up = lax.dynamic_index_in_dim(
        w_up.reshape(rows, shard_count, PIECES, fine), place, 2, False
    ).reshape(rows, CHUNK)
    part_down = lax.dynamic_slice_in_dim(w_down, place * fine, fine, 0)
    part_mlp = jnp.concatenate([part_up, part_down[:, :CHUNK], part_down[:, CHUNK:]], axis=0)

    in_full = around(part_in)
    small = around(small)
    cotangent_other = flip(flat_cotangent, 1)
    feature_weight = small[:, :rows].reshape(D, FEAT)
    vectors = wide(small[:, rows:].reshape(shard_count, 4, rows).transpose(1, 0, 2).reshape(4, D))
    blocks = feature_weight.reshape(D // GROUP, 4, HEAD, 2, HEAD)
    maps = (
        jnp.einsum("gaiwo,ab->wgaobi", blocks, jnp.eye(4, dtype=low_type))
        .reshape(2 * D // GROUP, GROUP, GROUP)
        .astype(low_type)
    )
    in_full = in_full.reshape(-1, CHUNK)
    in_full, part_mlp = lax.optimization_barrier((in_full, part_mlp))
    from_x, from_y = sides_of(in_full)
    in_other = flip(in_full, 1)
    steps = list(range(1, shard_count))
    soon = {step: spin(part_mlp, step) for step in steps[:1] + steps[2:]}
    in_halves, maps, vectors, soon, part_mlp = lax.optimization_barrier(
        (halves_of(from_x, from_y), maps, vectors, soon, part_mlp)
    )
    in_even = [in_full, from_x, from_y, diagonal_of(in_halves)]
    in_pieces = interleave(in_even, [in_other] + [flip(part, 1) for part in in_even[1:]])
    soon.update({step: spin(part_mlp, step) for step in steps[1:2]})
    here = lax.axis_index("shard")
    mlp_parts = [part_mlp[None]] + [soon[step][None] for step in steps]
    mlp_slots = [(here - step) % shard_count for step in range(shard_count)]

    normed, normed_t, queries, keyed, fk, fk_t, key_state, out_weight = call(
        keys_kernel,
        9,
        (
            whole((count, D)),
            whole((D, count)),
            whole((count, D)),
            whole((count, 2 * D)),
            whole((count, HEADS * FEAT)),
            whole((HEADS * FEAT, count)),
            whole((seqs, SLAB, FEAT)),
            whole((D, D)),
        ),
        scalar_first(3 + PIECES),
    )(spot, flat, vectors, maps, *in_pieces)
    prior, running = scan_first(key_state, 1)
    mlp_parts, queries = lax.optimization_barrier((mlp_parts, queries))
    mlp_full = place_parts(mlp_parts, mlp_slots).reshape(-1, CHUNK)
    mlp_full, queries = lax.optimization_barrier((mlp_full, queries))
    mlp_x, mlp_y = sides_of(mlp_full)
    fq, fq_t, partial = call(
        queries_kernel,
        7,
        (
            whole((count, HEADS * FEAT)),
            whole((HEADS * FEAT, count)),
            whole((seqs, length, HEADS * FEAT), wide_type),
        ),
    )(queries, keyed, fk_t, maps)
    running, partial = lax.optimization_barrier((running, partial))
    priors = scan_rest(prior, running, 1)
    mlp_halves, partial = lax.optimization_barrier((halves_of(mlp_x, mlp_y), partial))
    mlp_pieces = [mlp_full, mlp_x, mlp_y, diagonal_of(mlp_halves)]
    attended, inverse, resid, second, second_t = call(
        attend_kernel,
        5,
        (
            whole((count, D)),
            whole((count, D), wide_type),
            whole((count, D), wide_type),
            whole((count, D)),
            whole((D, count)),
        ),
    )(flat, vectors, partial, fq, out_weight, *priors)

    second_other = flip(second, 1)
    (
        out_sum,
        out_send,
        back_sum,
        back_send,
        hiddens,
        d_pres,
        second_other_t,
    ) = call(
        mlp_kernel,
        20,
        (
            whole((count, D), wide_type),
            whole((count, D)),
            whole((count, D), wide_type),
            whole((count, D)),
            whole((4, 2 * count, CHUNK)),
            whole((4, 2 * count, CHUNK)),
            whole((D, count)),
        ),
        [pl.BlockSpec(memory_space=pltpu.VMEM)] * 5 + anywhere[:4],
        [
            pltpu.VMEM((count, D), wide_type),
            pltpu.VMEM((count, D), wide_type),
            pltpu.VMEM((4, D, CHUNK), low_type),
            pltpu.VMEM((4, CHUNK, D), low_type),
            pltpu.SemaphoreType.DMA((4, 3 * shard_count)),
        ],
    )(second, second_other, flat_cotangent, cotangent_other, resid, *mlp_pieces)
    back_other = flip(back_send, 1)
    out_other = flip(out_send, 1)
    d_resid, d_resid_low, d_vectors_two, d_num, d_den, query_state = call(
        resid_kernel,
        5,
        (
            whole((count, D), wide_type),
            whole((count, D)),
            whole((2, D), wide_type),
            whole((count, D)),
            whole((count, D)),
            whole((seqs, SLAB, FEAT)),
        ),
    )(back_sum, back_other, resid, flat_cotangent, vectors, out_weight, attended, inverse, fq_t)
    later, running = scan_first(query_state, -1)
    normed_other_t = flip(normed_t, 1)
    attended_other = flip(attended, 1)
    second_t, query_state, normed_other_t, attended_other = lax.optimization_barrier(
        (second_t, query_state, normed_other_t, attended_other)
    )
    piece = lambda rows: tuple(
        whole((size, CHUNK)) for size in (rows, rows, rows, rows // 2, rows // 2)
    )
    mlp_grads = call(mlp_grads_kernel, 7, piece(2 * D))(
        second_t, second_other_t, flat_cotangent, cotangent_other, hiddens, d_pres
    )
    mlp_upper, mlp_lower, running, fk = lax.optimization_barrier(
        (mlp_grads[3], mlp_grads[4], running, fk)
    )
    laters = scan_rest(later, running, -1)
    mlp_to_x, mlp_to_y = flip(mlp_upper, 4), flip(mlp_lower, 2)
    d_uq_t, d_fk_t, d_values = call(
        local_kernel,
        10,
        (
            whole((D, count)),
            whole((HEADS * FEAT, count), wide_type),
            whole((count, D), wide_type),
        ),
    )(keyed, fq_t, fk, fk_t, d_num, d_den, *priors)
    add_sides = lambda parts, to_x, to_y: call(
        sides_kernel, 1, (whole(parts[1].shape), whole(parts[1].shape))
    )(parts[1], parts[2], to_x, to_y)
    mlp_sides = add_sides(mlp_grads, mlp_to_x, mlp_to_y)
    mlp_sides, d_uq_t = lax.optimization_barrier((mlp_sides, d_uq_t))
    mlp_joined = [flip(mlp_sides[0], 2), flip(mlp_sides[1], 4)]
    d_mixed, d_features, sends, _ = call(
        mixed_kernel,
        7,
        (
            whole((count, 3 * D)),
            whole((D, FEAT), wide_type),
            whole((PIECES // 2, count, CHUNK)),
            whole((D, count)),
        ),
        scalar_first(9 + len(laters)),
    )(spot, queries, keyed, fk, fk_t, maps, d_uq_t, d_fk_t, d_values, d_resid_low, *laters)
    received = flip(sends, 1)
    block_out, grad_tokens, d_vectors_one = call(
        input_kernel,
        8,
        (whole((count, D)), whole((count, D)), whole((2, D), wide_type)),
        scalar_first(6 + PIECES),
        [pltpu.VMEM((count, D), wide_type)],
    )(spot, flat, vectors, d_mixed, d_resid, out_sum, out_other, *in_pieces)
    received, d_vectors_one, d_mixed = lax.optimization_barrier((received, d_vectors_one, d_mixed))
    in_grads = call(in_grads_kernel, 7, piece(D), scalar_first(7))(
        spot, normed_t, normed_other_t, attended, attended_other, d_mixed, d_resid_low, received
    )
    in_to_x, in_to_y = flip(in_grads[3], 4), flip(in_grads[4], 2)
    in_sides = add_sides(in_grads, in_to_x, in_to_y)
    in_sides, mlp_joined = lax.optimization_barrier((in_sides, mlp_joined))
    in_joined = [flip(in_sides[0], 2), flip(in_sides[1], 4)]
    mlp_total = settle(*join_parts([mlp_grads[0], *mlp_joined]))
    mlp_sums = interleave(*spread(mlp_total))
    in_total = settle(*join_parts([in_grads[0], *in_joined]))
    in_sums = interleave(*spread(in_total))
    grad_qkv, grad_out = call(
        lay_in_kernel,
        2,
        (whole((rows, 3 * D), wide_type), whole((rows, D), wide_type)),
        scalar_first(PIECES),
    )(spot, *in_sums)
    grad_up, grad_down = call(
        lay_mlp_kernel,
        3,
        (whole((rows, 4 * D), wide_type), whole((PIECES, fine, D), wide_type)),
        scalar_first(PIECES),
        [pltpu.VMEM((PIECES, rows, CHUNK), low_type)],
    )(spot, *mlp_sums)
    grad_down = grad_down.reshape(-1, D)

    d_vectors = jnp.concatenate([d_vectors_one, d_vectors_two], axis=0)
    d_vectors = d_vectors.reshape(4, shard_count, rows).transpose(1, 0, 2)
    tiny = jnp.concatenate(
        [d_features.reshape(shard_count, rows, FEAT), d_vectors.reshape(shard_count, -1, FEAT)],
        axis=1,
    ).reshape(-1, FEAT)
    bit = 1
    while bit < lax.axis_size("rep"):
        tiny = tiny + wide(flip(low(tiny), bit))
        bit *= 2
    tiny = scatter_shards(tiny)
    grad_feature = tiny[:rows]
    d_vectors = tiny[rows:].reshape(4, rows)
    return (
        block_out.reshape(tokens.shape),
        grad_tokens.reshape(tokens.shape),
        d_vectors[0],
        d_vectors[1],
        grad_qkv,
        grad_feature,
        grad_out,
        d_vectors[2],
        d_vectors[3],
        grad_up,
        grad_down,
    )


def solution(mesh):
    placed = (
        P("rep", "shard", None),
        P("shard"),
        P("shard"),
        P("shard", None),
        P("shard", None),
        P("shard", None),
        P("shard"),
        P("shard"),
        P("shard", None),
        P("shard", None),
        P("rep", "shard", None),
    )
    return jax.shard_map(
        shards,
        mesh=mesh,
        in_specs=placed,
        out_specs=(
            P("rep", "shard", None),
            P("rep", "shard", None),
            P("shard"),
            P("shard"),
            P("shard", None),
            P("shard", None),
            P("shard", None),
            P("shard"),
            P("shard"),
            P("shard", None),
            P("shard", None),
        ),
        check_vma=False,
    )
```

```python
import jax
import jax.numpy as jnp
from jax import lax
from jax.experimental import pallas as pl
from jax.experimental.pallas import tpu as pltpu
from jax.sharding import PartitionSpec as P

D = 768
HEADS = 12
HEAD = 64
FEAT = 128
PAIRS = HEADS // 2
GROUP = 4 * HEAD
PIECES = 8
CHUNK = 4 * D // PIECES
QKV_BLOCKS = 3 * D // CHUNK
SLAB = (PAIRS + 1) * FEAT

norm_epsilon = 1e-05
low_type = jnp.bfloat16
wide_type = jnp.float32


def flip(value, bit):
    count = lax.axis_size("rep")
    return lax.ppermute(value, "rep", [(i, i ^ bit) for i in range(count)])


def spin(value, step):
    count = lax.axis_size("shard")
    return lax.ppermute(value, "shard", [(i, (i + step) % count) for i in range(count)])


def slide(value, step):
    count = lax.axis_size("shard")
    pairs = [(i, i + step) for i in range(count) if 0 <= i + step < count]
    return lax.ppermute(value, "shard", pairs)


def wide(value):
    return value.astype(wide_type)


def low(value):
    return value.astype(low_type)


def place_kernel(slots, *refs):
    parts, full = refs[:-1], refs[-1]
    for i, part in enumerate(parts):
        size = part.shape[0]
        full[pl.ds(slots[i] * size, size)] = part[...]


def place_parts(parts, slots):
    shape = (len(parts) * parts[0].shape[0],) + parts[0].shape[1:]
    slots = jnp.stack([jnp.asarray(slot, jnp.int32) for slot in slots])
    return call(place_kernel, 1, whole(shape, parts[0].dtype), scalar_first(len(parts)))(
        slots, *parts
    )


def around_parts(part):
    count, here = lax.axis_size("shard"), lax.axis_index("shard")
    parts = [part[None]] + [spin(part, step)[None] for step in range(1, count)]
    return parts, [(here - step) % count for step in range(count)]


def around(part):
    return place_parts(*around_parts(part))


def scan_first(state, direction):
    received = slide(state, direction)
    return received, low(wide(state) + wide(received))


def scan_rest(received, running, direction):
    found, step = [received], 2
    while step < lax.axis_size("shard"):
        found.append(slide(running, direction * step))
        running = low(wide(running) + wide(found[-1]))
        step *= 2
    return found


def sides_of(own):
    return flip(own, 2), flip(own, 4)


def halves_of(from_x, from_y):
    half = from_x.shape[0] // 2
    return from_x[:half], from_y[half:]


def diagonal_of(halves):
    return jnp.concatenate([flip(halves[0], 4), flip(halves[1], 2)], axis=0)


def share(own):
    parts = [own[None]] + [flip(own, bit)[None] for bit in (2, 4, 6)]
    even = place_parts(parts, [0, 1, 2, 3])
    return even, flip(even, 1)


def sides_kernel(x_part, y_part, to_x, to_y, x_sum, y_sum):
    half = to_x.shape[0]
    x_sum[:half] = low(wide(x_part[:half]) + wide(to_x[...]))
    x_sum[half:] = x_part[half:]
    y_sum[:half] = y_part[:half]
    y_sum[half:] = low(wide(y_part[half:]) + wide(to_y[...]))


def join_parts(parts):
    count, here = lax.axis_size("shard"), lax.axis_index("shard")
    bit = PIECES
    if bit < lax.axis_size("rep"):
        mine = sum(wide(part) for part in parts)
        while bit < lax.axis_size("rep"):
            mine = mine + wide(flip(low(mine), bit))
            bit *= 2
        parts = [mine]
    rows, columns = parts[0].shape
    rows //= count

    def kernel(spot, *refs):
        sources, outs = refs[: len(parts)], refs[len(parts) :]
        for step in range(count):
            block = lax.rem(spot[0] + step, count)
            chosen = pl.ds(pl.multiple_of(block * rows, rows), rows)
            total = wide(sources[0][chosen, :])
            for source in sources[1:]:
                total = total + wide(source[chosen, :])
            outs[step][...] = total if step == 0 else low(total)

    shapes = [whole((rows, columns), wide_type)] + [whole((rows, columns))] * (count - 1)
    return call(kernel, 2, tuple(shapes), scalar_first(len(parts)))(
        here.reshape(1).astype(jnp.int32), *parts
    )


def settle(own, received):
    def kernel(own, *refs):
        total = own[...]
        for ref in refs[:-1]:
            total = total + wide(ref[...])
        refs[-1][...] = low(total)

    return call(kernel, 1, whole(own.shape))(own, *received)


def dot(a, b):
    return jnp.dot(a, b, preferred_element_type=wide_type)


def dot_nt(a, b):
    return lax.dot_general(a, b, (((1,), (1,)), ((), ())), preferred_element_type=wide_type)


def dot_tn(a, b):
    return lax.dot_general(a, b, (((0,), (0,)), ((), ())), preferred_element_type=wide_type)


def normalize(rows):
    centred = rows - jnp.mean(rows, axis=-1, keepdims=True)
    scale = lax.rsqrt(jnp.mean(centred * centred, axis=-1, keepdims=True) + norm_epsilon)
    return centred * scale, scale


def norm_backward(grad, normal, scale, gain):
    e = grad * gain
    return scale * (
        e
        - jnp.mean(e, axis=-1, keepdims=True)
        - normal * jnp.mean(e * normal, axis=-1, keepdims=True)
    )


def lane_index(shape):
    return lax.broadcasted_iota(jnp.int32, shape, len(shape) - 1)


def row_index(shape):
    return lax.broadcasted_iota(jnp.int32, shape, len(shape) - 2)


def left_half(shape):
    return lane_index(shape) < HEAD


def aligned(index, unit):
    return pl.multiple_of(index * unit, unit)


def with_ones(pair):
    left = left_half(pair.shape)
    one = jnp.ones_like(pair)
    return jnp.where(left, pair, one), jnp.where(left, one, pair)


def pack_state(even, odd, p):
    lane = lane_index(even.shape)
    packed = jnp.where(lane < HEAD, even, odd)
    sums = jnp.where(lane == HEAD + 2 * p, even, jnp.where(lane == 2 * p + 1, odd, 0.0))
    return packed, sums


def unpack_state(packed, sums, p):
    shape = packed.shape
    lane, row = lane_index(shape), row_index(shape)
    pick_even = low(jnp.where((row == HEAD + 2 * p) & (lane >= HEAD), 1.0, 0.0))
    pick_odd = low(jnp.where((row == 2 * p + 1) & (lane < HEAD), 1.0, 0.0))
    even = jnp.where(lane < HEAD, packed, dot(sums, pick_even))
    odd = jnp.where(lane < HEAD, dot(sums, pick_odd), packed)
    return low(even), low(odd)


def added(refs, b, rows):
    total = wide(refs[0][b, rows, :])
    for ref in refs[1:]:
        total = total + wide(ref[b, rows, :])
    return total


def states_at(refs, b, p):
    packed = added(refs, b, pl.ds(aligned(p, FEAT), FEAT))
    sums = low(added(refs, b, slice(PAIRS * FEAT, SLAB)))
    return unpack_state(packed, sums, p)


def features(maps, base, columns, f_t, f):
    def group(g, carry):
        u_t = dot_nt(maps[base + g], columns[:, pl.ds(aligned(g, GROUP), GROUP)])
        for a in range(4):
            u = u_t[a * HEAD : (a + 1) * HEAD]
            up = jnp.exp(u - jnp.max(u, axis=0, keepdims=True))
            down = jnp.exp(jnp.min(u, axis=0, keepdims=True) - u)
            plus = up / jnp.sum(up, axis=0, keepdims=True)
            minus = down / jnp.sum(down, axis=0, keepdims=True)
            feature = low(jnp.concatenate([plus, minus], axis=0))
            rows = pl.ds(aligned(g * 4 + a, FEAT), FEAT)
            f_t[rows, :] = feature
            f[:, rows] = feature.T
        return carry

    lax.fori_loop(0, D // GROUP, group, 0)


def wanted(place, k, first, last):
    block = place[0] ^ k
    return block, (block >= first) & (block < last)


def each_piece(place, pieces, first, last, work):
    for k in range(PIECES):
        block, use = wanted(place, k, first, last)

        @pl.when(use)
        def _():
            work(block - first, pieces[k])


def chunk_at(index):
    return pl.ds(aligned(index, CHUNK), CHUNK)


def pair_at(index):
    return pl.ds(aligned(index, FEAT), FEAT)


VALUES = D // FEAT
QUERY_BLOCKS = D // CHUNK


def copy_rows(source, target):
    def step(i, carry):
        rows = pl.ds(aligned(i, 2 * HEAD), 2 * HEAD)
        target[rows, :] = source[rows, :]
        return carry

    lax.fori_loop(0, source.shape[0] // (2 * HEAD), step, 0)


def keys_kernel(place, tokens, vectors, maps, *refs):
    pieces = refs[:PIECES]
    normed, keyed, fk, fk_t, state, w_kv = refs[PIECES:]
    seqs = state.shape[0]
    length = tokens.shape[0] // seqs
    normal, _ = normalize(wide(tokens[...]))
    normed[...] = low(normal * vectors[0:1, :] + vectors[1:2, :])

    def keep(index, weight):
        copy_rows(weight, w_kv.at[index])

    each_piece(place, pieces, QUERY_BLOCKS, QKV_BLOCKS, keep)

    def project(index, carry):
        keyed[:, chunk_at(index)] = low(dot(normed[...], w_kv[index]))
        return carry

    lax.fori_loop(0, QKV_BLOCKS - QUERY_BLOCKS, project, 0)
    features(maps, D // GROUP, keyed, fk_t, fk)
    state_sums(state, length, lambda p, here: with_ones(keyed[here, pair_at(VALUES + p)]), fk_t)


def state_sums(state, length, sides, f_t):
    seqs = state.shape[0]

    def pair(p, sums):
        result = []
        for b in range(seqs):
            here = slice(b * length, (b + 1) * length)
            first, second = sides(p, here)
            even = dot(f_t[pair_at(2 * p), here], first)
            odd = dot(f_t[pair_at(2 * p + 1), here], second)
            packed, new = pack_state(even, odd, p)
            state[b, pair_at(p), :] = low(packed)
            result.append(sums[b] + new)
        return tuple(result)

    empty = tuple(jnp.zeros((FEAT, FEAT), wide_type) for _ in range(seqs))
    sums = lax.fori_loop(0, PAIRS, pair, empty)
    for b in range(seqs):
        state[b, PAIRS * FEAT :, :] = low(sums[b])


def queries_kernel(place, normed, keyed, fk_t, maps, *refs):
    pieces = refs[:PIECES]
    normed_t, queries, fq, fq_t, partial, w_out, w_q = refs[PIECES:]

    def keep(index, weight):
        copy_rows(weight, w_q.at[index])

    def keep_out(index, weight):
        copy_rows(weight, w_out.at[:, chunk_at(index)])

    each_piece(place, pieces, 0, QUERY_BLOCKS, keep)
    each_piece(place, pieces, QKV_BLOCKS, PIECES, keep_out)

    def project(index, carry):
        queries[:, chunk_at(index)] = low(dot(normed[...], w_q[index]))
        return carry

    lax.fori_loop(0, QUERY_BLOCKS, project, 0)
    normed_t[...] = normed[...].T
    features(maps, 0, queries, fq_t, fq)
    seqs, length, _ = partial.shape

    def pair(p, carry):
        for b in range(seqs):
            here = slice(b * length, (b + 1) * length)
            values = with_ones(keyed[here, pair_at(VALUES + p)])
            for side in range(2):
                rows = pair_at(2 * p + side)
                scores = dot(fq[here, rows], fk_t[rows, here])
                scores = jnp.where(row_index(scores.shape) >= lane_index(scores.shape), scores, 0.0)
                partial[b, :, rows] = dot(low(scores), values[side])
        return carry

    lax.fori_loop(0, PAIRS, pair, 0)


def attend_kernel(tokens, vectors, partial, fq, w_out, *refs):
    priors, (attended, inverse, resid, second, second_t) = refs[:-5], refs[-5:]
    seqs = priors[0].shape[0]
    length = tokens.shape[0] // seqs

    def pair(p, carry):
        for b in range(seqs):
            here = slice(b * length, (b + 1) * length)
            states = states_at(priors, b, p)
            found = []
            for side in range(2):
                rows = pair_at(2 * p + side)
                found.append(partial[b, :, rows] + dot(fq[here, rows], states[side]))
            left = left_half(found[0].shape)
            turned = [pltpu.roll(a, HEAD, 1) for a in found]
            over = 1.0 / jnp.where(left, turned[0], turned[1])
            attended[here, pair_at(p)] = low(jnp.where(left, found[0], found[1]) * over)
            inverse[here, pair_at(p)] = over
        return carry

    lax.fori_loop(0, PAIRS, pair, 0)
    resid[...] = wide(tokens[...]) + dot(attended[...], w_out[...])
    normal, _ = normalize(resid[...])
    second[...] = low(normal * vectors[2:3, :] + vectors[3:4, :])
    second_t[...] = second[...].T


def mlp_kernel(second, second_other, cotangent, cotangent_other, resid, attended, *refs):
    pieces = refs[:4]
    out_sum, out_send, back_sum, back_send, hiddens, d_pres, second_other_t, attended_t = refs[4:12]
    out_other, back_other, up, down, ready = refs[12:]
    count = second.shape[0]
    parts = grads_layout(second.shape[1], pieces[0].shape[0])

    def copies(k, source):
        listed = []
        for i, (src, dst) in enumerate(parts):
            if dst[0] == "up":
                target = up.at[k, pl.ds(dst[1], dst[2]), :]
            else:
                target = down.at[k, pl.ds(dst[1], dst[2]), pl.ds(dst[3], CHUNK)]
            listed.append(
                pltpu.make_async_copy(source.at[pl.ds(src, dst[2]), :], target, ready.at[k, i])
            )
        return listed

    for k in range(4):
        for copy in copies(k, pieces[k]):
            copy.start()
    out_sum[...] = resid[...]
    for total in (out_other, back_sum, back_other):
        total[...] = jnp.zeros_like(total)
    second_other_t[...] = second_other[...].T
    attended_t[...] = attended[...].T
    sides = (
        (second, cotangent, out_sum, back_sum),
        (second_other, cotangent_other, out_other, back_other),
    )

    def piece(k, carry):
        for copy in copies(k, pieces[0]):
            copy.wait()
        for side, (source, grad, out_total, back_total) in enumerate(sides):
            here = slice(side * count, (side + 1) * count)
            pre = dot(source[...], up[k])
            square = pre * pre
            bent = jnp.tanh(0.7978845608 * (pre + 0.044715 * square * pre))
            half = 0.5 * (1.0 + bent)
            hidden = low(pre * half)
            slope = half + (0.5 * 0.7978845608) * pre * (1.0 - bent * bent) * (
                1.0 + 3.0 * 0.044715 * square
            )
            hiddens[k, here] = hidden
            out_total[...] += dot(hidden, down[k])
            d_pre = low(dot_nt(grad[...], down[k]) * slope)
            d_pres[k, here] = d_pre
            back_total[...] += dot_nt(d_pre, up[k])
        return carry

    lax.fori_loop(0, 4, piece, 0)
    out_send[...] = low(out_other[...])
    back_send[...] = low(back_other[...])


def store_piece(outs, made, k):
    half = outs[3].shape[0]
    for i in range(3):

        @pl.when(k == i)
        def _():
            outs[i][...] = made[...]

    @pl.when(k == 3)
    def _():
        outs[3][...] = made[:half]
        outs[4][...] = made[half:]


def mlp_grads_kernel(second_t, second_other_t, cotangent, cotangent_other, hiddens, d_pres, *refs):
    outs, made = refs[:5], refs[5]
    count = cotangent.shape[0]
    own, other = slice(0, count), slice(count, 2 * count)

    def piece(k, carry):
        d_up = dot(second_t[...], d_pres[k, own]) + dot(second_other_t[...], d_pres[k, other])
        d_down = dot_tn(hiddens[k, own], cotangent[...])
        d_down = d_down + dot_tn(hiddens[k, other], cotangent_other[...])
        d_up, d_down = low(d_up), low(d_down)
        for src, dst in grads_layout(second_t.shape[0], made.shape[0]):
            rows = slice(dst[1], dst[1] + dst[2])
            if dst[0] == "up":
                made[src : src + dst[2], :] = d_up[rows]
            else:
                made[src : src + dst[2], :] = d_down[rows, dst[3] : dst[3] + CHUNK]
        store_piece(outs, made, k)
        return carry

    lax.fori_loop(0, 4, piece, 0)


def grads_layout(width, block):
    shards = block // CHUNK
    up_rows = width // shards
    down_rows = CHUNK // shards
    parts = []
    for s in range(shards):
        base = s * (up_rows + 2 * down_rows)
        parts.append((base, ("up", s * up_rows, up_rows)))
        for side in range(2):
            parts.append(
                (
                    base + up_rows + side * down_rows,
                    ("down", s * down_rows, down_rows, side * CHUNK),
                )
            )
    return parts


def resid_kernel(back_sum, back_other, resid, cotangent, vectors, w_out, attended, inverse, fq_t, *refs):
    d_resid, d_resid_low, d_vectors, d_num, d_den, state = refs
    seqs = state.shape[0]
    length = resid.shape[0] // seqs
    normal, scale = normalize(resid[...])
    grad = back_sum[...] + wide(back_other[...])
    d_vectors[0:1, :] = jnp.sum(grad * normal, axis=0, keepdims=True)
    d_vectors[1:2, :] = jnp.sum(grad, axis=0, keepdims=True)
    d_resid[...] = wide(cotangent[...]) + norm_backward(grad, normal, scale, vectors[2:3, :])
    d_resid_low[...] = low(d_resid[...])
    d_attended = dot_nt(d_resid_low[...], w_out[...])
    shape = (FEAT, FEAT)
    cross = low(
        jnp.where(left_half(shape) != (row_index(shape) < HEAD), -1.0 / HEAD, 0.0)
    )
    for p in range(PAIRS):
        columns = slice(p * FEAT, (p + 1) * FEAT)
        num = d_attended[:, columns] * inverse[:, columns]
        product = num * wide(attended[:, columns])
        top = low(product)
        rest = low(product - wide(top))
        d_num[:, columns] = low(num)
        d_den[:, columns] = low(dot(top, cross) + dot(rest, cross))

    state_sums(state, length, lambda p, here: joined(d_num, d_den, here, p), fq_t)


def joined(d_num, d_den, here, p):
    columns = pl.ds(aligned(p, FEAT), FEAT)
    num, den = d_num[here, columns], d_den[here, columns]
    left = left_half(num.shape)
    return jnp.where(left, num, den), jnp.where(left, den, num)


def softmax_backward(feature, grad):
    plus, minus = wide(feature[:HEAD]), wide(feature[HEAD:])
    d_plus, d_minus = grad[:HEAD], grad[HEAD:]
    d_plus = plus * (d_plus - jnp.sum(d_plus * plus, axis=0, keepdims=True))
    d_minus = minus * (d_minus - jnp.sum(d_minus * minus, axis=0, keepdims=True))
    return low(d_plus - d_minus)


def local_kernel(queries, keyed, maps, fq_t, fk, fk_t, d_num, d_den, *refs):
    priors, (d_fk_t, d_values, d_queries, d_features, d_uq_t) = refs[:-5], refs[-5:]
    seqs = priors[0].shape[0]
    length = keyed.shape[0] // seqs

    def pair(p, carry):
        for b in range(seqs):
            here = slice(b * length, (b + 1) * length)
            values = with_ones(keyed[here, pair_at(VALUES + p)])
            outer = joined(d_num, d_den, here, p)
            states = states_at(priors, b, p)
            found = []
            for side in range(2):
                rows = pl.ds(aligned(2 * p + side, FEAT), FEAT)
                q_t, k_t = fq_t[rows, here], fk_t[rows, here]
                link = dot_nt(outer[side], values[side])
                row, lane = row_index(link.shape), lane_index(link.shape)
                link = low(jnp.where(row >= lane, link, 0.0))
                d_q = dot_nt(k_t, link) + dot_nt(states[side], outer[side])
                d_uq_t[pl.ds(aligned(2 * p + side, HEAD), HEAD), here] = softmax_backward(q_t, d_q)
                d_fk_t[rows, here] = dot(q_t, link)
                scores = dot(fk[here, rows], q_t)
                scores = low(jnp.where(row <= lane, scores, 0.0))
                found.append(dot(scores, outer[side]))
            left = left_half(found[0].shape)
            d_values[here, pl.ds(aligned(p, FEAT), FEAT)] = jnp.where(left, found[0], found[1])
        return carry

    lax.fori_loop(0, PAIRS, pair, 0)
    feature_backward(d_uq_t, queries, maps, 0, d_queries, d_features, 0)


def feature_backward(d_u_t, source, maps, base, target, d_features, lane):
    def group(g, carry):
        d_u = d_u_t[pl.ds(aligned(g, GROUP), GROUP), :]
        columns = pl.ds(aligned(g, GROUP), GROUP)
        product = dot(d_u, source[:, columns]).T
        for a in range(4):
            block = slice(a * HEAD, (a + 1) * HEAD)
            rows = pl.ds(aligned(g * 4 + a, HEAD), HEAD)
            d_features[rows, lane : lane + HEAD] = product[block, block]
        target[:, columns] = low(dot(d_u.T, maps[base + g]))
        return carry

    lax.fori_loop(0, D // GROUP, group, 0)


def mixed_kernel(
    place, keyed, fk, fk_t, maps, d_fk_t, d_values, d_resid_low, d_queries, d_half, *refs
):
    laters, (d_keyed, d_features, sends, d_uk_t) = refs[:-4], refs[-4:]
    seqs = laters[0].shape[0]
    length = keyed.shape[0] // seqs

    def pair(p, carry):
        for b in range(seqs):
            here = slice(b * length, (b + 1) * length)
            values = with_ones(keyed[here, pair_at(VALUES + p)])
            states = states_at(laters, b, p)
            found = []
            for side in range(2):
                rows = pl.ds(aligned(2 * p + side, FEAT), FEAT)
                d_k = d_fk_t[rows, here] + dot_nt(states[side], values[side])
                d_uk_t[pl.ds(aligned(2 * p + side, HEAD), HEAD), here] = softmax_backward(
                    fk_t[rows, here], d_k
                )
                found.append(dot(fk[here, rows], states[side]))
            left = left_half(found[0].shape)
            total = d_values[here, pl.ds(aligned(p, FEAT), FEAT)] + jnp.where(
                left, found[0], found[1]
            )
            d_keyed[here, pair_at(VALUES + p)] = low(total)
        return carry

    lax.fori_loop(0, PAIRS, pair, 0)
    feature_backward(d_uk_t, keyed, maps, D // GROUP, d_keyed, d_features, HEAD)
    d_features[:, :HEAD] = d_half[:, :HEAD]

    def send(i, carry):
        own_column(place[0] ^ (2 * i + 1), sends.at[i], d_queries, d_keyed, d_resid_low)
        return carry

    lax.fori_loop(0, PIECES // 2, send, 0)


def own_column(block, target, d_queries, d_keyed, d_resid_low):
    @pl.when(block < QUERY_BLOCKS)
    def _():
        target[...] = d_queries[:, chunk_at(block)]

    @pl.when((block >= QUERY_BLOCKS) & (block < QKV_BLOCKS))
    def _():
        target[...] = d_keyed[:, chunk_at(block - QUERY_BLOCKS)]

    @pl.when(block >= QKV_BLOCKS)
    def _():
        target[...] = d_resid_low[:, chunk_at(block - QKV_BLOCKS)]


TINY_ROWS = 48
TINY_TILE = 16


def tiny_size(rows):
    return -(-(rows + 8) // TINY_ROWS) * TINY_ROWS


def in_grads_kernel(
    place, d_queries, d_keyed, d_resid_low, received, tiny, tiny_other, *refs
):
    sources, outs, (held, column, made, ready) = refs[:4], refs[4:9], refs[9:]
    shard_count, size, _ = tiny.shape
    rows = D // shard_count
    copies = [
        pltpu.make_async_copy(source, held.at[i], ready.at[i]) for i, source in enumerate(sources)
    ]
    for copy in copies:
        copy.start()
    for copy in copies:
        copy.wait()

    def piece(i, carry):
        block = place[0] ^ (2 * i)
        kind = 2 * jnp.where(block < QKV_BLOCKS, 0, 1)
        own_column(block, column, d_queries, d_keyed, d_resid_low)
        value = low(dot(held[kind], column[...]) + dot(held[kind + 1], received[i]))
        for s in range(shard_count):
            base = s * (rows + TINY_TILE)
            made[base : base + rows, :] = value[s * rows : (s + 1) * rows]
            for j in range(TINY_ROWS // TINY_TILE):
                target = (slice(base + rows, base + rows + TINY_TILE), slice(j * FEAT, (j + 1) * FEAT))
                made[target] = jnp.zeros((TINY_TILE, FEAT), low_type)

                @pl.when(block < size // TINY_ROWS)
                def _():
                    start = pl.multiple_of(block * TINY_ROWS + j * TINY_TILE, TINY_TILE)
                    spot = pl.ds(start, TINY_TILE)
                    made[target] = low(wide(tiny[s, spot, :]) + wide(tiny_other[s, spot, :]))

        store_piece(outs, made, i)
        return carry

    lax.fori_loop(0, PIECES // 2, piece, 0)


def input_kernel(tokens, vectors, d_queries, d_keyed, d_resid, out_sum, out_other, *refs):
    w_q, w_kv, d_features, d_vectors, block_out, grad_tokens, tiny, total = refs
    total[...] = jnp.zeros_like(total)
    block_out[...] = low(out_sum[...] + wide(out_other[...]))

    def add_from(source, weights):
        def add(index, carry):
            total[...] += dot_nt(source[:, chunk_at(index)], weights[index])
            return carry

        lax.fori_loop(0, weights.shape[0], add, 0)

    add_from(d_queries, w_q)
    add_from(d_keyed, w_kv)
    normal, scale = normalize(wide(tokens[...]))
    grad = total[...]
    grad_tokens[...] = low(d_resid[...] + norm_backward(grad, normal, scale, vectors[0:1, :]))
    gathered = [
        jnp.sum(grad * normal, axis=0, keepdims=True),
        jnp.sum(grad, axis=0, keepdims=True),
        d_vectors[0:1, :],
        d_vectors[1:2, :],
    ]
    shard_count, size, _ = tiny.shape
    rows = D // shard_count
    tiny[...] = jnp.zeros_like(tiny)
    for s in range(shard_count):
        tiny[s, :rows, :] = low(d_features[s * rows : (s + 1) * rows, :])
        lines = []
        for vector in gathered:
            line = vector[:, s * rows : (s + 1) * rows]
            gap = jnp.zeros((1, 2 * FEAT - rows), wide_type)
            line = jnp.concatenate([line, gap], axis=1)
            lines += [line[:, :FEAT], line[:, FEAT:]]
        tiny[s, rows : rows + 8, :] = low(jnp.concatenate(lines, axis=0))


def lay_in_kernel(place, even, odd, qkv, out, tiny):
    rows = qkv.shape[0]
    for k in range(PIECES):
        block = place[0] ^ k
        piece = (even, odd)[k % 2].at[k // 2]

        @pl.when(block < QKV_BLOCKS)
        def _():
            qkv[:, chunk_at(block)] = wide(piece[:rows])

        @pl.when(block >= QKV_BLOCKS)
        def _():
            out[:, chunk_at(block - QKV_BLOCKS)] = wide(piece[:rows])

        @pl.when(block < tiny.shape[0] // TINY_ROWS)
        def _():
            for j in range(TINY_ROWS // TINY_TILE):
                start = pl.multiple_of(block * TINY_ROWS + j * TINY_TILE, TINY_TILE)
                tiny[pl.ds(start, TINY_TILE), :] = wide(
                    piece[rows:, j * FEAT : (j + 1) * FEAT]
                )


def lay_mlp_kernel(place, even, odd, up, down, ordered):
    up_rows, down_rows = ordered.shape[1], down.shape[1]
    for k in range(PIECES):
        block = place[0] ^ k
        piece = (even, odd)[k % 2]
        ordered[block] = piece[k // 2, :up_rows, :]
        for side in range(2):
            start = up_rows + side * down_rows
            down[block, :, side * CHUNK : (side + 1) * CHUNK] = wide(
                piece[k // 2, start : start + down_rows, :]
            )
    for s in range(CHUNK // down_rows):
        columns = slice(s * down_rows, (s + 1) * down_rows)
        row = jnp.concatenate([ordered[r][:, columns] for r in range(PIECES)], axis=1)
        up[:, s * PIECES * down_rows : (s + 1) * PIECES * down_rows] = wide(row)


def whole(shape, dtype=low_type):
    return jax.ShapeDtypeStruct(shape, dtype)


def scalar_first(count):
    return [pl.BlockSpec(memory_space=pltpu.SMEM)] + [
        pl.BlockSpec(memory_space=pltpu.VMEM) for _ in range(count)
    ]


def call(kernel, weight, out_shape, in_specs=None, scratch=(), limit=8, **rest):
    if in_specs is not None:
        rest["in_specs"] = in_specs
    return pl.pallas_call(
        kernel,
        out_shape=out_shape,
        scratch_shapes=list(scratch),
        compiler_params=pltpu.CompilerParams(vmem_limit_bytes=limit << 20),
        cost_estimate=pl.CostEstimate(
            flops=weight * 2000 * 10**6, transcendentals=0, bytes_accessed=weight * 3 * 2000 * 10**3
        ),
        **rest,
    )


def interleave(even, odd):
    return [part for both in zip(even, odd) for part in both]


def shards(
    tokens,
    gain_attn,
    bias_attn,
    w_qkv,
    w_feature,
    w_out,
    gain_mlp,
    bias_mlp,
    w_up,
    w_down,
    cotangent,
):
    shard_count = lax.axis_size("shard")
    place = lax.axis_index("rep") % PIECES
    spot = place.reshape(1).astype(jnp.int32)
    seqs, length, _ = tokens.shape
    count = seqs * length
    rows = w_qkv.shape[0]
    fine = CHUNK // shard_count
    flat = tokens.reshape(count, D)
    flat_cotangent = cotangent.reshape(count, D)
    anywhere = [pl.BlockSpec(memory_space=pl.ANY)] * PIECES

    part_in = lax.dynamic_slice_in_dim(
        jnp.concatenate([w_qkv, w_out], axis=1), place * CHUNK, CHUNK, 1
    )
    vectors = jnp.concatenate([gain_attn, bias_attn, gain_mlp, bias_mlp]).reshape(-1, FEAT)
    small = jnp.concatenate([w_feature, vectors], axis=0)
    small_rows = -(-small.shape[0] // 24) * 8
    small = jnp.pad(small, ((0, 3 * small_rows - small.shape[0]), (0, 0)))
    small = jnp.concatenate(jnp.split(small, 3, axis=0), axis=1)
    part_in = jnp.concatenate([part_in, small], axis=0)
    part_up = lax.dynamic_index_in_dim(
        w_up.reshape(rows, shard_count, PIECES, fine), place, 2, False
    ).reshape(rows, CHUNK)
    part_down = lax.dynamic_slice_in_dim(w_down, place * fine, fine, 0)
    part_mlp = jnp.concatenate([part_up, part_down[:, :CHUNK], part_down[:, CHUNK:]], axis=0)

    here = lax.axis_index("shard")
    in_slots = jnp.stack([(here - step) % shard_count for step in range(shard_count)])
    in_spins = [part_in] + [spin(part_in, step) for step in range(1, shard_count)]

    def place_in_kernel(slots, *refs):
        parts, (full, rest) = refs[:-2], refs[-2:]
        for i, part in enumerate(parts):
            full[slots[i]] = part[:rows]
            rest[slots[i]] = part[rows:]

    in_full, small = call(
        place_in_kernel,
        1,
        (whole((shard_count, rows, CHUNK)), whole((shard_count, small_rows, CHUNK))),
        scalar_first(shard_count),
    )(in_slots.astype(jnp.int32), *in_spins)
    small = jnp.concatenate(jnp.split(small, 3, axis=2), axis=1)
    cotangent_other = flip(flat_cotangent, 1)
    feature_weight = small[:, :rows].reshape(D, FEAT)
    vectors = wide(small[:, rows : rows + 4 * rows // FEAT].reshape(shard_count, 4, rows).transpose(1, 0, 2).reshape(4, D))
    blocks = feature_weight.reshape(D // GROUP, 4, HEAD, 2, HEAD)
    maps = (
        jnp.einsum("gaiwo,ab->wgaobi", blocks, jnp.eye(4, dtype=low_type))
        .reshape(2 * D // GROUP, GROUP, GROUP)
        .astype(low_type)
    )
    in_full = in_full.reshape(-1, CHUNK)
    steps = list(range(1, shard_count))
    soon = {step: spin(part_mlp, step) for step in steps[:1]}
    in_full, part_mlp, soon = lax.optimization_barrier((in_full, part_mlp, soon))
    from_x, from_y = sides_of(in_full)
    in_other = flip(in_full, 1)
    soon.update({step: spin(part_mlp, step) for step in steps[1:2]})
    in_halves, maps, vectors, soon, part_mlp = lax.optimization_barrier(
        (halves_of(from_x, from_y), maps, vectors, soon, part_mlp)
    )
    soon.update({step: spin(part_mlp, step) for step in steps[2:]})
    diagonal, soon = lax.optimization_barrier((diagonal_of(in_halves), soon))
    in_even = [in_full, from_x, from_y, diagonal]
    in_pieces = interleave(in_even, [in_other] + [flip(part, 1) for part in in_even[1:]])
    here = lax.axis_index("shard")
    mlp_parts = [part_mlp[None]] + [soon[step][None] for step in steps]
    mlp_slots = [(here - step) % shard_count for step in range(shard_count)]

    normed, keyed, fk, fk_t, key_state, w_kv = call(
        keys_kernel,
        8,
        (
            whole((count, D)),
            whole((count, 2 * D)),
            whole((count, HEADS * FEAT)),
            whole((HEADS * FEAT, count)),
            whole((seqs, SLAB, FEAT)),
            whole((QKV_BLOCKS - QUERY_BLOCKS, D, CHUNK)),
        ),
        scalar_first(3 + PIECES),
    )(spot, flat, vectors, maps, *in_pieces)
    prior, running = scan_first(key_state, 1)
    mlp_parts, normed = lax.optimization_barrier((mlp_parts, normed))
    mlp_full = place_parts(mlp_parts, mlp_slots).reshape(-1, CHUNK)
    mlp_full, normed = lax.optimization_barrier((mlp_full, normed))
    mlp_x, mlp_y = sides_of(mlp_full)
    normed_t, queries, fq, fq_t, partial, out_weight, w_q = call(
        queries_kernel,
        9,
        (
            whole((D, count)),
            whole((count, D)),
            whole((count, HEADS * FEAT)),
            whole((HEADS * FEAT, count)),
            whole((seqs, length, HEADS * FEAT), wide_type),
            whole((D, D)),
            whole((QUERY_BLOCKS, D, CHUNK)),
        ),
        scalar_first(4 + PIECES),
    )(spot, normed, keyed, fk_t, maps, *in_pieces)
    running, partial = lax.optimization_barrier((running, partial))
    priors = scan_rest(prior, running, 1)
    mlp_halves, partial = lax.optimization_barrier((halves_of(mlp_x, mlp_y), partial))
    mlp_pieces = [mlp_full, mlp_x, mlp_y, diagonal_of(mlp_halves)]
    attended, inverse, resid, second, second_t = call(
        attend_kernel,
        5,
        (
            whole((count, D)),
            whole((count, D), wide_type),
            whole((count, D), wide_type),
            whole((count, D)),
            whole((D, count)),
        ),
    )(flat, vectors, partial, fq, out_weight, *priors)

    second_other = flip(second, 1)
    (
        out_sum,
        out_send,
        back_sum,
        back_send,
        hiddens,
        d_pres,
        second_other_t,
        attended_t,
    ) = call(
        mlp_kernel,
        20,
        (
            whole((count, D), wide_type),
            whole((count, D)),
            whole((count, D), wide_type),
            whole((count, D)),
            whole((4, 2 * count, CHUNK)),
            whole((4, 2 * count, CHUNK)),
            whole((D, count)),
            whole((D, count)),
        ),
        [pl.BlockSpec(memory_space=pltpu.VMEM)] * 6 + anywhere[:4],
        [
            pltpu.VMEM((count, D), wide_type),
            pltpu.VMEM((count, D), wide_type),
            pltpu.VMEM((4, D, CHUNK), low_type),
            pltpu.VMEM((4, CHUNK, D), low_type),
            pltpu.SemaphoreType.DMA((4, 3 * shard_count)),
        ],
        limit=18,
    )(second, second_other, flat_cotangent, cotangent_other, resid, attended, *mlp_pieces)
    back_other = flip(back_send, 1)
    out_other = flip(out_send, 1)
    d_resid, d_resid_low, d_vectors_two, d_num, d_den, query_state = call(
        resid_kernel,
        5,
        (
            whole((count, D), wide_type),
            whole((count, D)),
            whole((2, D), wide_type),
            whole((count, D)),
            whole((count, D)),
            whole((seqs, SLAB, FEAT)),
        ),
    )(back_sum, back_other, resid, flat_cotangent, vectors, out_weight, attended, inverse, fq_t)
    later, running = scan_first(query_state, -1)
    normed_other_t = flip(normed_t, 1)
    attended_other_t = flip(attended_t, 1)
    second_t, query_state, normed_other_t, attended_other_t, out_other = lax.optimization_barrier(
        (second_t, query_state, normed_other_t, attended_other_t, out_other)
    )
    piece = lambda rows: tuple(
        whole((size, CHUNK)) for size in (rows, rows, rows, rows // 2, rows // 2)
    )
    mlp_grads = call(
        mlp_grads_kernel, 7, piece(2 * D), scratch=[pltpu.VMEM((2 * D, CHUNK), low_type)]
    )(second_t, second_other_t, flat_cotangent, cotangent_other, hiddens, d_pres)
    mlp_upper, mlp_lower, running, fk = lax.optimization_barrier(
        (mlp_grads[3], mlp_grads[4], running, fk)
    )
    laters = scan_rest(later, running, -1)
    mlp_to_x, mlp_to_y = flip(mlp_upper, 4), flip(mlp_lower, 2)
    d_fk_t, d_values, d_queries, d_half, _ = call(
        local_kernel,
        10,
        (
            whole((HEADS * FEAT, count), wide_type),
            whole((count, D), wide_type),
            whole((count, D)),
            whole((D, FEAT), wide_type),
            whole((D, count)),
        ),
    )(queries, keyed, maps, fq_t, fk, fk_t, d_num, d_den, *priors)
    add_sides = lambda parts, to_x, to_y: call(
        sides_kernel, 1, (whole(parts[1].shape), whole(parts[1].shape))
    )(parts[1], parts[2], to_x, to_y)
    mlp_sides = add_sides(mlp_grads, mlp_to_x, mlp_to_y)
    mlp_sides, d_half = lax.optimization_barrier((mlp_sides, d_half))
    mlp_joined = [flip(mlp_sides[0], 2), flip(mlp_sides[1], 4)]
    d_keyed, d_features, sends, _ = call(
        mixed_kernel,
        7,
        (
            whole((count, 2 * D)),
            whole((D, FEAT), wide_type),
            whole((PIECES // 2, count, CHUNK)),
            whole((D, count)),
        ),
        scalar_first(9 + len(laters)),
    )(spot, keyed, fk, fk_t, maps, d_fk_t, d_values, d_resid_low, d_queries, d_half, *laters)
    received = flip(sends, 1)
    block_out, grad_tokens, tiny = call(
        input_kernel,
        7,
        (
            whole((count, D)),
            whole((count, D)),
            whole((shard_count, tiny_size(rows), FEAT)),
        ),
        scratch=[pltpu.VMEM((count, D), wide_type)],
    )(
        flat,
        vectors,
        d_queries,
        d_keyed,
        d_resid,
        out_sum,
        out_other,
        w_q,
        w_kv,
        d_features,
        d_vectors_two,
    )
    tiny_other = flip(tiny, 1)
    mlp_blocks = join_parts([mlp_grads[0], *mlp_joined])
    received, tiny_other, mlp_blocks = lax.optimization_barrier((received, tiny_other, mlp_blocks))
    in_grads = call(
        in_grads_kernel,
        7,
        piece(D + shard_count * TINY_TILE),
        scalar_first(6) + anywhere[:4],
        [
            pltpu.VMEM((4, D, count), low_type),
            pltpu.VMEM((count, CHUNK), low_type),
            pltpu.VMEM((D + shard_count * TINY_TILE, CHUNK), low_type),
            pltpu.SemaphoreType.DMA((4,)),
        ],
    )(
        spot,
        d_queries,
        d_keyed,
        d_resid_low,
        received,
        tiny,
        tiny_other,
        normed_t,
        normed_other_t,
        attended_t,
        attended_other_t,
    )
    in_to_x, in_to_y = flip(in_grads[3], 4), flip(in_grads[4], 2)
    mlp_received = [spin(part, step + 1) for step, part in enumerate(mlp_blocks[1:])]
    in_to_x, in_to_y, mlp_received[:1] = lax.optimization_barrier(
        (in_to_x, in_to_y, mlp_received[:1])
    )
    in_sides = add_sides(in_grads, in_to_x, in_to_y)
    in_joined = [flip(in_sides[0], 2), flip(in_sides[1], 4)]
    in_blocks = join_parts([in_grads[0], *in_joined])
    in_blocks, mlp_received = lax.optimization_barrier((in_blocks, mlp_received))
    mlp_sums = share(settle(mlp_blocks[0], mlp_received))
    in_received = [spin(part, step + 1) for step, part in enumerate(in_blocks[1:])]
    in_sums = share(settle(in_blocks[0], in_received))
    grad_up, grad_down = call(
        lay_mlp_kernel,
        3,
        (whole((rows, 4 * D), wide_type), whole((PIECES, fine, D), wide_type)),
        scalar_first(2),
        [pltpu.VMEM((PIECES, rows, CHUNK), low_type)],
    )(spot, *mlp_sums)
    grad_down = grad_down.reshape(-1, D)
    in_sums, grad_up, grad_down = lax.optimization_barrier((in_sums, grad_up, grad_down))
    grad_qkv, grad_out, tiny = call(
        lay_in_kernel,
        2,
        (
            whole((rows, 3 * D), wide_type),
            whole((rows, D), wide_type),
            whole((tiny_size(rows), FEAT), wide_type),
        ),
        scalar_first(2),
    )(spot, *in_sums)
    grad_feature = tiny[:rows]
    d_vectors = tiny[rows : rows + 8].reshape(4, 2 * FEAT)[:, :rows]
    return (
        block_out.reshape(tokens.shape),
        grad_tokens.reshape(tokens.shape),
        d_vectors[0],
        d_vectors[1],
        grad_qkv,
        grad_feature,
        grad_out,
        d_vectors[2],
        d_vectors[3],
        grad_up,
        grad_down,
    )


def solution(mesh):
    placed = (
        P("rep", "shard", None),
        P("shard"),
        P("shard"),
        P("shard", None),
        P("shard", None),
        P("shard", None),
        P("shard"),
        P("shard"),
        P("shard", None),
        P("shard", None),
        P("rep", "shard", None),
    )
    return jax.shard_map(
        shards,
        mesh=mesh,
        in_specs=placed,
        out_specs=(
            P("rep", "shard", None),
            P("rep", "shard", None),
            P("shard"),
            P("shard"),
            P("shard", None),
            P("shard", None),
            P("shard", None),
            P("shard"),
            P("shard"),
            P("shard", None),
            P("shard", None),
        ),
        check_vma=False,
    )
```

```python
import jax
import jax.numpy as jnp
from jax import lax
from jax.experimental import pallas as pl
from jax.experimental.pallas import tpu as pltpu
from jax.sharding import PartitionSpec as P

D = 768
HEADS = 12
HEAD = 64
FEAT = 128
PAIRS = HEADS // 2
GROUP = 4 * HEAD
PIECES = 8
CHUNK = 4 * D // PIECES
QKV_BLOCKS = 3 * D // CHUNK
SLAB = (PAIRS + 1) * FEAT

norm_epsilon = 1e-05
low_type = jnp.bfloat16
wide_type = jnp.float32


def flip(value, bit):
    count = lax.axis_size("rep")
    return lax.ppermute(value, "rep", [(i, i ^ bit) for i in range(count)])


def spin(value, step):
    count = lax.axis_size("shard")
    return lax.ppermute(value, "shard", [(i, (i + step) % count) for i in range(count)])


def slide(value, step):
    count = lax.axis_size("shard")
    pairs = [(i, i + step) for i in range(count) if 0 <= i + step < count]
    return lax.ppermute(value, "shard", pairs)


def wide(value):
    return value.astype(wide_type)


def low(value):
    return value.astype(low_type)


def place_kernel(slots, *refs):
    parts, full = refs[:-1], refs[-1]
    for i, part in enumerate(parts):
        size = part.shape[0]
        full[pl.ds(slots[i] * size, size)] = part[...]


def place_parts(parts, slots):
    shape = (len(parts) * parts[0].shape[0],) + parts[0].shape[1:]
    slots = jnp.stack([jnp.asarray(slot, jnp.int32) for slot in slots])
    return call(place_kernel, 1, whole(shape, parts[0].dtype), scalar_first(len(parts)))(
        slots, *parts
    )


def around_parts(part):
    count, here = lax.axis_size("shard"), lax.axis_index("shard")
    parts = [part[None]] + [spin(part, step)[None] for step in range(1, count)]
    return parts, [(here - step) % count for step in range(count)]


def around(part):
    return place_parts(*around_parts(part))


def scan_first(state, direction):
    received = slide(state, direction)
    return received, low(wide(state) + wide(received))


def scan_rest(received, running, direction):
    found, step = [received], 2
    while step < lax.axis_size("shard"):
        found.append(slide(running, direction * step))
        running = low(wide(running) + wide(found[-1]))
        step *= 2
    return found


def sides_of(own):
    return flip(own, 2), flip(own, 4)


def halves_of(from_x, from_y):
    half = from_x.shape[0] // 2
    return from_x[:half], from_y[half:]


def diagonal_of(halves):
    return jnp.concatenate([flip(halves[0], 4), flip(halves[1], 2)], axis=0)


def share_flips(own):
    return [own[None]] + [flip(own, bit)[None] for bit in (2, 4, 6)]


def share_pair(parts):
    even = place_parts(parts, [0, 1, 2, 3])
    return even, flip(even, 1)


def sides_kernel(x_part, y_part, to_x, to_y, x_sum, y_sum):
    half = to_x.shape[0]
    x_sum[:half] = low(wide(x_part[:half]) + wide(to_x[...]))
    x_sum[half:] = x_part[half:]
    y_sum[:half] = y_part[:half]
    y_sum[half:] = low(wide(y_part[half:]) + wide(to_y[...]))


def join_parts(parts):
    count, here = lax.axis_size("shard"), lax.axis_index("shard")
    bit = PIECES
    if bit < lax.axis_size("rep"):
        mine = sum(wide(part) for part in parts)
        while bit < lax.axis_size("rep"):
            mine = mine + wide(flip(low(mine), bit))
            bit *= 2
        parts = [mine]
    rows, columns = parts[0].shape
    rows //= count

    def kernel(spot, *refs):
        sources, outs = refs[: len(parts)], refs[len(parts) :]
        for step in range(count):
            block = lax.rem(spot[0] + step, count)
            chosen = pl.ds(pl.multiple_of(block * rows, rows), rows)
            total = wide(sources[0][chosen, :])
            for source in sources[1:]:
                total = total + wide(source[chosen, :])
            outs[step][...] = total if step == 0 else low(total)

    shapes = [whole((rows, columns), wide_type)] + [whole((rows, columns))] * (count - 1)
    return call(kernel, 2, tuple(shapes), scalar_first(len(parts)))(
        here.reshape(1).astype(jnp.int32), *parts
    )


def settle(own, received):
    def kernel(own, *refs):
        total = own[...]
        for ref in refs[:-1]:
            total = total + wide(ref[...])
        refs[-1][...] = low(total)

    return call(kernel, 1, whole(own.shape))(own, *received)


def dot(a, b):
    return jnp.dot(a, b, preferred_element_type=wide_type)


def dot_nt(a, b):
    return lax.dot_general(a, b, (((1,), (1,)), ((), ())), preferred_element_type=wide_type)


def dot_tn(a, b):
    return lax.dot_general(a, b, (((0,), (0,)), ((), ())), preferred_element_type=wide_type)


def normalize(rows):
    centred = rows - jnp.mean(rows, axis=-1, keepdims=True)
    scale = lax.rsqrt(jnp.mean(centred * centred, axis=-1, keepdims=True) + norm_epsilon)
    return centred * scale, scale


def norm_backward(grad, normal, scale, gain):
    e = grad * gain
    return scale * (
        e
        - jnp.mean(e, axis=-1, keepdims=True)
        - normal * jnp.mean(e * normal, axis=-1, keepdims=True)
    )


def lane_index(shape):
    return lax.broadcasted_iota(jnp.int32, shape, len(shape) - 1)


def row_index(shape):
    return lax.broadcasted_iota(jnp.int32, shape, len(shape) - 2)


def left_half(shape):
    return lane_index(shape) < HEAD


def aligned(index, unit):
    return pl.multiple_of(index * unit, unit)


def with_ones(pair):
    left = left_half(pair.shape)
    one = jnp.ones_like(pair)
    return jnp.where(left, pair, one), jnp.where(left, one, pair)


def pack_state(even, odd, p):
    lane = lane_index(even.shape)
    packed = jnp.where(lane < HEAD, even, odd)
    sums = jnp.where(lane == HEAD + 2 * p, even, jnp.where(lane == 2 * p + 1, odd, 0.0))
    return packed, sums


def unpack_state(packed, sums, p):
    shape = packed.shape
    lane, row = lane_index(shape), row_index(shape)
    pick_even = low(jnp.where((row == HEAD + 2 * p) & (lane >= HEAD), 1.0, 0.0))
    pick_odd = low(jnp.where((row == 2 * p + 1) & (lane < HEAD), 1.0, 0.0))
    even = jnp.where(lane < HEAD, packed, dot(sums, pick_even))
    odd = jnp.where(lane < HEAD, dot(sums, pick_odd), packed)
    return low(even), low(odd)


def added(refs, b, rows):
    total = wide(refs[0][b, rows, :])
    for ref in refs[1:]:
        total = total + wide(ref[b, rows, :])
    return total


def states_at(refs, b, p):
    packed = added(refs, b, pl.ds(aligned(p, FEAT), FEAT))
    sums = low(added(refs, b, slice(PAIRS * FEAT, SLAB)))
    return unpack_state(packed, sums, p)


def maps_kernel(small, maps, vectors, weight):
    shard_count, size, _ = small.shape
    rows = D // shard_count
    lines = 4 * rows // FEAT
    for s in range(shard_count):
        for j in range(3):
            count = min(size, rows - j * size)
            if count > 0:
                weight[s * rows + j * size : s * rows + j * size + count, :] = wide(
                    small[s, :count, j * FEAT : (j + 1) * FEAT]
                )
        flat = []
        for line in range(rows, rows + lines):
            j, row = line // size, line % size
            flat.append(wide(small[s, row : row + 1, j * FEAT : (j + 1) * FEAT]))
        flat = jnp.concatenate(flat, axis=1)
        for v in range(4):
            vectors[v : v + 1, s * rows : (s + 1) * rows] = flat[:, v * rows : (v + 1) * rows]
    gap = jnp.zeros((HEAD, HEAD), low_type)
    for head in range(HEADS):
        turned = low(weight[head * HEAD : (head + 1) * HEAD, :].T)
        g, a = head // 4, head % 4
        for which in range(2):
            block = turned[which * HEAD : (which + 1) * HEAD]
            maps[which * (D // GROUP) + g, a * HEAD : (a + 1) * HEAD, :] = jnp.concatenate(
                [block if a == b else gap for b in range(4)], axis=1
            )


def features(maps, base, columns, f_t, f):
    def group(g, carry):
        u_t = dot_nt(maps[base + g], columns[:, pl.ds(aligned(g, GROUP), GROUP)])
        for a in range(4):
            u = u_t[a * HEAD : (a + 1) * HEAD]
            up = jnp.exp(u - jnp.max(u, axis=0, keepdims=True))
            down = jnp.exp(jnp.min(u, axis=0, keepdims=True) - u)
            plus = up / jnp.sum(up, axis=0, keepdims=True)
            minus = down / jnp.sum(down, axis=0, keepdims=True)
            feature = low(jnp.concatenate([plus, minus], axis=0))
            rows = pl.ds(aligned(g * 4 + a, FEAT), FEAT)
            f_t[rows, :] = feature
            f[:, rows] = feature.T
        return carry

    lax.fori_loop(0, D // GROUP, group, 0)


def wanted(place, k, first, last):
    block = place[0] ^ k
    return block, (block >= first) & (block < last)


def each_piece(place, pieces, first, last, work):
    for k in range(PIECES):
        block, use = wanted(place, k, first, last)

        @pl.when(use)
        def _():
            work(block - first, pieces[k])


def chunk_at(index):
    return pl.ds(aligned(index, CHUNK), CHUNK)


def pair_at(index):
    return pl.ds(aligned(index, FEAT), FEAT)


VALUES = D // FEAT
QUERY_BLOCKS = D // CHUNK


def copy_rows(source, target):
    def step(i, carry):
        rows = pl.ds(aligned(i, 2 * HEAD), 2 * HEAD)
        target[rows, :] = source[rows, :]
        return carry

    lax.fori_loop(0, source.shape[0] // (2 * HEAD), step, 0)


def keys_kernel(place, tokens, vectors, maps, *refs):
    pieces = refs[:PIECES]
    normed, keyed, fk, fk_t, state, w_kv = refs[PIECES:]
    seqs = state.shape[0]
    length = tokens.shape[0] // seqs
    normal, _ = normalize(wide(tokens[...]))
    normed[...] = low(normal * vectors[0:1, :] + vectors[1:2, :])

    def keep(index, weight):
        copy_rows(weight, w_kv.at[index])

    each_piece(place, pieces, QUERY_BLOCKS, QKV_BLOCKS, keep)

    def project(index, carry):
        keyed[:, chunk_at(index)] = low(dot(normed[...], w_kv[index]))
        return carry

    lax.fori_loop(0, QKV_BLOCKS - QUERY_BLOCKS, project, 0)
    features(maps, D // GROUP, keyed, fk_t, fk)
    state_sums(state, length, lambda p, here: with_ones(keyed[here, pair_at(VALUES + p)]), fk_t)


def state_sums(state, length, sides, f_t):
    seqs = state.shape[0]

    def pair(p, sums):
        result = []
        for b in range(seqs):
            here = slice(b * length, (b + 1) * length)
            first, second = sides(p, here)
            even = dot(f_t[pair_at(2 * p), here], first)
            odd = dot(f_t[pair_at(2 * p + 1), here], second)
            packed, new = pack_state(even, odd, p)
            state[b, pair_at(p), :] = low(packed)
            result.append(sums[b] + new)
        return tuple(result)

    empty = tuple(jnp.zeros((FEAT, FEAT), wide_type) for _ in range(seqs))
    sums = lax.fori_loop(0, PAIRS, pair, empty)
    for b in range(seqs):
        state[b, PAIRS * FEAT :, :] = low(sums[b])


def queries_kernel(place, normed, keyed, fk_t, maps, *refs):
    pieces = refs[:PIECES]
    normed_t, queries, fq, fq_t, partial, w_out, w_q = refs[PIECES:]

    def keep(index, weight):
        copy_rows(weight, w_q.at[index])

    def keep_out(index, weight):
        copy_rows(weight, w_out.at[:, chunk_at(index)])

    each_piece(place, pieces, 0, QUERY_BLOCKS, keep)
    each_piece(place, pieces, QKV_BLOCKS, PIECES, keep_out)

    def project(index, carry):
        queries[:, chunk_at(index)] = low(dot(normed[...], w_q[index]))
        return carry

    lax.fori_loop(0, QUERY_BLOCKS, project, 0)
    normed_t[...] = normed[...].T
    features(maps, 0, queries, fq_t, fq)
    seqs, length, _ = partial.shape

    def pair(p, carry):
        for b in range(seqs):
            here = slice(b * length, (b + 1) * length)
            values = with_ones(keyed[here, pair_at(VALUES + p)])
            for side in range(2):
                rows = pair_at(2 * p + side)
                scores = dot(fq[here, rows], fk_t[rows, here])
                scores = jnp.where(row_index(scores.shape) >= lane_index(scores.shape), scores, 0.0)
                partial[b, :, rows] = dot(low(scores), values[side])
        return carry

    lax.fori_loop(0, PAIRS, pair, 0)


def attend_kernel(tokens, vectors, partial, fq, w_out, *refs):
    priors, (attended, inverse, resid, second, second_t) = refs[:-5], refs[-5:]
    seqs = priors[0].shape[0]
    length = tokens.shape[0] // seqs

    def pair(p, carry):
        for b in range(seqs):
            here = slice(b * length, (b + 1) * length)
            states = states_at(priors, b, p)
            found = []
            for side in range(2):
                rows = pair_at(2 * p + side)
                found.append(partial[b, :, rows] + dot(fq[here, rows], states[side]))
            left = left_half(found[0].shape)
            turned = [pltpu.roll(a, HEAD, 1) for a in found]
            over = 1.0 / jnp.where(left, turned[0], turned[1])
            attended[here, pair_at(p)] = low(jnp.where(left, found[0], found[1]) * over)
            inverse[here, pair_at(p)] = over
        return carry

    lax.fori_loop(0, PAIRS, pair, 0)
    resid[...] = wide(tokens[...]) + dot(attended[...], w_out[...])
    normal, _ = normalize(resid[...])
    second[...] = low(normal * vectors[2:3, :] + vectors[3:4, :])
    second_t[...] = second[...].T


def mlp_kernel(second, second_other, cotangent, cotangent_other, resid, attended, *refs):
    pieces = refs[:4]
    out_sum, out_send, back_sum, back_send, hiddens, d_pres, second_other_t, attended_t = refs[4:12]
    up, down, ready = refs[12:]
    count = second.shape[0]
    parts = grads_layout(second.shape[1], pieces[0].shape[0])

    def copies(k, source):
        listed = []
        for i, (src, dst) in enumerate(parts):
            if dst[0] == "up":
                target = up.at[pl.ds(dst[1], dst[2]), chunk_at(k)]
            else:
                start = pl.multiple_of(k * CHUNK + dst[1], dst[2])
                target = down.at[pl.ds(start, dst[2]), pl.ds(dst[3], CHUNK)]
            listed.append(
                pltpu.make_async_copy(source.at[pl.ds(src, dst[2]), :], target, ready.at[k, i])
            )
        return listed

    for k in range(4):
        for copy in copies(k, pieces[k]):
            copy.start()
    second_other_t[...] = second_other[...].T
    attended_t[...] = attended[...].T

    def piece(k, carry):
        for copy in copies(k, pieces[0]):
            copy.wait()
        columns = chunk_at(k)
        for side, (source, grad) in enumerate(
            ((second, cotangent), (second_other, cotangent_other))
        ):
            here = slice(side * count, (side + 1) * count)
            pre = dot(source[...], up[:, columns])
            square = pre * pre
            bent = jnp.tanh(pre * (0.7978845608 + (0.7978845608 * 0.044715) * square))
            half = 0.5 + 0.5 * bent
            slope = half + (half * (1.0 - bent)) * pre * (
                0.7978845608 + (3.0 * 0.7978845608 * 0.044715) * square
            )
            hiddens[here, columns] = low(pre * half)
            d_pres[here, columns] = low(dot_nt(grad[...], down[columns, :]) * slope)
        return carry

    lax.fori_loop(0, 4, piece, 0)
    tile = count // 2

    def own(i, carry):
        here = pl.ds(aligned(i, tile), tile)
        back_sum[here, :] = dot_nt(d_pres[here, :], up[...])
        out_sum[here, :] = resid[here, :] + dot(hiddens[here, :], down[...])
        return carry

    def other(i, carry):
        here, there = pl.ds(aligned(i, tile), tile), pl.ds(aligned(i + 2, tile), tile)
        back_send[here, :] = low(dot_nt(d_pres[there, :], up[...]))
        out_send[here, :] = low(dot(hiddens[there, :], down[...]))
        return carry

    lax.fori_loop(0, 2, own, 0)
    lax.fori_loop(0, 2, other, 0)


def store_piece(outs, made, k):
    half = outs[3].shape[0]
    for i in range(3):

        @pl.when(k == i)
        def _():
            outs[i][...] = made[...]

    @pl.when(k == 3)
    def _():
        outs[3][...] = made[:half]
        outs[4][...] = made[half:]


def mlp_grads_kernel(second_t, second_other_t, cotangent, cotangent_other, hiddens, d_pres, *refs):
    outs, made = refs[:5], refs[5]
    count = cotangent.shape[0]
    own, other = slice(0, count), slice(count, 2 * count)

    def piece(k, carry):
        columns = chunk_at(k)
        d_up = dot(second_t[...], d_pres[own, columns])
        d_up = d_up + dot(second_other_t[...], d_pres[other, columns])
        d_down = dot_tn(hiddens[own, columns], cotangent[...])
        d_down = d_down + dot_tn(hiddens[other, columns], cotangent_other[...])
        d_up, d_down = low(d_up), low(d_down)
        for src, dst in grads_layout(second_t.shape[0], made.shape[0]):
            rows = slice(dst[1], dst[1] + dst[2])
            if dst[0] == "up":
                made[src : src + dst[2], :] = d_up[rows]
            else:
                made[src : src + dst[2], :] = d_down[rows, dst[3] : dst[3] + CHUNK]
        store_piece(outs, made, k)
        return carry

    lax.fori_loop(0, 4, piece, 0)


def grads_layout(width, block):
    shards = block // CHUNK
    up_rows = width // shards
    down_rows = CHUNK // shards
    parts = []
    for s in range(shards):
        base = s * (up_rows + 2 * down_rows)
        parts.append((base, ("up", s * up_rows, up_rows)))
        for side in range(2):
            parts.append(
                (
                    base + up_rows + side * down_rows,
                    ("down", s * down_rows, down_rows, side * CHUNK),
                )
            )
    return parts


def resid_kernel(back_sum, back_other, resid, cotangent, vectors, w_out, attended, inverse, fq_t, *refs):
    d_resid, d_resid_low, d_vectors, d_num, d_den, state = refs
    seqs = state.shape[0]
    length = resid.shape[0] // seqs
    normal, scale = normalize(resid[...])
    grad = back_sum[...] + wide(back_other[...])
    d_vectors[0:1, :] = jnp.sum(grad * normal, axis=0, keepdims=True)
    d_vectors[1:2, :] = jnp.sum(grad, axis=0, keepdims=True)
    d_resid[...] = wide(cotangent[...]) + norm_backward(grad, normal, scale, vectors[2:3, :])
    d_resid_low[...] = low(d_resid[...])
    d_attended = dot_nt(d_resid_low[...], w_out[...])
    shape = (FEAT, FEAT)
    cross = low(
        jnp.where(left_half(shape) != (row_index(shape) < HEAD), -1.0 / HEAD, 0.0)
    )
    for p in range(PAIRS):
        columns = slice(p * FEAT, (p + 1) * FEAT)
        num = d_attended[:, columns] * inverse[:, columns]
        product = num * wide(attended[:, columns])
        top = low(product)
        rest = low(product - wide(top))
        d_num[:, columns] = low(num)
        d_den[:, columns] = low(dot(top, cross) + dot(rest, cross))

    state_sums(state, length, lambda p, here: joined(d_num, d_den, here, p), fq_t)


def joined(d_num, d_den, here, p):
    columns = pl.ds(aligned(p, FEAT), FEAT)
    num, den = d_num[here, columns], d_den[here, columns]
    left = left_half(num.shape)
    return jnp.where(left, num, den), jnp.where(left, den, num)


def softmax_backward(feature, grad):
    plus, minus = wide(feature[:HEAD]), wide(feature[HEAD:])
    d_plus, d_minus = grad[:HEAD], grad[HEAD:]
    d_plus = plus * (d_plus - jnp.sum(d_plus * plus, axis=0, keepdims=True))
    d_minus = minus * (d_minus - jnp.sum(d_minus * minus, axis=0, keepdims=True))
    return low(d_plus - d_minus)


def linked(outer, value):
    link = dot_nt(outer, value)
    return low(jnp.where(row_index(link.shape) >= lane_index(link.shape), link, 0.0))


def local_queries_kernel(queries, keyed, maps, fq_t, fk_t, d_num, d_den, *refs):
    priors, (d_queries, d_features, d_uq_t) = refs[:-3], refs[-3:]
    seqs = priors[0].shape[0]
    length = keyed.shape[0] // seqs

    def pair(p, carry):
        for b in range(seqs):
            here = slice(b * length, (b + 1) * length)
            values = with_ones(keyed[here, pair_at(VALUES + p)])
            outer = joined(d_num, d_den, here, p)
            states = states_at(priors, b, p)
            for side in range(2):
                rows = pair_at(2 * p + side)
                link = linked(outer[side], values[side])
                d_q = dot_nt(fk_t[rows, here], link) + dot_nt(states[side], outer[side])
                d_uq_t[pl.ds(aligned(2 * p + side, HEAD), HEAD), here] = softmax_backward(
                    fq_t[rows, here], d_q
                )
        return carry

    lax.fori_loop(0, PAIRS, pair, 0)
    feature_backward(d_uq_t, queries, maps, 0, d_queries, d_features, 0)


def local_keys_kernel(keyed, fq_t, fk, d_num, d_den, d_fk_t, d_values, *, seqs):
    length = keyed.shape[0] // seqs

    def pair(p, carry):
        for b in range(seqs):
            here = slice(b * length, (b + 1) * length)
            values = with_ones(keyed[here, pair_at(VALUES + p)])
            outer = joined(d_num, d_den, here, p)
            found = []
            for side in range(2):
                rows = pair_at(2 * p + side)
                q_t = fq_t[rows, here]
                d_fk_t[rows, here] = dot(q_t, linked(outer[side], values[side]))
                scores = dot(fk[here, rows], q_t)
                row, lane = row_index(scores.shape), lane_index(scores.shape)
                found.append(dot(low(jnp.where(row <= lane, scores, 0.0)), outer[side]))
            left = left_half(found[0].shape)
            d_values[here, pair_at(p)] = jnp.where(left, found[0], found[1])
        return carry

    lax.fori_loop(0, PAIRS, pair, 0)


def feature_backward(d_u_t, source, maps, base, target, d_features, lane):
    def group(g, carry):
        d_u = d_u_t[pl.ds(aligned(g, GROUP), GROUP), :]
        columns = pl.ds(aligned(g, GROUP), GROUP)
        product = dot(d_u, source[:, columns]).T
        for a in range(4):
            block = slice(a * HEAD, (a + 1) * HEAD)
            rows = pl.ds(aligned(g * 4 + a, HEAD), HEAD)
            d_features[rows, lane : lane + HEAD] = product[block, block]
        target[:, columns] = low(dot(d_u.T, maps[base + g]))
        return carry

    lax.fori_loop(0, D // GROUP, group, 0)


def mixed_kernel(
    place, keyed, fk, fk_t, maps, d_fk_t, d_values, d_resid_low, d_queries, d_half, *refs
):
    laters, (d_keyed, d_features, sends, d_uk_t) = refs[:-4], refs[-4:]
    seqs = laters[0].shape[0]
    length = keyed.shape[0] // seqs

    def pair(p, carry):
        for b in range(seqs):
            here = slice(b * length, (b + 1) * length)
            values = with_ones(keyed[here, pair_at(VALUES + p)])
            states = states_at(laters, b, p)
            found = []
            for side in range(2):
                rows = pl.ds(aligned(2 * p + side, FEAT), FEAT)
                d_k = d_fk_t[rows, here] + dot_nt(states[side], values[side])
                d_uk_t[pl.ds(aligned(2 * p + side, HEAD), HEAD), here] = softmax_backward(
                    fk_t[rows, here], d_k
                )
                found.append(dot(fk[here, rows], states[side]))
            left = left_half(found[0].shape)
            total = d_values[here, pl.ds(aligned(p, FEAT), FEAT)] + jnp.where(
                left, found[0], found[1]
            )
            d_keyed[here, pair_at(VALUES + p)] = low(total)
        return carry

    lax.fori_loop(0, PAIRS, pair, 0)
    feature_backward(d_uk_t, keyed, maps, D // GROUP, d_keyed, d_features, HEAD)
    d_features[:, :HEAD] = d_half[:, :HEAD]

    def send(i, carry):
        own_column(place[0] ^ (2 * i + 1), sends.at[i], d_queries, d_keyed, d_resid_low)
        return carry

    lax.fori_loop(0, PIECES // 2, send, 0)


def own_column(block, target, d_queries, d_keyed, d_resid_low):
    @pl.when(block < QUERY_BLOCKS)
    def _():
        target[...] = d_queries[:, chunk_at(block)]

    @pl.when((block >= QUERY_BLOCKS) & (block < QKV_BLOCKS))
    def _():
        target[...] = d_keyed[:, chunk_at(block - QUERY_BLOCKS)]

    @pl.when(block >= QKV_BLOCKS)
    def _():
        target[...] = d_resid_low[:, chunk_at(block - QKV_BLOCKS)]


TINY_ROWS = 48
TINY_TILE = 16


def tiny_size(rows):
    return -(-(rows + 8) // TINY_ROWS) * TINY_ROWS


def in_grads_kernel(
    place, d_queries, d_keyed, d_resid_low, received, tiny, tiny_other, *refs
):
    sources, outs, (held, column, made, ready) = refs[:4], refs[4:9], refs[9:]
    shard_count, size, _ = tiny.shape
    rows = D // shard_count
    copies = [
        pltpu.make_async_copy(source, held.at[i], ready.at[i]) for i, source in enumerate(sources)
    ]
    for copy in copies:
        copy.start()
    for copy in copies:
        copy.wait()

    def piece(i, carry):
        block = place[0] ^ (2 * i)
        kind = 2 * jnp.where(block < QKV_BLOCKS, 0, 1)
        own_column(block, column, d_queries, d_keyed, d_resid_low)
        value = low(dot(held[kind], column[...]) + dot(held[kind + 1], received[i]))
        for s in range(shard_count):
            base = s * (rows + TINY_TILE)
            made[base : base + rows, :] = value[s * rows : (s + 1) * rows]
            for j in range(TINY_ROWS // TINY_TILE):
                target = (slice(base + rows, base + rows + TINY_TILE), slice(j * FEAT, (j + 1) * FEAT))
                made[target] = jnp.zeros((TINY_TILE, FEAT), low_type)

                @pl.when(block < size // TINY_ROWS)
                def _():
                    start = pl.multiple_of(block * TINY_ROWS + j * TINY_TILE, TINY_TILE)
                    spot = pl.ds(start, TINY_TILE)
                    made[target] = low(wide(tiny[s, spot, :]) + wide(tiny_other[s, spot, :]))

        store_piece(outs, made, i)
        return carry

    lax.fori_loop(0, PIECES // 2, piece, 0)


def early_kernel(d_queries, w_q, total):
    total[...] = jnp.zeros_like(total)
    add_products(total, d_queries, w_q)


def add_products(total, source, weights):
    def add(index, carry):
        total[...] += dot_nt(source[:, chunk_at(index)], weights[index])
        return carry

    lax.fori_loop(0, weights.shape[0], add, 0)


def input_kernel(tokens, vectors, early, d_keyed, d_resid, out_sum, out_other, *refs):
    w_kv, d_features, d_vectors, block_out, grad_tokens, tiny, total = refs
    total[...] = early[...]
    block_out[...] = low(out_sum[...] + wide(out_other[...]))

    add_products(total, d_keyed, w_kv)
    normal, scale = normalize(wide(tokens[...]))
    grad = total[...]
    grad_tokens[...] = low(d_resid[...] + norm_backward(grad, normal, scale, vectors[0:1, :]))
    gathered = [
        jnp.sum(grad * normal, axis=0, keepdims=True),
        jnp.sum(grad, axis=0, keepdims=True),
        d_vectors[0:1, :],
        d_vectors[1:2, :],
    ]
    shard_count, size, _ = tiny.shape
    rows = D // shard_count
    tiny[...] = jnp.zeros_like(tiny)
    for s in range(shard_count):
        tiny[s, :rows, :] = low(d_features[s * rows : (s + 1) * rows, :])
        lines = []
        for vector in gathered:
            line = vector[:, s * rows : (s + 1) * rows]
            gap = jnp.zeros((1, 2 * FEAT - rows), wide_type)
            line = jnp.concatenate([line, gap], axis=1)
            lines += [line[:, :FEAT], line[:, FEAT:]]
        tiny[s, rows : rows + 8, :] = low(jnp.concatenate(lines, axis=0))


def lay_in_kernel(place, even, odd, qkv, out, tiny):
    rows = qkv.shape[0]
    for k in range(PIECES):
        block = place[0] ^ k
        piece = (even, odd)[k % 2].at[k // 2]

        @pl.when(block < QKV_BLOCKS)
        def _():
            qkv[:, chunk_at(block)] = wide(piece[:rows])

        @pl.when(block >= QKV_BLOCKS)
        def _():
            out[:, chunk_at(block - QKV_BLOCKS)] = wide(piece[:rows])

        @pl.when(block < tiny.shape[0] // TINY_ROWS)
        def _():
            for j in range(TINY_ROWS // TINY_TILE):
                start = pl.multiple_of(block * TINY_ROWS + j * TINY_TILE, TINY_TILE)
                tiny[pl.ds(start, TINY_TILE), :] = wide(
                    piece[rows:, j * FEAT : (j + 1) * FEAT]
                )


def lay_mlp_kernel(place, even, odd, up, down, ordered):
    up_rows, down_rows = ordered.shape[1], down.shape[1]
    for k in range(PIECES):
        block = place[0] ^ k
        piece = (even, odd)[k % 2]
        ordered[block] = piece[k // 2, :up_rows, :]
        for side in range(2):
            start = up_rows + side * down_rows
            down[block, :, side * CHUNK : (side + 1) * CHUNK] = wide(
                piece[k // 2, start : start + down_rows, :]
            )
    for s in range(CHUNK // down_rows):
        columns = slice(s * down_rows, (s + 1) * down_rows)
        row = jnp.concatenate([ordered[r][:, columns] for r in range(PIECES)], axis=1)
        up[:, s * PIECES * down_rows : (s + 1) * PIECES * down_rows] = wide(row)


def whole(shape, dtype=low_type):
    return jax.ShapeDtypeStruct(shape, dtype)


def scalar_first(count):
    return [pl.BlockSpec(memory_space=pltpu.SMEM)] + [
        pl.BlockSpec(memory_space=pltpu.VMEM) for _ in range(count)
    ]


def call(kernel, weight, out_shape, in_specs=None, scratch=(), limit=8, **rest):
    if in_specs is not None:
        rest["in_specs"] = in_specs
    return pl.pallas_call(
        kernel,
        out_shape=out_shape,
        scratch_shapes=list(scratch),
        compiler_params=pltpu.CompilerParams(vmem_limit_bytes=limit << 20),
        cost_estimate=pl.CostEstimate(
            flops=weight * 2000 * 10**6, transcendentals=0, bytes_accessed=weight * 3 * 2000 * 10**3
        ),
        **rest,
    )


def interleave(even, odd):
    return [part for both in zip(even, odd) for part in both]


def shards(
    tokens,
    gain_attn,
    bias_attn,
    w_qkv,
    w_feature,
    w_out,
    gain_mlp,
    bias_mlp,
    w_up,
    w_down,
    cotangent,
):
    shard_count = lax.axis_size("shard")
    place = lax.axis_index("rep") % PIECES
    spot = place.reshape(1).astype(jnp.int32)
    seqs, length, _ = tokens.shape
    count = seqs * length
    rows = w_qkv.shape[0]
    fine = CHUNK // shard_count
    flat = tokens.reshape(count, D)
    flat_cotangent = cotangent.reshape(count, D)
    anywhere = [pl.BlockSpec(memory_space=pl.ANY)] * PIECES

    part_in = lax.dynamic_slice_in_dim(
        jnp.concatenate([w_qkv, w_out], axis=1), place * CHUNK, CHUNK, 1
    )
    vectors = jnp.concatenate([gain_attn, bias_attn, gain_mlp, bias_mlp]).reshape(-1, FEAT)
    small = jnp.concatenate([w_feature, vectors], axis=0)
    small_rows = -(-small.shape[0] // 24) * 8
    small = jnp.pad(small, ((0, 3 * small_rows - small.shape[0]), (0, 0)))
    small = jnp.concatenate(jnp.split(small, 3, axis=0), axis=1)
    part_in = jnp.concatenate([part_in, small], axis=0)
    part_up = lax.dynamic_index_in_dim(
        w_up.reshape(rows, shard_count, PIECES, fine), place, 2, False
    ).reshape(rows, CHUNK)
    part_down = lax.dynamic_slice_in_dim(w_down, place * fine, fine, 0)
    part_mlp = jnp.concatenate([part_up, part_down[:, :CHUNK], part_down[:, CHUNK:]], axis=0)

    here = lax.axis_index("shard")
    in_slots = jnp.stack([(here - step) % shard_count for step in range(shard_count)])
    in_spins = [part_in] + [spin(part_in, step) for step in range(1, shard_count)]

    def place_in_kernel(slots, *refs):
        parts, (full, rest) = refs[:-2], refs[-2:]
        for i, part in enumerate(parts):
            full[slots[i]] = part[:rows]
            rest[slots[i]] = part[rows:]

    in_full, small = call(
        place_in_kernel,
        1,
        (whole((shard_count, rows, CHUNK)), whole((shard_count, small_rows, CHUNK))),
        scalar_first(shard_count),
    )(in_slots.astype(jnp.int32), *in_spins)
    cotangent_other = flip(flat_cotangent, 1)
    in_full, small = lax.optimization_barrier((in_full, small))
    maps, vectors = call(
        maps_kernel,
        15,
        (whole((2 * D // GROUP, GROUP, GROUP)), whole((4, D), wide_type)),
        scratch=[pltpu.VMEM((D, FEAT), wide_type)],
    )(small)
    in_full = in_full.reshape(-1, CHUNK)
    part_mlp, in_full = lax.optimization_barrier((part_mlp, in_full))
    steps = list(range(1, shard_count))
    from_x, from_y = sides_of(in_full)
    in_other = flip(in_full, 1)
    soon = {step: spin(part_mlp, step) for step in steps[:1] + steps[2:]}
    in_halves, maps, vectors, soon = lax.optimization_barrier(
        (halves_of(from_x, from_y), maps, vectors, soon)
    )
    soon.update({step: spin(soon[1], 1) for step in steps[1:2]})
    diagonal = diagonal_of(in_halves)
    diagonal, soon = lax.optimization_barrier((diagonal, soon))
    in_even = [in_full, from_x, from_y, diagonal]
    in_pieces = interleave(in_even, [in_other] + [flip(part, 1) for part in in_even[1:]])
    here = lax.axis_index("shard")
    mlp_parts = [part_mlp[None]] + [soon[step][None] for step in steps]
    mlp_slots = [(here - step) % shard_count for step in range(shard_count)]

    normed, keyed, fk, fk_t, key_state, w_kv = call(
        keys_kernel,
        8,
        (
            whole((count, D)),
            whole((count, 2 * D)),
            whole((count, HEADS * FEAT)),
            whole((HEADS * FEAT, count)),
            whole((seqs, SLAB, FEAT)),
            whole((QKV_BLOCKS - QUERY_BLOCKS, D, CHUNK)),
        ),
        scalar_first(3 + PIECES),
    )(spot, flat, vectors, maps, *in_pieces)
    prior, running = scan_first(key_state, 1)
    mlp_parts, normed = lax.optimization_barrier((mlp_parts, normed))
    mlp_full = place_parts(mlp_parts, mlp_slots).reshape(-1, CHUNK)
    mlp_full, normed = lax.optimization_barrier((mlp_full, normed))
    mlp_x, mlp_y = sides_of(mlp_full)
    normed_t, queries, fq, fq_t, partial, out_weight, w_q = call(
        queries_kernel,
        9,
        (
            whole((D, count)),
            whole((count, D)),
            whole((count, HEADS * FEAT)),
            whole((HEADS * FEAT, count)),
            whole((seqs, length, HEADS * FEAT), wide_type),
            whole((D, D)),
            whole((QUERY_BLOCKS, D, CHUNK)),
        ),
        scalar_first(4 + PIECES),
    )(spot, normed, keyed, fk_t, maps, *in_pieces)
    running, partial = lax.optimization_barrier((running, partial))
    priors = scan_rest(prior, running, 1)
    mlp_halves, partial = lax.optimization_barrier((halves_of(mlp_x, mlp_y), partial))
    mlp_pieces = [mlp_full, mlp_x, mlp_y, diagonal_of(mlp_halves)]
    attended, inverse, resid, second, second_t = call(
        attend_kernel,
        5,
        (
            whole((count, D)),
            whole((count, D), wide_type),
            whole((count, D), wide_type),
            whole((count, D)),
            whole((D, count)),
        ),
    )(flat, vectors, partial, fq, out_weight, *priors)

    second_other = flip(second, 1)
    (
        out_sum,
        out_send,
        back_sum,
        back_send,
        hiddens,
        d_pres,
        second_other_t,
        attended_t,
    ) = call(
        mlp_kernel,
        20,
        (
            whole((count, D), wide_type),
            whole((count, D)),
            whole((count, D), wide_type),
            whole((count, D)),
            whole((2 * count, 4 * CHUNK)),
            whole((2 * count, 4 * CHUNK)),
            whole((D, count)),
            whole((D, count)),
        ),
        [pl.BlockSpec(memory_space=pltpu.VMEM)] * 6 + anywhere[:4],
        [
            pltpu.VMEM((D, 4 * CHUNK), low_type),
            pltpu.VMEM((4 * CHUNK, D), low_type),
            pltpu.SemaphoreType.DMA((4, 3 * shard_count)),
        ],
        limit=18,
    )(second, second_other, flat_cotangent, cotangent_other, resid, attended, *mlp_pieces)
    back_other = flip(back_send, 1)
    out_other = flip(out_send, 1)
    d_resid, d_resid_low, d_vectors_two, d_num, d_den, query_state = call(
        resid_kernel,
        5,
        (
            whole((count, D), wide_type),
            whole((count, D)),
            whole((2, D), wide_type),
            whole((count, D)),
            whole((count, D)),
            whole((seqs, SLAB, FEAT)),
        ),
    )(back_sum, back_other, resid, flat_cotangent, vectors, out_weight, attended, inverse, fq_t)
    later, running = scan_first(query_state, -1)
    normed_other_t = flip(normed_t, 1)
    attended_other_t = flip(attended_t, 1)
    second_t, query_state, normed_other_t, attended_other_t, out_other = lax.optimization_barrier(
        (second_t, query_state, normed_other_t, attended_other_t, out_other)
    )
    piece = lambda rows: tuple(
        whole((size, CHUNK)) for size in (rows, rows, rows, rows // 2, rows // 2)
    )
    mlp_grads = call(
        mlp_grads_kernel, 7, piece(2 * D), scratch=[pltpu.VMEM((2 * D, CHUNK), low_type)]
    )(second_t, second_other_t, flat_cotangent, cotangent_other, hiddens, d_pres)
    mlp_to_x, mlp_to_y = flip(mlp_grads[3], 4), flip(mlp_grads[4], 2)
    running, fk_t = lax.optimization_barrier((running, fk_t))
    laters = scan_rest(later, running, -1)
    d_queries, d_half, _ = call(
        local_queries_kernel,
        6,
        (whole((count, D)), whole((D, FEAT), wide_type), whole((D, count))),
    )(queries, keyed, maps, fq_t, fk_t, d_num, d_den, *priors)
    mlp_to_x, mlp_to_y, d_half = lax.optimization_barrier((mlp_to_x, mlp_to_y, d_half))
    add_sides = lambda parts, to_x, to_y: call(
        sides_kernel, 1, (whole(parts[1].shape), whole(parts[1].shape))
    )(parts[1], parts[2], to_x, to_y)
    mlp_sides = add_sides(mlp_grads, mlp_to_x, mlp_to_y)
    mlp_sides, d_half, fk = lax.optimization_barrier((mlp_sides, d_half, fk))
    d_fk_t, d_values = call(
        lambda *refs: local_keys_kernel(*refs, seqs=seqs),
        5,
        (whole((HEADS * FEAT, count), wide_type), whole((count, D), wide_type)),
    )(keyed, fq_t, fk, d_num, d_den)
    mlp_joined = [flip(mlp_sides[0], 2), flip(mlp_sides[1], 4)]
    early = call(early_kernel, 2, whole((count, D), wide_type))(d_queries, w_q)
    early, d_half = lax.optimization_barrier((early, d_half))
    d_keyed, d_features, sends, _ = call(
        mixed_kernel,
        7,
        (
            whole((count, 2 * D)),
            whole((D, FEAT), wide_type),
            whole((PIECES // 2, count, CHUNK)),
            whole((D, count)),
        ),
        scalar_first(9 + len(laters)),
    )(spot, keyed, fk, fk_t, maps, d_fk_t, d_values, d_resid_low, d_queries, d_half, *laters)
    received = flip(sends, 1)
    block_out, grad_tokens, tiny = call(
        input_kernel,
        7,
        (
            whole((count, D)),
            whole((count, D)),
            whole((shard_count, tiny_size(rows), FEAT)),
        ),
        scratch=[pltpu.VMEM((count, D), wide_type)],
    )(
        flat,
        vectors,
        early,
        d_keyed,
        d_resid,
        out_sum,
        out_other,
        w_kv,
        d_features,
        d_vectors_two,
    )
    tiny_other = flip(tiny, 1)
    mlp_blocks = join_parts([mlp_grads[0], *mlp_joined])
    received, tiny_other, mlp_blocks = lax.optimization_barrier((received, tiny_other, mlp_blocks))
    in_grads = call(
        in_grads_kernel,
        7,
        piece(D + shard_count * TINY_TILE),
        scalar_first(6) + anywhere[:4],
        [
            pltpu.VMEM((4, D, count), low_type),
            pltpu.VMEM((count, CHUNK), low_type),
            pltpu.VMEM((D + shard_count * TINY_TILE, CHUNK), low_type),
            pltpu.SemaphoreType.DMA((4,)),
        ],
    )(
        spot,
        d_queries,
        d_keyed,
        d_resid_low,
        received,
        tiny,
        tiny_other,
        normed_t,
        normed_other_t,
        attended_t,
        attended_other_t,
    )
    in_to_x, in_to_y = flip(in_grads[3], 4), flip(in_grads[4], 2)
    mlp_received = [spin(part, step + 1) for step, part in enumerate(mlp_blocks[1:])]
    in_to_x, in_to_y, mlp_received[:1] = lax.optimization_barrier((in_to_x, in_to_y, mlp_received[:1]))
    in_sides = add_sides(in_grads, in_to_x, in_to_y)
    in_joined = [flip(in_sides[0], 2), flip(in_sides[1], 4)]
    in_joined, mlp_received = lax.optimization_barrier((in_joined, mlp_received))
    in_blocks = join_parts([in_grads[0], *in_joined])
    in_received = [spin(part, step + 1) for step, part in enumerate(in_blocks[1:])]
    in_received, mlp_received = lax.optimization_barrier((in_received, mlp_received))
    mlp_sums = share_pair(share_flips(settle(mlp_blocks[0], mlp_received)))
    in_flips = share_flips(settle(in_blocks[0], in_received))
    grad_up, grad_down = call(
        lay_mlp_kernel,
        3,
        (whole((rows, 4 * D), wide_type), whole((PIECES, fine, D), wide_type)),
        scalar_first(2),
        [pltpu.VMEM((PIECES, rows, CHUNK), low_type)],
    )(spot, *mlp_sums)
    grad_down = grad_down.reshape(-1, D)
    in_flips, grad_up, grad_down = lax.optimization_barrier((in_flips, grad_up, grad_down))
    in_sums = share_pair(in_flips)
    grad_qkv, grad_out, tiny = call(
        lay_in_kernel,
        2,
        (
            whole((rows, 3 * D), wide_type),
            whole((rows, D), wide_type),
            whole((tiny_size(rows), FEAT), wide_type),
        ),
        scalar_first(2),
    )(spot, *in_sums)
    grad_feature = tiny[:rows]
    d_vectors = tiny[rows : rows + 8].reshape(4, 2 * FEAT)[:, :rows]
    return (
        block_out.reshape(tokens.shape),
        grad_tokens.reshape(tokens.shape),
        d_vectors[0],
        d_vectors[1],
        grad_qkv,
        grad_feature,
        grad_out,
        d_vectors[2],
        d_vectors[3],
        grad_up,
        grad_down,
    )


def solution(mesh):
    placed = (
        P("rep", "shard", None),
        P("shard"),
        P("shard"),
        P("shard", None),
        P("shard", None),
        P("shard", None),
        P("shard"),
        P("shard"),
        P("shard", None),
        P("shard", None),
        P("rep", "shard", None),
    )
    return jax.shard_map(
        shards,
        mesh=mesh,
        in_specs=placed,
        out_specs=(
            P("rep", "shard", None),
            P("rep", "shard", None),
            P("shard"),
            P("shard"),
            P("shard", None),
            P("shard", None),
            P("shard", None),
            P("shard"),
            P("shard"),
            P("shard", None),
            P("shard", None),
        ),
        check_vma=False,
    )
```

```python
import jax
import jax.numpy as jnp
from jax import lax
from jax.experimental import pallas as pl
from jax.experimental.pallas import tpu as pltpu
from jax.sharding import PartitionSpec as P

D = 768
HEADS = 12
HEAD = 64
FEAT = 128
PAIRS = HEADS // 2
GROUP = 4 * HEAD
PIECES = 8
CHUNK = 4 * D // PIECES
QKV_BLOCKS = 3 * D // CHUNK
SLAB = (PAIRS + 1) * FEAT

norm_epsilon = 1e-05
low_type = jnp.bfloat16
wide_type = jnp.float32


def flip(value, bit):
    count = lax.axis_size("rep")
    return lax.ppermute(value, "rep", [(i, i ^ bit) for i in range(count)])


def spin(value, step):
    count = lax.axis_size("shard")
    return lax.ppermute(value, "shard", [(i, (i + step) % count) for i in range(count)])


def slide(value, step):
    count = lax.axis_size("shard")
    pairs = [(i, i + step) for i in range(count) if 0 <= i + step < count]
    return lax.ppermute(value, "shard", pairs)


def wide(value):
    return value.astype(wide_type)


def low(value):
    return value.astype(low_type)


def place_kernel(slots, *refs):
    parts, full = refs[:-1], refs[-1]
    for i, part in enumerate(parts):
        size = part.shape[0]
        full[pl.ds(slots[i] * size, size)] = part[...]


def place_parts(parts, slots):
    shape = (len(parts) * parts[0].shape[0],) + parts[0].shape[1:]
    slots = jnp.stack([jnp.asarray(slot, jnp.int32) for slot in slots])
    return call(place_kernel, 1, whole(shape, parts[0].dtype), scalar_first(len(parts)))(
        slots, *parts
    )


def around_parts(part):
    count, here = lax.axis_size("shard"), lax.axis_index("shard")
    parts = [part[None]] + [spin(part, step)[None] for step in range(1, count)]
    return parts, [(here - step) % count for step in range(count)]


def around(part):
    return place_parts(*around_parts(part))


def scan_first(state, direction):
    received = slide(state, direction)
    return received, low(wide(state) + wide(received))


def scan_rest(received, running, direction):
    found, step = [received], 2
    while step < lax.axis_size("shard"):
        found.append(slide(running, direction * step))
        running = low(wide(running) + wide(found[-1]))
        step *= 2
    return found


def sides_of(own):
    return flip(own, 2), flip(own, 4)


def halves_of(from_x, from_y):
    half = from_x.shape[0] // 2
    return from_x[:half], from_y[half:]


def diagonal_of(halves):
    return jnp.concatenate([flip(halves[0], 4), flip(halves[1], 2)], axis=0)


def share_flips(own):
    return [own[None]] + [flip(own, bit)[None] for bit in (2, 4, 6)]


def share_pair(parts):
    even = place_parts(parts, [0, 1, 2, 3])
    return even, flip(even, 1)


def sides_kernel(x_part, y_part, to_x, to_y, x_sum, y_sum):
    half = to_x.shape[0]
    x_sum[:half] = low(wide(x_part[:half]) + wide(to_x[...]))
    x_sum[half:] = x_part[half:]
    y_sum[:half] = y_part[:half]
    y_sum[half:] = low(wide(y_part[half:]) + wide(to_y[...]))


def join_parts(parts):
    count, here = lax.axis_size("shard"), lax.axis_index("shard")
    bit = PIECES
    if bit < lax.axis_size("rep"):
        mine = sum(wide(part) for part in parts)
        while bit < lax.axis_size("rep"):
            mine = mine + wide(flip(low(mine), bit))
            bit *= 2
        parts = [mine]
    rows, columns = parts[0].shape
    rows //= count

    def kernel(spot, *refs):
        sources, outs = refs[: len(parts)], refs[len(parts) :]
        for step in range(count):
            block = lax.rem(spot[0] + step, count)
            chosen = pl.ds(pl.multiple_of(block * rows, rows), rows)
            total = wide(sources[0][chosen, :])
            for source in sources[1:]:
                total = total + wide(source[chosen, :])
            outs[step][...] = total if step == 0 else low(total)

    shapes = [whole((rows, columns), wide_type)] + [whole((rows, columns))] * (count - 1)
    return call(kernel, 2, tuple(shapes), scalar_first(len(parts)))(
        here.reshape(1).astype(jnp.int32), *parts
    )


def settle(own, received, weight=1):
    def kernel(own, *refs):
        total = own[...]
        for ref in refs[:-1]:
            total = total + wide(ref[...])
        refs[-1][...] = low(total)

    return call(kernel, weight, whole(own.shape))(own, *received)


def dot(a, b):
    return jnp.dot(a, b, preferred_element_type=wide_type)


def dot_nt(a, b):
    return lax.dot_general(a, b, (((1,), (1,)), ((), ())), preferred_element_type=wide_type)


def dot_tn(a, b):
    return lax.dot_general(a, b, (((0,), (0,)), ((), ())), preferred_element_type=wide_type)


def normalize(rows):
    centred = rows - jnp.mean(rows, axis=-1, keepdims=True)
    scale = lax.rsqrt(jnp.mean(centred * centred, axis=-1, keepdims=True) + norm_epsilon)
    return centred * scale, scale


def norm_backward(grad, normal, scale, gain):
    e = grad * gain
    return scale * (
        e
        - jnp.mean(e, axis=-1, keepdims=True)
        - normal * jnp.mean(e * normal, axis=-1, keepdims=True)
    )


def lane_index(shape):
    return lax.broadcasted_iota(jnp.int32, shape, len(shape) - 1)


def row_index(shape):
    return lax.broadcasted_iota(jnp.int32, shape, len(shape) - 2)


def left_half(shape):
    return lane_index(shape) < HEAD


def aligned(index, unit):
    return pl.multiple_of(index * unit, unit)


def with_ones(pair):
    left = left_half(pair.shape)
    one = jnp.ones_like(pair)
    return jnp.where(left, pair, one), jnp.where(left, one, pair)


def pack_state(even, odd, p):
    lane = lane_index(even.shape)
    packed = jnp.where(lane < HEAD, even, odd)
    sums = jnp.where(lane == HEAD + 2 * p, even, jnp.where(lane == 2 * p + 1, odd, 0.0))
    return packed, sums


def unpack_state(packed, sums, p):
    shape = packed.shape
    lane, row = lane_index(shape), row_index(shape)
    pick_even = low(jnp.where((row == HEAD + 2 * p) & (lane >= HEAD), 1.0, 0.0))
    pick_odd = low(jnp.where((row == 2 * p + 1) & (lane < HEAD), 1.0, 0.0))
    even = jnp.where(lane < HEAD, packed, dot(sums, pick_even))
    odd = jnp.where(lane < HEAD, dot(sums, pick_odd), packed)
    return low(even), low(odd)


def added(refs, b, rows):
    total = wide(refs[0][b, rows, :])
    for ref in refs[1:]:
        total = total + wide(ref[b, rows, :])
    return total


def states_at(refs, b, p):
    packed = added(refs, b, pl.ds(aligned(p, FEAT), FEAT))
    sums = low(added(refs, b, slice(PAIRS * FEAT, SLAB)))
    return unpack_state(packed, sums, p)


def maps_kernel(small, maps, vectors, weight):
    shard_count, size, _ = small.shape
    rows = D // shard_count
    lines = 4 * rows // FEAT
    for s in range(shard_count):
        for j in range(3):
            count = min(size, rows - j * size)
            if count > 0:
                weight[s * rows + j * size : s * rows + j * size + count, :] = wide(
                    small[s, :count, j * FEAT : (j + 1) * FEAT]
                )
        flat = []
        for line in range(rows, rows + lines):
            j, row = line // size, line % size
            flat.append(wide(small[s, row : row + 1, j * FEAT : (j + 1) * FEAT]))
        flat = jnp.concatenate(flat, axis=1)
        for v in range(4):
            vectors[v : v + 1, s * rows : (s + 1) * rows] = flat[:, v * rows : (v + 1) * rows]
    gap = jnp.zeros((HEAD, HEAD), low_type)
    for head in range(HEADS):
        turned = low(weight[head * HEAD : (head + 1) * HEAD, :].T)
        g, a = head // 4, head % 4
        for which in range(2):
            block = turned[which * HEAD : (which + 1) * HEAD]
            maps[which * (D // GROUP) + g, a * HEAD : (a + 1) * HEAD, :] = jnp.concatenate(
                [block if a == b else gap for b in range(4)], axis=1
            )


def features(maps, base, columns, f_t, f):
    def group(g, carry):
        u_t = dot_nt(maps[base + g], columns[:, pl.ds(aligned(g, GROUP), GROUP)])
        for a in range(4):
            u = u_t[a * HEAD : (a + 1) * HEAD]
            up = jnp.exp(u - jnp.max(u, axis=0, keepdims=True))
            down = jnp.exp(jnp.min(u, axis=0, keepdims=True) - u)
            plus = up / jnp.sum(up, axis=0, keepdims=True)
            minus = down / jnp.sum(down, axis=0, keepdims=True)
            feature = low(jnp.concatenate([plus, minus], axis=0))
            rows = pl.ds(aligned(g * 4 + a, FEAT), FEAT)
            f_t[rows, :] = feature
            f[:, rows] = feature.T
        return carry

    lax.fori_loop(0, D // GROUP, group, 0)


def wanted(place, k, first, last):
    block = place[0] ^ k
    return block, (block >= first) & (block < last)


def each_piece(place, pieces, first, last, work):
    for k in range(PIECES):
        block, use = wanted(place, k, first, last)

        @pl.when(use)
        def _():
            work(block - first, pieces[k])


def chunk_at(index):
    return pl.ds(aligned(index, CHUNK), CHUNK)


def pair_at(index):
    return pl.ds(aligned(index, FEAT), FEAT)


VALUES = D // FEAT
QUERY_BLOCKS = D // CHUNK


def copy_rows(source, target):
    def step(i, carry):
        rows = pl.ds(aligned(i, 2 * HEAD), 2 * HEAD)
        target[rows, :] = source[rows, :]
        return carry

    lax.fori_loop(0, source.shape[0] // (2 * HEAD), step, 0)


def keys_kernel(place, tokens, vectors, maps, *refs):
    pieces = refs[:PIECES]
    normed, keyed, fk, fk_t, state, w_kv = refs[PIECES:]
    seqs = state.shape[0]
    length = tokens.shape[0] // seqs
    normal, _ = normalize(wide(tokens[...]))
    normed[...] = low(normal * vectors[0:1, :] + vectors[1:2, :])

    def keep(index, weight):
        copy_rows(weight, w_kv.at[index])

    each_piece(place, pieces, QUERY_BLOCKS, QKV_BLOCKS, keep)

    def project(index, carry):
        keyed[:, chunk_at(index)] = low(dot(normed[...], w_kv[index]))
        return carry

    lax.fori_loop(0, QKV_BLOCKS - QUERY_BLOCKS, project, 0)
    features(maps, D // GROUP, keyed, fk_t, fk)
    state_sums(state, length, lambda p, here: with_ones(keyed[here, pair_at(VALUES + p)]), fk_t)


def state_sums(state, length, sides, f_t):
    seqs = state.shape[0]

    def pair(p, sums):
        result = []
        for b in range(seqs):
            here = slice(b * length, (b + 1) * length)
            first, second = sides(p, here)
            even = dot(f_t[pair_at(2 * p), here], first)
            odd = dot(f_t[pair_at(2 * p + 1), here], second)
            packed, new = pack_state(even, odd, p)
            state[b, pair_at(p), :] = low(packed)
            result.append(sums[b] + new)
        return tuple(result)

    empty = tuple(jnp.zeros((FEAT, FEAT), wide_type) for _ in range(seqs))
    sums = lax.fori_loop(0, PAIRS, pair, empty)
    for b in range(seqs):
        state[b, PAIRS * FEAT :, :] = low(sums[b])


def queries_kernel(place, normed, keyed, fk_t, maps, *refs):
    pieces = refs[:PIECES]
    normed_t, queries, fq, fq_t, partial, w_out, w_q = refs[PIECES:]

    def keep(index, weight):
        copy_rows(weight, w_q.at[index])

    def keep_out(index, weight):
        copy_rows(weight, w_out.at[:, chunk_at(index)])

    each_piece(place, pieces, 0, QUERY_BLOCKS, keep)
    each_piece(place, pieces, QKV_BLOCKS, PIECES, keep_out)

    def project(index, carry):
        queries[:, chunk_at(index)] = low(dot(normed[...], w_q[index]))
        return carry

    lax.fori_loop(0, QUERY_BLOCKS, project, 0)
    normed_t[...] = normed[...].T
    features(maps, 0, queries, fq_t, fq)
    seqs, length, _ = partial.shape

    def pair(p, carry):
        for b in range(seqs):
            here = slice(b * length, (b + 1) * length)
            values = with_ones(keyed[here, pair_at(VALUES + p)])
            for side in range(2):
                rows = pair_at(2 * p + side)
                scores = dot(fq[here, rows], fk_t[rows, here])
                scores = jnp.where(row_index(scores.shape) >= lane_index(scores.shape), scores, 0.0)
                partial[b, :, rows] = dot(low(scores), values[side])
        return carry

    lax.fori_loop(0, PAIRS, pair, 0)


def attend_kernel(tokens, vectors, partial, fq, w_out, *refs):
    priors, (attended, inverse, resid, second, second_t) = refs[:-5], refs[-5:]
    seqs = priors[0].shape[0]
    length = tokens.shape[0] // seqs

    def pair(p, carry):
        for b in range(seqs):
            here = slice(b * length, (b + 1) * length)
            states = states_at(priors, b, p)
            found = []
            for side in range(2):
                rows = pair_at(2 * p + side)
                found.append(partial[b, :, rows] + dot(fq[here, rows], states[side]))
            left = left_half(found[0].shape)
            turned = [pltpu.roll(a, HEAD, 1) for a in found]
            over = 1.0 / jnp.where(left, turned[0], turned[1])
            attended[here, pair_at(p)] = low(jnp.where(left, found[0], found[1]) * over)
            inverse[here, pair_at(p)] = over
        return carry

    lax.fori_loop(0, PAIRS, pair, 0)
    resid[...] = wide(tokens[...]) + dot(attended[...], w_out[...])
    normal, _ = normalize(resid[...])
    second[...] = low(normal * vectors[2:3, :] + vectors[3:4, :])
    second_t[...] = second[...].T


def mlp_kernel(second, second_other, cotangent, cotangent_other, resid, attended, *refs):
    pieces = refs[:4]
    out_sum, out_send, back_sum, back_send, hiddens, d_pres, second_other_t, attended_t = refs[4:12]
    up, down, ready = refs[12:]
    count = second.shape[0]
    parts = grads_layout(second.shape[1], pieces[0].shape[0])

    def copies(k, source):
        listed = []
        for i, (src, dst) in enumerate(parts):
            if dst[0] == "up":
                target = up.at[pl.ds(dst[1], dst[2]), chunk_at(k)]
            else:
                start = pl.multiple_of(k * CHUNK + dst[1], dst[2])
                target = down.at[pl.ds(start, dst[2]), pl.ds(dst[3], CHUNK)]
            listed.append(
                pltpu.make_async_copy(source.at[pl.ds(src, dst[2]), :], target, ready.at[k, i])
            )
        return listed

    for k in range(4):
        for copy in copies(k, pieces[k]):
            copy.start()
    second_other_t[...] = second_other[...].T
    attended_t[...] = attended[...].T

    def piece(k, carry):
        for copy in copies(k, pieces[0]):
            copy.wait()
        columns = chunk_at(k)
        for side, (source, grad) in enumerate(
            ((second, cotangent), (second_other, cotangent_other))
        ):
            here = slice(side * count, (side + 1) * count)
            pre = dot(source[...], up[:, columns])
            square = pre * pre
            bent = jnp.tanh(pre * (0.7978845608 + (0.7978845608 * 0.044715) * square))
            half = 0.5 + 0.5 * bent
            slope = half + (half * (1.0 - bent)) * pre * (
                0.7978845608 + (3.0 * 0.7978845608 * 0.044715) * square
            )
            hiddens[here, columns] = low(pre * half)
            d_pres[here, columns] = low(dot_nt(grad[...], down[columns, :]) * slope)
        return carry

    lax.fori_loop(0, 4, piece, 0)
    tile = count // 2

    def own(i, carry):
        here = pl.ds(aligned(i, tile), tile)
        back_sum[here, :] = dot_nt(d_pres[here, :], up[...])
        out_sum[here, :] = resid[here, :] + dot(hiddens[here, :], down[...])
        return carry

    def other(i, carry):
        here, there = pl.ds(aligned(i, tile), tile), pl.ds(aligned(i + 2, tile), tile)
        back_send[here, :] = low(dot_nt(d_pres[there, :], up[...]))
        out_send[here, :] = low(dot(hiddens[there, :], down[...]))
        return carry

    lax.fori_loop(0, 2, own, 0)
    lax.fori_loop(0, 2, other, 0)


def store_piece(outs, made, k):
    half = outs[3].shape[0]
    for i in range(3):

        @pl.when(k == i)
        def _():
            outs[i][...] = made[...]

    @pl.when(k == 3)
    def _():
        outs[3][...] = made[:half]
        outs[4][...] = made[half:]


def mlp_grads_kernel(second_t, second_other_t, cotangent, cotangent_other, hiddens, d_pres, *refs):
    outs, made = refs[:5], refs[5]
    count = cotangent.shape[0]
    own, other = slice(0, count), slice(count, 2 * count)

    def piece(k, carry):
        columns = chunk_at(k)
        d_up = dot(second_t[...], d_pres[own, columns])
        d_up = d_up + dot(second_other_t[...], d_pres[other, columns])
        d_down = dot_tn(hiddens[own, columns], cotangent[...])
        d_down = d_down + dot_tn(hiddens[other, columns], cotangent_other[...])
        d_up, d_down = low(d_up), low(d_down)
        for src, dst in grads_layout(second_t.shape[0], made.shape[0]):
            rows = slice(dst[1], dst[1] + dst[2])
            if dst[0] == "up":
                made[src : src + dst[2], :] = d_up[rows]
            else:
                made[src : src + dst[2], :] = d_down[rows, dst[3] : dst[3] + CHUNK]
        store_piece(outs, made, k)
        return carry

    lax.fori_loop(0, 4, piece, 0)


def grads_layout(width, block):
    shards = block // CHUNK
    up_rows = width // shards
    down_rows = CHUNK // shards
    parts = []
    for s in range(shards):
        base = s * (up_rows + 2 * down_rows)
        parts.append((base, ("up", s * up_rows, up_rows)))
        for side in range(2):
            parts.append(
                (
                    base + up_rows + side * down_rows,
                    ("down", s * down_rows, down_rows, side * CHUNK),
                )
            )
    return parts


def resid_kernel(back_sum, back_other, resid, cotangent, vectors, w_out, attended, inverse, fq_t, *refs):
    d_resid, d_resid_low, d_vectors, d_num, d_den, state = refs
    seqs = state.shape[0]
    length = resid.shape[0] // seqs
    normal, scale = normalize(resid[...])
    grad = back_sum[...] + wide(back_other[...])
    d_vectors[0:1, :] = jnp.sum(grad * normal, axis=0, keepdims=True)
    d_vectors[1:2, :] = jnp.sum(grad, axis=0, keepdims=True)
    d_resid[...] = wide(cotangent[...]) + norm_backward(grad, normal, scale, vectors[2:3, :])
    d_resid_low[...] = low(d_resid[...])
    d_attended = dot_nt(d_resid_low[...], w_out[...])
    shape = (FEAT, FEAT)
    cross = low(
        jnp.where(left_half(shape) != (row_index(shape) < HEAD), -1.0 / HEAD, 0.0)
    )
    for p in range(PAIRS):
        columns = slice(p * FEAT, (p + 1) * FEAT)
        num = d_attended[:, columns] * inverse[:, columns]
        product = num * wide(attended[:, columns])
        top = low(product)
        rest = low(product - wide(top))
        d_num[:, columns] = low(num)
        d_den[:, columns] = low(dot(top, cross) + dot(rest, cross))

    state_sums(state, length, lambda p, here: joined(d_num, d_den, here, p), fq_t)


def joined(d_num, d_den, here, p):
    columns = pl.ds(aligned(p, FEAT), FEAT)
    num, den = d_num[here, columns], d_den[here, columns]
    left = left_half(num.shape)
    return jnp.where(left, num, den), jnp.where(left, den, num)


def softmax_backward(feature, grad):
    plus, minus = wide(feature[:HEAD]), wide(feature[HEAD:])
    d_plus, d_minus = grad[:HEAD], grad[HEAD:]
    d_plus = plus * (d_plus - jnp.sum(d_plus * plus, axis=0, keepdims=True))
    d_minus = minus * (d_minus - jnp.sum(d_minus * minus, axis=0, keepdims=True))
    return low(d_plus - d_minus)


def linked(outer, value):
    link = dot_nt(outer, value)
    return low(jnp.where(row_index(link.shape) >= lane_index(link.shape), link, 0.0))


def local_queries_kernel(queries, keyed, maps, fq_t, fk_t, d_num, d_den, *refs):
    priors, (d_queries, d_features, d_uq_t) = refs[:-3], refs[-3:]
    seqs = priors[0].shape[0]
    length = keyed.shape[0] // seqs

    def pair(p, carry):
        for b in range(seqs):
            here = slice(b * length, (b + 1) * length)
            values = with_ones(keyed[here, pair_at(VALUES + p)])
            outer = joined(d_num, d_den, here, p)
            states = states_at(priors, b, p)
            for side in range(2):
                rows = pair_at(2 * p + side)
                link = linked(outer[side], values[side])
                d_q = dot_nt(fk_t[rows, here], link) + dot_nt(states[side], outer[side])
                d_uq_t[pl.ds(aligned(2 * p + side, HEAD), HEAD), here] = softmax_backward(
                    fq_t[rows, here], d_q
                )
        return carry

    lax.fori_loop(0, PAIRS, pair, 0)
    feature_backward(d_uq_t, queries, maps, 0, d_queries, d_features, 0)


def local_keys_kernel(keyed, fq_t, fk, d_num, d_den, d_fk_t, d_values, *, seqs):
    length = keyed.shape[0] // seqs

    def pair(p, carry):
        for b in range(seqs):
            here = slice(b * length, (b + 1) * length)
            values = with_ones(keyed[here, pair_at(VALUES + p)])
            outer = joined(d_num, d_den, here, p)
            found = []
            for side in range(2):
                rows = pair_at(2 * p + side)
                q_t = fq_t[rows, here]
                d_fk_t[rows, here] = dot(q_t, linked(outer[side], values[side]))
                scores = dot(fk[here, rows], q_t)
                row, lane = row_index(scores.shape), lane_index(scores.shape)
                found.append(dot(low(jnp.where(row <= lane, scores, 0.0)), outer[side]))
            left = left_half(found[0].shape)
            d_values[here, pair_at(p)] = jnp.where(left, found[0], found[1])
        return carry

    lax.fori_loop(0, PAIRS, pair, 0)


def feature_backward(d_u_t, source, maps, base, target, d_features, lane):
    def group(g, carry):
        d_u = d_u_t[pl.ds(aligned(g, GROUP), GROUP), :]
        columns = pl.ds(aligned(g, GROUP), GROUP)
        product = dot(d_u, source[:, columns]).T
        for a in range(4):
            block = slice(a * HEAD, (a + 1) * HEAD)
            rows = pl.ds(aligned(g * 4 + a, HEAD), HEAD)
            d_features[rows, lane : lane + HEAD] = product[block, block]
        target[:, columns] = low(dot(d_u.T, maps[base + g]))
        return carry

    lax.fori_loop(0, D // GROUP, group, 0)


def mixed_kernel(
    place, keyed, fk, fk_t, maps, d_fk_t, d_values, d_resid_low, d_queries, d_half, *refs
):
    laters, (d_keyed, d_features, sends, d_uk_t) = refs[:-4], refs[-4:]
    seqs = laters[0].shape[0]
    length = keyed.shape[0] // seqs

    def pair(p, carry):
        for b in range(seqs):
            here = slice(b * length, (b + 1) * length)
            values = with_ones(keyed[here, pair_at(VALUES + p)])
            states = states_at(laters, b, p)
            found = []
            for side in range(2):
                rows = pl.ds(aligned(2 * p + side, FEAT), FEAT)
                d_k = d_fk_t[rows, here] + dot_nt(states[side], values[side])
                d_uk_t[pl.ds(aligned(2 * p + side, HEAD), HEAD), here] = softmax_backward(
                    fk_t[rows, here], d_k
                )
                found.append(dot(fk[here, rows], states[side]))
            left = left_half(found[0].shape)
            total = d_values[here, pl.ds(aligned(p, FEAT), FEAT)] + jnp.where(
                left, found[0], found[1]
            )
            d_keyed[here, pair_at(VALUES + p)] = low(total)
        return carry

    lax.fori_loop(0, PAIRS, pair, 0)
    feature_backward(d_uk_t, keyed, maps, D // GROUP, d_keyed, d_features, HEAD)
    d_features[:, :HEAD] = d_half[:, :HEAD]

    def send(i, carry):
        own_column(place[0] ^ (2 * i + 1), sends.at[i], d_queries, d_keyed, d_resid_low)
        return carry

    lax.fori_loop(0, PIECES // 2, send, 0)


def own_column(block, target, d_queries, d_keyed, d_resid_low):
    @pl.when(block < QUERY_BLOCKS)
    def _():
        target[...] = d_queries[:, chunk_at(block)]

    @pl.when((block >= QUERY_BLOCKS) & (block < QKV_BLOCKS))
    def _():
        target[...] = d_keyed[:, chunk_at(block - QUERY_BLOCKS)]

    @pl.when(block >= QKV_BLOCKS)
    def _():
        target[...] = d_resid_low[:, chunk_at(block - QKV_BLOCKS)]


TINY_ROWS = 48
TINY_TILE = 16


def tiny_size(rows):
    return -(-(rows + 8) // TINY_ROWS) * TINY_ROWS


def in_grads_kernel(
    place, d_queries, d_keyed, d_resid_low, received, tiny, tiny_other, *refs
):
    sources, outs, (held, column, made, ready) = refs[:4], refs[4:9], refs[9:]
    shard_count, size, _ = tiny.shape
    rows = D // shard_count
    copies = [
        pltpu.make_async_copy(source, held.at[i], ready.at[i]) for i, source in enumerate(sources)
    ]
    for copy in copies:
        copy.start()
    for copy in copies:
        copy.wait()

    def piece(i, carry):
        block = place[0] ^ (2 * i)
        kind = 2 * jnp.where(block < QKV_BLOCKS, 0, 1)
        own_column(block, column, d_queries, d_keyed, d_resid_low)
        value = low(dot(held[kind], column[...]) + dot(held[kind + 1], received[i]))
        for s in range(shard_count):
            base = s * (rows + TINY_TILE)
            made[base : base + rows, :] = value[s * rows : (s + 1) * rows]
            for j in range(TINY_ROWS // TINY_TILE):
                target = (slice(base + rows, base + rows + TINY_TILE), slice(j * FEAT, (j + 1) * FEAT))
                made[target] = jnp.zeros((TINY_TILE, FEAT), low_type)

                @pl.when(block < size // TINY_ROWS)
                def _():
                    start = pl.multiple_of(block * TINY_ROWS + j * TINY_TILE, TINY_TILE)
                    spot = pl.ds(start, TINY_TILE)
                    made[target] = low(wide(tiny[s, spot, :]) + wide(tiny_other[s, spot, :]))

        store_piece(outs, made, i)
        return carry

    lax.fori_loop(0, PIECES // 2, piece, 0)


def early_kernel(d_queries, w_q, total):
    total[...] = jnp.zeros_like(total)
    add_products(total, d_queries, w_q)


def add_products(total, source, weights):
    def add(index, carry):
        total[...] += dot_nt(source[:, chunk_at(index)], weights[index])
        return carry

    lax.fori_loop(0, weights.shape[0], add, 0)


def input_kernel(tokens, vectors, early, d_keyed, d_resid, out_sum, out_other, *refs):
    w_kv, d_features, d_vectors, block_out, grad_tokens, tiny, total = refs
    total[...] = early[...]
    block_out[...] = low(out_sum[...] + wide(out_other[...]))

    add_products(total, d_keyed, w_kv)
    normal, scale = normalize(wide(tokens[...]))
    grad = total[...]
    grad_tokens[...] = low(d_resid[...] + norm_backward(grad, normal, scale, vectors[0:1, :]))
    gathered = [
        jnp.sum(grad * normal, axis=0, keepdims=True),
        jnp.sum(grad, axis=0, keepdims=True),
        d_vectors[0:1, :],
        d_vectors[1:2, :],
    ]
    shard_count, size, _ = tiny.shape
    rows = D // shard_count
    tiny[...] = jnp.zeros_like(tiny)
    for s in range(shard_count):
        tiny[s, :rows, :] = low(d_features[s * rows : (s + 1) * rows, :])
        lines = []
        for vector in gathered:
            line = vector[:, s * rows : (s + 1) * rows]
            gap = jnp.zeros((1, 2 * FEAT - rows), wide_type)
            line = jnp.concatenate([line, gap], axis=1)
            lines += [line[:, :FEAT], line[:, FEAT:]]
        tiny[s, rows : rows + 8, :] = low(jnp.concatenate(lines, axis=0))


def lay_in_kernel(place, even, odd, qkv, out, tiny):
    rows = qkv.shape[0]
    for k in range(PIECES):
        block = place[0] ^ k
        piece = (even, odd)[k % 2].at[k // 2]

        @pl.when(block < QKV_BLOCKS)
        def _():
            qkv[:, chunk_at(block)] = wide(piece[:rows])

        @pl.when(block >= QKV_BLOCKS)
        def _():
            out[:, chunk_at(block - QKV_BLOCKS)] = wide(piece[:rows])

        @pl.when(block < tiny.shape[0] // TINY_ROWS)
        def _():
            for j in range(TINY_ROWS // TINY_TILE):
                start = pl.multiple_of(block * TINY_ROWS + j * TINY_TILE, TINY_TILE)
                tiny[pl.ds(start, TINY_TILE), :] = wide(
                    piece[rows:, j * FEAT : (j + 1) * FEAT]
                )


def lay_mlp_kernel(place, even, odd, up, down, ordered):
    up_rows, down_rows = ordered.shape[1], down.shape[1]
    for k in range(PIECES):
        block = place[0] ^ k
        piece = (even, odd)[k % 2]
        ordered[block] = piece[k // 2, :up_rows, :]
        for side in range(2):
            start = up_rows + side * down_rows
            down[block, :, side * CHUNK : (side + 1) * CHUNK] = wide(
                piece[k // 2, start : start + down_rows, :]
            )
    for s in range(CHUNK // down_rows):
        columns = slice(s * down_rows, (s + 1) * down_rows)
        row = jnp.concatenate([ordered[r][:, columns] for r in range(PIECES)], axis=1)
        up[:, s * PIECES * down_rows : (s + 1) * PIECES * down_rows] = wide(row)


def whole(shape, dtype=low_type):
    return jax.ShapeDtypeStruct(shape, dtype)


def scalar_first(count):
    return [pl.BlockSpec(memory_space=pltpu.SMEM)] + [
        pl.BlockSpec(memory_space=pltpu.VMEM) for _ in range(count)
    ]


def call(kernel, weight, out_shape, in_specs=None, scratch=(), limit=8, **rest):
    if in_specs is not None:
        rest["in_specs"] = in_specs
    return pl.pallas_call(
        kernel,
        out_shape=out_shape,
        scratch_shapes=list(scratch),
        compiler_params=pltpu.CompilerParams(vmem_limit_bytes=limit << 20),
        cost_estimate=pl.CostEstimate(
            flops=int(weight * 2000 * 10**6), transcendentals=0, bytes_accessed=int(weight * 6 * 10**6)
        ),
        **rest,
    )


def interleave(even, odd):
    return [part for both in zip(even, odd) for part in both]


def shards(
    tokens,
    gain_attn,
    bias_attn,
    w_qkv,
    w_feature,
    w_out,
    gain_mlp,
    bias_mlp,
    w_up,
    w_down,
    cotangent,
):
    shard_count = lax.axis_size("shard")
    place = lax.axis_index("rep") % PIECES
    spot = place.reshape(1).astype(jnp.int32)
    seqs, length, _ = tokens.shape
    count = seqs * length
    rows = w_qkv.shape[0]
    fine = CHUNK // shard_count
    flat = tokens.reshape(count, D)
    flat_cotangent = cotangent.reshape(count, D)
    anywhere = [pl.BlockSpec(memory_space=pl.ANY)] * PIECES

    part_in = lax.dynamic_slice_in_dim(
        jnp.concatenate([w_qkv, w_out], axis=1), place * CHUNK, CHUNK, 1
    )
    vectors = jnp.concatenate([gain_attn, bias_attn, gain_mlp, bias_mlp]).reshape(-1, FEAT)
    small = jnp.concatenate([w_feature, vectors], axis=0)
    small_rows = -(-small.shape[0] // 24) * 8
    small = jnp.pad(small, ((0, 3 * small_rows - small.shape[0]), (0, 0)))
    small = jnp.concatenate(jnp.split(small, 3, axis=0), axis=1)
    part_in = jnp.concatenate([part_in, small], axis=0)
    part_up = lax.dynamic_index_in_dim(
        w_up.reshape(rows, shard_count, PIECES, fine), place, 2, False
    ).reshape(rows, CHUNK)
    part_down = lax.dynamic_slice_in_dim(w_down, place * fine, fine, 0)
    part_mlp = jnp.concatenate([part_up, part_down[:, :CHUNK], part_down[:, CHUNK:]], axis=0)

    here = lax.axis_index("shard")
    in_slots = jnp.stack([(here - step) % shard_count for step in range(shard_count)])
    in_spins = [part_in] + [spin(part_in, step) for step in range(1, shard_count)]

    def place_in_kernel(slots, *refs):
        parts, (full, rest) = refs[:-2], refs[-2:]
        for i, part in enumerate(parts):
            full[slots[i]] = part[:rows]
            rest[slots[i]] = part[rows:]

    in_full, small = call(
        place_in_kernel,
        1,
        (whole((shard_count, rows, CHUNK)), whole((shard_count, small_rows, CHUNK))),
        scalar_first(shard_count),
    )(in_slots.astype(jnp.int32), *in_spins)
    cotangent_other = flip(flat_cotangent, 1)
    in_full, small = lax.optimization_barrier((in_full, small))
    maps, vectors = call(
        maps_kernel,
        15,
        (whole((2 * D // GROUP, GROUP, GROUP)), whole((4, D), wide_type)),
        scratch=[pltpu.VMEM((D, FEAT), wide_type)],
    )(small)
    in_full = in_full.reshape(-1, CHUNK)
    part_mlp, in_full = lax.optimization_barrier((part_mlp, in_full))
    steps = list(range(1, shard_count))
    from_x, from_y = sides_of(in_full)
    in_other = flip(in_full, 1)
    soon = {step: spin(part_mlp, step) for step in steps[:1] + steps[2:]}
    in_halves, maps, vectors, soon = lax.optimization_barrier(
        (halves_of(from_x, from_y), maps, vectors, soon)
    )
    soon.update({step: spin(soon[1], 1) for step in steps[1:2]})
    diagonal = diagonal_of(in_halves)
    diagonal, soon = lax.optimization_barrier((diagonal, soon))
    in_even = [in_full, from_x, from_y, diagonal]
    in_pieces = interleave(in_even, [in_other] + [flip(part, 1) for part in in_even[1:]])
    here = lax.axis_index("shard")
    mlp_parts = [part_mlp[None]] + [soon[step][None] for step in steps]
    mlp_slots = [(here - step) % shard_count for step in range(shard_count)]

    mlp_full = place_parts(mlp_parts, mlp_slots).reshape(-1, CHUNK)
    mlp_full, vectors = lax.optimization_barrier((mlp_full, vectors))
    normed, keyed, fk, fk_t, key_state, w_kv = call(
        keys_kernel,
        8,
        (
            whole((count, D)),
            whole((count, 2 * D)),
            whole((count, HEADS * FEAT)),
            whole((HEADS * FEAT, count)),
            whole((seqs, SLAB, FEAT)),
            whole((QKV_BLOCKS - QUERY_BLOCKS, D, CHUNK)),
        ),
        scalar_first(3 + PIECES),
    )(spot, flat, vectors, maps, *in_pieces)
    prior, running = scan_first(key_state, 1)
    mlp_x, mlp_y = sides_of(mlp_full)
    normed_t, queries, fq, fq_t, partial, out_weight, w_q = call(
        queries_kernel,
        9,
        (
            whole((D, count)),
            whole((count, D)),
            whole((count, HEADS * FEAT)),
            whole((HEADS * FEAT, count)),
            whole((seqs, length, HEADS * FEAT), wide_type),
            whole((D, D)),
            whole((QUERY_BLOCKS, D, CHUNK)),
        ),
        scalar_first(4 + PIECES),
    )(spot, normed, keyed, fk_t, maps, *in_pieces)
    running, partial = lax.optimization_barrier((running, partial))
    priors = scan_rest(prior, running, 1)
    mlp_halves, partial = lax.optimization_barrier((halves_of(mlp_x, mlp_y), partial))
    mlp_pieces = [mlp_full, mlp_x, mlp_y, diagonal_of(mlp_halves)]
    attended, inverse, resid, second, second_t = call(
        attend_kernel,
        5,
        (
            whole((count, D)),
            whole((count, D), wide_type),
            whole((count, D), wide_type),
            whole((count, D)),
            whole((D, count)),
        ),
    )(flat, vectors, partial, fq, out_weight, *priors)

    second_other = flip(second, 1)
    (
        out_sum,
        out_send,
        back_sum,
        back_send,
        hiddens,
        d_pres,
        second_other_t,
        attended_t,
    ) = call(
        mlp_kernel,
        20,
        (
            whole((count, D), wide_type),
            whole((count, D)),
            whole((count, D), wide_type),
            whole((count, D)),
            whole((2 * count, 4 * CHUNK)),
            whole((2 * count, 4 * CHUNK)),
            whole((D, count)),
            whole((D, count)),
        ),
        [pl.BlockSpec(memory_space=pltpu.VMEM)] * 6 + anywhere[:4],
        [
            pltpu.VMEM((D, 4 * CHUNK), low_type),
            pltpu.VMEM((4 * CHUNK, D), low_type),
            pltpu.SemaphoreType.DMA((4, 3 * shard_count)),
        ],
        limit=18,
    )(second, second_other, flat_cotangent, cotangent_other, resid, attended, *mlp_pieces)
    back_other = flip(back_send, 1)
    out_other = flip(out_send, 1)
    d_resid, d_resid_low, d_vectors_two, d_num, d_den, query_state = call(
        resid_kernel,
        5,
        (
            whole((count, D), wide_type),
            whole((count, D)),
            whole((2, D), wide_type),
            whole((count, D)),
            whole((count, D)),
            whole((seqs, SLAB, FEAT)),
        ),
    )(back_sum, back_other, resid, flat_cotangent, vectors, out_weight, attended, inverse, fq_t)
    later, running = scan_first(query_state, -1)
    normed_other_t = flip(normed_t, 1)
    attended_other_t = flip(attended_t, 1)
    second_t, query_state, normed_other_t, attended_other_t, out_other = lax.optimization_barrier(
        (second_t, query_state, normed_other_t, attended_other_t, out_other)
    )
    piece = lambda rows: tuple(
        whole((size, CHUNK)) for size in (rows, rows, rows, rows // 2, rows // 2)
    )
    mlp_grads = call(
        mlp_grads_kernel, 7, piece(2 * D), scratch=[pltpu.VMEM((2 * D, CHUNK), low_type)]
    )(second_t, second_other_t, flat_cotangent, cotangent_other, hiddens, d_pres)
    mlp_to_x, mlp_to_y = flip(mlp_grads[3], 4), flip(mlp_grads[4], 2)
    running, fk_t = lax.optimization_barrier((running, fk_t))
    laters = scan_rest(later, running, -1)
    d_queries, d_half, _ = call(
        local_queries_kernel,
        6,
        (whole((count, D)), whole((D, FEAT), wide_type), whole((D, count))),
    )(queries, keyed, maps, fq_t, fk_t, d_num, d_den, *priors)
    mlp_to_x, mlp_to_y, d_half = lax.optimization_barrier((mlp_to_x, mlp_to_y, d_half))
    add_sides = lambda parts, to_x, to_y: call(
        sides_kernel, 1, (whole(parts[1].shape), whole(parts[1].shape))
    )(parts[1], parts[2], to_x, to_y)
    mlp_sides = add_sides(mlp_grads, mlp_to_x, mlp_to_y)
    mlp_sides, d_half, fk = lax.optimization_barrier((mlp_sides, d_half, fk))
    d_fk_t, d_values = call(
        lambda *refs: local_keys_kernel(*refs, seqs=seqs),
        5,
        (whole((HEADS * FEAT, count), wide_type), whole((count, D), wide_type)),
    )(keyed, fq_t, fk, d_num, d_den)
    mlp_joined = [flip(mlp_sides[0], 2), flip(mlp_sides[1], 4)]
    early = call(early_kernel, 2, whole((count, D), wide_type))(d_queries, w_q)
    early, d_half = lax.optimization_barrier((early, d_half))
    d_keyed, d_features, sends, _ = call(
        mixed_kernel,
        7,
        (
            whole((count, 2 * D)),
            whole((D, FEAT), wide_type),
            whole((PIECES // 2, count, CHUNK)),
            whole((D, count)),
        ),
        scalar_first(9 + len(laters)),
    )(spot, keyed, fk, fk_t, maps, d_fk_t, d_values, d_resid_low, d_queries, d_half, *laters)
    received = flip(sends, 1)
    block_out, grad_tokens, tiny = call(
        input_kernel,
        7,
        (
            whole((count, D)),
            whole((count, D)),
            whole((shard_count, tiny_size(rows), FEAT)),
        ),
        scratch=[pltpu.VMEM((count, D), wide_type)],
    )(
        flat,
        vectors,
        early,
        d_keyed,
        d_resid,
        out_sum,
        out_other,
        w_kv,
        d_features,
        d_vectors_two,
    )
    tiny_other = flip(tiny, 1)
    mlp_blocks = join_parts([mlp_grads[0], *mlp_joined])
    received, tiny_other, mlp_blocks = lax.optimization_barrier((received, tiny_other, mlp_blocks))
    in_grads = call(
        in_grads_kernel,
        7,
        piece(D + shard_count * TINY_TILE),
        scalar_first(6) + anywhere[:4],
        [
            pltpu.VMEM((4, D, count), low_type),
            pltpu.VMEM((count, CHUNK), low_type),
            pltpu.VMEM((D + shard_count * TINY_TILE, CHUNK), low_type),
            pltpu.SemaphoreType.DMA((4,)),
        ],
    )(
        spot,
        d_queries,
        d_keyed,
        d_resid_low,
        received,
        tiny,
        tiny_other,
        normed_t,
        normed_other_t,
        attended_t,
        attended_other_t,
    )
    mlp_received = [spin(part, step + 1) for step, part in enumerate(mlp_blocks[1:])]
    in_upper, in_lower, mlp_received[:1] = lax.optimization_barrier(
        (in_grads[3], in_grads[4], mlp_received[:1])
    )
    in_to_x, in_to_y = flip(in_upper, 4), flip(in_lower, 2)
    in_to_x, in_to_y, mlp_received[2:] = lax.optimization_barrier(
        (in_to_x, in_to_y, mlp_received[2:])
    )
    in_sides = add_sides(in_grads, in_to_x, in_to_y)
    in_joined = [flip(in_sides[0], 2), flip(in_sides[1], 4)]
    in_joined, mlp_received = lax.optimization_barrier((in_joined, mlp_received))
    in_blocks = join_parts([in_grads[0], *in_joined])
    in_received = [spin(part, step + 1) for step, part in enumerate(in_blocks[1:])]
    in_blocks, mlp_received = lax.optimization_barrier((in_blocks, mlp_received))
    mlp_total = settle(mlp_blocks[0], mlp_received, 10)
    mlp_flips = share_flips(mlp_total)
    in_received, _ = lax.optimization_barrier((in_received, mlp_total))
    in_received[:1], mlp_flips[:2] = lax.optimization_barrier((in_received[:1], mlp_flips[:2]))
    mlp_sums = share_pair(mlp_flips)
    in_flips = share_flips(settle(in_blocks[0], in_received))
    grad_up, grad_down = call(
        lay_mlp_kernel,
        3,
        (whole((rows, 4 * D), wide_type), whole((PIECES, fine, D), wide_type)),
        scalar_first(2),
        [pltpu.VMEM((PIECES, rows, CHUNK), low_type)],
    )(spot, *mlp_sums)
    grad_down = grad_down.reshape(-1, D)
    in_flips, grad_up, grad_down = lax.optimization_barrier((in_flips, grad_up, grad_down))
    in_sums = share_pair(in_flips)
    grad_qkv, grad_out, tiny = call(
        lay_in_kernel,
        2,
        (
            whole((rows, 3 * D), wide_type),
            whole((rows, D), wide_type),
            whole((tiny_size(rows), FEAT), wide_type),
        ),
        scalar_first(2),
    )(spot, *in_sums)
    grad_feature = tiny[:rows]
    d_vectors = tiny[rows : rows + 8].reshape(4, 2 * FEAT)[:, :rows]
    return (
        block_out.reshape(tokens.shape),
        grad_tokens.reshape(tokens.shape),
        d_vectors[0],
        d_vectors[1],
        grad_qkv,
        grad_feature,
        grad_out,
        d_vectors[2],
        d_vectors[3],
        grad_up,
        grad_down,
    )


def solution(mesh):
    placed = (
        P("rep", "shard", None),
        P("shard"),
        P("shard"),
        P("shard", None),
        P("shard", None),
        P("shard", None),
        P("shard"),
        P("shard"),
        P("shard", None),
        P("shard", None),
        P("rep", "shard", None),
    )
    return jax.shard_map(
        shards,
        mesh=mesh,
        in_specs=placed,
        out_specs=(
            P("rep", "shard", None),
            P("rep", "shard", None),
            P("shard"),
            P("shard"),
            P("shard", None),
            P("shard", None),
            P("shard", None),
            P("shard"),
            P("shard"),
            P("shard", None),
            P("shard", None),
        ),
        check_vma=False,
    )
```

```python
import jax
import jax.numpy as jnp
from jax import lax
from jax.experimental import pallas as pl
from jax.experimental.pallas import tpu as pltpu
from jax.sharding import PartitionSpec as P

D = 768
HEADS = 12
HEAD = 64
FEAT = 128
PAIRS = HEADS // 2
GROUP = 4 * HEAD
PIECES = 8
CHUNK = 4 * D // PIECES
QKV_BLOCKS = 3 * D // CHUNK
EDGE = 16
SLAB = PAIRS * FEAT + 2 * EDGE

norm_epsilon = 1e-05
low_type = jnp.bfloat16
wide_type = jnp.float32


def flip(value, bit):
    count = lax.axis_size("rep")
    return lax.ppermute(value, "rep", [(i, i ^ bit) for i in range(count)])


def spin(value, step):
    count = lax.axis_size("shard")
    return lax.ppermute(value, "shard", [(i, (i + step) % count) for i in range(count)])


def slide(value, step):
    count = lax.axis_size("shard")
    pairs = [(i, i + step) for i in range(count) if 0 <= i + step < count]
    return lax.ppermute(value, "shard", pairs)


def wide(value):
    return value.astype(wide_type)


def low(value):
    return value.astype(low_type)


def place_kernel(slots, *refs):
    parts, full = refs[:-1], refs[-1]
    for i, part in enumerate(parts):
        size = part.shape[0]
        full[pl.ds(slots[i] * size, size)] = part[...]


def place_parts(parts, slots):
    shape = (len(parts) * parts[0].shape[0],) + parts[0].shape[1:]
    slots = jnp.stack([jnp.asarray(slot, jnp.int32) for slot in slots])
    return call(place_kernel, 1, whole(shape, parts[0].dtype), scalar_first(len(parts)))(
        slots, *parts
    )


def around_parts(part):
    count, here = lax.axis_size("shard"), lax.axis_index("shard")
    parts = [part[None]] + [spin(part, step)[None] for step in range(1, count)]
    return parts, [(here - step) % count for step in range(count)]


def around(part):
    return place_parts(*around_parts(part))


def scan_first(state, direction):
    received = slide(state, direction)
    return received, low(wide(state) + wide(received))


def scan_rest(received, running, direction):
    found, step = [received], 2
    while step < lax.axis_size("shard"):
        found.append(slide(running, direction * step))
        running = low(wide(running) + wide(found[-1]))
        step *= 2
    return found


def sides_of(own):
    return flip(own, 2), flip(own, 4)


def halves_of(from_x, from_y):
    half = from_x.shape[0] // 2
    return from_x[:half], from_y[half:]


def diagonal_of(halves):
    return jnp.concatenate([flip(halves[0], 4), flip(halves[1], 2)], axis=0)


def share_flips(own):
    return [own[None]] + [flip(own, bit)[None] for bit in (2, 4, 6)]


def share_pair(parts):
    even = place_parts(parts, [0, 1, 2, 3])
    return even, flip(even, 1)


def sides_kernel(x_part, y_part, to_x, to_y, x_sum, y_sum):
    half = to_x.shape[0]
    x_sum[:half] = low(wide(x_part[:half]) + wide(to_x[...]))
    x_sum[half:] = x_part[half:]
    y_sum[:half] = y_part[:half]
    y_sum[half:] = low(wide(y_part[half:]) + wide(to_y[...]))


def join_parts(parts):
    count, here = lax.axis_size("shard"), lax.axis_index("shard")
    bit = PIECES
    if bit < lax.axis_size("rep"):
        mine = sum(wide(part) for part in parts)
        while bit < lax.axis_size("rep"):
            mine = mine + wide(flip(low(mine), bit))
            bit *= 2
        parts = [mine]
    rows, columns = parts[0].shape
    rows //= count

    def kernel(spot, *refs):
        sources, outs = refs[: len(parts)], refs[len(parts) :]
        for step in range(count):
            block = lax.rem(spot[0] + step, count)
            chosen = pl.ds(pl.multiple_of(block * rows, rows), rows)
            total = wide(sources[0][chosen, :])
            for source in sources[1:]:
                total = total + wide(source[chosen, :])
            outs[step][...] = total if step == 0 else low(total)

    shapes = [whole((rows, columns), wide_type)] + [whole((rows, columns))] * (count - 1)
    return call(kernel, 2, tuple(shapes), scalar_first(len(parts)))(
        here.reshape(1).astype(jnp.int32), *parts
    )


def settle(own, received, weight=1):
    def kernel(own, *refs):
        total = own[...]
        for ref in refs[:-1]:
            total = total + wide(ref[...])
        refs[-1][...] = low(total)

    return call(kernel, weight, whole(own.shape))(own, *received)


def dot(a, b):
    return jnp.dot(a, b, preferred_element_type=wide_type)


def dot_nt(a, b):
    return lax.dot_general(a, b, (((1,), (1,)), ((), ())), preferred_element_type=wide_type)


def dot_tn(a, b):
    return lax.dot_general(a, b, (((0,), (0,)), ((), ())), preferred_element_type=wide_type)


def normalize(rows):
    centred = rows - jnp.mean(rows, axis=-1, keepdims=True)
    scale = lax.rsqrt(jnp.mean(centred * centred, axis=-1, keepdims=True) + norm_epsilon)
    return centred * scale, scale


def norm_backward(grad, normal, scale, gain):
    e = grad * gain
    return scale * (
        e
        - jnp.mean(e, axis=-1, keepdims=True)
        - normal * jnp.mean(e * normal, axis=-1, keepdims=True)
    )


def lane_index(shape):
    return lax.broadcasted_iota(jnp.int32, shape, len(shape) - 1)


def row_index(shape):
    return lax.broadcasted_iota(jnp.int32, shape, len(shape) - 2)


def left_half(shape):
    return lane_index(shape) < HEAD


def aligned(index, unit):
    return pl.multiple_of(index * unit, unit)


def with_ones(pair):
    left = left_half(pair.shape)
    one = jnp.ones_like(pair)
    return jnp.where(left, pair, one), jnp.where(left, one, pair)


def pack_state(even, odd, p):
    lane = lane_index(even.shape)
    packed = jnp.where(lane < HEAD, even, odd)
    sums = jnp.where(lane == HEAD + 2 * p, even, jnp.where(lane == 2 * p + 1, odd, 0.0))
    return packed, sums


def unpack_state(packed, sums, p):
    shape = packed.shape
    lane, row = lane_index(shape), row_index(shape)
    pick_even = low(jnp.where((row == HEAD + 2 * p) & (lane >= HEAD), 1.0, 0.0))
    pick_odd = low(jnp.where((row == 2 * p + 1) & (lane < HEAD), 1.0, 0.0))
    even = jnp.where(lane < HEAD, packed, dot(sums, pick_even))
    odd = jnp.where(lane < HEAD, dot(sums, pick_odd), packed)
    return low(even), low(odd)


def added(refs, b, rows):
    total = wide(refs[0][b, rows, :])
    for ref in refs[1:]:
        total = total + wide(ref[b, rows, :])
    return total


def sums_of(refs):
    found = []
    gap = jnp.zeros((HEAD - EDGE, FEAT), wide_type)
    for b in range(refs[0].shape[0]):
        edges = added(refs, b, slice(PAIRS * FEAT, SLAB))
        found.append(low(jnp.concatenate([edges[:EDGE], gap, edges[EDGE:], gap], axis=0).T))
    return found


def states_at(refs, b, p, sums):
    return unpack_state(added(refs, b, pair_at(p)), sums[b], p)


def maps_kernel(small, maps, vectors, weight):
    shard_count, size, _ = small.shape
    rows = D // shard_count
    lines = 4 * rows // FEAT
    for s in range(shard_count):
        for j in range(3):
            count = min(size, rows - j * size)
            if count > 0:
                weight[s * rows + j * size : s * rows + j * size + count, :] = wide(
                    small[s, :count, j * FEAT : (j + 1) * FEAT]
                )
        flat = []
        for line in range(rows, rows + lines):
            j, row = line // size, line % size
            flat.append(wide(small[s, row : row + 1, j * FEAT : (j + 1) * FEAT]))
        flat = jnp.concatenate(flat, axis=1)
        for v in range(4):
            vectors[v : v + 1, s * rows : (s + 1) * rows] = flat[:, v * rows : (v + 1) * rows]
    gap = jnp.zeros((HEAD, HEAD), low_type)
    for head in range(HEADS):
        turned = low(weight[head * HEAD : (head + 1) * HEAD, :].T)
        g, a = head // 4, head % 4
        for which in range(2):
            block = turned[which * HEAD : (which + 1) * HEAD]
            maps[which * (D // GROUP) + g, a * HEAD : (a + 1) * HEAD, :] = jnp.concatenate(
                [block if a == b else gap for b in range(4)], axis=1
            )


def features(maps, base, columns, f_t, f):
    def group(g, carry):
        u_t = dot_nt(maps[base + g], columns[:, pl.ds(aligned(g, GROUP), GROUP)])
        for a in range(4):
            u = u_t[a * HEAD : (a + 1) * HEAD]
            up = jnp.exp(u - jnp.max(u, axis=0, keepdims=True))
            down = jnp.exp(jnp.min(u, axis=0, keepdims=True) - u)
            plus = up / jnp.sum(up, axis=0, keepdims=True)
            minus = down / jnp.sum(down, axis=0, keepdims=True)
            feature = low(jnp.concatenate([plus, minus], axis=0))
            rows = pl.ds(aligned(g * 4 + a, FEAT), FEAT)
            f_t[rows, :] = feature
            f[:, rows] = feature.T
        return carry

    lax.fori_loop(0, D // GROUP, group, 0)


def wanted(place, k, first, last):
    block = place[0] ^ k
    return block, (block >= first) & (block < last)


def each_piece(place, pieces, first, last, work):
    for k in range(PIECES):
        block, use = wanted(place, k, first, last)

        @pl.when(use)
        def _():
            work(block - first, pieces[k])


def chunk_at(index):
    return pl.ds(aligned(index, CHUNK), CHUNK)


def pair_at(index):
    return pl.ds(aligned(index, FEAT), FEAT)


VALUES = D // FEAT
QUERY_BLOCKS = D // CHUNK


def copy_rows(source, target):
    def step(i, carry):
        rows = pl.ds(aligned(i, 2 * HEAD), 2 * HEAD)
        target[rows, :] = source[rows, :]
        return carry

    lax.fori_loop(0, source.shape[0] // (2 * HEAD), step, 0)


def keys_kernel(place, tokens, vectors, maps, *refs):
    pieces = refs[:PIECES]
    normed, keyed, fk, fk_t, state, w_kv = refs[PIECES:]
    seqs = state.shape[0]
    length = tokens.shape[0] // seqs
    normal, _ = normalize(wide(tokens[...]))
    normed[...] = low(normal * vectors[0:1, :] + vectors[1:2, :])

    def keep(index, weight):
        copy_rows(weight, w_kv.at[index])

    each_piece(place, pieces, QUERY_BLOCKS, QKV_BLOCKS, keep)

    def project(index, carry):
        keyed[:, chunk_at(index)] = low(dot(normed[...], w_kv[index]))
        return carry

    lax.fori_loop(0, QKV_BLOCKS - QUERY_BLOCKS, project, 0)
    features(maps, D // GROUP, keyed, fk_t, fk)
    state_sums(state, length, lambda p, here: with_ones(keyed[here, pair_at(VALUES + p)]), fk_t)


def state_sums(state, length, sides, f_t):
    seqs = state.shape[0]

    def pair(p, sums):
        result = []
        for b in range(seqs):
            here = slice(b * length, (b + 1) * length)
            first, second = sides(p, here)
            even = dot(f_t[pair_at(2 * p), here], first)
            odd = dot(f_t[pair_at(2 * p + 1), here], second)
            packed, new = pack_state(even, odd, p)
            state[b, pair_at(p), :] = low(packed)
            result.append(sums[b] + new)
        return tuple(result)

    empty = tuple(jnp.zeros((FEAT, FEAT), wide_type) for _ in range(seqs))
    sums = lax.fori_loop(0, PAIRS, pair, empty)
    for b in range(seqs):
        turned = low(sums[b].T)
        state[b, PAIRS * FEAT : PAIRS * FEAT + EDGE, :] = turned[:EDGE]
        state[b, PAIRS * FEAT + EDGE :, :] = turned[HEAD : HEAD + EDGE]


def queries_kernel(place, normed, keyed, fk_t, maps, *refs):
    pieces = refs[:PIECES]
    normed_t, queries, fq, fq_t, partial, w_out, w_q = refs[PIECES:]

    def keep(index, weight):
        copy_rows(weight, w_q.at[index])

    def keep_out(index, weight):
        copy_rows(weight, w_out.at[:, chunk_at(index)])

    each_piece(place, pieces, 0, QUERY_BLOCKS, keep)
    each_piece(place, pieces, QKV_BLOCKS, PIECES, keep_out)

    def project(index, carry):
        queries[:, chunk_at(index)] = low(dot(normed[...], w_q[index]))
        return carry

    lax.fori_loop(0, QUERY_BLOCKS, project, 0)
    normed_t[...] = normed[...].T
    features(maps, 0, queries, fq_t, fq)
    seqs, length, _ = partial.shape

    def pair(p, carry):
        for b in range(seqs):
            here = slice(b * length, (b + 1) * length)
            values = with_ones(keyed[here, pair_at(VALUES + p)])
            for side in range(2):
                rows = pair_at(2 * p + side)
                scores = dot(fq[here, rows], fk_t[rows, here])
                scores = jnp.where(row_index(scores.shape) >= lane_index(scores.shape), scores, 0.0)
                partial[b, :, rows] = dot(low(scores), values[side])
        return carry

    lax.fori_loop(0, PAIRS, pair, 0)


def attend_kernel(tokens, vectors, partial, fq, w_out, *refs):
    priors, (attended, inverse, resid, second, second_t) = refs[:-5], refs[-5:]
    seqs = priors[0].shape[0]
    length = tokens.shape[0] // seqs

    sums = sums_of(priors)

    def pair(p, carry):
        for b in range(seqs):
            here = slice(b * length, (b + 1) * length)
            states = states_at(priors, b, p, sums)
            found = []
            for side in range(2):
                rows = pair_at(2 * p + side)
                found.append(partial[b, :, rows] + dot(fq[here, rows], states[side]))
            left = left_half(found[0].shape)
            turned = [pltpu.roll(a, HEAD, 1) for a in found]
            over = 1.0 / jnp.where(left, turned[0], turned[1])
            attended[here, pair_at(p)] = low(jnp.where(left, found[0], found[1]) * over)
            inverse[here, pair_at(p)] = over
        return carry

    lax.fori_loop(0, PAIRS, pair, 0)
    resid[...] = wide(tokens[...]) + dot(attended[...], w_out[...])
    normal, _ = normalize(resid[...])
    second[...] = low(normal * vectors[2:3, :] + vectors[3:4, :])
    second_t[...] = second[...].T


def mlp_kernel(second, second_other, cotangent, cotangent_other, resid, attended, *refs):
    pieces = refs[:4]
    out_sum, out_send, back_sum, back_send, hiddens, d_pres, second_other_t, attended_t = refs[4:12]
    up, down, ready = refs[12:]
    count = second.shape[0]
    parts = grads_layout(second.shape[1], pieces[0].shape[0])

    def copies(k, source):
        listed = []
        for i, (src, dst) in enumerate(parts):
            if dst[0] == "up":
                target = up.at[pl.ds(dst[1], dst[2]), chunk_at(k)]
            else:
                start = pl.multiple_of(k * CHUNK + dst[1], dst[2])
                target = down.at[pl.ds(start, dst[2]), pl.ds(dst[3], CHUNK)]
            listed.append(
                pltpu.make_async_copy(source.at[pl.ds(src, dst[2]), :], target, ready.at[k, i])
            )
        return listed

    for k in range(4):
        for copy in copies(k, pieces[k]):
            copy.start()
    second_other_t[...] = second_other[...].T
    attended_t[...] = attended[...].T

    def piece(k, carry):
        for copy in copies(k, pieces[0]):
            copy.wait()
        columns = chunk_at(k)
        for side, (source, grad) in enumerate(
            ((second, cotangent), (second_other, cotangent_other))
        ):
            here = slice(side * count, (side + 1) * count)
            pre = dot(source[...], up[:, columns])
            square = pre * pre
            bent = jnp.tanh(pre * (0.7978845608 + (0.7978845608 * 0.044715) * square))
            half = 0.5 + 0.5 * bent
            slope = half + (half * (1.0 - bent)) * pre * (
                0.7978845608 + (3.0 * 0.7978845608 * 0.044715) * square
            )
            hiddens[here, columns] = low(pre * half)
            d_pres[here, columns] = low(dot_nt(grad[...], down[columns, :]) * slope)
        return carry

    lax.fori_loop(0, 4, piece, 0)
    tile = count // 2

    def own(i, carry):
        here = pl.ds(aligned(i, tile), tile)
        back_sum[here, :] = dot_nt(d_pres[here, :], up[...])
        out_sum[here, :] = resid[here, :] + dot(hiddens[here, :], down[...])
        return carry

    def other(i, carry):
        here, there = pl.ds(aligned(i, tile), tile), pl.ds(aligned(i + 2, tile), tile)
        back_send[here, :] = low(dot_nt(d_pres[there, :], up[...]))
        out_send[here, :] = low(dot(hiddens[there, :], down[...]))
        return carry

    lax.fori_loop(0, 2, own, 0)
    lax.fori_loop(0, 2, other, 0)


def store_piece(outs, made, k):
    half = outs[3].shape[0]
    for i in range(3):

        @pl.when(k == i)
        def _():
            outs[i][...] = made[...]

    @pl.when(k == 3)
    def _():
        outs[3][...] = made[:half]
        outs[4][...] = made[half:]


def mlp_grads_kernel(second_t, second_other_t, cotangent, cotangent_other, hiddens, d_pres, *refs):
    outs, made = refs[:5], refs[5]
    count = cotangent.shape[0]
    own, other = slice(0, count), slice(count, 2 * count)

    def piece(k, carry):
        columns = chunk_at(k)
        d_up = dot(second_t[...], d_pres[own, columns])
        d_up = d_up + dot(second_other_t[...], d_pres[other, columns])
        d_down = dot_tn(hiddens[own, columns], cotangent[...])
        d_down = d_down + dot_tn(hiddens[other, columns], cotangent_other[...])
        d_up, d_down = low(d_up), low(d_down)
        for src, dst in grads_layout(second_t.shape[0], made.shape[0]):
            rows = slice(dst[1], dst[1] + dst[2])
            if dst[0] == "up":
                made[src : src + dst[2], :] = d_up[rows]
            else:
                made[src : src + dst[2], :] = d_down[rows, dst[3] : dst[3] + CHUNK]
        store_piece(outs, made, k)
        return carry

    lax.fori_loop(0, 4, piece, 0)


def grads_layout(width, block):
    shards = block // CHUNK
    up_rows = width // shards
    down_rows = CHUNK // shards
    parts = []
    for s in range(shards):
        base = s * (up_rows + 2 * down_rows)
        parts.append((base, ("up", s * up_rows, up_rows)))
        for side in range(2):
            parts.append(
                (
                    base + up_rows + side * down_rows,
                    ("down", s * down_rows, down_rows, side * CHUNK),
                )
            )
    return parts


def resid_kernel(back_sum, back_other, resid, cotangent, vectors, w_out, attended, inverse, fq_t, *refs):
    d_resid, d_resid_low, d_vectors, d_num, d_den, state = refs
    seqs = state.shape[0]
    length = resid.shape[0] // seqs
    normal, scale = normalize(resid[...])
    grad = back_sum[...] + wide(back_other[...])
    d_vectors[0:1, :] = jnp.sum(grad * normal, axis=0, keepdims=True)
    d_vectors[1:2, :] = jnp.sum(grad, axis=0, keepdims=True)
    d_resid[...] = wide(cotangent[...]) + norm_backward(grad, normal, scale, vectors[2:3, :])
    d_resid_low[...] = low(d_resid[...])
    d_attended = dot_nt(d_resid_low[...], w_out[...])
    shape = (FEAT, FEAT)
    cross = low(
        jnp.where(left_half(shape) != (row_index(shape) < HEAD), -1.0 / HEAD, 0.0)
    )
    for p in range(PAIRS):
        columns = slice(p * FEAT, (p + 1) * FEAT)
        num = d_attended[:, columns] * inverse[:, columns]
        product = num * wide(attended[:, columns])
        top = low(product)
        rest = low(product - wide(top))
        d_num[:, columns] = low(num)
        d_den[:, columns] = low(dot(top, cross) + dot(rest, cross))

    state_sums(state, length, lambda p, here: joined(d_num, d_den, here, p), fq_t)


def joined(d_num, d_den, here, p):
    columns = pl.ds(aligned(p, FEAT), FEAT)
    num, den = d_num[here, columns], d_den[here, columns]
    left = left_half(num.shape)
    return jnp.where(left, num, den), jnp.where(left, den, num)


def softmax_backward(feature, grad):
    plus, minus = wide(feature[:HEAD]), wide(feature[HEAD:])
    d_plus, d_minus = grad[:HEAD], grad[HEAD:]
    d_plus = plus * (d_plus - jnp.sum(d_plus * plus, axis=0, keepdims=True))
    d_minus = minus * (d_minus - jnp.sum(d_minus * minus, axis=0, keepdims=True))
    return low(d_plus - d_minus)


def linked(outer, value):
    link = dot_nt(outer, value)
    return low(jnp.where(row_index(link.shape) >= lane_index(link.shape), link, 0.0))


def local_queries_kernel(queries, keyed, maps, fq_t, fk_t, d_num, d_den, *refs):
    priors, (d_queries, d_features, d_uq_t) = refs[:-3], refs[-3:]
    seqs = priors[0].shape[0]
    length = keyed.shape[0] // seqs

    sums = sums_of(priors)

    def pair(p, carry):
        for b in range(seqs):
            here = slice(b * length, (b + 1) * length)
            values = with_ones(keyed[here, pair_at(VALUES + p)])
            outer = joined(d_num, d_den, here, p)
            states = states_at(priors, b, p, sums)
            for side in range(2):
                rows = pair_at(2 * p + side)
                link = linked(outer[side], values[side])
                d_q = dot_nt(fk_t[rows, here], link) + dot_nt(states[side], outer[side])
                d_uq_t[pl.ds(aligned(2 * p + side, HEAD), HEAD), here] = softmax_backward(
                    fq_t[rows, here], d_q
                )
        return carry

    lax.fori_loop(0, PAIRS, pair, 0)
    feature_backward(d_uq_t, queries, maps, 0, d_queries, d_features, 0)


def local_keys_kernel(keyed, fq_t, fk, d_num, d_den, d_fk_t, d_values, *, seqs):
    length = keyed.shape[0] // seqs

    def pair(p, carry):
        for b in range(seqs):
            here = slice(b * length, (b + 1) * length)
            values = with_ones(keyed[here, pair_at(VALUES + p)])
            outer = joined(d_num, d_den, here, p)
            found = []
            for side in range(2):
                rows = pair_at(2 * p + side)
                q_t = fq_t[rows, here]
                d_fk_t[rows, here] = dot(q_t, linked(outer[side], values[side]))
                scores = dot(fk[here, rows], q_t)
                row, lane = row_index(scores.shape), lane_index(scores.shape)
                found.append(dot(low(jnp.where(row <= lane, scores, 0.0)), outer[side]))
            left = left_half(found[0].shape)
            d_values[here, pair_at(p)] = jnp.where(left, found[0], found[1])
        return carry

    lax.fori_loop(0, PAIRS, pair, 0)


def feature_backward(d_u_t, source, maps, base, target, d_features, lane):
    def group(g, carry):
        d_u = d_u_t[pl.ds(aligned(g, GROUP), GROUP), :]
        columns = pl.ds(aligned(g, GROUP), GROUP)
        product = dot(d_u, source[:, columns]).T
        for a in range(4):
            block = slice(a * HEAD, (a + 1) * HEAD)
            rows = pl.ds(aligned(g * 4 + a, HEAD), HEAD)
            d_features[rows, lane : lane + HEAD] = product[block, block]
        target[:, columns] = low(dot(d_u.T, maps[base + g]))
        return carry

    lax.fori_loop(0, D // GROUP, group, 0)


def mixed_kernel(
    place, keyed, fk, fk_t, maps, d_fk_t, d_values, d_resid_low, d_queries, d_half, *refs
):
    laters, (d_keyed, d_features, sends, d_uk_t) = refs[:-4], refs[-4:]
    seqs = laters[0].shape[0]
    length = keyed.shape[0] // seqs

    sums = sums_of(laters)

    def pair(p, carry):
        for b in range(seqs):
            here = slice(b * length, (b + 1) * length)
            values = with_ones(keyed[here, pair_at(VALUES + p)])
            states = states_at(laters, b, p, sums)
            found = []
            for side in range(2):
                rows = pl.ds(aligned(2 * p + side, FEAT), FEAT)
                d_k = d_fk_t[rows, here] + dot_nt(states[side], values[side])
                d_uk_t[pl.ds(aligned(2 * p + side, HEAD), HEAD), here] = softmax_backward(
                    fk_t[rows, here], d_k
                )
                found.append(dot(fk[here, rows], states[side]))
            left = left_half(found[0].shape)
            total = d_values[here, pl.ds(aligned(p, FEAT), FEAT)] + jnp.where(
                left, found[0], found[1]
            )
            d_keyed[here, pair_at(VALUES + p)] = low(total)
        return carry

    lax.fori_loop(0, PAIRS, pair, 0)
    feature_backward(d_uk_t, keyed, maps, D // GROUP, d_keyed, d_features, HEAD)
    d_features[:, :HEAD] = d_half[:, :HEAD]

    def send(i, carry):
        own_column(place[0] ^ (2 * i + 1), sends.at[i], d_queries, d_keyed, d_resid_low)
        return carry

    lax.fori_loop(0, PIECES // 2, send, 0)


def own_column(block, target, d_queries, d_keyed, d_resid_low):
    @pl.when(block < QUERY_BLOCKS)
    def _():
        target[...] = d_queries[:, chunk_at(block)]

    @pl.when((block >= QUERY_BLOCKS) & (block < QKV_BLOCKS))
    def _():
        target[...] = d_keyed[:, chunk_at(block - QUERY_BLOCKS)]

    @pl.when(block >= QKV_BLOCKS)
    def _():
        target[...] = d_resid_low[:, chunk_at(block - QKV_BLOCKS)]


TINY_ROWS = 48
TINY_TILE = 16


def tiny_size(rows):
    return -(-(rows + 8) // TINY_ROWS) * TINY_ROWS


def in_grads_kernel(
    place, d_queries, d_keyed, d_resid_low, received, tiny, tiny_other, *refs
):
    sources, outs, (held, column, made, ready) = refs[:4], refs[4:9], refs[9:]
    shard_count, size, _ = tiny.shape
    rows = D // shard_count
    copies = [
        pltpu.make_async_copy(source, held.at[i], ready.at[i]) for i, source in enumerate(sources)
    ]
    for copy in copies:
        copy.start()
    for copy in copies:
        copy.wait()

    def piece(i, carry):
        block = place[0] ^ (2 * i)
        kind = 2 * jnp.where(block < QKV_BLOCKS, 0, 1)
        own_column(block, column, d_queries, d_keyed, d_resid_low)
        value = low(dot(held[kind], column[...]) + dot(held[kind + 1], received[i]))
        for s in range(shard_count):
            base = s * (rows + TINY_TILE)
            made[base : base + rows, :] = value[s * rows : (s + 1) * rows]
            for j in range(TINY_ROWS // TINY_TILE):
                target = (slice(base + rows, base + rows + TINY_TILE), slice(j * FEAT, (j + 1) * FEAT))
                made[target] = jnp.zeros((TINY_TILE, FEAT), low_type)

                @pl.when(block < size // TINY_ROWS)
                def _():
                    start = pl.multiple_of(block * TINY_ROWS + j * TINY_TILE, TINY_TILE)
                    spot = pl.ds(start, TINY_TILE)
                    made[target] = low(wide(tiny[s, spot, :]) + wide(tiny_other[s, spot, :]))

        store_piece(outs, made, i)
        return carry

    lax.fori_loop(0, PIECES // 2, piece, 0)


def early_kernel(d_queries, w_q, total):
    total[...] = jnp.zeros_like(total)
    add_products(total, d_queries, w_q)


def add_products(total, source, weights):
    def add(index, carry):
        total[...] += dot_nt(source[:, chunk_at(index)], weights[index])
        return carry

    lax.fori_loop(0, weights.shape[0], add, 0)


def input_kernel(tokens, vectors, early, d_keyed, d_resid, out_sum, out_other, *refs):
    w_kv, d_features, d_vectors, block_out, grad_tokens, tiny, total = refs
    total[...] = early[...]
    block_out[...] = low(out_sum[...] + wide(out_other[...]))

    add_products(total, d_keyed, w_kv)
    normal, scale = normalize(wide(tokens[...]))
    grad = total[...]
    grad_tokens[...] = low(d_resid[...] + norm_backward(grad, normal, scale, vectors[0:1, :]))
    gathered = [
        jnp.sum(grad * normal, axis=0, keepdims=True),
        jnp.sum(grad, axis=0, keepdims=True),
        d_vectors[0:1, :],
        d_vectors[1:2, :],
    ]
    shard_count, size, _ = tiny.shape
    rows = D // shard_count
    tiny[...] = jnp.zeros_like(tiny)
    for s in range(shard_count):
        tiny[s, :rows, :] = low(d_features[s * rows : (s + 1) * rows, :])
        lines = []
        for vector in gathered:
            line = vector[:, s * rows : (s + 1) * rows]
            gap = jnp.zeros((1, 2 * FEAT - rows), wide_type)
            line = jnp.concatenate([line, gap], axis=1)
            lines += [line[:, :FEAT], line[:, FEAT:]]
        tiny[s, rows : rows + 8, :] = low(jnp.concatenate(lines, axis=0))


def lay_in_kernel(place, even, odd, qkv, out, feature, rest):
    rows = qkv.shape[0]
    for k in range(PIECES):
        block = place[0] ^ k
        piece = (even, odd)[k % 2].at[k // 2]

        @pl.when(block < QKV_BLOCKS)
        def _():
            qkv[:, chunk_at(block)] = wide(piece[:rows])

        @pl.when(block >= QKV_BLOCKS)
        def _():
            out[:, chunk_at(block - QKV_BLOCKS)] = wide(piece[:rows])

        for j in range(TINY_ROWS // TINY_TILE):

            @pl.when(block < rows // TINY_ROWS)
            def _():
                start = pl.multiple_of(block * TINY_ROWS + j * TINY_TILE, TINY_TILE)
                feature[pl.ds(start, TINY_TILE), :] = wide(
                    piece[rows:, j * FEAT : (j + 1) * FEAT]
                )

        @pl.when(block == rows // TINY_ROWS)
        def _():
            rest[...] = wide(piece[rows : rows + 8, :FEAT])


def lay_mlp_kernel(place, even, odd, up, down, ordered):
    up_rows, down_rows = ordered.shape[1], down.shape[1]
    for k in range(PIECES):
        block = place[0] ^ k
        piece = (even, odd)[k % 2]
        ordered[block] = piece[k // 2, :up_rows, :]
        for side in range(2):
            start = up_rows + side * down_rows
            down[block, :, side * CHUNK : (side + 1) * CHUNK] = wide(
                piece[k // 2, start : start + down_rows, :]
            )
    for s in range(CHUNK // down_rows):
        columns = slice(s * down_rows, (s + 1) * down_rows)
        row = jnp.concatenate([ordered[r][:, columns] for r in range(PIECES)], axis=1)
        up[:, s * PIECES * down_rows : (s + 1) * PIECES * down_rows] = wide(row)


def whole(shape, dtype=low_type):
    return jax.ShapeDtypeStruct(shape, dtype)


def scalar_first(count):
    return [pl.BlockSpec(memory_space=pltpu.SMEM)] + [
        pl.BlockSpec(memory_space=pltpu.VMEM) for _ in range(count)
    ]


def call(kernel, weight, out_shape, in_specs=None, scratch=(), limit=8, **rest):
    if in_specs is not None:
        rest["in_specs"] = in_specs
    return pl.pallas_call(
        kernel,
        out_shape=out_shape,
        scratch_shapes=list(scratch),
        compiler_params=pltpu.CompilerParams(vmem_limit_bytes=limit << 20),
        cost_estimate=pl.CostEstimate(
            flops=int(weight * 2000 * 10**6), transcendentals=0, bytes_accessed=int(weight * 6 * 10**6)
        ),
        **rest,
    )


def interleave(even, odd):
    return [part for both in zip(even, odd) for part in both]


def shards(
    tokens,
    gain_attn,
    bias_attn,
    w_qkv,
    w_feature,
    w_out,
    gain_mlp,
    bias_mlp,
    w_up,
    w_down,
    cotangent,
):
    shard_count = lax.axis_size("shard")
    place = lax.axis_index("rep") % PIECES
    spot = place.reshape(1).astype(jnp.int32)
    seqs, length, _ = tokens.shape
    count = seqs * length
    rows = w_qkv.shape[0]
    fine = CHUNK // shard_count
    flat = tokens.reshape(count, D)
    flat_cotangent = cotangent.reshape(count, D)
    anywhere = [pl.BlockSpec(memory_space=pl.ANY)] * PIECES

    part_in = lax.dynamic_slice_in_dim(
        jnp.concatenate([w_qkv, w_out], axis=1), place * CHUNK, CHUNK, 1
    )
    vectors = jnp.concatenate([gain_attn, bias_attn, gain_mlp, bias_mlp]).reshape(-1, FEAT)
    small = jnp.concatenate([w_feature, vectors], axis=0)
    small_rows = -(-small.shape[0] // 24) * 8
    small = jnp.pad(small, ((0, 3 * small_rows - small.shape[0]), (0, 0)))
    small = jnp.concatenate(jnp.split(small, 3, axis=0), axis=1)
    part_in = jnp.concatenate([part_in, small], axis=0)
    part_up = lax.dynamic_index_in_dim(
        w_up.reshape(rows, shard_count, PIECES, fine), place, 2, False
    ).reshape(rows, CHUNK)
    part_down = lax.dynamic_slice_in_dim(w_down, place * fine, fine, 0)
    part_mlp = jnp.concatenate([part_up, part_down[:, :CHUNK], part_down[:, CHUNK:]], axis=0)

    here = lax.axis_index("shard")
    in_slots = jnp.stack([(here - step) % shard_count for step in range(shard_count)])
    in_spins = [part_in] + [spin(part_in, step) for step in range(1, shard_count)]

    def place_in_kernel(slots, *refs):
        parts, (full, rest) = refs[:-2], refs[-2:]
        for i, part in enumerate(parts):
            full[slots[i]] = part[:rows]
            rest[slots[i]] = part[rows:]

    in_full, small = call(
        place_in_kernel,
        1,
        (whole((shard_count, rows, CHUNK)), whole((shard_count, small_rows, CHUNK))),
        scalar_first(shard_count),
    )(in_slots.astype(jnp.int32), *in_spins)
    cotangent_other = flip(flat_cotangent, 1)
    in_full, small = lax.optimization_barrier((in_full, small))
    maps, vectors = call(
        maps_kernel,
        15,
        (whole((2 * D // GROUP, GROUP, GROUP)), whole((4, D), wide_type)),
        scratch=[pltpu.VMEM((D, FEAT), wide_type)],
    )(small)
    in_full = in_full.reshape(-1, CHUNK)
    part_mlp, in_full = lax.optimization_barrier((part_mlp, in_full))
    steps = list(range(1, shard_count))
    from_x, from_y = sides_of(in_full)
    in_other = flip(in_full, 1)
    soon = {step: spin(part_mlp, step) for step in steps[:1] + steps[2:]}
    in_halves, maps, vectors, soon = lax.optimization_barrier(
        (halves_of(from_x, from_y), maps, vectors, soon)
    )
    soon.update({step: spin(soon[1], 1) for step in steps[1:2]})
    diagonal = diagonal_of(in_halves)
    diagonal, soon = lax.optimization_barrier((diagonal, soon))
    in_even = [in_full, from_x, from_y, diagonal]
    in_pieces = interleave(in_even, [in_other] + [flip(part, 1) for part in in_even[1:]])
    here = lax.axis_index("shard")
    mlp_parts = [part_mlp[None]] + [soon[step][None] for step in steps]
    mlp_slots = [(here - step) % shard_count for step in range(shard_count)]

    mlp_full = place_parts(mlp_parts, mlp_slots).reshape(-1, CHUNK)
    mlp_full, vectors = lax.optimization_barrier((mlp_full, vectors))
    normed, keyed, fk, fk_t, key_state, w_kv = call(
        keys_kernel,
        8,
        (
            whole((count, D)),
            whole((count, 2 * D)),
            whole((count, HEADS * FEAT)),
            whole((HEADS * FEAT, count)),
            whole((seqs, SLAB, FEAT)),
            whole((QKV_BLOCKS - QUERY_BLOCKS, D, CHUNK)),
        ),
        scalar_first(3 + PIECES),
    )(spot, flat, vectors, maps, *in_pieces)
    prior, running = scan_first(key_state, 1)
    mlp_x, mlp_y = sides_of(mlp_full)
    normed_t, queries, fq, fq_t, partial, out_weight, w_q = call(
        queries_kernel,
        9,
        (
            whole((D, count)),
            whole((count, D)),
            whole((count, HEADS * FEAT)),
            whole((HEADS * FEAT, count)),
            whole((seqs, length, HEADS * FEAT), wide_type),
            whole((D, D)),
            whole((QUERY_BLOCKS, D, CHUNK)),
        ),
        scalar_first(4 + PIECES),
    )(spot, normed, keyed, fk_t, maps, *in_pieces)
    running, partial = lax.optimization_barrier((running, partial))
    priors = scan_rest(prior, running, 1)
    mlp_halves, partial = lax.optimization_barrier((halves_of(mlp_x, mlp_y), partial))
    mlp_pieces = [mlp_full, mlp_x, mlp_y, diagonal_of(mlp_halves)]
    attended, inverse, resid, second, second_t = call(
        attend_kernel,
        5,
        (
            whole((count, D)),
            whole((count, D), wide_type),
            whole((count, D), wide_type),
            whole((count, D)),
            whole((D, count)),
        ),
    )(flat, vectors, partial, fq, out_weight, *priors)

    second_other = flip(second, 1)
    (
        out_sum,
        out_send,
        back_sum,
        back_send,
        hiddens,
        d_pres,
        second_other_t,
        attended_t,
    ) = call(
        mlp_kernel,
        20,
        (
            whole((count, D), wide_type),
            whole((count, D)),
            whole((count, D), wide_type),
            whole((count, D)),
            whole((2 * count, 4 * CHUNK)),
            whole((2 * count, 4 * CHUNK)),
            whole((D, count)),
            whole((D, count)),
        ),
        [pl.BlockSpec(memory_space=pltpu.VMEM)] * 6 + anywhere[:4],
        [
            pltpu.VMEM((D, 4 * CHUNK), low_type),
            pltpu.VMEM((4 * CHUNK, D), low_type),
            pltpu.SemaphoreType.DMA((4, 3 * shard_count)),
        ],
        limit=18,
    )(second, second_other, flat_cotangent, cotangent_other, resid, attended, *mlp_pieces)
    back_other = flip(back_send, 1)
    out_other = flip(out_send, 1)
    d_resid, d_resid_low, d_vectors_two, d_num, d_den, query_state = call(
        resid_kernel,
        5,
        (
            whole((count, D), wide_type),
            whole((count, D)),
            whole((2, D), wide_type),
            whole((count, D)),
            whole((count, D)),
            whole((seqs, SLAB, FEAT)),
        ),
    )(back_sum, back_other, resid, flat_cotangent, vectors, out_weight, attended, inverse, fq_t)
    later, running = scan_first(query_state, -1)
    normed_other_t = flip(normed_t, 1)
    attended_other_t = flip(attended_t, 1)
    second_t, query_state, normed_other_t, attended_other_t, out_other = lax.optimization_barrier(
        (second_t, query_state, normed_other_t, attended_other_t, out_other)
    )
    piece = lambda rows: tuple(
        whole((size, CHUNK)) for size in (rows, rows, rows, rows // 2, rows // 2)
    )
    mlp_grads = call(
        mlp_grads_kernel, 7, piece(2 * D), scratch=[pltpu.VMEM((2 * D, CHUNK), low_type)]
    )(second_t, second_other_t, flat_cotangent, cotangent_other, hiddens, d_pres)
    mlp_to_x, mlp_to_y = flip(mlp_grads[3], 4), flip(mlp_grads[4], 2)
    running, fk_t = lax.optimization_barrier((running, fk_t))
    laters = scan_rest(later, running, -1)
    d_queries, d_half, _ = call(
        local_queries_kernel,
        6,
        (whole((count, D)), whole((D, FEAT), wide_type), whole((D, count))),
    )(queries, keyed, maps, fq_t, fk_t, d_num, d_den, *priors)
    mlp_to_x, mlp_to_y, d_half = lax.optimization_barrier((mlp_to_x, mlp_to_y, d_half))
    add_sides = lambda parts, to_x, to_y: call(
        sides_kernel, 1, (whole(parts[1].shape), whole(parts[1].shape))
    )(parts[1], parts[2], to_x, to_y)
    mlp_sides = add_sides(mlp_grads, mlp_to_x, mlp_to_y)
    mlp_sides, d_half, fk = lax.optimization_barrier((mlp_sides, d_half, fk))
    d_fk_t, d_values = call(
        lambda *refs: local_keys_kernel(*refs, seqs=seqs),
        5,
        (whole((HEADS * FEAT, count), wide_type), whole((count, D), wide_type)),
    )(keyed, fq_t, fk, d_num, d_den)
    mlp_joined = [flip(mlp_sides[0], 2), flip(mlp_sides[1], 4)]
    early = call(early_kernel, 2, whole((count, D), wide_type))(d_queries, w_q)
    early, d_half = lax.optimization_barrier((early, d_half))
    d_keyed, d_features, sends, _ = call(
        mixed_kernel,
        7,
        (
            whole((count, 2 * D)),
            whole((D, FEAT), wide_type),
            whole((PIECES // 2, count, CHUNK)),
            whole((D, count)),
        ),
        scalar_first(9 + len(laters)),
    )(spot, keyed, fk, fk_t, maps, d_fk_t, d_values, d_resid_low, d_queries, d_half, *laters)
    received = flip(sends, 1)
    block_out, grad_tokens, tiny = call(
        input_kernel,
        7,
        (
            whole((count, D)),
            whole((count, D)),
            whole((shard_count, tiny_size(rows), FEAT)),
        ),
        scratch=[pltpu.VMEM((count, D), wide_type)],
    )(
        flat,
        vectors,
        early,
        d_keyed,
        d_resid,
        out_sum,
        out_other,
        w_kv,
        d_features,
        d_vectors_two,
    )
    tiny_other = flip(tiny, 1)
    mlp_blocks = join_parts([mlp_grads[0], *mlp_joined])
    received, tiny_other, mlp_blocks = lax.optimization_barrier((received, tiny_other, mlp_blocks))
    in_grads = call(
        in_grads_kernel,
        7,
        piece(D + shard_count * TINY_TILE),
        scalar_first(6) + anywhere[:4],
        [
            pltpu.VMEM((4, D, count), low_type),
            pltpu.VMEM((count, CHUNK), low_type),
            pltpu.VMEM((D + shard_count * TINY_TILE, CHUNK), low_type),
            pltpu.SemaphoreType.DMA((4,)),
        ],
    )(
        spot,
        d_queries,
        d_keyed,
        d_resid_low,
        received,
        tiny,
        tiny_other,
        normed_t,
        normed_other_t,
        attended_t,
        attended_other_t,
    )
    mlp_received = [spin(part, step + 1) for step, part in enumerate(mlp_blocks[1:])]
    in_upper, in_lower, mlp_received[:1] = lax.optimization_barrier(
        (in_grads[3], in_grads[4], mlp_received[:1])
    )
    in_to_x, in_to_y = flip(in_upper, 4), flip(in_lower, 2)
    in_to_x, in_to_y, mlp_received[2:] = lax.optimization_barrier(
        (in_to_x, in_to_y, mlp_received[2:])
    )
    in_sides = add_sides(in_grads, in_to_x, in_to_y)
    in_joined = [flip(in_sides[0], 2), flip(in_sides[1], 4)]
    in_joined, mlp_received = lax.optimization_barrier((in_joined, mlp_received))
    in_blocks = join_parts([in_grads[0], *in_joined])
    in_received = [spin(part, step + 1) for step, part in enumerate(in_blocks[1:])]
    in_blocks, mlp_received = lax.optimization_barrier((in_blocks, mlp_received))
    mlp_total = settle(mlp_blocks[0], mlp_received, 10)
    mlp_flips = share_flips(mlp_total)
    in_received, _ = lax.optimization_barrier((in_received, mlp_total))
    in_received[:1], mlp_flips[:2] = lax.optimization_barrier((in_received[:1], mlp_flips[:2]))
    mlp_sums = share_pair(mlp_flips)
    in_flips = share_flips(settle(in_blocks[0], in_received))
    grad_up, grad_down = call(
        lay_mlp_kernel,
        3,
        (whole((rows, 4 * D), wide_type), whole((PIECES, fine, D), wide_type)),
        scalar_first(2),
        [pltpu.VMEM((PIECES, rows, CHUNK), low_type)],
    )(spot, *mlp_sums)
    grad_down = grad_down.reshape(-1, D)
    in_flips, grad_up, grad_down = lax.optimization_barrier((in_flips, grad_up, grad_down))
    in_sums = share_pair(in_flips)
    grad_qkv, grad_out, grad_feature, d_vectors = call(
        lay_in_kernel,
        2,
        (
            whole((rows, 3 * D), wide_type),
            whole((rows, D), wide_type),
            whole((rows, FEAT), wide_type),
            whole((8, FEAT), wide_type),
        ),
        scalar_first(2),
    )(spot, *in_sums)
    d_vectors = d_vectors.reshape(4, 2 * FEAT)[:, :rows]
    return (
        block_out.reshape(tokens.shape),
        grad_tokens.reshape(tokens.shape),
        d_vectors[0],
        d_vectors[1],
        grad_qkv,
        grad_feature,
        grad_out,
        d_vectors[2],
        d_vectors[3],
        grad_up,
        grad_down,
    )


def solution(mesh):
    placed = (
        P("rep", "shard", None),
        P("shard"),
        P("shard"),
        P("shard", None),
        P("shard", None),
        P("shard", None),
        P("shard"),
        P("shard"),
        P("shard", None),
        P("shard", None),
        P("rep", "shard", None),
    )
    return jax.shard_map(
        shards,
        mesh=mesh,
        in_specs=placed,
        out_specs=(
            P("rep", "shard", None),
            P("rep", "shard", None),
            P("shard"),
            P("shard"),
            P("shard", None),
            P("shard", None),
            P("shard", None),
            P("shard"),
            P("shard"),
            P("shard", None),
            P("shard", None),
        ),
        check_vma=False,
    )
```

```python
import jax
import jax.numpy as jnp
from jax import lax
from jax.experimental import pallas as pl
from jax.experimental.pallas import tpu as pltpu
from jax.sharding import PartitionSpec as P

D = 768
HEADS = 12
HEAD = 64
FEAT = 128
PAIRS = HEADS // 2
GROUP = 4 * HEAD
PIECES = 8
CHUNK = 4 * D // PIECES
QKV_BLOCKS = 3 * D // CHUNK
EDGE = 16
SLAB = PAIRS * FEAT + 2 * EDGE

norm_epsilon = 1e-05
low_type = jnp.bfloat16
wide_type = jnp.float32


def flip(value, bit):
    count = lax.axis_size("rep")
    return lax.ppermute(value, "rep", [(i, i ^ bit) for i in range(count)])


def spin(value, step):
    count = lax.axis_size("shard")
    return lax.ppermute(value, "shard", [(i, (i + step) % count) for i in range(count)])


def slide(value, step):
    count = lax.axis_size("shard")
    pairs = [(i, i + step) for i in range(count) if 0 <= i + step < count]
    return lax.ppermute(value, "shard", pairs)


def wide(value):
    return value.astype(wide_type)


def low(value):
    return value.astype(low_type)


def place_kernel(slots, *refs):
    parts, full = refs[:-1], refs[-1]
    for i, part in enumerate(parts):
        size = part.shape[0]
        full[pl.ds(slots[i] * size, size)] = part[...]


def place_parts(parts, slots):
    shape = (len(parts) * parts[0].shape[0],) + parts[0].shape[1:]
    slots = jnp.stack([jnp.asarray(slot, jnp.int32) for slot in slots])
    return call(place_kernel, 1, whole(shape, parts[0].dtype), scalar_first(len(parts)))(
        slots, *parts
    )


def around_parts(part):
    count, here = lax.axis_size("shard"), lax.axis_index("shard")
    parts = [part[None]] + [spin(part, step)[None] for step in range(1, count)]
    return parts, [(here - step) % count for step in range(count)]


def around(part):
    return place_parts(*around_parts(part))


def scan_first(state, direction):
    received = slide(state, direction)
    return received, low(wide(state) + wide(received))


def scan_rest(received, running, direction):
    found, step = [received], 2
    while step < lax.axis_size("shard"):
        found.append(slide(running, direction * step))
        running = low(wide(running) + wide(found[-1]))
        step *= 2
    return found


def sides_of(own):
    return flip(own, 2), flip(own, 4)


def halves_of(from_x, from_y):
    half = from_x.shape[0] // 2
    return from_x[:half], from_y[half:]


def diagonal_of(halves):
    return jnp.concatenate([flip(halves[0], 4), flip(halves[1], 2)], axis=0)


def share_flips(own):
    return [own[None]] + [flip(own, bit)[None] for bit in (2, 4, 6)]


def share_pair(parts):
    even = place_parts(parts, [0, 1, 2, 3])
    return even, flip(even, 1)


def sides_kernel(x_part, y_part, to_x, to_y, x_sum, y_sum):
    half = to_x.shape[0]
    x_sum[:half] = low(wide(x_part[:half]) + wide(to_x[...]))
    x_sum[half:] = x_part[half:]
    y_sum[:half] = y_part[:half]
    y_sum[half:] = low(wide(y_part[half:]) + wide(to_y[...]))


def join_parts(parts):
    count, here = lax.axis_size("shard"), lax.axis_index("shard")
    bit = PIECES
    if bit < lax.axis_size("rep"):
        mine = sum(wide(part) for part in parts)
        while bit < lax.axis_size("rep"):
            mine = mine + wide(flip(low(mine), bit))
            bit *= 2
        parts = [mine]
    rows, columns = parts[0].shape
    rows //= count

    def kernel(spot, *refs):
        sources, outs = refs[: len(parts)], refs[len(parts) :]
        for step in range(count):
            block = lax.rem(spot[0] + step, count)
            chosen = pl.ds(pl.multiple_of(block * rows, rows), rows)
            total = wide(sources[0][chosen, :])
            for source in sources[1:]:
                total = total + wide(source[chosen, :])
            outs[step][...] = total if step == 0 else low(total)

    shapes = [whole((rows, columns), wide_type)] + [whole((rows, columns))] * (count - 1)
    return call(kernel, 2, tuple(shapes), scalar_first(len(parts)))(
        here.reshape(1).astype(jnp.int32), *parts
    )


def settle(own, received, weight=1):
    def kernel(own, *refs):
        total = own[...]
        for ref in refs[:-1]:
            total = total + wide(ref[...])
        refs[-1][...] = low(total)

    return call(kernel, weight, whole(own.shape))(own, *received)


def dot(a, b):
    return jnp.dot(a, b, preferred_element_type=wide_type)


def dot_nt(a, b):
    return lax.dot_general(a, b, (((1,), (1,)), ((), ())), preferred_element_type=wide_type)


def dot_tn(a, b):
    return lax.dot_general(a, b, (((0,), (0,)), ((), ())), preferred_element_type=wide_type)


def normalize(rows):
    centred = rows - jnp.mean(rows, axis=-1, keepdims=True)
    scale = lax.rsqrt(jnp.mean(centred * centred, axis=-1, keepdims=True) + norm_epsilon)
    return centred * scale, scale


def norm_backward(grad, normal, scale, gain):
    e = grad * gain
    return scale * (
        e
        - jnp.mean(e, axis=-1, keepdims=True)
        - normal * jnp.mean(e * normal, axis=-1, keepdims=True)
    )


def lane_index(shape):
    return lax.broadcasted_iota(jnp.int32, shape, len(shape) - 1)


def row_index(shape):
    return lax.broadcasted_iota(jnp.int32, shape, len(shape) - 2)


def left_half(shape):
    return lane_index(shape) < HEAD


def aligned(index, unit):
    return pl.multiple_of(index * unit, unit)


def with_ones(pair):
    left = left_half(pair.shape)
    one = jnp.ones_like(pair)
    return jnp.where(left, pair, one), jnp.where(left, one, pair)


def pack_state(even, odd, p):
    lane = lane_index(even.shape)
    packed = jnp.where(lane < HEAD, even, odd)
    sums = jnp.where(lane == HEAD + 2 * p, even, jnp.where(lane == 2 * p + 1, odd, 0.0))
    return packed, sums


def unpack_state(packed, sums, p):
    shape = packed.shape
    lane, row = lane_index(shape), row_index(shape)
    pick_even = low(jnp.where((row == HEAD + 2 * p) & (lane >= HEAD), 1.0, 0.0))
    pick_odd = low(jnp.where((row == 2 * p + 1) & (lane < HEAD), 1.0, 0.0))
    even = jnp.where(lane < HEAD, packed, dot(sums, pick_even))
    odd = jnp.where(lane < HEAD, dot(sums, pick_odd), packed)
    return low(even), low(odd)


def added(refs, b, rows):
    total = wide(refs[0][b, rows, :])
    for ref in refs[1:]:
        total = total + wide(ref[b, rows, :])
    return total


def sums_of(refs):
    found = []
    gap = jnp.zeros((HEAD - EDGE, FEAT), wide_type)
    for b in range(refs[0].shape[0]):
        edges = added(refs, b, slice(PAIRS * FEAT, SLAB))
        found.append(low(jnp.concatenate([edges[:EDGE], gap, edges[EDGE:], gap], axis=0).T))
    return found


def states_at(refs, b, p, sums):
    return unpack_state(added(refs, b, pair_at(p)), sums[b], p)


def maps_kernel(small, maps, vectors, weight):
    shard_count, size, _ = small.shape
    rows = D // shard_count
    lines = 4 * rows // FEAT
    for s in range(shard_count):
        for j in range(3):
            count = min(size, rows - j * size)
            if count > 0:
                weight[s * rows + j * size : s * rows + j * size + count, :] = wide(
                    small[s, :count, j * FEAT : (j + 1) * FEAT]
                )
        flat = []
        for line in range(rows, rows + lines):
            j, row = line // size, line % size
            flat.append(wide(small[s, row : row + 1, j * FEAT : (j + 1) * FEAT]))
        flat = jnp.concatenate(flat, axis=1)
        for v in range(4):
            vectors[v : v + 1, s * rows : (s + 1) * rows] = flat[:, v * rows : (v + 1) * rows]
    gap = jnp.zeros((HEAD, HEAD), low_type)
    for head in range(HEADS):
        turned = low(weight[head * HEAD : (head + 1) * HEAD, :].T)
        g, a = head // 4, head % 4
        for which in range(2):
            block = turned[which * HEAD : (which + 1) * HEAD]
            maps[which * (D // GROUP) + g, a * HEAD : (a + 1) * HEAD, :] = jnp.concatenate(
                [block if a == b else gap for b in range(4)], axis=1
            )


def features(maps, base, columns, f_t, f):
    def group(g, carry):
        u_t = dot_nt(maps[base + g], columns[:, pl.ds(aligned(g, GROUP), GROUP)])
        for a in range(4):
            u = u_t[a * HEAD : (a + 1) * HEAD]
            up = jnp.exp(u - jnp.max(u, axis=0, keepdims=True))
            down = jnp.exp(jnp.min(u, axis=0, keepdims=True) - u)
            plus = up / jnp.sum(up, axis=0, keepdims=True)
            minus = down / jnp.sum(down, axis=0, keepdims=True)
            feature = low(jnp.concatenate([plus, minus], axis=0))
            rows = pl.ds(aligned(g * 4 + a, FEAT), FEAT)
            f_t[rows, :] = feature
            f[:, rows] = feature.T
        return carry

    lax.fori_loop(0, D // GROUP, group, 0)


def wanted(place, k, first, last):
    block = place[0] ^ k
    return block, (block >= first) & (block < last)


def each_piece(place, pieces, first, last, work):
    for k in range(PIECES):
        block, use = wanted(place, k, first, last)

        @pl.when(use)
        def _():
            work(block - first, pieces[k])


def chunk_at(index):
    return pl.ds(aligned(index, CHUNK), CHUNK)


def pair_at(index):
    return pl.ds(aligned(index, FEAT), FEAT)


VALUES = D // FEAT
QUERY_BLOCKS = D // CHUNK


def copy_rows(source, target):
    def step(i, carry):
        rows = pl.ds(aligned(i, 2 * HEAD), 2 * HEAD)
        target[rows, :] = source[rows, :]
        return carry

    lax.fori_loop(0, source.shape[0] // (2 * HEAD), step, 0)


def keys_kernel(place, tokens, vectors, maps, *refs):
    pieces = refs[:PIECES]
    normed, keyed, fk, fk_t, state, w_kv = refs[PIECES:]
    seqs = state.shape[0]
    length = tokens.shape[0] // seqs
    normal, _ = normalize(wide(tokens[...]))
    normed[...] = low(normal * vectors[0:1, :] + vectors[1:2, :])

    def keep(index, weight):
        copy_rows(weight, w_kv.at[index])

    each_piece(place, pieces, QUERY_BLOCKS, QKV_BLOCKS, keep)

    def project(index, carry):
        keyed[:, chunk_at(index)] = low(dot(normed[...], w_kv[index]))
        return carry

    lax.fori_loop(0, QKV_BLOCKS - QUERY_BLOCKS, project, 0)
    features(maps, D // GROUP, keyed, fk_t, fk)
    state_sums(state, length, lambda p, here: with_ones(keyed[here, pair_at(VALUES + p)]), fk_t)


def state_sums(state, length, sides, f_t):
    seqs = state.shape[0]

    def pair(p, sums):
        result = []
        for b in range(seqs):
            here = slice(b * length, (b + 1) * length)
            first, second = sides(p, here)
            even = dot(f_t[pair_at(2 * p), here], first)
            odd = dot(f_t[pair_at(2 * p + 1), here], second)
            packed, new = pack_state(even, odd, p)
            state[b, pair_at(p), :] = low(packed)
            result.append(sums[b] + new)
        return tuple(result)

    empty = tuple(jnp.zeros((FEAT, FEAT), wide_type) for _ in range(seqs))
    sums = lax.fori_loop(0, PAIRS, pair, empty)
    for b in range(seqs):
        turned = low(sums[b].T)
        state[b, PAIRS * FEAT : PAIRS * FEAT + EDGE, :] = turned[:EDGE]
        state[b, PAIRS * FEAT + EDGE :, :] = turned[HEAD : HEAD + EDGE]


def queries_kernel(place, normed, keyed, fk_t, maps, *refs):
    pieces = refs[:PIECES]
    normed_t, queries, fq, fq_t, partial, w_out, w_q = refs[PIECES:]

    def keep(index, weight):
        copy_rows(weight, w_q.at[index])

    def keep_out(index, weight):
        copy_rows(weight, w_out.at[:, chunk_at(index)])

    each_piece(place, pieces, 0, QUERY_BLOCKS, keep)
    each_piece(place, pieces, QKV_BLOCKS, PIECES, keep_out)

    def project(index, carry):
        queries[:, chunk_at(index)] = low(dot(normed[...], w_q[index]))
        return carry

    lax.fori_loop(0, QUERY_BLOCKS, project, 0)
    normed_t[...] = normed[...].T
    features(maps, 0, queries, fq_t, fq)
    seqs, length, _ = partial.shape

    def pair(p, carry):
        for b in range(seqs):
            here = slice(b * length, (b + 1) * length)
            values = with_ones(keyed[here, pair_at(VALUES + p)])
            for side in range(2):
                rows = pair_at(2 * p + side)
                scores = dot(fq[here, rows], fk_t[rows, here])
                scores = jnp.where(row_index(scores.shape) >= lane_index(scores.shape), scores, 0.0)
                partial[b, :, rows] = dot(low(scores), values[side])
        return carry

    lax.fori_loop(0, PAIRS, pair, 0)


def attend_kernel(tokens, vectors, partial, fq, w_out, *refs):
    priors, (attended, attended_t, inverse, resid, second, second_t) = refs[:-6], refs[-6:]
    seqs = priors[0].shape[0]
    length = tokens.shape[0] // seqs

    sums = sums_of(priors)

    def pair(p, carry):
        for b in range(seqs):
            here = slice(b * length, (b + 1) * length)
            states = states_at(priors, b, p, sums)
            found = []
            for side in range(2):
                rows = pair_at(2 * p + side)
                found.append(partial[b, :, rows] + dot(fq[here, rows], states[side]))
            left = left_half(found[0].shape)
            turned = [pltpu.roll(a, HEAD, 1) for a in found]
            over = 1.0 / jnp.where(left, turned[0], turned[1])
            attended[here, pair_at(p)] = low(jnp.where(left, found[0], found[1]) * over)
            inverse[here, pair_at(p)] = over
        return carry

    lax.fori_loop(0, PAIRS, pair, 0)
    resid[...] = wide(tokens[...]) + dot(attended[...], w_out[...])
    normal, _ = normalize(resid[...])
    second[...] = low(normal * vectors[2:3, :] + vectors[3:4, :])
    second_t[...] = second[...].T
    attended_t[...] = attended[...].T


def mlp_kernel(second, second_other, cotangent, cotangent_other, resid, *refs):
    pieces = refs[:4]
    out_sum, out_send, back_sum, back_send, hiddens, d_pres = refs[4:10]
    up, down, ready = refs[10:]
    count = second.shape[0]
    parts = grads_layout(second.shape[1], pieces[0].shape[0])

    def copies(k, source):
        listed = []
        for i, (src, dst) in enumerate(parts):
            if dst[0] == "up":
                target = up.at[pl.ds(dst[1], dst[2]), chunk_at(k)]
            else:
                start = pl.multiple_of(k * CHUNK + dst[1], dst[2])
                target = down.at[pl.ds(start, dst[2]), pl.ds(dst[3], CHUNK)]
            listed.append(
                pltpu.make_async_copy(source.at[pl.ds(src, dst[2]), :], target, ready.at[k, i])
            )
        return listed

    for k in range(4):
        for copy in copies(k, pieces[k]):
            copy.start()

    def piece(k, carry):
        for copy in copies(k, pieces[0]):
            copy.wait()
        columns = chunk_at(k)
        for side, (source, grad) in enumerate(
            ((second, cotangent), (second_other, cotangent_other))
        ):
            here = slice(side * count, (side + 1) * count)
            pre = dot(source[...], up[:, columns])
            square = pre * pre
            bent = jnp.tanh(pre * (0.7978845608 + (0.7978845608 * 0.044715) * square))
            half = 0.5 + 0.5 * bent
            slope = half + (half * (1.0 - bent)) * pre * (
                0.7978845608 + (3.0 * 0.7978845608 * 0.044715) * square
            )
            hiddens[here, columns] = low(pre * half)
            d_pres[here, columns] = low(dot_nt(grad[...], down[columns, :]) * slope)
        return carry

    lax.fori_loop(0, 4, piece, 0)
    tile = count // 2

    def own(i, carry):
        here = pl.ds(aligned(i, tile), tile)
        back_sum[here, :] = dot_nt(d_pres[here, :], up[...])
        out_sum[here, :] = resid[here, :] + dot(hiddens[here, :], down[...])
        return carry

    def other(i, carry):
        here, there = pl.ds(aligned(i, tile), tile), pl.ds(aligned(i + 2, tile), tile)
        back_send[here, :] = low(dot_nt(d_pres[there, :], up[...]))
        out_send[here, :] = low(dot(hiddens[there, :], down[...]))
        return carry

    lax.fori_loop(0, 2, own, 0)
    lax.fori_loop(0, 2, other, 0)


def store_piece(outs, made, k):
    half = outs[3].shape[0]
    for i in range(3):

        @pl.when(k == i)
        def _():
            outs[i][...] = made[...]

    @pl.when(k == 3)
    def _():
        outs[3][...] = made[:half]
        outs[4][...] = made[half:]


def mlp_grads_kernel(second_t, second_other, cotangent, cotangent_other, hiddens, d_pres, *refs):
    outs, made, second_other_t = refs[:5], refs[5], refs[6]
    second_other_t[...] = second_other[...].T
    count = cotangent.shape[0]
    own, other = slice(0, count), slice(count, 2 * count)

    def piece(k, carry):
        columns = chunk_at(k)
        d_up = dot(second_t[...], d_pres[own, columns])
        d_up = d_up + dot(second_other_t[...], d_pres[other, columns])
        d_down = dot_tn(hiddens[own, columns], cotangent[...])
        d_down = d_down + dot_tn(hiddens[other, columns], cotangent_other[...])
        d_up, d_down = low(d_up), low(d_down)
        for src, dst in grads_layout(second_t.shape[0], made.shape[0]):
            rows = slice(dst[1], dst[1] + dst[2])
            if dst[0] == "up":
                made[src : src + dst[2], :] = d_up[rows]
            else:
                made[src : src + dst[2], :] = d_down[rows, dst[3] : dst[3] + CHUNK]
        store_piece(outs, made, k)
        return carry

    lax.fori_loop(0, 4, piece, 0)


def grads_layout(width, block):
    shards = block // CHUNK
    up_rows = width // shards
    down_rows = CHUNK // shards
    parts = []
    for s in range(shards):
        base = s * (up_rows + 2 * down_rows)
        parts.append((base, ("up", s * up_rows, up_rows)))
        for side in range(2):
            parts.append(
                (
                    base + up_rows + side * down_rows,
                    ("down", s * down_rows, down_rows, side * CHUNK),
                )
            )
    return parts


def resid_kernel(back_sum, back_other, resid, cotangent, vectors, w_out, attended, inverse, fq_t, *refs):
    d_resid, d_resid_low, d_vectors, d_num, d_den, state = refs
    seqs = state.shape[0]
    length = resid.shape[0] // seqs
    normal, scale = normalize(resid[...])
    grad = back_sum[...] + wide(back_other[...])
    d_vectors[0:1, :] = jnp.sum(grad * normal, axis=0, keepdims=True)
    d_vectors[1:2, :] = jnp.sum(grad, axis=0, keepdims=True)
    d_resid[...] = wide(cotangent[...]) + norm_backward(grad, normal, scale, vectors[2:3, :])
    d_resid_low[...] = low(d_resid[...])
    d_attended = dot_nt(d_resid_low[...], w_out[...])
    shape = (FEAT, FEAT)
    cross = low(
        jnp.where(left_half(shape) != (row_index(shape) < HEAD), -1.0 / HEAD, 0.0)
    )
    for p in range(PAIRS):
        columns = slice(p * FEAT, (p + 1) * FEAT)
        num = d_attended[:, columns] * inverse[:, columns]
        product = num * wide(attended[:, columns])
        top = low(product)
        rest = low(product - wide(top))
        d_num[:, columns] = low(num)
        d_den[:, columns] = low(dot(top, cross) + dot(rest, cross))

    state_sums(state, length, lambda p, here: joined(d_num, d_den, here, p), fq_t)


def joined(d_num, d_den, here, p):
    columns = pl.ds(aligned(p, FEAT), FEAT)
    num, den = d_num[here, columns], d_den[here, columns]
    left = left_half(num.shape)
    return jnp.where(left, num, den), jnp.where(left, den, num)


def softmax_backward(feature, grad):
    plus, minus = wide(feature[:HEAD]), wide(feature[HEAD:])
    d_plus, d_minus = grad[:HEAD], grad[HEAD:]
    d_plus = plus * (d_plus - jnp.sum(d_plus * plus, axis=0, keepdims=True))
    d_minus = minus * (d_minus - jnp.sum(d_minus * minus, axis=0, keepdims=True))
    return low(d_plus - d_minus)


def linked(outer, value):
    link = dot_nt(outer, value)
    return low(jnp.where(row_index(link.shape) >= lane_index(link.shape), link, 0.0))


def local_queries_kernel(queries, keyed, maps, fq_t, fk_t, d_num, d_den, *refs):
    priors, (d_queries, d_features, d_uq_t) = refs[:-3], refs[-3:]
    seqs = priors[0].shape[0]
    length = keyed.shape[0] // seqs

    sums = sums_of(priors)

    def pair(p, carry):
        for b in range(seqs):
            here = slice(b * length, (b + 1) * length)
            values = with_ones(keyed[here, pair_at(VALUES + p)])
            outer = joined(d_num, d_den, here, p)
            states = states_at(priors, b, p, sums)
            for side in range(2):
                rows = pair_at(2 * p + side)
                link = linked(outer[side], values[side])
                d_q = dot_nt(fk_t[rows, here], link) + dot_nt(states[side], outer[side])
                d_uq_t[pl.ds(aligned(2 * p + side, HEAD), HEAD), here] = softmax_backward(
                    fq_t[rows, here], d_q
                )
        return carry

    lax.fori_loop(0, PAIRS, pair, 0)
    feature_backward(d_uq_t, queries, maps, 0, d_queries, d_features, 0)


def local_keys_kernel(keyed, fq_t, fk, d_num, d_den, d_fk_t, d_values, *, seqs):
    length = keyed.shape[0] // seqs

    def pair(p, carry):
        for b in range(seqs):
            here = slice(b * length, (b + 1) * length)
            values = with_ones(keyed[here, pair_at(VALUES + p)])
            outer = joined(d_num, d_den, here, p)
            found = []
            for side in range(2):
                rows = pair_at(2 * p + side)
                q_t = fq_t[rows, here]
                d_fk_t[rows, here] = dot(q_t, linked(outer[side], values[side]))
                scores = dot(fk[here, rows], q_t)
                row, lane = row_index(scores.shape), lane_index(scores.shape)
                found.append(dot(low(jnp.where(row <= lane, scores, 0.0)), outer[side]))
            left = left_half(found[0].shape)
            d_values[here, pair_at(p)] = jnp.where(left, found[0], found[1])
        return carry

    lax.fori_loop(0, PAIRS, pair, 0)


def feature_backward(d_u_t, source, maps, base, target, d_features, lane):
    def group(g, carry):
        d_u = d_u_t[pl.ds(aligned(g, GROUP), GROUP), :]
        columns = pl.ds(aligned(g, GROUP), GROUP)
        product = dot(d_u, source[:, columns]).T
        for a in range(4):
            block = slice(a * HEAD, (a + 1) * HEAD)
            rows = pl.ds(aligned(g * 4 + a, HEAD), HEAD)
            d_features[rows, lane : lane + HEAD] = product[block, block]
        target[:, columns] = low(dot(d_u.T, maps[base + g]))
        return carry

    lax.fori_loop(0, D // GROUP, group, 0)


def mixed_kernel(
    place, keyed, fk, fk_t, maps, d_fk_t, d_values, d_resid_low, d_queries, d_half, *refs
):
    laters, (d_keyed, d_features, sends, d_uk_t) = refs[:-4], refs[-4:]
    seqs = laters[0].shape[0]
    length = keyed.shape[0] // seqs

    sums = sums_of(laters)

    def pair(p, carry):
        for b in range(seqs):
            here = slice(b * length, (b + 1) * length)
            values = with_ones(keyed[here, pair_at(VALUES + p)])
            states = states_at(laters, b, p, sums)
            found = []
            for side in range(2):
                rows = pl.ds(aligned(2 * p + side, FEAT), FEAT)
                d_k = d_fk_t[rows, here] + dot_nt(states[side], values[side])
                d_uk_t[pl.ds(aligned(2 * p + side, HEAD), HEAD), here] = softmax_backward(
                    fk_t[rows, here], d_k
                )
                found.append(dot(fk[here, rows], states[side]))
            left = left_half(found[0].shape)
            total = d_values[here, pl.ds(aligned(p, FEAT), FEAT)] + jnp.where(
                left, found[0], found[1]
            )
            d_keyed[here, pair_at(VALUES + p)] = low(total)
        return carry

    lax.fori_loop(0, PAIRS, pair, 0)
    feature_backward(d_uk_t, keyed, maps, D // GROUP, d_keyed, d_features, HEAD)
    d_features[:, :HEAD] = d_half[:, :HEAD]

    def send(i, carry):
        own_column(place[0] ^ (2 * i + 1), sends.at[i], d_queries, d_keyed, d_resid_low)
        return carry

    lax.fori_loop(0, PIECES // 2, send, 0)


def own_column(block, target, d_queries, d_keyed, d_resid_low):
    @pl.when(block < QUERY_BLOCKS)
    def _():
        target[...] = d_queries[:, chunk_at(block)]

    @pl.when((block >= QUERY_BLOCKS) & (block < QKV_BLOCKS))
    def _():
        target[...] = d_keyed[:, chunk_at(block - QUERY_BLOCKS)]

    @pl.when(block >= QKV_BLOCKS)
    def _():
        target[...] = d_resid_low[:, chunk_at(block - QKV_BLOCKS)]


TINY_ROWS = 48
TINY_TILE = 16


def tiny_size(rows):
    return -(-(rows + 8) // TINY_ROWS) * TINY_ROWS


def in_grads_kernel(
    place, d_queries, d_keyed, d_resid_low, received, tiny, tiny_other, *refs
):
    sources, outs, (held, column, made, ready) = refs[:4], refs[4:9], refs[9:]
    shard_count, size, _ = tiny.shape
    rows = D // shard_count
    copies = [
        pltpu.make_async_copy(source, held.at[i], ready.at[i]) for i, source in enumerate(sources)
    ]
    for copy in copies:
        copy.start()
    for copy in copies:
        copy.wait()

    def piece(i, carry):
        block = place[0] ^ (2 * i)
        kind = 2 * jnp.where(block < QKV_BLOCKS, 0, 1)
        own_column(block, column, d_queries, d_keyed, d_resid_low)
        value = low(dot(held[kind], column[...]) + dot(held[kind + 1], received[i]))
        for s in range(shard_count):
            base = s * (rows + TINY_TILE)
            made[base : base + rows, :] = value[s * rows : (s + 1) * rows]
            for j in range(TINY_ROWS // TINY_TILE):
                target = (slice(base + rows, base + rows + TINY_TILE), slice(j * FEAT, (j + 1) * FEAT))
                made[target] = jnp.zeros((TINY_TILE, FEAT), low_type)

                @pl.when(block < size // TINY_ROWS)
                def _():
                    start = pl.multiple_of(block * TINY_ROWS + j * TINY_TILE, TINY_TILE)
                    spot = pl.ds(start, TINY_TILE)
                    made[target] = low(wide(tiny[s, spot, :]) + wide(tiny_other[s, spot, :]))

        store_piece(outs, made, i)
        return carry

    lax.fori_loop(0, PIECES // 2, piece, 0)


def early_kernel(d_queries, w_q, total):
    total[...] = jnp.zeros_like(total)
    add_products(total, d_queries, w_q)


def add_products(total, source, weights):
    def add(index, carry):
        total[...] += dot_nt(source[:, chunk_at(index)], weights[index])
        return carry

    lax.fori_loop(0, weights.shape[0], add, 0)


def input_kernel(tokens, vectors, early, d_keyed, d_resid, out_sum, out_other, *refs):
    w_kv, d_features, d_vectors, block_out, grad_tokens, tiny, total = refs
    total[...] = early[...]
    block_out[...] = low(out_sum[...] + wide(out_other[...]))

    add_products(total, d_keyed, w_kv)
    normal, scale = normalize(wide(tokens[...]))
    grad = total[...]
    grad_tokens[...] = low(d_resid[...] + norm_backward(grad, normal, scale, vectors[0:1, :]))
    gathered = [
        jnp.sum(grad * normal, axis=0, keepdims=True),
        jnp.sum(grad, axis=0, keepdims=True),
        d_vectors[0:1, :],
        d_vectors[1:2, :],
    ]
    shard_count, size, _ = tiny.shape
    rows = D // shard_count
    tiny[...] = jnp.zeros_like(tiny)
    for s in range(shard_count):
        tiny[s, :rows, :] = low(d_features[s * rows : (s + 1) * rows, :])
        lines = []
        for vector in gathered:
            line = vector[:, s * rows : (s + 1) * rows]
            gap = jnp.zeros((1, 2 * FEAT - rows), wide_type)
            line = jnp.concatenate([line, gap], axis=1)
            lines += [line[:, :FEAT], line[:, FEAT:]]
        tiny[s, rows : rows + 8, :] = low(jnp.concatenate(lines, axis=0))


def lay_in_kernel(place, even, odd, qkv, out, feature, rest):
    rows = qkv.shape[0]
    for k in range(PIECES):
        block = place[0] ^ k
        piece = (even, odd)[k % 2].at[k // 2]

        @pl.when(block < QKV_BLOCKS)
        def _():
            qkv[:, chunk_at(block)] = wide(piece[:rows])

        @pl.when(block >= QKV_BLOCKS)
        def _():
            out[:, chunk_at(block - QKV_BLOCKS)] = wide(piece[:rows])

        for j in range(TINY_ROWS // TINY_TILE):

            @pl.when(block < rows // TINY_ROWS)
            def _():
                start = pl.multiple_of(block * TINY_ROWS + j * TINY_TILE, TINY_TILE)
                feature[pl.ds(start, TINY_TILE), :] = wide(
                    piece[rows:, j * FEAT : (j + 1) * FEAT]
                )

        @pl.when(block == rows // TINY_ROWS)
        def _():
            rest[...] = wide(piece[rows : rows + 8, :FEAT])


def lay_mlp_kernel(place, even, odd, up, down, ordered):
    up_rows, down_rows = ordered.shape[1], down.shape[1]
    for k in range(PIECES):
        block = place[0] ^ k
        piece = (even, odd)[k % 2]
        ordered[block] = piece[k // 2, :up_rows, :]
        for side in range(2):
            start = up_rows + side * down_rows
            down[block, :, side * CHUNK : (side + 1) * CHUNK] = wide(
                piece[k // 2, start : start + down_rows, :]
            )
    for s in range(CHUNK // down_rows):
        columns = slice(s * down_rows, (s + 1) * down_rows)
        row = jnp.concatenate([ordered[r][:, columns] for r in range(PIECES)], axis=1)
        up[:, s * PIECES * down_rows : (s + 1) * PIECES * down_rows] = wide(row)


def whole(shape, dtype=low_type):
    return jax.ShapeDtypeStruct(shape, dtype)


def scalar_first(count):
    return [pl.BlockSpec(memory_space=pltpu.SMEM)] + [
        pl.BlockSpec(memory_space=pltpu.VMEM) for _ in range(count)
    ]


def call(kernel, weight, out_shape, in_specs=None, scratch=(), limit=8, **rest):
    if in_specs is not None:
        rest["in_specs"] = in_specs
    return pl.pallas_call(
        kernel,
        out_shape=out_shape,
        scratch_shapes=list(scratch),
        compiler_params=pltpu.CompilerParams(vmem_limit_bytes=limit << 20),
        cost_estimate=pl.CostEstimate(
            flops=int(weight * 2000 * 10**6), transcendentals=0, bytes_accessed=int(weight * 6 * 10**6)
        ),
        **rest,
    )


def interleave(even, odd):
    return [part for both in zip(even, odd) for part in both]


def shards(
    tokens,
    gain_attn,
    bias_attn,
    w_qkv,
    w_feature,
    w_out,
    gain_mlp,
    bias_mlp,
    w_up,
    w_down,
    cotangent,
):
    shard_count = lax.axis_size("shard")
    place = lax.axis_index("rep") % PIECES
    spot = place.reshape(1).astype(jnp.int32)
    seqs, length, _ = tokens.shape
    count = seqs * length
    rows = w_qkv.shape[0]
    fine = CHUNK // shard_count
    flat = tokens.reshape(count, D)
    flat_cotangent = cotangent.reshape(count, D)
    anywhere = [pl.BlockSpec(memory_space=pl.ANY)] * PIECES

    part_in = lax.dynamic_slice_in_dim(
        jnp.concatenate([w_qkv, w_out], axis=1), place * CHUNK, CHUNK, 1
    )
    vectors = jnp.concatenate([gain_attn, bias_attn, gain_mlp, bias_mlp]).reshape(-1, FEAT)
    small = jnp.concatenate([w_feature, vectors], axis=0)
    small_rows = -(-small.shape[0] // 24) * 8
    small = jnp.pad(small, ((0, 3 * small_rows - small.shape[0]), (0, 0)))
    small = jnp.concatenate(jnp.split(small, 3, axis=0), axis=1)
    part_in = jnp.concatenate([part_in, small], axis=0)
    part_up = lax.dynamic_index_in_dim(
        w_up.reshape(rows, shard_count, PIECES, fine), place, 2, False
    ).reshape(rows, CHUNK)
    part_down = lax.dynamic_slice_in_dim(w_down, place * fine, fine, 0)
    part_mlp = jnp.concatenate([part_up, part_down[:, :CHUNK], part_down[:, CHUNK:]], axis=0)

    here = lax.axis_index("shard")
    in_slots = jnp.stack([(here - step) % shard_count for step in range(shard_count)])
    in_spins = [part_in] + [spin(part_in, step) for step in range(1, shard_count)]

    def place_in_kernel(slots, *refs):
        parts, (full, rest) = refs[:-2], refs[-2:]
        for i, part in enumerate(parts):
            full[slots[i]] = part[:rows]
            rest[slots[i]] = part[rows:]

    in_full, small = call(
        place_in_kernel,
        1,
        (whole((shard_count, rows, CHUNK)), whole((shard_count, small_rows, CHUNK))),
        scalar_first(shard_count),
    )(in_slots.astype(jnp.int32), *in_spins)
    cotangent_other = flip(flat_cotangent, 1)
    in_full, small = lax.optimization_barrier((in_full, small))
    maps, vectors = call(
        maps_kernel,
        15,
        (whole((2 * D // GROUP, GROUP, GROUP)), whole((4, D), wide_type)),
        scratch=[pltpu.VMEM((D, FEAT), wide_type)],
    )(small)
    in_full = in_full.reshape(-1, CHUNK)
    part_mlp, in_full = lax.optimization_barrier((part_mlp, in_full))
    steps = list(range(1, shard_count))
    from_x, from_y = sides_of(in_full)
    in_other = flip(in_full, 1)
    soon = {step: spin(part_mlp, step) for step in steps[:1] + steps[2:]}
    in_halves, maps, vectors, soon = lax.optimization_barrier(
        (halves_of(from_x, from_y), maps, vectors, soon)
    )
    soon.update({step: spin(soon[1], 1) for step in steps[1:2]})
    diagonal = diagonal_of(in_halves)
    diagonal, soon = lax.optimization_barrier((diagonal, soon))
    in_even = [in_full, from_x, from_y, diagonal]
    in_pieces = interleave(in_even, [in_other] + [flip(part, 1) for part in in_even[1:]])
    here = lax.axis_index("shard")
    mlp_parts = [part_mlp[None]] + [soon[step][None] for step in steps]
    mlp_slots = [(here - step) % shard_count for step in range(shard_count)]

    mlp_full = place_parts(mlp_parts, mlp_slots).reshape(-1, CHUNK)
    mlp_full, vectors = lax.optimization_barrier((mlp_full, vectors))
    normed, keyed, fk, fk_t, key_state, w_kv = call(
        keys_kernel,
        8,
        (
            whole((count, D)),
            whole((count, 2 * D)),
            whole((count, HEADS * FEAT)),
            whole((HEADS * FEAT, count)),
            whole((seqs, SLAB, FEAT)),
            whole((QKV_BLOCKS - QUERY_BLOCKS, D, CHUNK)),
        ),
        scalar_first(3 + PIECES),
    )(spot, flat, vectors, maps, *in_pieces)
    prior, running = scan_first(key_state, 1)
    mlp_x, mlp_y = sides_of(mlp_full)
    normed_t, queries, fq, fq_t, partial, out_weight, w_q = call(
        queries_kernel,
        9,
        (
            whole((D, count)),
            whole((count, D)),
            whole((count, HEADS * FEAT)),
            whole((HEADS * FEAT, count)),
            whole((seqs, length, HEADS * FEAT), wide_type),
            whole((D, D)),
            whole((QUERY_BLOCKS, D, CHUNK)),
        ),
        scalar_first(4 + PIECES),
    )(spot, normed, keyed, fk_t, maps, *in_pieces)
    running, partial = lax.optimization_barrier((running, partial))
    priors = scan_rest(prior, running, 1)
    mlp_halves, partial = lax.optimization_barrier((halves_of(mlp_x, mlp_y), partial))
    mlp_pieces = [mlp_full, mlp_x, mlp_y, diagonal_of(mlp_halves)]
    attended, attended_t, inverse, resid, second, second_t = call(
        attend_kernel,
        5,
        (
            whole((count, D)),
            whole((D, count)),
            whole((count, D), wide_type),
            whole((count, D), wide_type),
            whole((count, D)),
            whole((D, count)),
        ),
    )(flat, vectors, partial, fq, out_weight, *priors)

    second_other = flip(second, 1)
    (
        out_sum,
        out_send,
        back_sum,
        back_send,
        hiddens,
        d_pres,
    ) = call(
        mlp_kernel,
        20,
        (
            whole((count, D), wide_type),
            whole((count, D)),
            whole((count, D), wide_type),
            whole((count, D)),
            whole((2 * count, 4 * CHUNK)),
            whole((2 * count, 4 * CHUNK)),
        ),
        [pl.BlockSpec(memory_space=pltpu.VMEM)] * 5 + anywhere[:4],
        [
            pltpu.VMEM((D, 4 * CHUNK), low_type),
            pltpu.VMEM((4 * CHUNK, D), low_type),
            pltpu.SemaphoreType.DMA((4, 3 * shard_count)),
        ],
        limit=18,
    )(second, second_other, flat_cotangent, cotangent_other, resid, *mlp_pieces)
    back_other = flip(back_send, 1)
    out_other = flip(out_send, 1)
    d_resid, d_resid_low, d_vectors_two, d_num, d_den, query_state = call(
        resid_kernel,
        5,
        (
            whole((count, D), wide_type),
            whole((count, D)),
            whole((2, D), wide_type),
            whole((count, D)),
            whole((count, D)),
            whole((seqs, SLAB, FEAT)),
        ),
    )(back_sum, back_other, resid, flat_cotangent, vectors, out_weight, attended, inverse, fq_t)
    later, running = scan_first(query_state, -1)
    normed_other_t = flip(normed_t, 1)
    attended_other_t = flip(attended_t, 1)
    second_t, query_state, normed_other_t, attended_other_t, out_other = lax.optimization_barrier(
        (second_t, query_state, normed_other_t, attended_other_t, out_other)
    )
    piece = lambda rows: tuple(
        whole((size, CHUNK)) for size in (rows, rows, rows, rows // 2, rows // 2)
    )
    mlp_grads = call(
        mlp_grads_kernel, 7, piece(2 * D), scratch=[pltpu.VMEM((2 * D, CHUNK), low_type), pltpu.VMEM((D, count), low_type)]
    )(second_t, second_other, flat_cotangent, cotangent_other, hiddens, d_pres)
    mlp_to_x, mlp_to_y = flip(mlp_grads[3], 4), flip(mlp_grads[4], 2)
    running, fk_t = lax.optimization_barrier((running, fk_t))
    laters = scan_rest(later, running, -1)
    d_queries, d_half, _ = call(
        local_queries_kernel,
        6,
        (whole((count, D)), whole((D, FEAT), wide_type), whole((D, count))),
    )(queries, keyed, maps, fq_t, fk_t, d_num, d_den, *priors)
    mlp_to_x, mlp_to_y, d_half = lax.optimization_barrier((mlp_to_x, mlp_to_y, d_half))
    add_sides = lambda parts, to_x, to_y: call(
        sides_kernel, 1, (whole(parts[1].shape), whole(parts[1].shape))
    )(parts[1], parts[2], to_x, to_y)
    mlp_sides = add_sides(mlp_grads, mlp_to_x, mlp_to_y)
    mlp_sides, d_half, fk = lax.optimization_barrier((mlp_sides, d_half, fk))
    d_fk_t, d_values = call(
        lambda *refs: local_keys_kernel(*refs, seqs=seqs),
        5,
        (whole((HEADS * FEAT, count), wide_type), whole((count, D), wide_type)),
    )(keyed, fq_t, fk, d_num, d_den)
    mlp_joined = [flip(mlp_sides[0], 2), flip(mlp_sides[1], 4)]
    early = call(early_kernel, 2, whole((count, D), wide_type))(d_queries, w_q)
    early, d_half = lax.optimization_barrier((early, d_half))
    d_keyed, d_features, sends, _ = call(
        mixed_kernel,
        7,
        (
            whole((count, 2 * D)),
            whole((D, FEAT), wide_type),
            whole((PIECES // 2, count, CHUNK)),
            whole((D, count)),
        ),
        scalar_first(9 + len(laters)),
    )(spot, keyed, fk, fk_t, maps, d_fk_t, d_values, d_resid_low, d_queries, d_half, *laters)
    received = flip(sends, 1)
    block_out, grad_tokens, tiny = call(
        input_kernel,
        7,
        (
            whole((count, D)),
            whole((count, D)),
            whole((shard_count, tiny_size(rows), FEAT)),
        ),
        scratch=[pltpu.VMEM((count, D), wide_type)],
    )(
        flat,
        vectors,
        early,
        d_keyed,
        d_resid,
        out_sum,
        out_other,
        w_kv,
        d_features,
        d_vectors_two,
    )
    tiny_other = flip(tiny, 1)
    mlp_blocks = join_parts([mlp_grads[0], *mlp_joined])
    received, tiny_other, mlp_blocks = lax.optimization_barrier((received, tiny_other, mlp_blocks))
    in_grads = call(
        in_grads_kernel,
        7,
        piece(D + shard_count * TINY_TILE),
        scalar_first(6) + anywhere[:4],
        [
            pltpu.VMEM((4, D, count), low_type),
            pltpu.VMEM((count, CHUNK), low_type),
            pltpu.VMEM((D + shard_count * TINY_TILE, CHUNK), low_type),
            pltpu.SemaphoreType.DMA((4,)),
        ],
    )(
        spot,
        d_queries,
        d_keyed,
        d_resid_low,
        received,
        tiny,
        tiny_other,
        normed_t,
        normed_other_t,
        attended_t,
        attended_other_t,
    )
    mlp_received = [spin(part, step + 1) for step, part in enumerate(mlp_blocks[1:])]
    in_upper, in_lower, mlp_received[:1] = lax.optimization_barrier(
        (in_grads[3], in_grads[4], mlp_received[:1])
    )
    in_to_x, in_to_y = flip(in_upper, 4), flip(in_lower, 2)
    in_to_x, in_to_y, mlp_received[2:] = lax.optimization_barrier(
        (in_to_x, in_to_y, mlp_received[2:])
    )
    in_sides = add_sides(in_grads, in_to_x, in_to_y)
    in_joined = [flip(in_sides[0], 2), flip(in_sides[1], 4)]
    in_joined, mlp_received = lax.optimization_barrier((in_joined, mlp_received))
    in_blocks = join_parts([in_grads[0], *in_joined])
    in_received = [spin(part, step + 1) for step, part in enumerate(in_blocks[1:])]
    in_blocks, mlp_received = lax.optimization_barrier((in_blocks, mlp_received))
    mlp_total = settle(mlp_blocks[0], mlp_received, 10)
    mlp_flips = share_flips(mlp_total)
    in_received, _ = lax.optimization_barrier((in_received, mlp_total))
    in_received[:1], mlp_flips[:2] = lax.optimization_barrier((in_received[:1], mlp_flips[:2]))
    mlp_sums = share_pair(mlp_flips)
    in_flips = share_flips(settle(in_blocks[0], in_received))
    grad_up, grad_down = call(
        lay_mlp_kernel,
        3,
        (whole((rows, 4 * D), wide_type), whole((PIECES, fine, D), wide_type)),
        scalar_first(2),
        [pltpu.VMEM((PIECES, rows, CHUNK), low_type)],
    )(spot, *mlp_sums)
    grad_down = grad_down.reshape(-1, D)
    in_flips, grad_up, grad_down = lax.optimization_barrier((in_flips, grad_up, grad_down))
    in_sums = share_pair(in_flips)
    grad_qkv, grad_out, grad_feature, d_vectors = call(
        lay_in_kernel,
        2,
        (
            whole((rows, 3 * D), wide_type),
            whole((rows, D), wide_type),
            whole((rows, FEAT), wide_type),
            whole((8, FEAT), wide_type),
        ),
        scalar_first(2),
    )(spot, *in_sums)
    d_vectors = d_vectors.reshape(4, 2 * FEAT)[:, :rows]
    return (
        block_out.reshape(tokens.shape),
        grad_tokens.reshape(tokens.shape),
        d_vectors[0],
        d_vectors[1],
        grad_qkv,
        grad_feature,
        grad_out,
        d_vectors[2],
        d_vectors[3],
        grad_up,
        grad_down,
    )


def solution(mesh):
    placed = (
        P("rep", "shard", None),
        P("shard"),
        P("shard"),
        P("shard", None),
        P("shard", None),
        P("shard", None),
        P("shard"),
        P("shard"),
        P("shard", None),
        P("shard", None),
        P("rep", "shard", None),
    )
    return jax.shard_map(
        shards,
        mesh=mesh,
        in_specs=placed,
        out_specs=(
            P("rep", "shard", None),
            P("rep", "shard", None),
            P("shard"),
            P("shard"),
            P("shard", None),
            P("shard", None),
            P("shard", None),
            P("shard"),
            P("shard"),
            P("shard", None),
            P("shard", None),
        ),
        check_vma=False,
    )
```

```python
import jax
import jax.numpy as jnp
from jax import lax
from jax.experimental import pallas as pl
from jax.experimental.pallas import tpu as pltpu
from jax.sharding import PartitionSpec as P

D = 768
HEADS = 12
HEAD = 64
FEAT = 128
PAIRS = HEADS // 2
GROUP = 4 * HEAD
PIECES = 8
CHUNK = 4 * D // PIECES
QKV_BLOCKS = 3 * D // CHUNK
EDGE = 16
SLAB = PAIRS * FEAT + 2 * EDGE

norm_epsilon = 1e-05
low_type = jnp.bfloat16
wide_type = jnp.float32


def flip(value, bit):
    count = lax.axis_size("rep")
    return lax.ppermute(value, "rep", [(i, i ^ bit) for i in range(count)])


def spin(value, step):
    count = lax.axis_size("shard")
    return lax.ppermute(value, "shard", [(i, (i + step) % count) for i in range(count)])


def slide(value, step):
    count = lax.axis_size("shard")
    pairs = [(i, i + step) for i in range(count) if 0 <= i + step < count]
    return lax.ppermute(value, "shard", pairs)


def wide(value):
    return value.astype(wide_type)


def low(value):
    return value.astype(low_type)


def place_kernel(slots, *refs):
    parts, full = refs[:-1], refs[-1]
    for i, part in enumerate(parts):
        size = part.shape[0]
        full[pl.ds(slots[i] * size, size)] = part[...]


def place_parts(parts, slots):
    shape = (len(parts) * parts[0].shape[0],) + parts[0].shape[1:]
    slots = jnp.stack([jnp.asarray(slot, jnp.int32) for slot in slots])
    return call(place_kernel, 1, whole(shape, parts[0].dtype), scalar_first(len(parts)))(
        slots, *parts
    )


def around_parts(part):
    count, here = lax.axis_size("shard"), lax.axis_index("shard")
    parts = [part[None]] + [spin(part, step)[None] for step in range(1, count)]
    return parts, [(here - step) % count for step in range(count)]


def around(part):
    return place_parts(*around_parts(part))


def scan_first(state, direction):
    received = slide(state, direction)
    return received, low(wide(state) + wide(received))


def scan_rest(received, running, direction):
    found, step = [received], 2
    while step < lax.axis_size("shard"):
        found.append(slide(running, direction * step))
        running = low(wide(running) + wide(found[-1]))
        step *= 2
    return found


def sides_of(own):
    return flip(own, 2), flip(own, 4)


def halves_of(from_x, from_y):
    half = from_x.shape[0] // 2
    return from_x[:half], from_y[half:]


def diagonal_of(halves):
    return jnp.concatenate([flip(halves[0], 4), flip(halves[1], 2)], axis=0)


def share_flips(own):
    return [own[None]] + [flip(own, bit)[None] for bit in (2, 4, 6)]


def share_pair(parts):
    even = place_parts(parts, [0, 1, 2, 3])
    return even, flip(even, 1)


def sides_kernel(x_part, y_part, to_x, to_y, x_sum, y_sum):
    half = to_x.shape[0]
    x_sum[:half] = low(wide(x_part[:half]) + wide(to_x[...]))
    x_sum[half:] = x_part[half:]
    y_sum[:half] = y_part[:half]
    y_sum[half:] = low(wide(y_part[half:]) + wide(to_y[...]))


def join_parts(parts):
    count, here = lax.axis_size("shard"), lax.axis_index("shard")
    bit = PIECES
    if bit < lax.axis_size("rep"):
        mine = sum(wide(part) for part in parts)
        while bit < lax.axis_size("rep"):
            mine = mine + wide(flip(low(mine), bit))
            bit *= 2
        parts = [mine]
    rows, columns = parts[0].shape
    rows //= count

    def kernel(spot, *refs):
        sources, outs = refs[: len(parts)], refs[len(parts) :]
        for step in range(count):
            block = lax.rem(spot[0] + step, count)
            chosen = pl.ds(pl.multiple_of(block * rows, rows), rows)
            total = wide(sources[0][chosen, :])
            for source in sources[1:]:
                total = total + wide(source[chosen, :])
            outs[step][...] = total if step == 0 else low(total)

    shapes = [whole((rows, columns), wide_type)] + [whole((rows, columns))] * (count - 1)
    return call(kernel, 2, tuple(shapes), scalar_first(len(parts)))(
        here.reshape(1).astype(jnp.int32), *parts
    )


def settle(own, received, weight=1):
    def kernel(own, *refs):
        total = own[...]
        for ref in refs[:-1]:
            total = total + wide(ref[...])
        refs[-1][...] = low(total)

    return call(kernel, weight, whole(own.shape))(own, *received)


def dot(a, b):
    return jnp.dot(a, b, preferred_element_type=wide_type)


def dot_nt(a, b):
    return lax.dot_general(a, b, (((1,), (1,)), ((), ())), preferred_element_type=wide_type)


def dot_tn(a, b):
    return lax.dot_general(a, b, (((0,), (0,)), ((), ())), preferred_element_type=wide_type)


def normalize(rows):
    centred = rows - jnp.mean(rows, axis=-1, keepdims=True)
    scale = lax.rsqrt(jnp.mean(centred * centred, axis=-1, keepdims=True) + norm_epsilon)
    return centred * scale, scale


def norm_backward(grad, normal, scale, gain):
    e = grad * gain
    return scale * (
        e
        - jnp.mean(e, axis=-1, keepdims=True)
        - normal * jnp.mean(e * normal, axis=-1, keepdims=True)
    )


def lane_index(shape):
    return lax.broadcasted_iota(jnp.int32, shape, len(shape) - 1)


def row_index(shape):
    return lax.broadcasted_iota(jnp.int32, shape, len(shape) - 2)


def left_half(shape):
    return lane_index(shape) < HEAD


def aligned(index, unit):
    return pl.multiple_of(index * unit, unit)


def with_ones(pair):
    left = left_half(pair.shape)
    one = jnp.ones_like(pair)
    return jnp.where(left, pair, one), jnp.where(left, one, pair)


def pack_state(even, odd, p):
    lane = lane_index(even.shape)
    packed = jnp.where(lane < HEAD, even, odd)
    sums = jnp.where(lane == HEAD + 2 * p, even, jnp.where(lane == 2 * p + 1, odd, 0.0))
    return packed, sums


def unpack_state(packed, sums, p):
    shape = packed.shape
    lane, row = lane_index(shape), row_index(shape)
    pick_even = low(jnp.where((row == HEAD + 2 * p) & (lane >= HEAD), 1.0, 0.0))
    pick_odd = low(jnp.where((row == 2 * p + 1) & (lane < HEAD), 1.0, 0.0))
    even = jnp.where(lane < HEAD, packed, dot(sums, pick_even))
    odd = jnp.where(lane < HEAD, dot(sums, pick_odd), packed)
    return low(even), low(odd)


def added(refs, b, rows):
    total = wide(refs[0][b, rows, :])
    for ref in refs[1:]:
        total = total + wide(ref[b, rows, :])
    return total


def sums_of(refs):
    found = []
    gap = jnp.zeros((HEAD - EDGE, FEAT), wide_type)
    for b in range(refs[0].shape[0]):
        edges = added(refs, b, slice(PAIRS * FEAT, SLAB))
        found.append(low(jnp.concatenate([edges[:EDGE], gap, edges[EDGE:], gap], axis=0).T))
    return found


def states_at(refs, b, p, sums):
    return unpack_state(added(refs, b, pair_at(p)), sums[b], p)


def maps_kernel(small, maps, vectors, weight):
    shard_count, size, _ = small.shape
    rows = D // shard_count
    lines = 4 * rows // FEAT
    for s in range(shard_count):
        for j in range(3):
            count = min(size, rows - j * size)
            if count > 0:
                weight[s * rows + j * size : s * rows + j * size + count, :] = wide(
                    small[s, :count, j * FEAT : (j + 1) * FEAT]
                )
        flat = []
        for line in range(rows, rows + lines):
            j, row = line // size, line % size
            flat.append(wide(small[s, row : row + 1, j * FEAT : (j + 1) * FEAT]))
        flat = jnp.concatenate(flat, axis=1)
        for v in range(4):
            vectors[v : v + 1, s * rows : (s + 1) * rows] = flat[:, v * rows : (v + 1) * rows]
    gap = jnp.zeros((HEAD, HEAD), low_type)
    for head in range(HEADS):
        turned = low(weight[head * HEAD : (head + 1) * HEAD, :].T)
        g, a = head // 4, head % 4
        for which in range(2):
            block = turned[which * HEAD : (which + 1) * HEAD]
            maps[which * (D // GROUP) + g, a * HEAD : (a + 1) * HEAD, :] = jnp.concatenate(
                [block if a == b else gap for b in range(4)], axis=1
            )


def features(maps, base, columns, f_t, f):
    def group(g, carry):
        u_t = dot_nt(maps[base + g], columns[:, pl.ds(aligned(g, GROUP), GROUP)])
        for a in range(4):
            u = u_t[a * HEAD : (a + 1) * HEAD]
            up = jnp.exp(u - jnp.max(u, axis=0, keepdims=True))
            down = jnp.exp(jnp.min(u, axis=0, keepdims=True) - u)
            plus = up / jnp.sum(up, axis=0, keepdims=True)
            minus = down / jnp.sum(down, axis=0, keepdims=True)
            feature = low(jnp.concatenate([plus, minus], axis=0))
            rows = pl.ds(aligned(g * 4 + a, FEAT), FEAT)
            f_t[rows, :] = feature
            f[:, rows] = feature.T
        return carry

    lax.fori_loop(0, D // GROUP, group, 0)


def wanted(place, k, first, last):
    block = place[0] ^ k
    return block, (block >= first) & (block < last)


def each_piece(place, pieces, first, last, work):
    for k in range(PIECES):
        block, use = wanted(place, k, first, last)

        @pl.when(use)
        def _():
            work(block - first, pieces[k])


def chunk_at(index):
    return pl.ds(aligned(index, CHUNK), CHUNK)


def pair_at(index):
    return pl.ds(aligned(index, FEAT), FEAT)


VALUES = D // FEAT
QUERY_BLOCKS = D // CHUNK


def copy_rows(source, target):
    def step(i, carry):
        rows = pl.ds(aligned(i, 2 * HEAD), 2 * HEAD)
        target[rows, :] = source[rows, :]
        return carry

    lax.fori_loop(0, source.shape[0] // (2 * HEAD), step, 0)


def keys_kernel(place, tokens, vectors, maps, *refs):
    pieces = refs[:PIECES]
    normed, keyed, fk, fk_t, state, w_kv = refs[PIECES:]
    seqs = state.shape[0]
    length = tokens.shape[0] // seqs
    normal, _ = normalize(wide(tokens[...]))
    normed[...] = low(normal * vectors[0:1, :] + vectors[1:2, :])

    def keep(index, weight):
        copy_rows(weight, w_kv.at[index])

    each_piece(place, pieces, QUERY_BLOCKS, QKV_BLOCKS, keep)

    def project(index, carry):
        keyed[:, chunk_at(index)] = low(dot(normed[...], w_kv[index]))
        return carry

    lax.fori_loop(0, QKV_BLOCKS - QUERY_BLOCKS, project, 0)
    features(maps, D // GROUP, keyed, fk_t, fk)
    state_sums(state, length, lambda p, here: with_ones(keyed[here, pair_at(VALUES + p)]), fk_t)


def state_sums(state, length, sides, f_t):
    seqs = state.shape[0]

    def pair(p, sums):
        result = []
        for b in range(seqs):
            here = slice(b * length, (b + 1) * length)
            first, second = sides(p, here)
            even = dot(f_t[pair_at(2 * p), here], first)
            odd = dot(f_t[pair_at(2 * p + 1), here], second)
            packed, new = pack_state(even, odd, p)
            state[b, pair_at(p), :] = low(packed)
            result.append(sums[b] + new)
        return tuple(result)

    empty = tuple(jnp.zeros((FEAT, FEAT), wide_type) for _ in range(seqs))
    sums = lax.fori_loop(0, PAIRS, pair, empty)
    for b in range(seqs):
        turned = low(sums[b].T)
        state[b, PAIRS * FEAT : PAIRS * FEAT + EDGE, :] = turned[:EDGE]
        state[b, PAIRS * FEAT + EDGE :, :] = turned[HEAD : HEAD + EDGE]


def queries_kernel(place, normed, keyed, fk_t, maps, *refs):
    pieces = refs[:PIECES]
    normed_t, queries, fq, fq_t, partial, w_out, w_q = refs[PIECES:]

    def keep(index, weight):
        copy_rows(weight, w_q.at[index])

    def keep_out(index, weight):
        copy_rows(weight, w_out.at[:, chunk_at(index)])

    each_piece(place, pieces, 0, QUERY_BLOCKS, keep)
    each_piece(place, pieces, QKV_BLOCKS, PIECES, keep_out)

    def project(index, carry):
        queries[:, chunk_at(index)] = low(dot(normed[...], w_q[index]))
        return carry

    lax.fori_loop(0, QUERY_BLOCKS, project, 0)
    normed_t[...] = normed[...].T
    features(maps, 0, queries, fq_t, fq)
    seqs, length, _ = partial.shape

    def pair(p, carry):
        for b in range(seqs):
            here = slice(b * length, (b + 1) * length)
            values = with_ones(keyed[here, pair_at(VALUES + p)])
            for side in range(2):
                rows = pair_at(2 * p + side)
                scores = dot(fq[here, rows], fk_t[rows, here])
                scores = jnp.where(row_index(scores.shape) >= lane_index(scores.shape), scores, 0.0)
                partial[b, :, rows] = dot(low(scores), values[side])
        return carry

    lax.fori_loop(0, PAIRS, pair, 0)


def attend_kernel(tokens, vectors, partial, fq, w_out, *refs):
    priors, (attended, inverse, resid, second, second_t) = refs[:-5], refs[-5:]
    seqs = priors[0].shape[0]
    length = tokens.shape[0] // seqs

    sums = sums_of(priors)

    def pair(p, carry):
        for b in range(seqs):
            here = slice(b * length, (b + 1) * length)
            states = states_at(priors, b, p, sums)
            found = []
            for side in range(2):
                rows = pair_at(2 * p + side)
                found.append(partial[b, :, rows] + dot(fq[here, rows], states[side]))
            left = left_half(found[0].shape)
            turned = [pltpu.roll(a, HEAD, 1) for a in found]
            over = 1.0 / jnp.where(left, turned[0], turned[1])
            attended[here, pair_at(p)] = low(jnp.where(left, found[0], found[1]) * over)
            inverse[here, pair_at(p)] = over
        return carry

    lax.fori_loop(0, PAIRS, pair, 0)
    resid[...] = wide(tokens[...]) + dot(attended[...], w_out[...])
    normal, _ = normalize(resid[...])
    second[...] = low(normal * vectors[2:3, :] + vectors[3:4, :])
    second_t[...] = second[...].T


def mlp_kernel(second, second_other, cotangent, cotangent_other, resid, attended, *refs):
    pieces = refs[:4]
    out_sum, out_send, back_sum, back_send, hiddens, d_pres, second_other_t, attended_t = refs[4:12]
    up, down, ready = refs[12:]
    count = second.shape[0]
    parts = grads_layout(second.shape[1], pieces[0].shape[0])

    def copies(k, source):
        listed = []
        for i, (src, dst) in enumerate(parts):
            if dst[0] == "up":
                target = up.at[pl.ds(dst[1], dst[2]), chunk_at(k)]
            else:
                start = pl.multiple_of(k * CHUNK + dst[1], dst[2])
                target = down.at[pl.ds(start, dst[2]), pl.ds(dst[3], CHUNK)]
            listed.append(
                pltpu.make_async_copy(source.at[pl.ds(src, dst[2]), :], target, ready.at[k, i])
            )
        return listed

    for k in range(4):
        for copy in copies(k, pieces[k]):
            copy.start()
    second_other_t[...] = second_other[...].T
    attended_t[...] = attended[...].T

    def piece(k, carry):
        for copy in copies(k, pieces[0]):
            copy.wait()
        columns = chunk_at(k)
        for side, (source, grad) in enumerate(
            ((second, cotangent), (second_other, cotangent_other))
        ):
            here = slice(side * count, (side + 1) * count)
            pre = dot(source[...], up[:, columns])
            square = pre * pre
            bent = jnp.tanh(pre * (0.7978845608 + (0.7978845608 * 0.044715) * square))
            half = 0.5 + 0.5 * bent
            slope = half + (half * (1.0 - bent)) * pre * (
                0.7978845608 + (3.0 * 0.7978845608 * 0.044715) * square
            )
            hiddens[here, columns] = low(pre * half)
            d_pres[here, columns] = low(dot_nt(grad[...], down[columns, :]) * slope)
        return carry

    lax.fori_loop(0, 4, piece, 0)
    tile = count // 2

    def own(i, carry):
        here = pl.ds(aligned(i, tile), tile)
        back_sum[here, :] = dot_nt(d_pres[here, :], up[...])
        out_sum[here, :] = resid[here, :] + dot(hiddens[here, :], down[...])
        return carry

    def other(i, carry):
        here, there = pl.ds(aligned(i, tile), tile), pl.ds(aligned(i + 2, tile), tile)
        back_send[here, :] = low(dot_nt(d_pres[there, :], up[...]))
        out_send[here, :] = low(dot(hiddens[there, :], down[...]))
        return carry

    lax.fori_loop(0, 2, own, 0)
    lax.fori_loop(0, 2, other, 0)


def store_piece(outs, made, k):
    half = outs[3].shape[0]
    for i in range(3):

        @pl.when(k == i)
        def _():
            outs[i][...] = made[...]

    @pl.when(k == 3)
    def _():
        outs[3][...] = made[:half]
        outs[4][...] = made[half:]


def mlp_grads_kernel(second_t, second_other_t, cotangent, cotangent_other, hiddens, d_pres, *refs):
    outs, made = refs[:5], refs[5]
    count = cotangent.shape[0]
    own, other = slice(0, count), slice(count, 2 * count)

    def piece(k, carry):
        columns = chunk_at(k)
        d_up = dot(second_t[...], d_pres[own, columns])
        d_up = d_up + dot(second_other_t[...], d_pres[other, columns])
        d_down = dot_tn(hiddens[own, columns], cotangent[...])
        d_down = d_down + dot_tn(hiddens[other, columns], cotangent_other[...])
        d_up, d_down = low(d_up), low(d_down)
        for src, dst in grads_layout(second_t.shape[0], made.shape[0]):
            rows = slice(dst[1], dst[1] + dst[2])
            if dst[0] == "up":
                made[src : src + dst[2], :] = d_up[rows]
            else:
                made[src : src + dst[2], :] = d_down[rows, dst[3] : dst[3] + CHUNK]
        store_piece(outs, made, k)
        return carry

    lax.fori_loop(0, 4, piece, 0)


def grads_layout(width, block):
    shards = block // CHUNK
    up_rows = width // shards
    down_rows = CHUNK // shards
    parts = []
    for s in range(shards):
        base = s * (up_rows + 2 * down_rows)
        parts.append((base, ("up", s * up_rows, up_rows)))
        for side in range(2):
            parts.append(
                (
                    base + up_rows + side * down_rows,
                    ("down", s * down_rows, down_rows, side * CHUNK),
                )
            )
    return parts


def resid_kernel(back_sum, back_other, resid, cotangent, vectors, w_out, attended, inverse, fq_t, *refs):
    d_resid, d_resid_low, d_vectors, d_num, d_den, state = refs
    seqs = state.shape[0]
    length = resid.shape[0] // seqs
    normal, scale = normalize(resid[...])
    grad = back_sum[...] + wide(back_other[...])
    d_vectors[0:1, :] = jnp.sum(grad * normal, axis=0, keepdims=True)
    d_vectors[1:2, :] = jnp.sum(grad, axis=0, keepdims=True)
    d_resid[...] = wide(cotangent[...]) + norm_backward(grad, normal, scale, vectors[2:3, :])
    d_resid_low[...] = low(d_resid[...])
    d_attended = dot_nt(d_resid_low[...], w_out[...])
    shape = (FEAT, FEAT)
    cross = low(
        jnp.where(left_half(shape) != (row_index(shape) < HEAD), -1.0 / HEAD, 0.0)
    )
    for p in range(PAIRS):
        columns = slice(p * FEAT, (p + 1) * FEAT)
        num = d_attended[:, columns] * inverse[:, columns]
        product = num * wide(attended[:, columns])
        top = low(product)
        rest = low(product - wide(top))
        d_num[:, columns] = low(num)
        d_den[:, columns] = low(dot(top, cross) + dot(rest, cross))

    state_sums(state, length, lambda p, here: joined(d_num, d_den, here, p), fq_t)


def joined(d_num, d_den, here, p):
    columns = pl.ds(aligned(p, FEAT), FEAT)
    num, den = d_num[here, columns], d_den[here, columns]
    left = left_half(num.shape)
    return jnp.where(left, num, den), jnp.where(left, den, num)


def softmax_backward(feature, grad):
    plus, minus = wide(feature[:HEAD]), wide(feature[HEAD:])
    d_plus, d_minus = grad[:HEAD], grad[HEAD:]
    d_plus = plus * (d_plus - jnp.sum(d_plus * plus, axis=0, keepdims=True))
    d_minus = minus * (d_minus - jnp.sum(d_minus * minus, axis=0, keepdims=True))
    return low(d_plus - d_minus)


def linked(outer, value):
    link = dot_nt(outer, value)
    return low(jnp.where(row_index(link.shape) >= lane_index(link.shape), link, 0.0))


def local_queries_kernel(queries, keyed, maps, fq_t, fk_t, d_num, d_den, *refs):
    priors, (d_queries, d_features, d_uq_t) = refs[:-3], refs[-3:]
    seqs = priors[0].shape[0]
    length = keyed.shape[0] // seqs

    sums = sums_of(priors)

    def pair(p, carry):
        for b in range(seqs):
            here = slice(b * length, (b + 1) * length)
            values = with_ones(keyed[here, pair_at(VALUES + p)])
            outer = joined(d_num, d_den, here, p)
            states = states_at(priors, b, p, sums)
            for side in range(2):
                rows = pair_at(2 * p + side)
                link = linked(outer[side], values[side])
                d_q = dot_nt(fk_t[rows, here], link) + dot_nt(states[side], outer[side])
                d_uq_t[pl.ds(aligned(2 * p + side, HEAD), HEAD), here] = softmax_backward(
                    fq_t[rows, here], d_q
                )
        return carry

    lax.fori_loop(0, PAIRS, pair, 0)
    feature_backward(d_uq_t, queries, maps, 0, d_queries, d_features, 0)


def local_keys_kernel(keyed, fq_t, fk, d_num, d_den, d_fk_t, d_values, *, seqs):
    length = keyed.shape[0] // seqs

    def pair(p, carry):
        for b in range(seqs):
            here = slice(b * length, (b + 1) * length)
            values = with_ones(keyed[here, pair_at(VALUES + p)])
            outer = joined(d_num, d_den, here, p)
            found = []
            for side in range(2):
                rows = pair_at(2 * p + side)
                q_t = fq_t[rows, here]
                d_fk_t[rows, here] = dot(q_t, linked(outer[side], values[side]))
                scores = dot(fk[here, rows], q_t)
                row, lane = row_index(scores.shape), lane_index(scores.shape)
                found.append(dot(low(jnp.where(row <= lane, scores, 0.0)), outer[side]))
            left = left_half(found[0].shape)
            d_values[here, pair_at(p)] = jnp.where(left, found[0], found[1])
        return carry

    lax.fori_loop(0, PAIRS, pair, 0)


def feature_backward(d_u_t, source, maps, base, target, d_features, lane):
    def group(g, carry):
        d_u = d_u_t[pl.ds(aligned(g, GROUP), GROUP), :]
        columns = pl.ds(aligned(g, GROUP), GROUP)
        product = dot(d_u, source[:, columns]).T
        for a in range(4):
            block = slice(a * HEAD, (a + 1) * HEAD)
            rows = pl.ds(aligned(g * 4 + a, HEAD), HEAD)
            d_features[rows, lane : lane + HEAD] = product[block, block]
        target[:, columns] = low(dot(d_u.T, maps[base + g]))
        return carry

    lax.fori_loop(0, D // GROUP, group, 0)


def mixed_kernel(
    place, keyed, fk, fk_t, maps, d_fk_t, d_values, d_resid_low, d_queries, d_half, *refs
):
    laters, (d_keyed, d_features, sends, d_uk_t) = refs[:-4], refs[-4:]
    seqs = laters[0].shape[0]
    length = keyed.shape[0] // seqs

    sums = sums_of(laters)

    def pair(p, carry):
        for b in range(seqs):
            here = slice(b * length, (b + 1) * length)
            values = with_ones(keyed[here, pair_at(VALUES + p)])
            states = states_at(laters, b, p, sums)
            found = []
            for side in range(2):
                rows = pl.ds(aligned(2 * p + side, FEAT), FEAT)
                d_k = d_fk_t[rows, here] + dot_nt(states[side], values[side])
                d_uk_t[pl.ds(aligned(2 * p + side, HEAD), HEAD), here] = softmax_backward(
                    fk_t[rows, here], d_k
                )
                found.append(dot(fk[here, rows], states[side]))
            left = left_half(found[0].shape)
            total = d_values[here, pl.ds(aligned(p, FEAT), FEAT)] + jnp.where(
                left, found[0], found[1]
            )
            d_keyed[here, pair_at(VALUES + p)] = low(total)
        return carry

    lax.fori_loop(0, PAIRS, pair, 0)
    feature_backward(d_uk_t, keyed, maps, D // GROUP, d_keyed, d_features, HEAD)
    d_features[:, :HEAD] = d_half[:, :HEAD]

    def send(i, carry):
        own_column(place[0] ^ (2 * i + 1), sends.at[i], d_queries, d_keyed, d_resid_low)
        return carry

    lax.fori_loop(0, PIECES // 2, send, 0)


def own_column(block, target, d_queries, d_keyed, d_resid_low):
    @pl.when(block < QUERY_BLOCKS)
    def _():
        target[...] = d_queries[:, chunk_at(block)]

    @pl.when((block >= QUERY_BLOCKS) & (block < QKV_BLOCKS))
    def _():
        target[...] = d_keyed[:, chunk_at(block - QUERY_BLOCKS)]

    @pl.when(block >= QKV_BLOCKS)
    def _():
        target[...] = d_resid_low[:, chunk_at(block - QKV_BLOCKS)]


TINY_ROWS = 48
TINY_TILE = 16


def tiny_size(rows):
    return -(-(rows + 8) // TINY_ROWS) * TINY_ROWS


def in_grads_kernel(
    place, d_queries, d_keyed, d_resid_low, received, tiny, tiny_other, *refs
):
    sources, outs, (held, column, made, ready) = refs[:4], refs[4:9], refs[9:]
    shard_count, size, _ = tiny.shape
    rows = D // shard_count
    copies = [
        pltpu.make_async_copy(source, held.at[i], ready.at[i]) for i, source in enumerate(sources)
    ]
    for copy in copies:
        copy.start()
    for copy in copies:
        copy.wait()

    def piece(i, carry):
        block = place[0] ^ (2 * i)
        kind = 2 * jnp.where(block < QKV_BLOCKS, 0, 1)
        own_column(block, column, d_queries, d_keyed, d_resid_low)
        value = low(dot(held[kind], column[...]) + dot(held[kind + 1], received[i]))
        for s in range(shard_count):
            base = s * (rows + TINY_TILE)
            made[base : base + rows, :] = value[s * rows : (s + 1) * rows]
            for j in range(TINY_ROWS // TINY_TILE):
                target = (slice(base + rows, base + rows + TINY_TILE), slice(j * FEAT, (j + 1) * FEAT))
                made[target] = jnp.zeros((TINY_TILE, FEAT), low_type)

                @pl.when(block < size // TINY_ROWS)
                def _():
                    start = pl.multiple_of(block * TINY_ROWS + j * TINY_TILE, TINY_TILE)
                    spot = pl.ds(start, TINY_TILE)
                    made[target] = low(wide(tiny[s, spot, :]) + wide(tiny_other[s, spot, :]))

        store_piece(outs, made, i)
        return carry

    lax.fori_loop(0, PIECES // 2, piece, 0)


def early_kernel(d_queries, w_q, total):
    total[...] = jnp.zeros_like(total)
    add_products(total, d_queries, w_q)


def add_products(total, source, weights):
    def add(index, carry):
        total[...] += dot_nt(source[:, chunk_at(index)], weights[index])
        return carry

    lax.fori_loop(0, weights.shape[0], add, 0)


def input_kernel(tokens, vectors, early, d_keyed, d_resid, out_sum, out_other, *refs):
    w_kv, d_features, d_vectors, block_out, grad_tokens, tiny, total = refs
    total[...] = early[...]
    block_out[...] = low(out_sum[...] + wide(out_other[...]))

    add_products(total, d_keyed, w_kv)
    normal, scale = normalize(wide(tokens[...]))
    grad = total[...]
    grad_tokens[...] = low(d_resid[...] + norm_backward(grad, normal, scale, vectors[0:1, :]))
    gathered = [
        jnp.sum(grad * normal, axis=0, keepdims=True),
        jnp.sum(grad, axis=0, keepdims=True),
        d_vectors[0:1, :],
        d_vectors[1:2, :],
    ]
    shard_count, size, _ = tiny.shape
    rows = D // shard_count
    tiny[...] = jnp.zeros_like(tiny)
    for s in range(shard_count):
        tiny[s, :rows, :] = low(d_features[s * rows : (s + 1) * rows, :])
        lines = []
        for vector in gathered:
            line = vector[:, s * rows : (s + 1) * rows]
            gap = jnp.zeros((1, 2 * FEAT - rows), wide_type)
            line = jnp.concatenate([line, gap], axis=1)
            lines += [line[:, :FEAT], line[:, FEAT:]]
        tiny[s, rows : rows + 8, :] = low(jnp.concatenate(lines, axis=0))


def lay_in_kernel(place, even, odd, qkv, out, feature, rest):
    rows = qkv.shape[0]
    for k in range(PIECES):
        block = place[0] ^ k
        piece = (even, odd)[k % 2].at[k // 2]

        @pl.when(block < QKV_BLOCKS)
        def _():
            qkv[:, chunk_at(block)] = wide(piece[:rows])

        @pl.when(block >= QKV_BLOCKS)
        def _():
            out[:, chunk_at(block - QKV_BLOCKS)] = wide(piece[:rows])

        for j in range(TINY_ROWS // TINY_TILE):

            @pl.when(block < rows // TINY_ROWS)
            def _():
                start = pl.multiple_of(block * TINY_ROWS + j * TINY_TILE, TINY_TILE)
                feature[pl.ds(start, TINY_TILE), :] = wide(
                    piece[rows:, j * FEAT : (j + 1) * FEAT]
                )

        @pl.when(block == rows // TINY_ROWS)
        def _():
            rest[...] = wide(piece[rows : rows + 8, :FEAT])


def lay_mlp_kernel(place, even, odd, up, down, ordered):
    up_rows, down_rows = ordered.shape[1], down.shape[1]
    for k in range(PIECES):
        block = place[0] ^ k
        piece = (even, odd)[k % 2]
        ordered[block] = piece[k // 2, :up_rows, :]
        for side in range(2):
            start = up_rows + side * down_rows
            down[block, :, side * CHUNK : (side + 1) * CHUNK] = wide(
                piece[k // 2, start : start + down_rows, :]
            )
    for s in range(CHUNK // down_rows):
        columns = slice(s * down_rows, (s + 1) * down_rows)
        row = jnp.concatenate([ordered[r][:, columns] for r in range(PIECES)], axis=1)
        up[:, s * PIECES * down_rows : (s + 1) * PIECES * down_rows] = wide(row)


def whole(shape, dtype=low_type):
    return jax.ShapeDtypeStruct(shape, dtype)


def scalar_first(count):
    return [pl.BlockSpec(memory_space=pltpu.SMEM)] + [
        pl.BlockSpec(memory_space=pltpu.VMEM) for _ in range(count)
    ]


def call(kernel, weight, out_shape, in_specs=None, scratch=(), limit=12, **rest):
    if in_specs is not None:
        rest["in_specs"] = in_specs
    return pl.pallas_call(
        kernel,
        out_shape=out_shape,
        scratch_shapes=list(scratch),
        compiler_params=pltpu.CompilerParams(vmem_limit_bytes=limit << 20),
        cost_estimate=pl.CostEstimate(
            flops=int(weight * 2000 * 10**6), transcendentals=0, bytes_accessed=int(weight * 6 * 10**6)
        ),
        **rest,
    )


def interleave(even, odd):
    return [part for both in zip(even, odd) for part in both]


def shards(
    tokens,
    gain_attn,
    bias_attn,
    w_qkv,
    w_feature,
    w_out,
    gain_mlp,
    bias_mlp,
    w_up,
    w_down,
    cotangent,
):
    shard_count = lax.axis_size("shard")
    place = lax.axis_index("rep") % PIECES
    spot = place.reshape(1).astype(jnp.int32)
    seqs, length, _ = tokens.shape
    count = seqs * length
    rows = w_qkv.shape[0]
    fine = CHUNK // shard_count
    flat = tokens.reshape(count, D)
    flat_cotangent = cotangent.reshape(count, D)
    anywhere = [pl.BlockSpec(memory_space=pl.ANY)] * PIECES

    part_in = lax.dynamic_slice_in_dim(
        jnp.concatenate([w_qkv, w_out], axis=1), place * CHUNK, CHUNK, 1
    )
    vectors = jnp.concatenate([gain_attn, bias_attn, gain_mlp, bias_mlp]).reshape(-1, FEAT)
    small = jnp.concatenate([w_feature, vectors], axis=0)
    small_rows = -(-small.shape[0] // 24) * 8
    small = jnp.pad(small, ((0, 3 * small_rows - small.shape[0]), (0, 0)))
    small = jnp.concatenate(jnp.split(small, 3, axis=0), axis=1)
    part_in = jnp.concatenate([part_in, small], axis=0)
    part_up = lax.dynamic_index_in_dim(
        w_up.reshape(rows, shard_count, PIECES, fine), place, 2, False
    ).reshape(rows, CHUNK)
    part_down = lax.dynamic_slice_in_dim(w_down, place * fine, fine, 0)
    part_mlp = jnp.concatenate([part_up, part_down[:, :CHUNK], part_down[:, CHUNK:]], axis=0)

    here = lax.axis_index("shard")
    in_slots = jnp.stack([(here - step) % shard_count for step in range(shard_count)])
    in_spins = [part_in] + [spin(part_in, step) for step in range(1, shard_count)]

    def place_in_kernel(slots, *refs):
        parts, (full, rest) = refs[:-2], refs[-2:]
        for i, part in enumerate(parts):
            full[slots[i]] = part[:rows]
            rest[slots[i]] = part[rows:]

    in_full, small = call(
        place_in_kernel,
        1,
        (whole((shard_count, rows, CHUNK)), whole((shard_count, small_rows, CHUNK))),
        scalar_first(shard_count),
    )(in_slots.astype(jnp.int32), *in_spins)
    cotangent_other = flip(flat_cotangent, 1)
    in_full, small = lax.optimization_barrier((in_full, small))
    maps, vectors = call(
        maps_kernel,
        15,
        (whole((2 * D // GROUP, GROUP, GROUP)), whole((4, D), wide_type)),
        scratch=[pltpu.VMEM((D, FEAT), wide_type)],
    )(small)
    in_full = in_full.reshape(-1, CHUNK)
    part_mlp, in_full = lax.optimization_barrier((part_mlp, in_full))
    steps = list(range(1, shard_count))
    from_x, from_y = sides_of(in_full)
    in_other = flip(in_full, 1)
    soon = {step: spin(part_mlp, step) for step in steps[:1] + steps[2:]}
    in_halves, maps, vectors, soon = lax.optimization_barrier(
        (halves_of(from_x, from_y), maps, vectors, soon)
    )
    soon.update({step: spin(soon[1], 1) for step in steps[1:2]})
    diagonal = diagonal_of(in_halves)
    diagonal, soon = lax.optimization_barrier((diagonal, soon))
    in_even = [in_full, from_x, from_y, diagonal]
    in_pieces = interleave(in_even, [in_other] + [flip(part, 1) for part in in_even[1:]])
    here = lax.axis_index("shard")
    mlp_parts = [part_mlp[None]] + [soon[step][None] for step in steps]
    mlp_slots = [(here - step) % shard_count for step in range(shard_count)]

    mlp_full = place_parts(mlp_parts, mlp_slots).reshape(-1, CHUNK)
    mlp_full, vectors = lax.optimization_barrier((mlp_full, vectors))
    normed, keyed, fk, fk_t, key_state, w_kv = call(
        keys_kernel,
        8,
        (
            whole((count, D)),
            whole((count, 2 * D)),
            whole((count, HEADS * FEAT)),
            whole((HEADS * FEAT, count)),
            whole((seqs, SLAB, FEAT)),
            whole((QKV_BLOCKS - QUERY_BLOCKS, D, CHUNK)),
        ),
        scalar_first(3 + PIECES),
    )(spot, flat, vectors, maps, *in_pieces)
    prior, running = scan_first(key_state, 1)
    mlp_x, mlp_y = sides_of(mlp_full)
    normed_t, queries, fq, fq_t, partial, out_weight, w_q = call(
        queries_kernel,
        9,
        (
            whole((D, count)),
            whole((count, D)),
            whole((count, HEADS * FEAT)),
            whole((HEADS * FEAT, count)),
            whole((seqs, length, HEADS * FEAT), wide_type),
            whole((D, D)),
            whole((QUERY_BLOCKS, D, CHUNK)),
        ),
        scalar_first(4 + PIECES),
    )(spot, normed, keyed, fk_t, maps, *in_pieces)
    running, partial = lax.optimization_barrier((running, partial))
    priors = scan_rest(prior, running, 1)
    mlp_halves, partial = lax.optimization_barrier((halves_of(mlp_x, mlp_y), partial))
    mlp_pieces = [mlp_full, mlp_x, mlp_y, diagonal_of(mlp_halves)]
    attended, inverse, resid, second, second_t = call(
        attend_kernel,
        5,
        (
            whole((count, D)),
            whole((count, D), wide_type),
            whole((count, D), wide_type),
            whole((count, D)),
            whole((D, count)),
        ),
    )(flat, vectors, partial, fq, out_weight, *priors)

    second_other = flip(second, 1)
    (
        out_sum,
        out_send,
        back_sum,
        back_send,
        hiddens,
        d_pres,
        second_other_t,
        attended_t,
    ) = call(
        mlp_kernel,
        20,
        (
            whole((count, D), wide_type),
            whole((count, D)),
            whole((count, D), wide_type),
            whole((count, D)),
            whole((2 * count, 4 * CHUNK)),
            whole((2 * count, 4 * CHUNK)),
            whole((D, count)),
            whole((D, count)),
        ),
        [pl.BlockSpec(memory_space=pltpu.VMEM)] * 6 + anywhere[:4],
        [
            pltpu.VMEM((D, 4 * CHUNK), low_type),
            pltpu.VMEM((4 * CHUNK, D), low_type),
            pltpu.SemaphoreType.DMA((4, 3 * shard_count)),
        ],
        limit=18,
    )(second, second_other, flat_cotangent, cotangent_other, resid, attended, *mlp_pieces)
    back_other = flip(back_send, 1)
    out_other = flip(out_send, 1)
    d_resid, d_resid_low, d_vectors_two, d_num, d_den, query_state = call(
        resid_kernel,
        5,
        (
            whole((count, D), wide_type),
            whole((count, D)),
            whole((2, D), wide_type),
            whole((count, D)),
            whole((count, D)),
            whole((seqs, SLAB, FEAT)),
        ),
    )(back_sum, back_other, resid, flat_cotangent, vectors, out_weight, attended, inverse, fq_t)
    later, running = scan_first(query_state, -1)
    normed_other_t = flip(normed_t, 1)
    attended_other_t = flip(attended_t, 1)
    second_t, query_state, normed_other_t, attended_other_t, out_other = lax.optimization_barrier(
        (second_t, query_state, normed_other_t, attended_other_t, out_other)
    )
    piece = lambda rows: tuple(
        whole((size, CHUNK)) for size in (rows, rows, rows, rows // 2, rows // 2)
    )
    mlp_grads = call(
        mlp_grads_kernel, 7, piece(2 * D), scratch=[pltpu.VMEM((2 * D, CHUNK), low_type)]
    )(second_t, second_other_t, flat_cotangent, cotangent_other, hiddens, d_pres)
    mlp_to_x, mlp_to_y = flip(mlp_grads[3], 4), flip(mlp_grads[4], 2)
    running, fk_t = lax.optimization_barrier((running, fk_t))
    laters = scan_rest(later, running, -1)
    d_queries, d_half, _ = call(
        local_queries_kernel,
        6,
        (whole((count, D)), whole((D, FEAT), wide_type), whole((D, count))),
    )(queries, keyed, maps, fq_t, fk_t, d_num, d_den, *priors)
    mlp_to_x, mlp_to_y, d_half = lax.optimization_barrier((mlp_to_x, mlp_to_y, d_half))
    add_sides = lambda parts, to_x, to_y: call(
        sides_kernel, 1, (whole(parts[1].shape), whole(parts[1].shape))
    )(parts[1], parts[2], to_x, to_y)
    mlp_sides = add_sides(mlp_grads, mlp_to_x, mlp_to_y)
    mlp_sides, d_half, fk = lax.optimization_barrier((mlp_sides, d_half, fk))
    d_fk_t, d_values = call(
        lambda *refs: local_keys_kernel(*refs, seqs=seqs),
        5,
        (whole((HEADS * FEAT, count), wide_type), whole((count, D), wide_type)),
    )(keyed, fq_t, fk, d_num, d_den)
    mlp_joined = [flip(mlp_sides[0], 2), flip(mlp_sides[1], 4)]
    early = call(early_kernel, 2, whole((count, D), wide_type))(d_queries, w_q)
    early, d_half = lax.optimization_barrier((early, d_half))
    d_keyed, d_features, sends, _ = call(
        mixed_kernel,
        7,
        (
            whole((count, 2 * D)),
            whole((D, FEAT), wide_type),
            whole((PIECES // 2, count, CHUNK)),
            whole((D, count)),
        ),
        scalar_first(9 + len(laters)),
    )(spot, keyed, fk, fk_t, maps, d_fk_t, d_values, d_resid_low, d_queries, d_half, *laters)
    received = flip(sends, 1)
    block_out, grad_tokens, tiny = call(
        input_kernel,
        7,
        (
            whole((count, D)),
            whole((count, D)),
            whole((shard_count, tiny_size(rows), FEAT)),
        ),
        scratch=[pltpu.VMEM((count, D), wide_type)],
    )(
        flat,
        vectors,
        early,
        d_keyed,
        d_resid,
        out_sum,
        out_other,
        w_kv,
        d_features,
        d_vectors_two,
    )
    tiny_other = flip(tiny, 1)
    mlp_blocks = join_parts([mlp_grads[0], *mlp_joined])
    received, tiny_other, mlp_blocks = lax.optimization_barrier((received, tiny_other, mlp_blocks))
    in_grads = call(
        in_grads_kernel,
        7,
        piece(D + shard_count * TINY_TILE),
        scalar_first(6) + anywhere[:4],
        [
            pltpu.VMEM((4, D, count), low_type),
            pltpu.VMEM((count, CHUNK), low_type),
            pltpu.VMEM((D + shard_count * TINY_TILE, CHUNK), low_type),
            pltpu.SemaphoreType.DMA((4,)),
        ],
    )(
        spot,
        d_queries,
        d_keyed,
        d_resid_low,
        received,
        tiny,
        tiny_other,
        normed_t,
        normed_other_t,
        attended_t,
        attended_other_t,
    )
    mlp_received = [spin(part, step + 1) for step, part in enumerate(mlp_blocks[1:])]
    in_upper, in_lower, mlp_received[:1] = lax.optimization_barrier(
        (in_grads[3], in_grads[4], mlp_received[:1])
    )
    in_to_x, in_to_y = flip(in_upper, 4), flip(in_lower, 2)
    in_to_x, in_to_y, mlp_received[2:] = lax.optimization_barrier(
        (in_to_x, in_to_y, mlp_received[2:])
    )
    in_sides = add_sides(in_grads, in_to_x, in_to_y)
    in_joined = [flip(in_sides[0], 2), flip(in_sides[1], 4)]
    in_joined, mlp_received = lax.optimization_barrier((in_joined, mlp_received))
    in_blocks = join_parts([in_grads[0], *in_joined])
    in_received = [spin(part, step + 1) for step, part in enumerate(in_blocks[1:])]
    in_blocks, mlp_received = lax.optimization_barrier((in_blocks, mlp_received))
    mlp_total = settle(mlp_blocks[0], mlp_received, 10)
    mlp_flips = share_flips(mlp_total)
    in_received, _ = lax.optimization_barrier((in_received, mlp_total))
    in_received[:1], mlp_flips[:2] = lax.optimization_barrier((in_received[:1], mlp_flips[:2]))
    mlp_sums = share_pair(mlp_flips)
    in_flips = share_flips(settle(in_blocks[0], in_received))
    grad_up, grad_down = call(
        lay_mlp_kernel,
        3,
        (whole((rows, 4 * D), wide_type), whole((PIECES, fine, D), wide_type)),
        scalar_first(2),
        [pltpu.VMEM((PIECES, rows, CHUNK), low_type)],
    )(spot, *mlp_sums)
    grad_down = grad_down.reshape(-1, D)
    in_flips, grad_up, grad_down = lax.optimization_barrier((in_flips, grad_up, grad_down))
    in_sums = share_pair(in_flips)
    grad_qkv, grad_out, grad_feature, d_vectors = call(
        lay_in_kernel,
        2,
        (
            whole((rows, 3 * D), wide_type),
            whole((rows, D), wide_type),
            whole((rows, FEAT), wide_type),
            whole((8, FEAT), wide_type),
        ),
        scalar_first(2),
    )(spot, *in_sums)
    d_vectors = d_vectors.reshape(4, 2 * FEAT)[:, :rows]
    return (
        block_out.reshape(tokens.shape),
        grad_tokens.reshape(tokens.shape),
        d_vectors[0],
        d_vectors[1],
        grad_qkv,
        grad_feature,
        grad_out,
        d_vectors[2],
        d_vectors[3],
        grad_up,
        grad_down,
    )


def solution(mesh):
    placed = (
        P("rep", "shard", None),
        P("shard"),
        P("shard"),
        P("shard", None),
        P("shard", None),
        P("shard", None),
        P("shard"),
        P("shard"),
        P("shard", None),
        P("shard", None),
        P("rep", "shard", None),
    )
    return jax.shard_map(
        shards,
        mesh=mesh,
        in_specs=placed,
        out_specs=(
            P("rep", "shard", None),
            P("rep", "shard", None),
            P("shard"),
            P("shard"),
            P("shard", None),
            P("shard", None),
            P("shard", None),
            P("shard"),
            P("shard"),
            P("shard", None),
            P("shard", None),
        ),
        check_vma=False,
    )
```
